32 devices in a mesh: shard: 2 (over y), ctx: 4 (over x, core), tp: 4 (over z).
Axes of the slice: x: 2, y: 2, z: 4, core: 2. Of those that a mesh axis runs over, the one named last changes fastest.
Arguments:
- layer_input: bfloat16 [12, 1024, 768], P('shard', 'ctx'), may hold values from -6 to 6
- segment_ids: int32 [12, 1024], P('shard'), may hold values from 0 to 15, never falling along the last dimension, each value on 1 to 512 neighbouring positions
- query_proj: bfloat16 [768, 768], P('shard', 'tp'), may hold values from -0.21875 to 0.21875
- query_bias: bfloat16 [768], P('tp'), may hold values from -4 to 4
- key_proj: bfloat16 [768, 768], P('shard', 'tp'), may hold values from -0.21875 to 0.21875
- value_proj: bfloat16 [768, 768], P('shard', 'tp'), may hold values from -0.21875 to 0.21875
- value_bias: bfloat16 [768], P('tp'), may hold values from -3 to 3
- out_proj: bfloat16 [768, 768], P('tp', 'shard'), may hold values from -1.5 to 1.5
- out_bias: bfloat16 [768], replicated, may hold values from -3 to 3
- attn_gain: bfloat16 [768], replicated, may hold values from 0.099609375 to 1.8984375
- attn_shift: bfloat16 [768], replicated, may hold values from -3 to 3
- up_proj: bfloat16 [768, 3072], P('shard', 'tp'), may hold values from -0.21875 to 0.21875
- up_bias: bfloat16 [3072], P('tp'), may hold values from -3 to 3
- down_proj: bfloat16 [3072, 768], P('tp', 'shard'), may hold values from -0.109375 to 0.109375
- down_bias: bfloat16 [768], replicated, may hold values from -3 to 3
- ffn_gain: bfloat16 [768], replicated, may hold values from 0.099609375 to 1.8984375
- ffn_shift: bfloat16 [768], replicated, may hold values from -3 to 3
- out_cotangent: bfloat16 [12, 1024, 768], P('shard', 'ctx'), may hold values from -6 to 6
Outputs:
- layer_output: bfloat16 [12, 1024, 768], P('shard', 'ctx')
- input_grad: float32 [12, 1024, 768], P('shard', 'ctx')
- query_proj_grad: float32 [768, 768], P('shard', 'tp')
- query_bias_grad: float32 [768], P('tp')
- key_proj_grad: float32 [768, 768], P('shard', 'tp')
- value_proj_grad: float32 [768, 768], P('shard', 'tp')
- value_bias_grad: float32 [768], P('tp')
- out_proj_grad: float32 [768, 768], P('tp', 'shard')
- out_bias_grad: float32 [768], replicated
- attn_gain_grad: float32 [768], replicated
- attn_shift_grad: float32 [768], replicated
- up_proj_grad: float32 [768, 3072], P('shard', 'tp')
- up_bias_grad: float32 [3072], P('tp')
- down_proj_grad: float32 [3072, 768], P('tp', 'shard')
- down_bias_grad: float32 [768], replicated
- ffn_gain_grad: float32 [768], replicated
- ffn_shift_grad: float32 [768], replicated
The draws below stay inside these ranges and needn't reach their ends.
Inputs may be any that keep to these rules, and one draw needn't show every extreme that they name: `segment_ids`: within a sequence the ids never fall; each of the 16 documents has 1 to 512 tokens, and one has exactly 512.
All inputs are finite; a program needn't handle non-finite values.
Results may differ from the reference program's by a relative error of at most 0.04.
Values may be sent and summed in bfloat16 or wider, within the bound.
No kernel may reach another device: no remote copies, remote signals or barrier semaphores. Data moves between devices by JAX's collectives and lax.ppermute only.
A program may use at most 192 MiB of HBM per device.

```python
import math
import jax
import jax.numpy as jnp
import numpy as np
from jax import lax

D = 768
HEADS = 12
HEAD_DIM = 64
FF = 3072
DOCS = 16
SEQ = 1024
SEQS = 12


def steps_of(rng, shape, shards, least, largest):
    factor_of = 1.0
    for position, shards_of in shards:
        draws = jax.random.uniform(jax.random.fold_in(jax.random.fold_in(rng, 6), position), (shards_of,), jnp.float32, least / len(shards), largest / len(shards))
        factor_of = factor_of * jnp.repeat(jnp.exp(draws), shape[position] // shards_of).reshape((-1,) + (1,) * (len(shape) - 1 - position))
    return factor_of


def length_profile(count, total, most, lean):
    weights = [(1 << 20) // math.isqrt(standing ** lean) + 1 for standing in range(2, count + 1)]
    spare, given = total - most - (count - 1), [1] * (count - 1)
    while spare > 0:
        free = [i for i in range(count - 1) if given[i] < most]
        mass, budget = sum([weights[i] for i in free]), spare
        for i in free:
            extra = min(most - given[i], max(1, budget * weights[i] // mass), spare)
            given[i] = given[i] + extra
            spare = spare - extra
    return np.array([most] + given)


def ragged(rng, amount, total, reach, skew):
    if amount == 2:
        one = jax.random.randint(rng, (), max(1, total - reach), min(reach, total - 1) + 1)
        return jnp.stack([one, total - one])
    lengths = jnp.asarray(length_profile(amount, total, reach, skew), jnp.int32)
    couples = (amount - 1) // 2
    donor, taker = lengths[1:1 + 2 * couples:2], lengths[2:2 + 2 * couples:2]
    room = jnp.minimum(donor - 1, reach - taker)
    shifted = jax.random.randint(jax.random.fold_in(rng, 1), (couples,), 0, 1 << 20) % (room + 1)
    lengths = lengths.at[1:1 + 2 * couples:2].set(donor - shifted).at[2:2 + 2 * couples:2].set(taker + shifted)
    return lengths[jax.random.permutation(jax.random.fold_in(rng, 2), amount)]


def centred(rng, dims, scale, bound, cuts=(), held_as=jnp.bfloat16):
    loudness = steps_of(rng, dims, cuts, -0.22, 0.18) if cuts else 1.0
    values = jax.random.normal(rng, dims, jnp.float32) * scale * loudness
    return jnp.minimum(jnp.maximum(values, -bound), bound).astype(held_as)


def setup_inputs(seed: int = 0) -> dict:
    arg_keys = jax.random.split(jax.random.key(seed), 19)
    layer_input = centred(arg_keys[0], (SEQS, SEQ, D), 1.0, 6.0, ((0, 2), (1, 4)))
    segment_ids = jax.vmap(lambda own: jnp.searchsorted(jnp.cumsum(ragged(own, DOCS, SEQ, SEQ // 2, 2)), jnp.arange(SEQ), side="right"))(jax.random.split(arg_keys[1], SEQS)).reshape((SEQS, SEQ)).astype(jnp.int32)
    query_proj = centred(arg_keys[2], (D, D), D ** -0.5, 0.21875, ((0, 2), (1, 4)))
    query_bias = centred(arg_keys[3], (D,), 1.0, 4.0, ((0, 4),))
    key_proj = centred(arg_keys[4], (D, D), D ** -0.5, 0.21875, ((0, 2), (1, 4)))
    value_proj = centred(arg_keys[5], (D, D), D ** -0.5, 0.21875, ((0, 2), (1, 4)))
    value_bias = centred(arg_keys[6], (D,), 0.5, 3.0, ((0, 4),))
    out_proj = centred(arg_keys[7], (D, D), 16 ** -0.5, 1.5, ((0, 4), (1, 2)))
    out_bias = centred(arg_keys[8], (D,), 0.5, 3.0)
    attn_gain = jnp.clip(1.0 + 0.18 * jax.random.normal(arg_keys[9], (D,), jnp.float32), 0.099609375, 1.8984375).astype(jnp.bfloat16)
    attn_shift = centred(arg_keys[10], (D,), 0.5, 3.0)
    up_proj = centred(arg_keys[11], (D, FF), D ** -0.5, 0.21875, ((0, 2), (1, 4)))
    up_bias = centred(arg_keys[12], (FF,), 0.5, 3.0, ((0, 4),))
    down_proj = centred(arg_keys[13], (FF, D), FF ** -0.5, 0.109375, ((0, 4), (1, 2)))
    down_bias = centred(arg_keys[14], (D,), 0.5, 3.0)
    ffn_gain = jnp.clip(1.0 + 0.18 * jax.random.normal(arg_keys[15], (D,), jnp.float32), 0.099609375, 1.8984375).astype(jnp.bfloat16)
    ffn_shift = centred(arg_keys[16], (D,), 0.5, 3.0)
    out_cotangent = centred(arg_keys[17], (SEQS, SEQ, D), 1.0, 6.0, ((0, 2), (1, 4)))
    return dict(layer_input=layer_input, segment_ids=segment_ids, query_proj=query_proj, query_bias=query_bias, key_proj=key_proj, value_proj=value_proj, value_bias=value_bias, out_proj=out_proj, out_bias=out_bias, attn_gain=attn_gain, attn_shift=attn_shift, up_proj=up_proj, up_bias=up_bias, down_proj=down_proj, down_bias=down_bias, ffn_gain=ffn_gain, ffn_shift=ffn_shift, out_cotangent=out_cotangent)


@jax.custom_vjp
def low(v):
    return lax.optimization_barrier(v.astype(jnp.bfloat16)).astype(jnp.float32)

@jax.custom_vjp
def low_back(v):
    return v

def low_keep(v):
    return (low(v), None)

def low_pass(kept, grad):
    return (grad,)

def back_keep(v):
    return (v, None)

def back_low(kept, grad):
    return (low(grad),)
low.defvjp(low_keep, low_pass)
low_back.defvjp(back_keep, back_low)
eps_norm = 1e-12

def matmul(left, right):
    return jnp.dot(left, right, precision=lax.Precision.HIGHEST, preferred_element_type=jnp.float32)

def norm_rows(resid, norm_gain, norm_shift):
    center = resid - lax.optimization_barrier(jnp.mean(resid, axis=-1, keepdims=True))
    spread = lax.optimization_barrier(jnp.mean(center * center, axis=-1, keepdims=True))
    return center * lax.rsqrt(spread + eps_norm) * norm_gain + norm_shift

def attend_head(queries, key_rows, value_rows, doc_ids):
    same_doc = doc_ids[:, None] == doc_ids[None, :]
    scores = low_back(matmul(queries, key_rows.T))
    masked = jnp.where(same_doc, scores, jnp.float32(-1e+30))
    top_score = lax.optimization_barrier(jnp.max(masked, axis=-1, keepdims=True))
    expo = jnp.exp(masked - top_score)
    probs = expo / lax.optimization_barrier(jnp.sum(expo, axis=-1, keepdims=True))
    return matmul(low(probs), value_rows)

def forward(params, inputs, doc_ids, per_group):
    query_proj, query_bias, key_proj, value_proj, value_bias, out_proj, out_bias, attn_gain, attn_shift, up_proj, up_bias, down_proj, down_bias, ffn_gain, ffn_shift = params
    token_rows = inputs.reshape(per_group * SEQ, D)
    scale = 1.0 / math.sqrt(HEAD_DIM)
    queries = low_back(low((matmul(token_rows, query_proj) + query_bias) * scale))
    key_rows = low_back(low(matmul(token_rows, key_proj)))
    value_rows = low_back(low(matmul(token_rows, value_proj) + value_bias))

    def by_head(matrix):
        return matrix.reshape(per_group, SEQ, HEADS, HEAD_DIM).transpose(0, 2, 1, 3).reshape(per_group * HEADS, SEQ, HEAD_DIM)
    head_docs = jnp.repeat(doc_ids, HEADS, axis=0)
    head_step = jax.checkpoint(attend_head)
    mixed = lax.map(lambda item: head_step(item[0], item[1], item[2], item[3]), (by_head(queries), by_head(key_rows), by_head(value_rows), head_docs))
    mixed = mixed.reshape(per_group, HEADS, SEQ, HEAD_DIM).transpose(0, 2, 1, 3).reshape(per_group * SEQ, D)
    mixed = low_back(low(mixed))
    attended = low_back(matmul(mixed, out_proj) + out_bias)
    hidden = norm_rows(token_rows + attended, attn_gain, attn_shift)
    pre_act = low_back(matmul(low(hidden), up_proj) + up_bias)
    acts = low(jax.nn.gelu(pre_act, approximate=False))
    ffn_out = low_back(matmul(acts, down_proj) + down_bias)
    return norm_rows(hidden + ffn_out, ffn_gain, ffn_shift)

def reference(layer_input, segment_ids, query_proj, query_bias, key_proj, value_proj, value_bias, out_proj, out_bias, attn_gain, attn_shift, up_proj, up_bias, down_proj, down_bias, ffn_gain, ffn_shift, out_cotangent):
    params = tuple((p.astype(jnp.float32) for p in (query_proj, query_bias, key_proj, value_proj, value_bias, out_proj, out_bias, attn_gain, attn_shift, up_proj, up_bias, down_proj, down_bias, ffn_gain, ffn_shift)))
    per_group = math.gcd(SEQS, max(1, 4096 // SEQ))
    groups = SEQS // per_group
    inputs = layer_input.astype(jnp.float32).reshape(groups, per_group, SEQ, D)
    cotan = out_cotangent.astype(jnp.float32).reshape(groups, per_group, SEQ, D)
    doc_groups = segment_ids.reshape(groups, per_group, SEQ)

    def group_step(totals, item):
        block_in, block_docs, block_cot = item
        result, pullback = jax.vjp(lambda prm, inp: forward(prm, inp, block_docs, per_group), params, block_in)
        grad_params, grad_in = pullback(block_cot.reshape(per_group * SEQ, D))
        totals = jax.tree.map(jnp.add, totals, grad_params)
        return (totals, (result.reshape(per_group, SEQ, D).astype(jnp.bfloat16), grad_in))
    zeros = jax.tree.map(jnp.zeros_like, params)
    totals, (outputs, grads_in) = lax.scan(group_step, zeros, (inputs, doc_groups, cotan))
    return (outputs.reshape(SEQS, SEQ, D), grads_in.reshape(SEQS, SEQ, D), totals[0], totals[1], totals[2], totals[3], totals[4], totals[5], totals[6], totals[7], totals[8], totals[9], totals[10], totals[11], totals[12], totals[13], totals[14])
```

```python
from functools import partial
import math

import jax
import jax.numpy as jnp
from jax import lax
from jax.experimental import pallas as pl
from jax.experimental.pallas import tpu as pltpu
from jax.sharding import PartitionSpec as P

HEAD_DIM = 64


eps_norm = 1e-12
far_below = -1e30


def contract_rows(left, right):
    return lax.dot_general(
        left, right, (((0,), (0,)), ((), ())), preferred_element_type=jnp.float32
    )


def contract_last(left, right):
    return lax.dot_general(
        left, right, (((1,), (1,)), ((), ())), preferred_element_type=jnp.float32
    )


def norm_forward(resid, norm_gain, norm_shift):
    center = resid - jnp.mean(resid, axis=-1, keepdims=True)
    inv_std = lax.rsqrt(jnp.mean(center * center, axis=-1, keepdims=True) + eps_norm)
    normed = center * inv_std
    return (normed * norm_gain + norm_shift, normed, inv_std)


def norm_backward(grad_out, normed, inv_std, norm_gain):
    grad_normed = grad_out * norm_gain
    grad_in = inv_std * (
        grad_normed
        - jnp.mean(grad_normed, axis=-1, keepdims=True)
        - normed * jnp.mean(grad_normed * normed, axis=-1, keepdims=True)
    )
    return (grad_in, jnp.sum(grad_out * normed, axis=0), jnp.sum(grad_out, axis=0))


def split_heads(matrix):
    return matrix.reshape(matrix.shape[0], matrix.shape[1] // HEAD_DIM, HEAD_DIM)


def scores_of(queries, keys_all, query_docs, key_docs):
    scores = jnp.einsum(
        "qhd,khd->hqk",
        split_heads(queries),
        split_heads(keys_all),
        preferred_element_type=jnp.float32,
    )
    same_doc = (query_docs[:, None] == key_docs[None, :])[None]
    return jnp.where(same_doc, scores, jnp.float32(far_below))


def attend_forward(item):
    queries, keys_all, values_all, query_docs, key_docs = item
    scores = scores_of(queries, keys_all, query_docs, key_docs)
    top_score = jnp.max(scores, axis=-1, keepdims=True)
    expo = jnp.exp(scores - top_score)
    total = jnp.sum(expo, axis=-1, keepdims=True)
    probs = (expo / total).astype(jnp.bfloat16)
    mixed = jnp.einsum(
        "hqk,khd->qhd", probs, split_heads(values_all), preferred_element_type=jnp.float32
    )
    return (
        mixed.reshape(queries.shape).astype(jnp.bfloat16),
        (top_score + jnp.log(total))[:, :, 0],
    )


def score_grads(queries, keys_all, values_all, query_docs, key_docs, grad_mixed, log_total):
    scores = scores_of(queries, keys_all, query_docs, key_docs)
    probs = jnp.exp(scores - log_total[:, :, None])
    grad_probs = jnp.einsum(
        "qhd,khd->hqk",
        split_heads(grad_mixed),
        split_heads(values_all),
        preferred_element_type=jnp.float32,
    )
    inner = jnp.sum(grad_probs * probs, axis=-1)
    grad_scores = (probs * (grad_probs - inner[:, :, None])).astype(jnp.bfloat16)
    return (probs, grad_scores, inner)


def attend_backward(item):
    queries, keys_all, values_all, query_docs, key_docs, grad_mixed, log_total = item
    probs, grad_scores, inner = score_grads(
        queries, keys_all, values_all, query_docs, key_docs, grad_mixed, log_total
    )
    grad_heads = split_heads(grad_mixed)
    grad_queries = jnp.einsum(
        "hqk,khd->qhd", grad_scores, split_heads(keys_all), preferred_element_type=jnp.float32
    )
    grad_keys = jnp.einsum(
        "hqk,qhd->khd", grad_scores, split_heads(queries), preferred_element_type=jnp.float32
    )
    grad_values = jnp.einsum(
        "hqk,qhd->khd", probs.astype(jnp.bfloat16), grad_heads, preferred_element_type=jnp.float32
    )
    return (
        grad_queries.reshape(queries.shape).astype(jnp.bfloat16),
        grad_keys.reshape(keys_all.shape),
        grad_values.reshape(values_all.shape),
    )


def general_shards(
    layer_input,
    segment_ids,
    query_proj,
    query_bias,
    key_proj,
    value_proj,
    value_bias,
    out_proj,
    out_bias,
    attn_gain,
    attn_shift,
    up_proj,
    up_bias,
    down_proj,
    down_bias,
    ffn_gain,
    ffn_shift,
    out_cotangent,
):
    seq_here, ctx_rows, width = layer_input.shape
    scale = 1.0 / math.sqrt(HEAD_DIM)
    full_query, full_key, full_value, full_out, full_up, full_down = (
        lax.all_gather(query_proj, "shard", axis=0, tiled=True),
        lax.all_gather(key_proj, "shard", axis=0, tiled=True),
        lax.all_gather(value_proj, "shard", axis=0, tiled=True),
        lax.all_gather(out_proj, "shard", axis=1, tiled=True),
        lax.all_gather(up_proj, "shard", axis=0, tiled=True),
        lax.all_gather(down_proj, "shard", axis=1, tiled=True),
    )
    local_width = full_query.shape[1]
    joined_proj = jnp.concatenate([full_query, full_key, full_value], axis=1)
    rows_in = layer_input.reshape(seq_here * ctx_rows, width)
    projected = jnp.dot(rows_in, joined_proj, preferred_element_type=jnp.float32)
    shaped = (seq_here, ctx_rows, local_width)
    queries = (
        ((projected[:, :local_width] + query_bias) * scale).astype(jnp.bfloat16).reshape(shaped)
    )
    keys_mine = projected[:, local_width : 2 * local_width].astype(jnp.bfloat16).reshape(shaped)
    values_mine = (
        (projected[:, 2 * local_width :] + value_bias).astype(jnp.bfloat16).reshape(shaped)
    )
    keys_all, values_all = (
        lax.all_gather(keys_mine, "ctx", axis=1, tiled=True),
        lax.all_gather(values_mine, "ctx", axis=1, tiled=True),
    )
    query_docs = lax.dynamic_slice_in_dim(
        segment_ids, lax.axis_index("ctx") * ctx_rows, ctx_rows, 1
    )
    mixed, log_total = lax.map(
        attend_forward, (queries, keys_all, values_all, query_docs, segment_ids)
    )
    mixed_rows = mixed.reshape(-1, local_width)
    attended = (
        lax.psum(
            jnp.dot(mixed_rows, full_out, preferred_element_type=jnp.float32).astype(jnp.bfloat16),
            "tp",
        ).astype(jnp.float32)
        + out_bias
    )
    hidden, normed_one, inv_one = norm_forward(
        rows_in.astype(jnp.float32) + attended, attn_gain, attn_shift
    )
    hidden_low = hidden.astype(jnp.bfloat16)
    pre_act = jnp.dot(hidden_low, full_up, preferred_element_type=jnp.float32) + up_bias
    acts_low = jax.nn.gelu(pre_act, approximate=False).astype(jnp.bfloat16)
    ffn_out = (
        lax.psum(
            jnp.dot(acts_low, full_down, preferred_element_type=jnp.float32).astype(jnp.bfloat16),
            "tp",
        ).astype(jnp.float32)
        + down_bias
    )
    output_rows, normed_two, inv_two = norm_forward(hidden + ffn_out, ffn_gain, ffn_shift)
    layer_output = output_rows.astype(jnp.bfloat16).reshape(layer_input.shape)
    grad_out = out_cotangent.reshape(-1, width).astype(jnp.float32)
    grad_two, ffn_gain_grad, ffn_shift_grad = norm_backward(grad_out, normed_two, inv_two, ffn_gain)
    grad_ffn = grad_two.astype(jnp.bfloat16)
    down_bias_grad = jnp.sum(grad_ffn, axis=0, dtype=jnp.float32)
    down_part = contract_rows(acts_low, grad_ffn)
    grad_acts = contract_last(grad_ffn, full_down)
    _, gelu_back = jax.vjp(partial(jax.nn.gelu, approximate=False), pre_act)
    grad_pre = gelu_back(grad_acts)[0].astype(jnp.bfloat16)
    up_bias_grad = jnp.sum(grad_pre, axis=0, dtype=jnp.float32)
    up_part = contract_rows(hidden_low, grad_pre)
    grad_hidden = grad_two + lax.psum(
        contract_last(grad_pre, full_up).astype(jnp.bfloat16), "tp"
    ).astype(jnp.float32)
    grad_one, attn_gain_grad, attn_shift_grad = norm_backward(
        grad_hidden, normed_one, inv_one, attn_gain
    )
    grad_attn = grad_one.astype(jnp.bfloat16)
    out_bias_grad = jnp.sum(grad_attn, axis=0, dtype=jnp.float32)
    out_part = contract_rows(mixed_rows, grad_attn)
    grad_mixed = contract_last(grad_attn, full_out).astype(jnp.bfloat16).reshape(shaped)
    keys_back, values_back = (
        lax.all_gather(keys_mine, "ctx", axis=1, tiled=True),
        lax.all_gather(values_mine, "ctx", axis=1, tiled=True),
    )
    grad_queries, grad_keys_all, grad_values_all = lax.map(
        attend_backward,
        (queries, keys_back, values_back, query_docs, segment_ids, grad_mixed, log_total),
    )
    grad_keys, grad_values = (
        lax.psum_scatter(
            grad_keys_all.astype(jnp.bfloat16), "ctx", scatter_dimension=1, tiled=True
        ).astype(jnp.float32),
        lax.psum_scatter(
            grad_values_all.astype(jnp.bfloat16), "ctx", scatter_dimension=1, tiled=True
        ).astype(jnp.float32),
    )
    grad_keys = grad_keys.astype(jnp.bfloat16).reshape(-1, local_width)
    grad_values = grad_values.astype(jnp.bfloat16).reshape(-1, local_width)
    grad_scaled = grad_queries.reshape(-1, local_width) * jnp.bfloat16(scale)
    grad_joined = jnp.concatenate([grad_scaled, grad_keys, grad_values], axis=1)
    joined_part = contract_rows(rows_in, grad_joined)
    query_part = joined_part[:, :local_width]
    key_part = joined_part[:, local_width : 2 * local_width]
    value_part = joined_part[:, 2 * local_width :]
    query_bias_grad = jnp.sum(grad_scaled, axis=0, dtype=jnp.float32)
    value_bias_grad = jnp.sum(grad_values, axis=0, dtype=jnp.float32)
    back_terms = contract_last(grad_joined, joined_proj)
    input_grad = (
        grad_one + lax.psum(back_terms.astype(jnp.bfloat16), "tp").astype(jnp.float32)
    ).reshape(layer_input.shape)
    sliced = (
        lax.psum_scatter(
            query_part.astype(jnp.bfloat16), "shard", scatter_dimension=0, tiled=True
        ).astype(jnp.float32),
        lax.psum_scatter(
            key_part.astype(jnp.bfloat16), "shard", scatter_dimension=0, tiled=True
        ).astype(jnp.float32),
        lax.psum_scatter(
            value_part.astype(jnp.bfloat16), "shard", scatter_dimension=0, tiled=True
        ).astype(jnp.float32),
        lax.psum_scatter(
            out_part.astype(jnp.bfloat16), "shard", scatter_dimension=1, tiled=True
        ).astype(jnp.float32),
        lax.psum_scatter(
            up_part.astype(jnp.bfloat16), "shard", scatter_dimension=0, tiled=True
        ).astype(jnp.float32),
        lax.psum_scatter(
            down_part.astype(jnp.bfloat16), "shard", scatter_dimension=1, tiled=True
        ).astype(jnp.float32),
    )
    reduced = (
        lax.psum(sliced[0].astype(jnp.bfloat16), "ctx").astype(jnp.float32),
        lax.psum(sliced[1].astype(jnp.bfloat16), "ctx").astype(jnp.float32),
        lax.psum(sliced[2].astype(jnp.bfloat16), "ctx").astype(jnp.float32),
        lax.psum(sliced[3].astype(jnp.bfloat16), "ctx").astype(jnp.float32),
        lax.psum(sliced[4].astype(jnp.bfloat16), "ctx").astype(jnp.float32),
        lax.psum(sliced[5].astype(jnp.bfloat16), "ctx").astype(jnp.float32),
    )
    small = lax.psum(
        (
            query_bias_grad,
            value_bias_grad,
            out_bias_grad,
            attn_gain_grad,
            attn_shift_grad,
            up_bias_grad,
            down_bias_grad,
            ffn_gain_grad,
            ffn_shift_grad,
        ),
        ("shard", "ctx"),
    )
    return (
        layer_output,
        input_grad,
        reduced[0],
        small[0],
        reduced[1],
        reduced[2],
        small[1],
        reduced[3],
        small[2],
        small[3],
        small[4],
        reduced[4],
        small[5],
        reduced[5],
        small[6],
        small[7],
        small[8],
    )


PAIR = 2 * HEAD_DIM
QBLOCK = 128


def dot32(left, right):
    return jnp.dot(left, right, preferred_element_type=jnp.float32)


def stack_heads(rows):
    lane = lax.broadcasted_iota(jnp.int32, rows.shape, 1)
    nought = jnp.zeros_like(rows)
    return jnp.concatenate(
        [jnp.where(lane < HEAD_DIM, rows, nought), jnp.where(lane >= HEAD_DIM, rows, nought)], axis=0
    )


def unstack_heads(wide):
    return jnp.concatenate([wide[:HEAD_DIM, :QBLOCK], wide[HEAD_DIM:, QBLOCK:]], axis=0).T


def masked_scores(span, queries, keys, key_docs, query_docs):
    scores = contract_last(keys, queries)
    same = key_docs == query_docs
    return jnp.where(jnp.concatenate([same, same], axis=1), scores, jnp.float32(far_below))


def attend_kernel(span, q_ref, k_ref, v_ref, kd_ref, qd_ref, o_ref, l_ref):
    first = pl.multiple_of(pl.program_id(1) * QBLOCK, QBLOCK)
    keys = k_ref[pl.ds(first, span), :]
    values = v_ref[pl.ds(first, span), :]
    scores = masked_scores(
        span, stack_heads(q_ref[...]), keys, kd_ref[pl.ds(first, span), :], qd_ref[0]
    )
    top = jnp.max(scores, axis=0, keepdims=True)
    expo = jnp.exp(scores - top)
    total = jnp.sum(expo, axis=0, keepdims=True)
    probs = (expo * (1.0 / total)).astype(jnp.bfloat16)
    o_ref[...] = unstack_heads(contract_rows(values, probs)).astype(jnp.bfloat16)
    l_ref[0, 0] = top + jnp.log(total)


def attend_back_kernel(
    span, q_ref, k_ref, v_ref, kd_ref, qd_ref, do_ref, l_ref, dq_ref, dk_ref, dv_ref, dk_acc, dv_acc
):
    step = pl.program_id(1)

    @pl.when(step == 0)
    def _():
        dk_acc[...] = jnp.zeros_like(dk_acc)
        dv_acc[...] = jnp.zeros_like(dv_acc)

    first = pl.multiple_of(step * QBLOCK, QBLOCK)
    here = pl.ds(first, span)
    keys = k_ref[here, :]
    values = v_ref[here, :]
    queries = stack_heads(q_ref[...])
    grads = stack_heads(do_ref[...])
    scores = masked_scores(span, queries, keys, kd_ref[here, :], qd_ref[0])
    probs = jnp.exp(scores - l_ref[0, 0])
    grad_probs = contract_last(values, grads)
    inner = jnp.sum(grad_probs * probs, axis=0, keepdims=True)
    grad_scores = (probs * (grad_probs - inner)).astype(jnp.bfloat16)
    dq_ref[...] = unstack_heads(contract_rows(keys, grad_scores)).astype(jnp.bfloat16)
    dk_acc[here, :] += dot32(grad_scores, queries)
    dv_acc[here, :] += dot32(probs.astype(jnp.bfloat16), grads)

    @pl.when(step == pl.num_programs(1) - 1)
    def _():
        dk_ref[...] = dk_acc[...].astype(jnp.bfloat16)
        dv_ref[...] = dv_acc[...].astype(jnp.bfloat16)


def attention_specs(window):
    rows = pl.BlockSpec((QBLOCK, PAIR), lambda h, i: (i, h))
    keys = pl.BlockSpec((window, PAIR), lambda h, i: (0, h))
    key_docs = pl.BlockSpec((window, QBLOCK), lambda h, i: (0, 0))
    query_docs = pl.BlockSpec((1, 1, QBLOCK), lambda h, i: (i, 0, 0))
    logs = pl.BlockSpec((1, 1, 1, 2 * QBLOCK), lambda h, i: (h, i, 0, 0))
    return rows, keys, key_docs, query_docs, logs


def attend(queries, keys, values, key_docs, query_docs, reach):
    count, width = queries.shape
    window = keys.shape[0]
    blocks, pairs, span = count // QBLOCK, width // PAIR, QBLOCK + 2 * reach
    rows, key_spec, kd_spec, qd_spec, logs = attention_specs(window)
    return pl.pallas_call(
        partial(attend_kernel, span),
        grid=(pairs, blocks),
        in_specs=[rows, key_spec, key_spec, kd_spec, qd_spec],
        out_specs=[rows, logs],
        out_shape=[
            jax.ShapeDtypeStruct((count, width), jnp.bfloat16),
            jax.ShapeDtypeStruct((pairs, blocks, 1, 2 * QBLOCK), jnp.float32),
        ],
        compiler_params=pltpu.CompilerParams(vmem_limit_bytes=40 << 20),
        cost_estimate=pl.CostEstimate(
            flops=16 * count * span * width, bytes_accessed=8 << 20, transcendentals=0
        ),
        name="attend",
    )(queries, keys, values, key_docs, query_docs)


def attend_back(queries, keys, values, key_docs, query_docs, grads, logs_in, reach):
    count, width = queries.shape
    window = keys.shape[0]
    blocks, pairs, span = count // QBLOCK, width // PAIR, QBLOCK + 2 * reach
    rows, key_spec, kd_spec, qd_spec, logs = attention_specs(window)
    return pl.pallas_call(
        partial(attend_back_kernel, span),
        grid=(pairs, blocks),
        in_specs=[rows, key_spec, key_spec, kd_spec, qd_spec, rows, logs],
        out_specs=[rows, key_spec, key_spec],
        out_shape=[
            jax.ShapeDtypeStruct((count, width), jnp.bfloat16),
            jax.ShapeDtypeStruct((window, width), jnp.bfloat16),
            jax.ShapeDtypeStruct((window, width), jnp.bfloat16),
        ],
        scratch_shapes=[
            pltpu.VMEM((window, PAIR), jnp.float32),
            pltpu.VMEM((window, PAIR), jnp.float32),
        ],
        compiler_params=pltpu.CompilerParams(vmem_limit_bytes=40 << 20),
        cost_estimate=pl.CostEstimate(
            flops=40 * count * span * width, bytes_accessed=12 << 20, transcendentals=0
        ),
        name="attend_back",
    )(queries, keys, values, key_docs, query_docs, grads, logs_in)


def ctx_swap(array, bit):
    return lax.ppermute(array, "ctx", [(i, i ^ bit) for i in range(4)])


def core_swap(array):
    return ctx_swap(array, 1)


def across_swap(array):
    return ctx_swap(array, 2)


def in_order(flag, mine, other):
    return jnp.where(flag == 0, mine, other), jnp.where(flag == 0, other, mine)


def chain_pairs():
    def at(across, core, tp):
        return (2 * across + core) * 4 + tp

    pairs = []
    for group in (0, 2):
        path = [(0, group), (0, group + 1), (1, group + 1), (1, group)]
        for (across, tp), (next_across, next_tp) in zip(path[:-1], path[1:]):
            pairs.append((at(across, 1, tp), at(next_across, 0, next_tp)))
            pairs.append((at(next_across, 0, next_tp), at(across, 1, tp)))
    return pairs


def span_shards(
    layer_input,
    segment_ids,
    query_proj,
    query_bias,
    key_proj,
    value_proj,
    value_bias,
    out_proj,
    out_bias,
    attn_gain,
    attn_shift,
    up_proj,
    up_bias,
    down_proj,
    down_bias,
    ffn_gain,
    ffn_shift,
    out_cotangent,
):
    seqs, block, width = layer_input.shape
    length = segment_ids.shape[1]
    reach = length // 2
    count = seqs * block // 4
    window = count + 2 * reach
    scale = 1.0 / math.sqrt(HEAD_DIM)
    bf16, f32 = jnp.bfloat16, jnp.float32
    ctx, tp = lax.axis_index("ctx"), lax.axis_index("tp")
    core, across, side = ctx & 1, ctx >> 1, tp & 1
    place = 2 * across + (side ^ across)
    odd = across ^ side
    both = ("tp", "shard")

    half = query_proj.shape[0] // 2
    own_in = lax.dynamic_slice_in_dim(
        jnp.concatenate([query_proj, key_proj, value_proj], axis=1), core * half, half, 0
    )
    in_mine = lax.all_gather(own_in, both, axis=0, tiled=False)
    in_lo, in_hi = in_order(core, in_mine, core_swap(in_mine))
    heads = query_proj.shape[1]
    joined = jnp.stack(
        [in_lo.reshape(4, 2, half, 3, heads), in_hi.reshape(4, 2, half, 3, heads)], axis=2
    )
    joined = joined.transpose(4, 1, 2, 3, 0, 5).reshape(3, width, 4 * heads)
    full_query, full_key, full_value = joined[0], joined[1], joined[2]

    cut = up_proj.shape[1] // 2
    out_half = out_proj.shape[0] // 2
    own_rest = jnp.concatenate(
        [
            lax.dynamic_slice_in_dim(up_proj, core * cut, cut, 1),
            lax.dynamic_slice_in_dim(down_proj, core * cut, cut, 0),
            lax.dynamic_slice_in_dim(out_proj, core * out_half, out_half, 0),
        ],
        axis=0,
    )
    rest = lax.all_gather(own_rest, both, axis=0, tiled=False).reshape(4, 2, -1, cut)
    up_here = rest[:, :, :cut].transpose(1, 2, 0, 3).reshape(width, 4 * cut)
    down_here = rest[:, :, cut : 2 * cut].transpose(0, 2, 1, 3).reshape(4 * cut, width)
    out_mine = rest[:, :, 2 * cut :]
    out_lo, out_hi = in_order(core, out_mine, core_swap(out_mine))
    full_out = (
        jnp.stack([out_lo, out_hi], axis=1).transpose(0, 1, 3, 2, 4).reshape(width, width)
    )
    biases = lax.all_gather(
        jnp.concatenate(
            [query_bias, value_bias, lax.dynamic_slice_in_dim(up_bias, core * cut, cut, 0)]
        ),
        "tp",
        axis=0,
        tiled=False,
    )
    full_query_bias = biases[:, :heads].reshape(-1)
    full_value_bias = biases[:, heads : 2 * heads].reshape(-1)
    up_bias_here = biases[:, 2 * heads :].reshape(-1)

    first_seq = 3 * (tp >> 1)
    mine = lax.dynamic_slice_in_dim(layer_input, first_seq + across, 2, 0)
    theirs = across_swap(lax.dynamic_slice_in_dim(layer_input, first_seq + 1 - across, 2, 0))
    pair = jnp.stack([mine, theirs])
    pair_lo, pair_hi = in_order(core, pair, core_swap(pair))
    quads = jnp.stack([pair_lo, pair_hi], axis=1)
    quads = jnp.where(across == 0, quads, quads[::-1])
    near = quads.transpose(2, 0, 1, 3, 4).reshape(2 * length, width)
    start = 2 * count * place + count * core - length * across
    edge = jnp.zeros((reach, width), bf16)
    in_window = lax.dynamic_slice_in_dim(
        jnp.concatenate([edge, near, edge], axis=0), start, window, 0
    )
    ids = lax.dynamic_slice_in_dim(segment_ids, first_seq + across, 2, 0)
    ids = (ids + jnp.array([[0], [1 << 16]], jnp.int32)).reshape(-1)
    no_doc = jnp.full((reach,), -1, jnp.int32)
    window_docs = lax.dynamic_slice_in_dim(
        jnp.concatenate([no_doc, ids, no_doc]), start, window, 0
    )
    key_docs = jnp.broadcast_to(window_docs[:, None], (window, QBLOCK))
    query_docs = window_docs[reach : reach + count].reshape(-1, 1, QBLOCK)
    rows_in = in_window[reach : reach + count]

    queries = ((dot32(rows_in, full_query) + full_query_bias) * scale).astype(bf16)
    keys = dot32(in_window, full_key).astype(bf16)
    values = (dot32(in_window, full_value) + full_value_bias).astype(bf16)
    mixed, logs = attend(queries, keys, values, key_docs, query_docs, reach)
    attended = dot32(mixed, full_out) + out_bias
    hidden, normed_one, inv_one = norm_forward(
        rows_in.astype(f32) + attended, attn_gain, attn_shift
    )
    hidden_low = hidden.astype(bf16)
    hidden_both = jnp.concatenate(in_order(core, hidden_low, core_swap(hidden_low)), axis=0)
    pre_act = dot32(hidden_both, up_here) + up_bias_here
    cdf = 0.5 * (1.0 + lax.erf(pre_act * math.sqrt(0.5)))
    acts_low = (pre_act * cdf).astype(bf16)
    slope = cdf + pre_act * (jnp.exp(-0.5 * pre_act * pre_act) * (1.0 / math.sqrt(2 * math.pi)))

    def chip_sum(partial_rows):
        low, high = partial_rows[:count], partial_rows[count:]
        keep = jnp.where(core == 0, low, high)
        give = jnp.where(core == 0, high, low).astype(bf16)
        return keep + core_swap(give).astype(f32)

    ffn_out = chip_sum(dot32(acts_low, down_here)) + down_bias
    output_rows, normed_two, inv_two = norm_forward(hidden + ffn_out, ffn_gain, ffn_shift)

    def deliver(rows):
        chip = jnp.concatenate(in_order(core, rows, core_swap(rows)), axis=0)
        kept = lax.dynamic_slice_in_dim(chip, odd * block + core * block, block, 0)
        half_block = block // 2
        sent = lax.dynamic_slice_in_dim(
            chip, (1 - odd) * 2 * block + core * half_block, half_block, 0
        )
        packed = jnp.concatenate([kept, across_swap(sent)], axis=0)
        every = lax.all_gather(packed, "tp", axis=0, tiled=False)
        halves = every[:, block:]
        lo, hi = in_order(core, halves, core_swap(halves))
        moved = jnp.concatenate([lo, hi], axis=1)
        kept_all = every[:, :block]
        from_side = 1 ^ across ^ core
        parts = []
        for group in (0, 2):
            foreign = lax.dynamic_index_in_dim(moved, group + from_side, 0, keepdims=False)
            near_one, mid_one = kept_all[group], kept_all[group + 1]
            parts += [
                jnp.where(across == 0, near_one, foreign),
                mid_one,
                jnp.where(across == 0, foreign, near_one),
            ]
        return jnp.stack(parts)

    layer_output = deliver(output_rows.astype(bf16))

    cot_mine = lax.dynamic_slice_in_dim(out_cotangent, first_seq + across, 2, 0)
    cot_theirs = across_swap(
        lax.dynamic_slice_in_dim(out_cotangent, first_seq + 1 - across, 2, 0)
    )
    cot_pair = jnp.stack([cot_mine, cot_theirs])
    cot_lo, cot_hi = in_order(core, cot_pair, core_swap(cot_pair))
    cots = jnp.stack([cot_lo, cot_hi], axis=1)
    cots = jnp.where(across == 0, cots, cots[::-1])
    cots = cots.transpose(2, 0, 1, 3, 4).reshape(2 * length, width)
    grad_out = lax.dynamic_slice_in_dim(cots, start, count, 0).astype(f32)

    grad_two, ffn_gain_grad, ffn_shift_grad = norm_backward(grad_out, normed_two, inv_two, ffn_gain)
    grad_ffn = grad_two.astype(bf16)
    down_bias_grad = jnp.sum(grad_ffn, axis=0, dtype=f32)
    grad_ffn_both = jnp.concatenate(in_order(core, grad_ffn, core_swap(grad_ffn)), axis=0)
    down_part = contract_rows(acts_low, grad_ffn_both)
    grad_pre = (slope * contract_last(grad_ffn_both, down_here)).astype(bf16)
    up_bias_part = jnp.sum(grad_pre, axis=0, dtype=f32)
    up_part = contract_rows(hidden_both, grad_pre)
    grad_hidden = grad_two + chip_sum(contract_last(grad_pre, up_here))
    grad_one, attn_gain_grad, attn_shift_grad = norm_backward(
        grad_hidden, normed_one, inv_one, attn_gain
    )
    grad_attn = grad_one.astype(bf16)
    out_bias_grad = jnp.sum(grad_attn, axis=0, dtype=f32)
    out_part = contract_rows(mixed, grad_attn).astype(bf16)
    grad_mixed = contract_last(grad_attn, full_out).astype(bf16)
    grad_queries, grad_keys, grad_values = attend_back(
        queries, keys, values, key_docs, query_docs, grad_mixed, logs, reach
    )
    grad_scaled = grad_queries * bf16(scale)
    grad_near = (contract_last(grad_keys, full_key) + contract_last(grad_values, full_value)).astype(
        bf16
    )
    give = jnp.where(core == 0, grad_near[count + reach :], grad_near[:reach])
    keep = jnp.where(core == 0, grad_near[: count + reach], grad_near[reach:]).astype(f32)
    got = core_swap(give[: 2 * reach]).astype(f32)
    shared = reach - count
    own_sum = jnp.where(core == 0, keep[reach:] + got[shared:], keep[:count] + got[:count])
    onward = jnp.where(
        core == 0,
        jnp.concatenate([keep[:count], keep[count:reach] + got[:shared]], axis=0),
        jnp.concatenate([keep[count : count + shared] + got[count:], keep[count + shared :]], axis=0),
    ).astype(bf16)
    arrived = lax.ppermute(onward, ("ctx", "tp"), chain_pairs())
    passed = core_swap(jnp.where(core == 0, arrived[count:], arrived[:shared])).astype(f32)
    own_sum = own_sum + jnp.where(core == 0, arrived[:count], arrived[shared:]).astype(f32)
    rest_rows = jnp.zeros((count - shared, width), f32)
    own_sum = own_sum + jnp.where(
        core == 0,
        jnp.concatenate([rest_rows, passed], axis=0),
        jnp.concatenate([passed, rest_rows], axis=0),
    )
    grad_rows = grad_one + own_sum + contract_last(grad_scaled, full_query)
    input_grad = deliver(grad_rows.astype(bf16)).astype(f32)

    query_part = contract_rows(rows_in, grad_scaled)
    key_part = contract_rows(in_window, grad_keys)
    value_part = contract_rows(in_window, grad_values)
    in_part = jnp.stack([query_part, key_part, value_part]).astype(bf16)
    in_part = in_part.reshape(3, 2, 2, half, 4, heads).transpose(2, 4, 1, 3, 0, 5)
    in_part = in_part.reshape(2, 8 * half, 3 * heads)
    out_part = out_part.reshape(4, 2, out_half, 2, cut).transpose(1, 0, 3, 2, 4)

    def core_sum(parts):
        return (
            jnp.where(core == 0, parts[0], parts[1]).astype(f32)
            + core_swap(jnp.where(core == 0, parts[1], parts[0])).astype(f32)
        ).astype(bf16)

    def finish(scattered):
        total = (scattered.astype(f32) + across_swap(scattered).astype(f32)).astype(bf16)
        return in_order(core, total, core_swap(total))

    in_done = lax.psum_scatter(core_sum(in_part), both, scatter_dimension=0, tiled=True)
    in_grads = jnp.concatenate(finish(in_done), axis=0).astype(f32)
    rest_part = jnp.concatenate(
        [
            up_part.astype(bf16).reshape(2, cut, 4, cut).transpose(2, 0, 1, 3),
            down_part.astype(bf16).reshape(4, cut, 2, cut).transpose(0, 2, 1, 3),
            core_sum(out_part),
        ],
        axis=2,
    ).reshape(-1, cut)
    rest_done = lax.psum_scatter(rest_part, both, scatter_dimension=0, tiled=True)
    rest_lo, rest_hi = finish(rest_done)
    up_grad = jnp.concatenate([rest_lo[:cut], rest_hi[:cut]], axis=1).astype(f32)
    down_grad = jnp.concatenate([rest_lo[cut : 2 * cut], rest_hi[cut : 2 * cut]], axis=0).astype(f32)
    out_grad = jnp.concatenate([rest_lo[2 * cut :], rest_hi[2 * cut :]], axis=0).astype(f32)

    up_bias_all = jnp.stack(
        [jnp.where(core == 0, up_bias_part, 0.0), jnp.where(core == 1, up_bias_part, 0.0)]
    )
    small = lax.psum(
        jnp.concatenate(
            [
                jnp.sum(grad_scaled, axis=0, dtype=f32),
                jnp.sum(grad_values, axis=0, dtype=f32),
                out_bias_grad,
                attn_gain_grad,
                attn_shift_grad,
                down_bias_grad,
                ffn_gain_grad,
                ffn_shift_grad,
                up_bias_all.reshape(-1),
            ]
        ),
        ("shard", "ctx", "tp"),
    )
    flat = small[: 8 * width].reshape(8, width)
    query_bias_grad = lax.dynamic_slice_in_dim(flat[0], tp * heads, heads, 0)
    value_bias_grad = lax.dynamic_slice_in_dim(flat[1], tp * heads, heads, 0)
    up_bias_grad = lax.dynamic_index_in_dim(
        small[8 * width :].reshape(2, 4, cut), tp, 1, keepdims=False
    ).reshape(-1)
    return (
        layer_output,
        input_grad,
        in_grads[:, :heads],
        query_bias_grad,
        in_grads[:, heads : 2 * heads],
        in_grads[:, 2 * heads :],
        value_bias_grad,
        out_grad,
        flat[2],
        flat[3],
        flat[4],
        up_grad,
        up_bias_grad,
        down_grad,
        flat[5],
        flat[6],
        flat[7],
    )


def pick_plan(mesh):
    shape = dict(mesh.shape)

    def plan(layer_input, segment_ids, *others):
        seqs, block, _ = layer_input.shape
        fits = (
            (shape["shard"], shape["ctx"], shape["tp"]) == (2, 4, 4)
            and seqs == 6
            and segment_ids.shape[1] == 4 * block
            and block == 2 * QBLOCK
        )
        chosen = span_shards if fits else general_shards
        return chosen(layer_input, segment_ids, *others)

    return plan


def solution(mesh):
    return jax.shard_map(
        pick_plan(mesh),
        mesh=mesh,
        in_specs=(
            P("shard", "ctx", None),
            P("shard", None),
            P("shard", "tp"),
            P("tp"),
            P("shard", "tp"),
            P("shard", "tp"),
            P("tp"),
            P("tp", "shard"),
            P(),
            P(),
            P(),
            P("shard", "tp"),
            P("tp"),
            P("tp", "shard"),
            P(),
            P(),
            P(),
            P("shard", "ctx", None),
        ),
        out_specs=(
            P("shard", "ctx", None),
            P("shard", "ctx", None),
            P("shard", "tp"),
            P("tp"),
            P("shard", "tp"),
            P("shard", "tp"),
            P("tp"),
            P("tp", "shard"),
            P(),
            P(),
            P(),
            P("shard", "tp"),
            P("tp"),
            P("tp", "shard"),
            P(),
            P(),
            P(),
        ),
        check_vma=False,
    )
```

```python
from functools import partial
import math

import jax
import jax.numpy as jnp
from jax import lax
from jax.experimental import pallas as pl
from jax.experimental.pallas import tpu as pltpu
from jax.sharding import PartitionSpec as P

HEAD_DIM = 64


eps_norm = 1e-12
far_below = -1e30


def contract_rows(left, right):
    return lax.dot_general(
        left, right, (((0,), (0,)), ((), ())), preferred_element_type=jnp.float32
    )


def contract_last(left, right):
    return lax.dot_general(
        left, right, (((1,), (1,)), ((), ())), preferred_element_type=jnp.float32
    )


def norm_forward(resid, norm_gain, norm_shift):
    center = resid - jnp.mean(resid, axis=-1, keepdims=True)
    inv_std = lax.rsqrt(jnp.mean(center * center, axis=-1, keepdims=True) + eps_norm)
    normed = center * inv_std
    return (normed * norm_gain + norm_shift, normed, inv_std)


def norm_backward(grad_out, normed, inv_std, norm_gain):
    grad_normed = grad_out * norm_gain
    grad_in = inv_std * (
        grad_normed
        - jnp.mean(grad_normed, axis=-1, keepdims=True)
        - normed * jnp.mean(grad_normed * normed, axis=-1, keepdims=True)
    )
    return (grad_in, jnp.sum(grad_out * normed, axis=0), jnp.sum(grad_out, axis=0))


def split_heads(matrix):
    return matrix.reshape(matrix.shape[0], matrix.shape[1] // HEAD_DIM, HEAD_DIM)


def scores_of(queries, keys_all, query_docs, key_docs):
    scores = jnp.einsum(
        "qhd,khd->hqk",
        split_heads(queries),
        split_heads(keys_all),
        preferred_element_type=jnp.float32,
    )
    same_doc = (query_docs[:, None] == key_docs[None, :])[None]
    return jnp.where(same_doc, scores, jnp.float32(far_below))


def attend_forward(item):
    queries, keys_all, values_all, query_docs, key_docs = item
    scores = scores_of(queries, keys_all, query_docs, key_docs)
    top_score = jnp.max(scores, axis=-1, keepdims=True)
    expo = jnp.exp(scores - top_score)
    total = jnp.sum(expo, axis=-1, keepdims=True)
    probs = (expo / total).astype(jnp.bfloat16)
    mixed = jnp.einsum(
        "hqk,khd->qhd", probs, split_heads(values_all), preferred_element_type=jnp.float32
    )
    return (
        mixed.reshape(queries.shape).astype(jnp.bfloat16),
        (top_score + jnp.log(total))[:, :, 0],
    )


def score_grads(queries, keys_all, values_all, query_docs, key_docs, grad_mixed, log_total):
    scores = scores_of(queries, keys_all, query_docs, key_docs)
    probs = jnp.exp(scores - log_total[:, :, None])
    grad_probs = jnp.einsum(
        "qhd,khd->hqk",
        split_heads(grad_mixed),
        split_heads(values_all),
        preferred_element_type=jnp.float32,
    )
    inner = jnp.sum(grad_probs * probs, axis=-1)
    grad_scores = (probs * (grad_probs - inner[:, :, None])).astype(jnp.bfloat16)
    return (probs, grad_scores, inner)


def attend_backward(item):
    queries, keys_all, values_all, query_docs, key_docs, grad_mixed, log_total = item
    probs, grad_scores, inner = score_grads(
        queries, keys_all, values_all, query_docs, key_docs, grad_mixed, log_total
    )
    grad_heads = split_heads(grad_mixed)
    grad_queries = jnp.einsum(
        "hqk,khd->qhd", grad_scores, split_heads(keys_all), preferred_element_type=jnp.float32
    )
    grad_keys = jnp.einsum(
        "hqk,qhd->khd", grad_scores, split_heads(queries), preferred_element_type=jnp.float32
    )
    grad_values = jnp.einsum(
        "hqk,qhd->khd", probs.astype(jnp.bfloat16), grad_heads, preferred_element_type=jnp.float32
    )
    return (
        grad_queries.reshape(queries.shape).astype(jnp.bfloat16),
        grad_keys.reshape(keys_all.shape),
        grad_values.reshape(values_all.shape),
    )


def general_shards(
    layer_input,
    segment_ids,
    query_proj,
    query_bias,
    key_proj,
    value_proj,
    value_bias,
    out_proj,
    out_bias,
    attn_gain,
    attn_shift,
    up_proj,
    up_bias,
    down_proj,
    down_bias,
    ffn_gain,
    ffn_shift,
    out_cotangent,
):
    seq_here, ctx_rows, width = layer_input.shape
    scale = 1.0 / math.sqrt(HEAD_DIM)
    full_query, full_key, full_value, full_out, full_up, full_down = (
        lax.all_gather(query_proj, "shard", axis=0, tiled=True),
        lax.all_gather(key_proj, "shard", axis=0, tiled=True),
        lax.all_gather(value_proj, "shard", axis=0, tiled=True),
        lax.all_gather(out_proj, "shard", axis=1, tiled=True),
        lax.all_gather(up_proj, "shard", axis=0, tiled=True),
        lax.all_gather(down_proj, "shard", axis=1, tiled=True),
    )
    local_width = full_query.shape[1]
    joined_proj = jnp.concatenate([full_query, full_key, full_value], axis=1)
    rows_in = layer_input.reshape(seq_here * ctx_rows, width)
    projected = jnp.dot(rows_in, joined_proj, preferred_element_type=jnp.float32)
    shaped = (seq_here, ctx_rows, local_width)
    queries = (
        ((projected[:, :local_width] + query_bias) * scale).astype(jnp.bfloat16).reshape(shaped)
    )
    keys_mine = projected[:, local_width : 2 * local_width].astype(jnp.bfloat16).reshape(shaped)
    values_mine = (
        (projected[:, 2 * local_width :] + value_bias).astype(jnp.bfloat16).reshape(shaped)
    )
    keys_all, values_all = (
        lax.all_gather(keys_mine, "ctx", axis=1, tiled=True),
        lax.all_gather(values_mine, "ctx", axis=1, tiled=True),
    )
    query_docs = lax.dynamic_slice_in_dim(
        segment_ids, lax.axis_index("ctx") * ctx_rows, ctx_rows, 1
    )
    mixed, log_total = lax.map(
        attend_forward, (queries, keys_all, values_all, query_docs, segment_ids)
    )
    mixed_rows = mixed.reshape(-1, local_width)
    attended = (
        lax.psum(
            jnp.dot(mixed_rows, full_out, preferred_element_type=jnp.float32).astype(jnp.bfloat16),
            "tp",
        ).astype(jnp.float32)
        + out_bias
    )
    hidden, normed_one, inv_one = norm_forward(
        rows_in.astype(jnp.float32) + attended, attn_gain, attn_shift
    )
    hidden_low = hidden.astype(jnp.bfloat16)
    pre_act = jnp.dot(hidden_low, full_up, preferred_element_type=jnp.float32) + up_bias
    acts_low = jax.nn.gelu(pre_act, approximate=False).astype(jnp.bfloat16)
    ffn_out = (
        lax.psum(
            jnp.dot(acts_low, full_down, preferred_element_type=jnp.float32).astype(jnp.bfloat16),
            "tp",
        ).astype(jnp.float32)
        + down_bias
    )
    output_rows, normed_two, inv_two = norm_forward(hidden + ffn_out, ffn_gain, ffn_shift)
    layer_output = output_rows.astype(jnp.bfloat16).reshape(layer_input.shape)
    grad_out = out_cotangent.reshape(-1, width).astype(jnp.float32)
    grad_two, ffn_gain_grad, ffn_shift_grad = norm_backward(grad_out, normed_two, inv_two, ffn_gain)
    grad_ffn = grad_two.astype(jnp.bfloat16)
    down_bias_grad = jnp.sum(grad_ffn, axis=0, dtype=jnp.float32)
    down_part = contract_rows(acts_low, grad_ffn)
    grad_acts = contract_last(grad_ffn, full_down)
    _, gelu_back = jax.vjp(partial(jax.nn.gelu, approximate=False), pre_act)
    grad_pre = gelu_back(grad_acts)[0].astype(jnp.bfloat16)
    up_bias_grad = jnp.sum(grad_pre, axis=0, dtype=jnp.float32)
    up_part = contract_rows(hidden_low, grad_pre)
    grad_hidden = grad_two + lax.psum(
        contract_last(grad_pre, full_up).astype(jnp.bfloat16), "tp"
    ).astype(jnp.float32)
    grad_one, attn_gain_grad, attn_shift_grad = norm_backward(
        grad_hidden, normed_one, inv_one, attn_gain
    )
    grad_attn = grad_one.astype(jnp.bfloat16)
    out_bias_grad = jnp.sum(grad_attn, axis=0, dtype=jnp.float32)
    out_part = contract_rows(mixed_rows, grad_attn)
    grad_mixed = contract_last(grad_attn, full_out).astype(jnp.bfloat16).reshape(shaped)
    keys_back, values_back = (
        lax.all_gather(keys_mine, "ctx", axis=1, tiled=True),
        lax.all_gather(values_mine, "ctx", axis=1, tiled=True),
    )
    grad_queries, grad_keys_all, grad_values_all = lax.map(
        attend_backward,
        (queries, keys_back, values_back, query_docs, segment_ids, grad_mixed, log_total),
    )
    grad_keys, grad_values = (
        lax.psum_scatter(
            grad_keys_all.astype(jnp.bfloat16), "ctx", scatter_dimension=1, tiled=True
        ).astype(jnp.float32),
        lax.psum_scatter(
            grad_values_all.astype(jnp.bfloat16), "ctx", scatter_dimension=1, tiled=True
        ).astype(jnp.float32),
    )
    grad_keys = grad_keys.astype(jnp.bfloat16).reshape(-1, local_width)
    grad_values = grad_values.astype(jnp.bfloat16).reshape(-1, local_width)
    grad_scaled = grad_queries.reshape(-1, local_width) * jnp.bfloat16(scale)
    grad_joined = jnp.concatenate([grad_scaled, grad_keys, grad_values], axis=1)
    joined_part = contract_rows(rows_in, grad_joined)
    query_part = joined_part[:, :local_width]
    key_part = joined_part[:, local_width : 2 * local_width]
    value_part = joined_part[:, 2 * local_width :]
    query_bias_grad = jnp.sum(grad_scaled, axis=0, dtype=jnp.float32)
    value_bias_grad = jnp.sum(grad_values, axis=0, dtype=jnp.float32)
    back_terms = contract_last(grad_joined, joined_proj)
    input_grad = (
        grad_one + lax.psum(back_terms.astype(jnp.bfloat16), "tp").astype(jnp.float32)
    ).reshape(layer_input.shape)
    sliced = (
        lax.psum_scatter(
            query_part.astype(jnp.bfloat16), "shard", scatter_dimension=0, tiled=True
        ).astype(jnp.float32),
        lax.psum_scatter(
            key_part.astype(jnp.bfloat16), "shard", scatter_dimension=0, tiled=True
        ).astype(jnp.float32),
        lax.psum_scatter(
            value_part.astype(jnp.bfloat16), "shard", scatter_dimension=0, tiled=True
        ).astype(jnp.float32),
        lax.psum_scatter(
            out_part.astype(jnp.bfloat16), "shard", scatter_dimension=1, tiled=True
        ).astype(jnp.float32),
        lax.psum_scatter(
            up_part.astype(jnp.bfloat16), "shard", scatter_dimension=0, tiled=True
        ).astype(jnp.float32),
        lax.psum_scatter(
            down_part.astype(jnp.bfloat16), "shard", scatter_dimension=1, tiled=True
        ).astype(jnp.float32),
    )
    reduced = (
        lax.psum(sliced[0].astype(jnp.bfloat16), "ctx").astype(jnp.float32),
        lax.psum(sliced[1].astype(jnp.bfloat16), "ctx").astype(jnp.float32),
        lax.psum(sliced[2].astype(jnp.bfloat16), "ctx").astype(jnp.float32),
        lax.psum(sliced[3].astype(jnp.bfloat16), "ctx").astype(jnp.float32),
        lax.psum(sliced[4].astype(jnp.bfloat16), "ctx").astype(jnp.float32),
        lax.psum(sliced[5].astype(jnp.bfloat16), "ctx").astype(jnp.float32),
    )
    small = lax.psum(
        (
            query_bias_grad,
            value_bias_grad,
            out_bias_grad,
            attn_gain_grad,
            attn_shift_grad,
            up_bias_grad,
            down_bias_grad,
            ffn_gain_grad,
            ffn_shift_grad,
        ),
        ("shard", "ctx"),
    )
    return (
        layer_output,
        input_grad,
        reduced[0],
        small[0],
        reduced[1],
        reduced[2],
        small[1],
        reduced[3],
        small[2],
        small[3],
        small[4],
        reduced[4],
        small[5],
        reduced[5],
        small[6],
        small[7],
        small[8],
    )


PAIR = 2 * HEAD_DIM
QBLOCK = 128


def dot32(left, right):
    return jnp.dot(left, right, preferred_element_type=jnp.float32)


def stack_heads(rows):
    lane = lax.broadcasted_iota(jnp.int32, rows.shape, 1)
    nought = jnp.zeros_like(rows)
    return jnp.concatenate(
        [jnp.where(lane < HEAD_DIM, rows, nought), jnp.where(lane >= HEAD_DIM, rows, nought)], axis=0
    )


def unstack_heads(wide):
    return jnp.concatenate([wide[:HEAD_DIM, :QBLOCK], wide[HEAD_DIM:, QBLOCK:]], axis=0).T


def masked_scores(span, queries, keys, key_docs, query_docs):
    scores = contract_last(keys, queries)
    same = key_docs == query_docs
    return jnp.where(jnp.concatenate([same, same], axis=1), scores, jnp.float32(far_below))


def attend_kernel(span, q_ref, k_ref, v_ref, kd_ref, qd_ref, o_ref, l_ref):
    first = pl.multiple_of(pl.program_id(1) * QBLOCK, QBLOCK)
    keys = k_ref[pl.ds(first, span), :]
    values = v_ref[pl.ds(first, span), :]
    scores = masked_scores(
        span, stack_heads(q_ref[...]), keys, kd_ref[pl.ds(first, span), :], qd_ref[0]
    )
    top = jnp.max(scores, axis=0, keepdims=True)
    expo = jnp.exp(scores - top)
    total = jnp.sum(expo, axis=0, keepdims=True)
    probs = (expo * (1.0 / total)).astype(jnp.bfloat16)
    o_ref[...] = unstack_heads(contract_rows(values, probs)).astype(jnp.bfloat16)
    l_ref[0, 0] = top + jnp.log(total)


def attend_back_kernel(
    span, q_ref, k_ref, v_ref, kd_ref, qd_ref, do_ref, l_ref, dq_ref, dk_ref, dv_ref, dk_acc, dv_acc
):
    step = pl.program_id(1)

    @pl.when(step == 0)
    def _():
        dk_acc[...] = jnp.zeros_like(dk_acc)
        dv_acc[...] = jnp.zeros_like(dv_acc)

    first = pl.multiple_of(step * QBLOCK, QBLOCK)
    here = pl.ds(first, span)
    keys = k_ref[here, :]
    values = v_ref[here, :]
    queries = stack_heads(q_ref[...])
    grads = stack_heads(do_ref[...])
    scores = masked_scores(span, queries, keys, kd_ref[here, :], qd_ref[0])
    probs = jnp.exp(scores - l_ref[0, 0])
    grad_probs = contract_last(values, grads)
    inner = jnp.sum(grad_probs * probs, axis=0, keepdims=True)
    grad_scores = (probs * (grad_probs - inner)).astype(jnp.bfloat16)
    grad_queries = unstack_heads(contract_rows(keys, grad_scores))
    dq_ref[...] = (grad_queries * (1.0 / math.sqrt(HEAD_DIM))).astype(jnp.bfloat16)
    dk_acc[here, :] += dot32(grad_scores, queries)
    dv_acc[here, :] += dot32(probs.astype(jnp.bfloat16), grads)

    @pl.when(step == pl.num_programs(1) - 1)
    def _():
        dk_ref[...] = dk_acc[...].astype(jnp.bfloat16)
        dv_ref[...] = dv_acc[...].astype(jnp.bfloat16)


def attention_specs(window):
    rows = pl.BlockSpec((QBLOCK, PAIR), lambda h, i: (i, h))
    keys = pl.BlockSpec((window, PAIR), lambda h, i: (0, h))
    key_docs = pl.BlockSpec((window, QBLOCK), lambda h, i: (0, 0))
    query_docs = pl.BlockSpec((1, 1, QBLOCK), lambda h, i: (i, 0, 0))
    logs = pl.BlockSpec((1, 1, 1, 2 * QBLOCK), lambda h, i: (h, i, 0, 0))
    return rows, keys, key_docs, query_docs, logs


def attend(queries, keys, values, key_docs, query_docs, reach):
    count, width = queries.shape
    window = keys.shape[0]
    blocks, pairs, span = count // QBLOCK, width // PAIR, QBLOCK + 2 * reach
    rows, key_spec, kd_spec, qd_spec, logs = attention_specs(window)
    return pl.pallas_call(
        partial(attend_kernel, span),
        grid=(pairs, blocks),
        in_specs=[rows, key_spec, key_spec, kd_spec, qd_spec],
        out_specs=[rows, logs],
        out_shape=[
            jax.ShapeDtypeStruct((count, width), jnp.bfloat16),
            jax.ShapeDtypeStruct((pairs, blocks, 1, 2 * QBLOCK), jnp.float32),
        ],
        compiler_params=pltpu.CompilerParams(vmem_limit_bytes=40 << 20),
        cost_estimate=pl.CostEstimate(
            flops=16 * count * span * width, bytes_accessed=8 << 20, transcendentals=0
        ),
        name="attend",
    )(queries, keys, values, key_docs, query_docs)


def attend_back(queries, keys, values, key_docs, query_docs, grads, logs_in, reach):
    count, width = queries.shape
    window = keys.shape[0]
    blocks, pairs, span = count // QBLOCK, width // PAIR, QBLOCK + 2 * reach
    rows, key_spec, kd_spec, qd_spec, logs = attention_specs(window)
    return pl.pallas_call(
        partial(attend_back_kernel, span),
        grid=(pairs, blocks),
        in_specs=[rows, key_spec, key_spec, kd_spec, qd_spec, rows, logs],
        out_specs=[rows, key_spec, key_spec],
        out_shape=[
            jax.ShapeDtypeStruct((count, width), jnp.bfloat16),
            jax.ShapeDtypeStruct((window, width), jnp.bfloat16),
            jax.ShapeDtypeStruct((window, width), jnp.bfloat16),
        ],
        scratch_shapes=[
            pltpu.VMEM((window, PAIR), jnp.float32),
            pltpu.VMEM((window, PAIR), jnp.float32),
        ],
        compiler_params=pltpu.CompilerParams(vmem_limit_bytes=40 << 20),
        cost_estimate=pl.CostEstimate(
            flops=40 * count * span * width, bytes_accessed=12 << 20, transcendentals=0
        ),
        name="attend_back",
    )(queries, keys, values, key_docs, query_docs, grads, logs_in)


def half_cols(position, half):
    return pl.ds(pl.multiple_of(position * half, half), half)


def add_or_set(first, ref, index, terms):
    @pl.when(first)
    def _():
        ref[index] = terms

    @pl.when(jnp.logical_not(first))
    def _():
        ref[index] += terms


def ffn_kernel(
    place_ref, hb_ref, up_ref, down_ref, bias_ref, acts_ref, slope_ref, own_ref, other_ref, total
):
    step = pl.program_id(0)
    half = up_ref.shape[3]
    count = own_ref.shape[0]
    near, far = half_cols(place_ref[1], half), half_cols(1 - place_ref[1], half)
    pre_act = dot32(hb_ref[:, near], up_ref[0, 0]) + dot32(hb_ref[:, far], up_ref[0, 1])
    pre_act += bias_ref[0]
    cdf = 0.5 * (1.0 + lax.erf(pre_act * math.sqrt(0.5)))
    bell = jnp.exp(-0.5 * pre_act * pre_act) * (1.0 / math.sqrt(2 * math.pi))
    acts = (pre_act * cdf).astype(jnp.bfloat16)
    acts_ref[...] = acts
    slope_ref[...] = (cdf + pre_act * bell).astype(jnp.bfloat16)
    add_or_set(step == 0, total, (slice(None), near), dot32(acts, down_ref[0, 0]))
    add_or_set(step == 0, total, (slice(None), far), dot32(acts, down_ref[0, 1]))

    @pl.when(step == pl.num_programs(0) - 1)
    def _():
        own_ref[...] = total[:count]
        other_ref[...] = total[count:].astype(jnp.bfloat16)


def ffn_back_kernel(
    place_ref,
    dz_ref,
    hb_ref,
    acts_ref,
    slope_ref,
    up_ref,
    down_ref,
    own_ref,
    other_ref,
    up_ref_out,
    down_ref_out,
    sums_ref,
    total,
):
    step = pl.program_id(0)
    half = up_ref.shape[3]
    count = own_ref.shape[0]
    near, far = half_cols(place_ref[1], half), half_cols(1 - place_ref[1], half)
    grad_acts = contract_last(dz_ref[:, near], down_ref[0, 0])
    grad_acts += contract_last(dz_ref[:, far], down_ref[0, 1])
    grad_pre = (slope_ref[...].astype(jnp.float32) * grad_acts).astype(jnp.bfloat16)
    sums_ref[0] = jnp.sum(grad_pre.astype(jnp.float32), axis=0, keepdims=True)
    add_or_set(step == 0, total, (slice(None), near), contract_last(grad_pre, up_ref[0, 0]))
    add_or_set(step == 0, total, (slice(None), far), contract_last(grad_pre, up_ref[0, 1]))
    for side, cols in enumerate((near, far)):
        up_grad = contract_rows(hb_ref[:, cols], grad_pre).astype(jnp.bfloat16)
        down_grad = contract_rows(acts_ref[...], dz_ref[:, cols]).astype(jnp.bfloat16)
        for x, place in enumerate((place_ref[3], 1 - place_ref[3])):
            rows = slice(x * half // 2, (x + 1) * half // 2)
            up_ref_out[place, side, 0] = up_grad[rows]
            down_ref_out[side, place, 0] = down_grad[rows]

    @pl.when(step == pl.num_programs(0) - 1)
    def _():
        own_ref[...] = total[:count]
        other_ref[...] = total[count:].astype(jnp.bfloat16)


def whole(shape):
    return pl.BlockSpec(shape, lambda *_: (0,) * len(shape))


def ffn(place, rows, weights, bias):
    both, width = rows.shape
    tps, shards, _, half = weights.shape
    count = both // 2
    matrix = (1, shards, half, half)
    block = pl.BlockSpec((both, half), lambda i, _: (0, i))
    return pl.pallas_call(
        ffn_kernel,
        grid_spec=pltpu.PrefetchScalarGridSpec(
            num_scalar_prefetch=1,
            grid=(tps,),
            in_specs=[
                whole((both, width)),
                pl.BlockSpec(matrix, lambda i, _: (i, 0, 0, 0)),
                pl.BlockSpec(matrix, lambda i, _: (i, 0, 1, 0)),
                pl.BlockSpec((1, 1, half), lambda i, _: (i, 0, 0)),
            ],
            out_specs=[block, block, whole((count, width)), whole((count, width))],
            scratch_shapes=[pltpu.VMEM((both, width), jnp.float32)],
        ),
        out_shape=[
            jax.ShapeDtypeStruct((both, tps * half), jnp.bfloat16),
            jax.ShapeDtypeStruct((both, tps * half), jnp.bfloat16),
            jax.ShapeDtypeStruct((count, width), jnp.float32),
            jax.ShapeDtypeStruct((count, width), jnp.bfloat16),
        ],
        compiler_params=pltpu.CompilerParams(vmem_limit_bytes=40 << 20),
        cost_estimate=pl.CostEstimate(
            flops=12 * both * width * tps * half, bytes_accessed=12 << 20, transcendentals=0
        ),
        name="ffn",
    )(place, rows, weights, weights, bias)


def ffn_back(place, grads, rows, acts, slope, weights):
    both, width = rows.shape
    tps, shards, _, half = weights.shape
    count = both // 2
    matrix = (1, shards, half, half)
    block = pl.BlockSpec((both, half), lambda i, _: (0, i))

    def source(i, place_ref):
        return (place_ref[2] + tps - i) % tps

    parts = pl.BlockSpec(
        (2, 2, 1, half // 2, half), lambda i, at: (0, 0, source(i, at), 0, 0)
    )
    return pl.pallas_call(
        ffn_back_kernel,
        grid_spec=pltpu.PrefetchScalarGridSpec(
            num_scalar_prefetch=1,
            grid=(tps,),
            in_specs=[
                whole((both, width)),
                whole((both, width)),
                block,
                block,
                pl.BlockSpec(matrix, lambda i, _: (i, 0, 0, 0)),
                pl.BlockSpec(matrix, lambda i, _: (i, 0, 1, 0)),
            ],
            out_specs=[
                whole((count, width)),
                whole((count, width)),
                parts,
                parts,
                pl.BlockSpec((1, 1, half), lambda i, at: (source(i, at), 0, 0)),
            ],
            scratch_shapes=[pltpu.VMEM((both, width), jnp.float32)],
        ),
        out_shape=[
            jax.ShapeDtypeStruct((count, width), jnp.float32),
            jax.ShapeDtypeStruct((count, width), jnp.bfloat16),
            jax.ShapeDtypeStruct((2, 2, tps, half // 2, half), jnp.bfloat16),
            jax.ShapeDtypeStruct((2, 2, tps, half // 2, half), jnp.bfloat16),
            jax.ShapeDtypeStruct((tps, 1, half), jnp.float32),
        ],
        compiler_params=pltpu.CompilerParams(vmem_limit_bytes=48 << 20),
        cost_estimate=pl.CostEstimate(
            flops=12 * both * width * tps * half, bytes_accessed=20 << 20, transcendentals=0
        ),
        name="ffn_back",
    )(place, grads, rows, acts, slope, weights, weights)


def project_kernel(
    place_ref, w_mine, w_other, x_mine, x_other, bias_ref, q_ref, k_ref, v_ref, x_ref, wt
):
    core, shard, tp, across, start = (place_ref[i] for i in range(5))
    depth = w_mine.shape[3]
    width = x_ref.shape[1]
    part = width // 8
    length = 4 * x_mine.shape[2]
    reach = length // 2
    for c, source in enumerate((w_mine, w_other)):
        for y in (0, 1):
            cols = half_cols(shard + y - 2 * shard * y, depth)
            for k in range(4):
                row = ((tp + 4 - k) & 3) * 2 + core + c - 2 * core * c
                rows = pl.ds(pl.multiple_of(row * part, part), part)
                for m in range(3):
                    wt[m, rows, cols] = source[y, k, m * part : (m + 1) * part]
    for i in range(x_ref.shape[0] // QBLOCK):
        row = start - reach + i * QBLOCK
        inside = jnp.logical_and(row >= 0, row < 2 * length)
        at = jnp.where(inside, row, 0) // QBLOCK
        seq, block, piece = at // 8, (at // 2) & 3, at & 1
        here = jnp.where((block >> 1) == across, 0, 1)
        rows = pl.ds(pl.multiple_of(piece * QBLOCK, QBLOCK), QBLOCK)
        mine, other = x_mine[here, seq, rows], x_other[here, seq, rows]
        found = jnp.where((block & 1) == core, mine, other)
        x_ref[i * QBLOCK : (i + 1) * QBLOCK] = jnp.where(inside, found, jnp.zeros_like(found))
    count = q_ref.shape[0]
    scaled = contract_last(x_ref[reach : reach + count], wt[0]) + bias_ref[0:1]
    q_ref[...] = (scaled * (1.0 / math.sqrt(HEAD_DIM))).astype(jnp.bfloat16)
    chunk = x_ref.shape[0] // 4

    @pl.loop(0, 4)
    def _(step):
        rows = pl.ds(pl.multiple_of(step * chunk, 32), chunk)
        k_ref[rows] = contract_last(x_ref[rows], wt[1]).astype(jnp.bfloat16)
        v_ref[rows] = (contract_last(x_ref[rows], wt[2]) + bias_ref[1:2]).astype(jnp.bfloat16)


def project(place, w_mine, w_other, x_mine, x_other, biases, count, window):
    width = x_mine.shape[-1]
    return pl.pallas_call(
        project_kernel,
        in_specs=[pl.BlockSpec(memory_space=pltpu.SMEM)]
        + [pl.BlockSpec(memory_space=pltpu.VMEM)] * 5,
        out_specs=[pl.BlockSpec(memory_space=pltpu.VMEM)] * 5,
        out_shape=[
            jax.ShapeDtypeStruct((count, width), jnp.bfloat16),
            jax.ShapeDtypeStruct((window, width), jnp.bfloat16),
            jax.ShapeDtypeStruct((window, width), jnp.bfloat16),
            jax.ShapeDtypeStruct((window, width), jnp.bfloat16),
            jax.ShapeDtypeStruct((3, width, width), jnp.bfloat16),
        ],
        compiler_params=pltpu.CompilerParams(vmem_limit_bytes=40 << 20),
        cost_estimate=pl.CostEstimate(
            flops=4 * window * width * width, bytes_accessed=16 << 20, transcendentals=0
        ),
        name="project",
    )(place, w_mine, w_other, x_mine, x_other, biases)


def norm_pieces(resid):
    center = resid - jnp.mean(resid, axis=-1, keepdims=True)
    inv_std = lax.rsqrt(jnp.mean(center * center, axis=-1, keepdims=True) + eps_norm)
    return center * inv_std, inv_std


def norm_pull(grad_out, normed, inv_std, gain):
    grad_normed = grad_out * gain
    return inv_std * (
        grad_normed
        - jnp.mean(grad_normed, axis=-1, keepdims=True)
        - normed * jnp.mean(grad_normed * normed, axis=-1, keepdims=True)
    )


def row_sum(rows):
    return jnp.sum(rows, axis=0, keepdims=True)


def attend_out_kernel(
    place_ref, o_ref, x_ref, w_mine, w_other, vec_ref, h_ref, hb_ref, n_ref, i_ref, wo_ref
):
    core, shard, tp = (place_ref[i] for i in range(3))
    part, depth = w_mine.shape[2:]
    for c, source in enumerate((w_mine, w_other)):
        for y in (0, 1):
            cols = half_cols(shard + y - 2 * shard * y, depth)
            for k in range(4):
                row = ((tp + 4 - k) & 3) * 2 + core + c - 2 * core * c
                rows = pl.ds(pl.multiple_of(row * part, part), part)
                wo_ref[rows, cols] = source[k, y]
    resid = x_ref[...].astype(jnp.float32) + dot32(o_ref[...], wo_ref[...]) + vec_ref[0:1]
    normed, inv_std = norm_pieces(resid)
    hidden = normed * vec_ref[1:2] + vec_ref[2:3]
    h_ref[...] = hidden
    hb_ref[...] = hidden.astype(jnp.bfloat16)
    n_ref[...] = normed
    i_ref[...] = jnp.broadcast_to(inv_std, i_ref.shape)


def attend_out(place, mixed, rows, w_mine, w_other, vectors):
    count, width = mixed.shape
    vmem = pl.BlockSpec(memory_space=pltpu.VMEM)
    return pl.pallas_call(
        attend_out_kernel,
        in_specs=[pl.BlockSpec(memory_space=pltpu.SMEM)] + [vmem] * 5,
        out_specs=[vmem] * 5,
        out_shape=[
            jax.ShapeDtypeStruct((count, width), jnp.float32),
            jax.ShapeDtypeStruct((count, width), jnp.bfloat16),
            jax.ShapeDtypeStruct((count, width), jnp.float32),
            jax.ShapeDtypeStruct((count, QBLOCK), jnp.float32),
            jax.ShapeDtypeStruct((width, width), jnp.bfloat16),
        ],
        compiler_params=pltpu.CompilerParams(vmem_limit_bytes=40 << 20),
        cost_estimate=pl.CostEstimate(
            flops=2 * count * width * width, bytes_accessed=8 << 20, transcendentals=0
        ),
        name="attend_out",
    )(place, mixed, rows, w_mine, w_other, vectors)


def ffn_norm_kernel(h_ref, own_ref, got_ref, g_ref, vec_ref, y_ref, dr_ref, dz_ref, sums_ref):
    resid = h_ref[...] + own_ref[...] + got_ref[...].astype(jnp.float32) + vec_ref[0:1]
    normed, inv_std = norm_pieces(resid)
    y_ref[...] = (normed * vec_ref[1:2] + vec_ref[2:3]).astype(jnp.bfloat16)
    grad_out = g_ref[...].astype(jnp.float32)
    grad = norm_pull(grad_out, normed, inv_std, vec_ref[1:2])
    low = grad.astype(jnp.bfloat16)
    dr_ref[...] = grad
    dz_ref[...] = low
    sums_ref[0:1] = row_sum(low.astype(jnp.float32))
    sums_ref[1:2] = row_sum(grad_out * normed)
    sums_ref[2:3] = row_sum(grad_out)


def ffn_norm(hidden, own, got, cots, vectors):
    count, width = hidden.shape
    vmem = pl.BlockSpec(memory_space=pltpu.VMEM)
    return pl.pallas_call(
        ffn_norm_kernel,
        in_specs=[vmem] * 5,
        out_specs=[vmem] * 4,
        out_shape=[
            jax.ShapeDtypeStruct((count, width), jnp.bfloat16),
            jax.ShapeDtypeStruct((count, width), jnp.float32),
            jax.ShapeDtypeStruct((count, width), jnp.bfloat16),
            jax.ShapeDtypeStruct((3, width), jnp.float32),
        ],
        compiler_params=pltpu.CompilerParams(vmem_limit_bytes=40 << 20),
        cost_estimate=pl.CostEstimate(
            flops=30 * count * width, bytes_accessed=7 << 20, transcendentals=0
        ),
        name="ffn_norm",
    )(hidden, own, got, cots, vectors)


def attend_norm_kernel(
    dr_ref, own_ref, got_ref, n_ref, i_ref, vec_ref, wo_ref, out_ref, da_ref, do_ref, sums_ref
):
    grad_out = dr_ref[...] + own_ref[...] + got_ref[...].astype(jnp.float32)
    normed = n_ref[...]
    grad = norm_pull(grad_out, normed, i_ref[:, :1], vec_ref[1:2])
    low = grad.astype(jnp.bfloat16)
    out_ref[...] = grad
    da_ref[...] = low
    do_ref[...] = contract_last(low, wo_ref[...]).astype(jnp.bfloat16)
    sums_ref[0:1] = row_sum(low.astype(jnp.float32))
    sums_ref[1:2] = row_sum(grad_out * normed)
    sums_ref[2:3] = row_sum(grad_out)


def attend_norm(grads, own, got, normed, inv_std, vectors, weights):
    count, width = grads.shape
    vmem = pl.BlockSpec(memory_space=pltpu.VMEM)
    return pl.pallas_call(
        attend_norm_kernel,
        in_specs=[vmem] * 7,
        out_specs=[vmem] * 4,
        out_shape=[
            jax.ShapeDtypeStruct((count, width), jnp.float32),
            jax.ShapeDtypeStruct((count, width), jnp.bfloat16),
            jax.ShapeDtypeStruct((count, width), jnp.bfloat16),
            jax.ShapeDtypeStruct((3, width), jnp.float32),
        ],
        compiler_params=pltpu.CompilerParams(vmem_limit_bytes=40 << 20),
        cost_estimate=pl.CostEstimate(
            flops=2 * count * width * width, bytes_accessed=9 << 20, transcendentals=0
        ),
        name="attend_norm",
    )(grads, own, got, normed, inv_std, vectors, weights)


def attn_grads_kernel(
    place_ref, dq_ref, dk_ref, dv_ref, o_ref, da_ref, x_ref, w_ref, sums_ref, parts_ref
):
    core, shard, across = place_ref[0], place_ref[1], place_ref[3]
    depth = parts_ref.shape[5]
    part = depth // 4
    sides = (
        (dq_ref, x_ref),
        (dk_ref, w_ref),
        (dv_ref, w_ref),
        (o_ref, da_ref),
    )
    for m, (left, right) in enumerate(sides):
        grad = contract_rows(left[...], right[...]).astype(jnp.bfloat16)
        group = across if m < 2 else 1 - across
        rows = slice((m % 2) * part, (m % 2 + 1) * part)
        for z in (0, 1):
            for c in (0, 1):
                piece = grad[(2 * z + c) * part : (2 * z + c + 1) * part]
                to = c + core - 2 * c * core
                parts_ref[to, group, shard, z, rows] = piece[:, :depth]
                parts_ref[to, group, 1 - shard, z, rows] = piece[:, depth:]
    extra = sums_ref.shape[3]
    for c in (0, 1):
        for y in (0, 1):
            parts_ref[c, across, y, :, 2 * part :] = sums_ref[c, 0]
            parts_ref[c, 1 - across, y, :, 2 * part :] = sums_ref[c, 1]


def attn_grads(place, grad_queries, grad_keys, grad_values, mixed, grad_attn, rows, near, sums):
    count, width = rows.shape
    window = near.shape[0]
    depth = width // 2
    extra = sums.shape[3]
    high = depth // 2 + extra
    cols = pl.BlockSpec((count, depth), lambda i, _: (0, i))
    near_cols = pl.BlockSpec((window, depth), lambda i, _: (0, i))
    return pl.pallas_call(
        attn_grads_kernel,
        grid_spec=pltpu.PrefetchScalarGridSpec(
            num_scalar_prefetch=1,
            grid=(2,),
            in_specs=[
                cols,
                near_cols,
                near_cols,
                cols,
                whole((count, width)),
                whole((count, width)),
                whole((window, width)),
                pl.BlockSpec((2, 2, 2, extra, depth), lambda i, _: (0, 0, i, 0, 0)),
            ],
            out_specs=pl.BlockSpec((2, 2, 2, 2, high, depth), lambda i, _: (0, 0, 0, i, 0, 0)),
        ),
        out_shape=jax.ShapeDtypeStruct((2, 2, 2, 4, high, depth), jnp.bfloat16),
        compiler_params=pltpu.CompilerParams(vmem_limit_bytes=48 << 20),
        cost_estimate=pl.CostEstimate(
            flops=4 * (window + count) * width * width, bytes_accessed=16 << 20, transcendentals=0
        ),
        name="attn_grads",
    )(place, grad_queries, grad_keys, grad_values, mixed, grad_attn, rows, near, sums)


def span_grads_kernel(
    place_ref, dq_ref, dk_ref, dv_ref, w_ref, base_ref, own_ref, onward_ref, give_ref
):
    core = place_ref[0]
    count, reach = own_ref.shape[0], give_ref.shape[0]

    def near(rows):
        return dot32(dk_ref[rows], w_ref[1]) + dot32(dv_ref[rows], w_ref[2])

    far = count + reach
    low = pl.ds(pl.multiple_of(core * far, QBLOCK), reach)
    high = pl.ds(pl.multiple_of((1 - core) * far, QBLOCK), reach)
    give_ref[...] = near(high).astype(jnp.bfloat16)
    onward_ref[...] = near(low).astype(jnp.bfloat16)
    own_ref[...] = base_ref[...] + dot32(dq_ref[...], w_ref[0]) + near(pl.ds(reach, count))


def span_grads(place, grad_queries, grad_keys, grad_values, weights, base):
    count, width = base.shape
    reach = (grad_keys.shape[0] - count) // 2
    vmem = pl.BlockSpec(memory_space=pltpu.VMEM)
    return pl.pallas_call(
        span_grads_kernel,
        in_specs=[pl.BlockSpec(memory_space=pltpu.SMEM)] + [vmem] * 5,
        out_specs=[vmem] * 3,
        out_shape=[
            jax.ShapeDtypeStruct((count, width), jnp.float32),
            jax.ShapeDtypeStruct((reach, width), jnp.bfloat16),
            jax.ShapeDtypeStruct((reach, width), jnp.bfloat16),
        ],
        compiler_params=pltpu.CompilerParams(vmem_limit_bytes=40 << 20),
        cost_estimate=pl.CostEstimate(
            flops=4 * (count + 2 * reach) * width * width,
            bytes_accessed=12 << 20,
            transcendentals=0,
        ),
        name="span_grads",
    )(place, grad_queries, grad_keys, grad_values, weights, base)


def ctx_swap(array, bit):
    return lax.ppermute(array, "ctx", [(i, i ^ bit) for i in range(4)])


def core_swap(array):
    return ctx_swap(array, 1)


def tie(*arrays):
    return lax.optimization_barrier(arrays)


def across_swap(array):
    return ctx_swap(array, 2)


def in_order(flag, mine, other):
    return jnp.where(flag == 0, mine, other), jnp.where(flag == 0, other, mine)


def at(across, core, tp):
    return (2 * across + core) * 4 + tp


def across_pairs():
    pairs = []
    for tp in range(4):
        for across in (0, 1):
            core = across ^ (tp & 1)
            pairs.append((at(1 - across, core, tp), at(across, core, tp)))
    return pairs


def tp_shifts(array):
    return [
        lax.ppermute(array, "tp", [(i, (i + shift) % 4) for i in range(4)]) for shift in (1, 2, 3)
    ]


def by_tp(array, shifted):
    one, two, three = shifted
    line = jnp.stack([three, two, one, array, three, two, one])
    return lax.dynamic_slice_in_dim(line, 3 - lax.axis_index("tp"), 4, 0)


def shard_swap(array):
    return lax.ppermute(array, "shard", [(0, 1), (1, 0)])


def low_sum(left, right):
    return (left.astype(jnp.float32) + right.astype(jnp.float32)).astype(jnp.bfloat16)


def scatter_tp_start(parts):
    tp = lax.axis_index("tp")
    moved = [lax.dynamic_index_in_dim(parts, tp, 0, keepdims=False)]
    for shift in (1, 2, 3):
        sent = lax.dynamic_index_in_dim(parts, (tp + shift) & 3, 0, keepdims=False)
        moved.append(lax.ppermute(sent, "tp", [(i, (i + shift) % 4) for i in range(4)]))
    return moved


def scatter_tp_end(moved):
    return sum(part.astype(jnp.float32) for part in moved).astype(jnp.bfloat16)


def chain_pairs():
    pairs = []
    for group in (0, 2):
        path = [(0, group), (0, group + 1), (1, group + 1), (1, group)]
        for (across, tp), (next_across, next_tp) in zip(path[:-1], path[1:]):
            pairs.append((at(across, 1, tp), at(next_across, 0, next_tp)))
            pairs.append((at(next_across, 0, next_tp), at(across, 1, tp)))
    return pairs


def span_shards(
    layer_input,
    segment_ids,
    query_proj,
    query_bias,
    key_proj,
    value_proj,
    value_bias,
    out_proj,
    out_bias,
    attn_gain,
    attn_shift,
    up_proj,
    up_bias,
    down_proj,
    down_bias,
    ffn_gain,
    ffn_shift,
    out_cotangent,
):
    seqs, block, width = layer_input.shape
    length = segment_ids.shape[1]
    reach = length // 2
    count = seqs * block // 4
    window = count + 2 * reach
    bf16, f32 = jnp.bfloat16, jnp.float32
    ctx, tp = lax.axis_index("ctx"), lax.axis_index("tp")
    shard = lax.axis_index("shard")
    core, across, side = ctx & 1, ctx >> 1, tp & 1
    place = 2 * across + (side ^ across)
    odd = across ^ side

    heads = query_proj.shape[1]
    half = heads // 2
    depth = query_proj.shape[0]
    cut = up_proj.shape[1] // 2
    own_in = lax.dynamic_slice_in_dim(
        jnp.stack([query_proj.T, key_proj.T, value_proj.T]), core * half, half, 1
    ).reshape(3 * half, depth)
    own_biases = jnp.stack(
        [
            jnp.concatenate([query_bias, value_bias]),
            lax.dynamic_slice_in_dim(up_bias, core * cut, cut, 0),
        ]
    )
    own_in = jnp.concatenate([own_in, own_biases, jnp.zeros((14, depth), bf16)], axis=0)
    out_half = out_proj.shape[0] // 2
    own_rest = jnp.concatenate(
        [
            lax.dynamic_slice_in_dim(up_proj, core * cut, cut, 1),
            lax.dynamic_slice_in_dim(down_proj, core * cut, cut, 0),
            lax.dynamic_slice_in_dim(out_proj, core * out_half, out_half, 0),
        ],
        axis=0,
    )
    first_seq = 3 * (tp >> 1)
    mine = lax.dynamic_slice_in_dim(layer_input, first_seq + across, 2, 0)
    theirs = across_swap(lax.dynamic_slice_in_dim(layer_input, first_seq + 1 - across, 2, 0))
    in_shifted = tp_shifts(own_in)
    rest_far = [shard_swap(own_rest)]
    *in_shifted, theirs, rest_far[0] = tie(*in_shifted, theirs, rest_far[0])
    in_near = jnp.stack([own_in] + in_shifted)
    rest_near = [own_rest] + tp_shifts(tie(own_rest, in_near)[0])
    in_far, rest_near[1] = tie(shard_swap(in_near), rest_near[1])
    in_mine = jnp.stack([in_near, in_far])
    in_other = core_swap(in_mine)
    bias_rows = in_mine[0, :, 3 * half]
    in_biases = by_tp(bias_rows[0], [bias_rows[1], bias_rows[2], bias_rows[3]]).astype(f32)
    in_biases = jnp.stack([in_biases[:, :heads].reshape(-1), in_biases[:, heads:].reshape(-1)])
    up_bias_here = in_mine[0, :, 3 * half + 1].reshape(4, 1, cut).astype(f32)

    pair = jnp.stack([mine, theirs])
    pair_other = core_swap(pair)
    start = 2 * count * place + count * core - length * across
    ids = lax.dynamic_slice_in_dim(segment_ids, first_seq + across, 2, 0)
    ids = (ids + jnp.array([[0], [1 << 16]], jnp.int32)).reshape(-1)
    no_doc = jnp.full((reach,), -1, jnp.int32)
    window_docs = lax.dynamic_slice_in_dim(
        jnp.concatenate([no_doc, ids, no_doc]), start, window, 0
    )
    key_docs = jnp.broadcast_to(window_docs[:, None], (window, QBLOCK))
    query_docs = window_docs[reach : reach + count].reshape(-1, 1, QBLOCK)

    place = jnp.stack([core, shard, tp, across, start])
    far_one = shard_swap(rest_near[1])
    queries, keys, values, in_window, weights_t = project(
        place, in_mine, in_other, pair, pair_other, in_biases, count, window
    )
    rows_in = in_window[reach : reach + count]
    queries, rest_near[3], far_one = tie(queries, rest_near[3], far_one)
    far_three = shard_swap(rest_near[3])
    mixed, logs = attend(queries, keys, values, key_docs, query_docs, reach)
    mixed, far_three, rest_near[2] = tie(mixed, far_three, rest_near[2])
    far_two = shard_swap(rest_near[2])
    rest_far += [far_one, far_two, far_three]
    rest = jnp.stack([jnp.stack(both) for both in zip(rest_near, rest_far)])
    out_mine = rest[:, :, 2 * cut :]
    attn_vectors = jnp.stack([out_bias, attn_gain, attn_shift]).astype(f32)
    hidden, hidden_low, normed_one, inv_one, full_out = attend_out(
        place, mixed, rows_in, out_mine, core_swap(out_mine), attn_vectors
    )
    hidden_both = jnp.concatenate([hidden_low, core_swap(hidden_low)], axis=0)
    acts, slope, ffn_own, ffn_other = ffn(place, hidden_both, rest, up_bias_here)

    def deliver_start(rows):
        chip = jnp.concatenate(in_order(core, rows, core_swap(rows)), axis=0)
        kept = lax.dynamic_slice_in_dim(chip, odd * block + core * block, block, 0)
        half_block = block // 2
        sent = lax.dynamic_slice_in_dim(
            chip, (1 - odd) * 2 * block + core * half_block, half_block, 0
        )
        packed = jnp.concatenate([kept, across_swap(sent)], axis=0)
        return packed, tp_shifts(packed)

    def deliver_end(packed, shifted):
        every = by_tp(packed, shifted)
        halves = every[:, block:]
        lo, hi = in_order(core, halves, core_swap(halves))
        moved = jnp.concatenate([lo, hi], axis=1)
        kept_all = every[:, :block]
        from_side = 1 ^ across ^ core
        parts = []
        for group in (0, 2):
            foreign = lax.dynamic_index_in_dim(moved, group + from_side, 0, keepdims=False)
            near_one, mid_one = kept_all[group], kept_all[group + 1]
            parts += [
                jnp.where(across == 0, near_one, foreign),
                mid_one,
                jnp.where(across == 0, foreign, near_one),
            ]
        return jnp.stack(parts)

    near_cot = lax.dynamic_index_in_dim(
        out_cotangent, first_seq + odd + across, 0, keepdims=False
    )
    far_cot = lax.ppermute(
        lax.dynamic_index_in_dim(out_cotangent, first_seq + 2 - 2 * across, 0, keepdims=False),
        ("ctx", "tp"),
        across_pairs(),
    )
    cot_pair = jnp.stack([near_cot, far_cot])
    cot_swapped = core_swap(cot_pair)
    low_cot, high_cot = in_order(core, near_cot, cot_swapped[0])
    far_cot = jnp.where(core == odd, far_cot, cot_swapped[1])
    chip_cot = jnp.where(
        odd == 0,
        jnp.concatenate([low_cot, high_cot, far_cot], axis=0),
        jnp.concatenate([far_cot, low_cot, high_cot], axis=0),
    )
    cot_rows = lax.dynamic_slice_in_dim(chip_cot, core * count, count, 0)


    ffn_vectors = jnp.stack([down_bias, ffn_gain, ffn_shift]).astype(f32)
    output_rows, grad_two, grad_ffn, ffn_sums = ffn_norm(
        hidden, ffn_own, core_swap(ffn_other), cot_rows, ffn_vectors
    )
    grad_ffn_both = jnp.concatenate([grad_ffn, core_swap(grad_ffn)], axis=0)
    out_packed, out_shifted = deliver_start(output_rows)
    grad_ffn_both, out_packed = lax.optimization_barrier((grad_ffn_both, out_packed))
    back_own, back_other, up_parts, down_parts, up_sums = ffn_back(
        place, grad_ffn_both, hidden_both, acts, slope, rest
    )
    back_own, out_shifted[0] = tie(back_own, out_shifted[0])
    grad_one, grad_attn, grad_mixed, attn_sums = attend_norm(
        grad_two, back_own, core_swap(back_other), normed_one, inv_one, attn_vectors, full_out
    )
    up_got = across_swap(up_parts[1])
    down_got = shard_swap(down_parts[1])
    grad_scaled, grad_keys, grad_values = attend_back(
        queries, keys, values, key_docs, query_docs, grad_mixed, logs, reach
    )
    grad_keys, grad_values, up_got, down_got = tie(grad_keys, grad_values, up_got, down_got)
    up_parts = low_sum(up_parts[0], up_got)
    down_parts = low_sum(down_parts[0], down_got)
    up_got = shard_swap(up_parts[1])
    down_got = across_swap(down_parts[1])
    own_sum, onward, give = span_grads(
        place, grad_scaled, grad_keys, grad_values, weights_t, grad_one
    )
    got = core_swap(give)
    got, *out_shifted = tie(got, *out_shifted)
    shared = reach - count
    to_own = lax.dynamic_slice_in_dim(got, (1 - core) * shared, count, 0)
    to_next = lax.dynamic_slice_in_dim(got, core * count, shared, 0)
    next_at = (1 - core) * count
    to_next = low_sum(lax.dynamic_slice_in_dim(onward, next_at, shared, 0), to_next)
    onward = lax.dynamic_update_slice_in_dim(onward, to_next, next_at, 0)
    arrived = lax.ppermute(onward, ("ctx", "tp"), chain_pairs())
    head_sums = jnp.concatenate(
        [
            jnp.sum(grad_scaled, axis=0, dtype=f32).reshape(4, 1, heads),
            jnp.sum(grad_values, axis=0, dtype=f32).reshape(4, 1, heads),
        ],
        axis=2,
    )
    row_sums = jnp.concatenate([attn_sums, ffn_sums], axis=0).reshape(12, depth)
    sums = jnp.concatenate(
        [head_sums, jnp.broadcast_to(row_sums, (4, 12, depth))], axis=1
    ).astype(bf16)
    up_sums = up_sums.astype(bf16)
    no_sum = jnp.zeros_like(up_sums)
    sums = jnp.stack(
        [
            jnp.concatenate([sums, up_sums, no_sum, no_sum], axis=1),
            jnp.concatenate([sums, no_sum, no_sum, no_sum], axis=1),
        ]
    )
    sums = sums.reshape(2, 4, 2, 8, depth).transpose(0, 2, 1, 3, 4)
    grad_keys, onward = tie(grad_keys, onward)
    attn_parts = attn_grads(
        place,
        grad_scaled,
        grad_keys,
        grad_values,
        mixed,
        grad_attn,
        rows_in,
        in_window,
        sums,
    )
    arrived, up_got, down_got, attn_parts = tie(arrived, up_got, down_got, attn_parts)
    ffn_parts = jnp.concatenate(
        [low_sum(up_parts[0], up_got), low_sum(down_parts[0], down_got)], axis=1
    )
    ffn_near = scatter_tp_start(ffn_parts)
    attn_parts = low_sum(attn_parts[0], core_swap(attn_parts[1]))
    passed = core_swap(lax.dynamic_slice_in_dim(arrived, next_at, shared, 0)).astype(f32)
    own_sum += to_own.astype(f32)
    own_sum += lax.dynamic_slice_in_dim(arrived, core * shared, count, 0).astype(f32)
    rest_rows = jnp.zeros((count - shared, width), f32)
    own_sum += jnp.where(
        core == 0,
        jnp.concatenate([rest_rows, passed], axis=0),
        jnp.concatenate([passed, rest_rows], axis=0),
    )
    own_sum, attn_parts = tie(own_sum, attn_parts)
    attn_got = across_swap(attn_parts[1])
    in_packed, in_moved = deliver_start(own_sum.astype(bf16))
    attn_got, ffn_near = tie(attn_got, ffn_near)
    attn_mid = low_sum(attn_parts[0], attn_got)
    attn_got = shard_swap(attn_mid[1])
    ffn_low = scatter_tp_end(ffn_near)
    ffn_got = across_swap(ffn_low)
    in_moved, attn_got, ffn_got = tie(in_moved, attn_got, ffn_got)
    attn_near = scatter_tp_start(low_sum(attn_mid[0], attn_got))
    layer_output = deliver_end(out_packed, out_shifted)
    input_grad = deliver_end(in_packed, in_moved).astype(f32)


    def spread(low, got):
        mine = jnp.stack(in_order(across, low, got))
        return in_order(core, mine, core_swap(mine))

    ffn_lo, ffn_hi = spread(ffn_low, ffn_got)
    attn_low = scatter_tp_end(attn_near)
    attn_lo, attn_hi = spread(attn_low, across_swap(attn_low))
    quarter = cut // 2
    up_grad, down_grad = (
        [part[:, at : at + quarter].reshape(cut, cut) for part in (ffn_lo, ffn_hi)]
        for at in (0, quarter)
    )
    up_grad = jnp.concatenate(up_grad, axis=1).astype(f32)
    down_grad = jnp.concatenate(down_grad, axis=0).astype(f32)
    weight_grads = [
        jnp.concatenate(
            [part[m // 2, (m % 2) * half : (m % 2 + 1) * half] for part in (attn_lo, attn_hi)], axis=0
        ).astype(f32)
        for m in range(4)
    ]
    sums = attn_lo[:, 2 * half :].astype(f32).reshape(16, depth)
    row_sums = sums[1:13].reshape(6, width)
    up_bias_grad = jnp.concatenate([sums[13], attn_hi[1, 2 * half + 5].astype(f32)])
    return (
        layer_output,
        input_grad,
        weight_grads[0].T,
        sums[0, :heads],
        weight_grads[1].T,
        weight_grads[2].T,
        sums[0, heads:],
        weight_grads[3],
        row_sums[0],
        row_sums[1],
        row_sums[2],
        up_grad,
        up_bias_grad,
        down_grad,
        row_sums[3],
        row_sums[4],
        row_sums[5],
    )


def pick_plan(mesh):
    shape = dict(mesh.shape)

    def plan(layer_input, segment_ids, *others):
        seqs, block, _ = layer_input.shape
        fits = (
            (shape["shard"], shape["ctx"], shape["tp"]) == (2, 4, 4)
            and seqs == 6
            and segment_ids.shape[1] == 4 * block
            and block == 2 * QBLOCK
        )
        chosen = span_shards if fits else general_shards
        return chosen(layer_input, segment_ids, *others)

    return plan


def solution(mesh):
    return jax.shard_map(
        pick_plan(mesh),
        mesh=mesh,
        in_specs=(
            P("shard", "ctx", None),
            P("shard", None),
            P("shard", "tp"),
            P("tp"),
            P("shard", "tp"),
            P("shard", "tp"),
            P("tp"),
            P("tp", "shard"),
            P(),
            P(),
            P(),
            P("shard", "tp"),
            P("tp"),
            P("tp", "shard"),
            P(),
            P(),
            P(),
            P("shard", "ctx", None),
        ),
        out_specs=(
            P("shard", "ctx", None),
            P("shard", "ctx", None),
            P("shard", "tp"),
            P("tp"),
            P("shard", "tp"),
            P("shard", "tp"),
            P("tp"),
            P("tp", "shard"),
            P(),
            P(),
            P(),
            P("shard", "tp"),
            P("tp"),
            P("tp", "shard"),
            P(),
            P(),
            P(),
        ),
        check_vma=False,
    )
```

```python
from functools import partial
import math

import jax
import jax.numpy as jnp
from jax import lax
from jax.experimental import pallas as pl
from jax.experimental.pallas import tpu as pltpu
from jax.sharding import PartitionSpec as P

HEAD_DIM = 64


eps_norm = 1e-12
far_below = -1e30


def contract_rows(left, right):
    return lax.dot_general(
        left, right, (((0,), (0,)), ((), ())), preferred_element_type=jnp.float32
    )


def contract_last(left, right):
    return lax.dot_general(
        left, right, (((1,), (1,)), ((), ())), preferred_element_type=jnp.float32
    )


def norm_forward(resid, norm_gain, norm_shift):
    center = resid - jnp.mean(resid, axis=-1, keepdims=True)
    inv_std = lax.rsqrt(jnp.mean(center * center, axis=-1, keepdims=True) + eps_norm)
    normed = center * inv_std
    return (normed * norm_gain + norm_shift, normed, inv_std)


def norm_backward(grad_out, normed, inv_std, norm_gain):
    grad_normed = grad_out * norm_gain
    grad_in = inv_std * (
        grad_normed
        - jnp.mean(grad_normed, axis=-1, keepdims=True)
        - normed * jnp.mean(grad_normed * normed, axis=-1, keepdims=True)
    )
    return (grad_in, jnp.sum(grad_out * normed, axis=0), jnp.sum(grad_out, axis=0))


def split_heads(matrix):
    return matrix.reshape(matrix.shape[0], matrix.shape[1] // HEAD_DIM, HEAD_DIM)


def scores_of(queries, keys_all, query_docs, key_docs):
    scores = jnp.einsum(
        "qhd,khd->hqk",
        split_heads(queries),
        split_heads(keys_all),
        preferred_element_type=jnp.float32,
    )
    same_doc = (query_docs[:, None] == key_docs[None, :])[None]
    return jnp.where(same_doc, scores, jnp.float32(far_below))


def attend_forward(item):
    queries, keys_all, values_all, query_docs, key_docs = item
    scores = scores_of(queries, keys_all, query_docs, key_docs)
    top_score = jnp.max(scores, axis=-1, keepdims=True)
    expo = jnp.exp(scores - top_score)
    total = jnp.sum(expo, axis=-1, keepdims=True)
    probs = (expo / total).astype(jnp.bfloat16)
    mixed = jnp.einsum(
        "hqk,khd->qhd", probs, split_heads(values_all), preferred_element_type=jnp.float32
    )
    return (
        mixed.reshape(queries.shape).astype(jnp.bfloat16),
        (top_score + jnp.log(total))[:, :, 0],
    )


def score_grads(queries, keys_all, values_all, query_docs, key_docs, grad_mixed, log_total):
    scores = scores_of(queries, keys_all, query_docs, key_docs)
    probs = jnp.exp(scores - log_total[:, :, None])
    grad_probs = jnp.einsum(
        "qhd,khd->hqk",
        split_heads(grad_mixed),
        split_heads(values_all),
        preferred_element_type=jnp.float32,
    )
    inner = jnp.sum(grad_probs * probs, axis=-1)
    grad_scores = (probs * (grad_probs - inner[:, :, None])).astype(jnp.bfloat16)
    return (probs, grad_scores, inner)


def attend_backward(item):
    queries, keys_all, values_all, query_docs, key_docs, grad_mixed, log_total = item
    probs, grad_scores, inner = score_grads(
        queries, keys_all, values_all, query_docs, key_docs, grad_mixed, log_total
    )
    grad_heads = split_heads(grad_mixed)
    grad_queries = jnp.einsum(
        "hqk,khd->qhd", grad_scores, split_heads(keys_all), preferred_element_type=jnp.float32
    )
    grad_keys = jnp.einsum(
        "hqk,qhd->khd", grad_scores, split_heads(queries), preferred_element_type=jnp.float32
    )
    grad_values = jnp.einsum(
        "hqk,qhd->khd", probs.astype(jnp.bfloat16), grad_heads, preferred_element_type=jnp.float32
    )
    return (
        grad_queries.reshape(queries.shape).astype(jnp.bfloat16),
        grad_keys.reshape(keys_all.shape),
        grad_values.reshape(values_all.shape),
    )


def general_shards(
    layer_input,
    segment_ids,
    query_proj,
    query_bias,
    key_proj,
    value_proj,
    value_bias,
    out_proj,
    out_bias,
    attn_gain,
    attn_shift,
    up_proj,
    up_bias,
    down_proj,
    down_bias,
    ffn_gain,
    ffn_shift,
    out_cotangent,
):
    seq_here, ctx_rows, width = layer_input.shape
    scale = 1.0 / math.sqrt(HEAD_DIM)
    full_query, full_key, full_value, full_out, full_up, full_down = (
        lax.all_gather(query_proj, "shard", axis=0, tiled=True),
        lax.all_gather(key_proj, "shard", axis=0, tiled=True),
        lax.all_gather(value_proj, "shard", axis=0, tiled=True),
        lax.all_gather(out_proj, "shard", axis=1, tiled=True),
        lax.all_gather(up_proj, "shard", axis=0, tiled=True),
        lax.all_gather(down_proj, "shard", axis=1, tiled=True),
    )
    local_width = full_query.shape[1]
    joined_proj = jnp.concatenate([full_query, full_key, full_value], axis=1)
    rows_in = layer_input.reshape(seq_here * ctx_rows, width)
    projected = jnp.dot(rows_in, joined_proj, preferred_element_type=jnp.float32)
    shaped = (seq_here, ctx_rows, local_width)
    queries = (
        ((projected[:, :local_width] + query_bias) * scale).astype(jnp.bfloat16).reshape(shaped)
    )
    keys_mine = projected[:, local_width : 2 * local_width].astype(jnp.bfloat16).reshape(shaped)
    values_mine = (
        (projected[:, 2 * local_width :] + value_bias).astype(jnp.bfloat16).reshape(shaped)
    )
    keys_all, values_all = (
        lax.all_gather(keys_mine, "ctx", axis=1, tiled=True),
        lax.all_gather(values_mine, "ctx", axis=1, tiled=True),
    )
    query_docs = lax.dynamic_slice_in_dim(
        segment_ids, lax.axis_index("ctx") * ctx_rows, ctx_rows, 1
    )
    mixed, log_total = lax.map(
        attend_forward, (queries, keys_all, values_all, query_docs, segment_ids)
    )
    mixed_rows = mixed.reshape(-1, local_width)
    attended = (
        lax.psum(
            jnp.dot(mixed_rows, full_out, preferred_element_type=jnp.float32).astype(jnp.bfloat16),
            "tp",
        ).astype(jnp.float32)
        + out_bias
    )
    hidden, normed_one, inv_one = norm_forward(
        rows_in.astype(jnp.float32) + attended, attn_gain, attn_shift
    )
    hidden_low = hidden.astype(jnp.bfloat16)
    pre_act = jnp.dot(hidden_low, full_up, preferred_element_type=jnp.float32) + up_bias
    acts_low = jax.nn.gelu(pre_act, approximate=False).astype(jnp.bfloat16)
    ffn_out = (
        lax.psum(
            jnp.dot(acts_low, full_down, preferred_element_type=jnp.float32).astype(jnp.bfloat16),
            "tp",
        ).astype(jnp.float32)
        + down_bias
    )
    output_rows, normed_two, inv_two = norm_forward(hidden + ffn_out, ffn_gain, ffn_shift)
    layer_output = output_rows.astype(jnp.bfloat16).reshape(layer_input.shape)
    grad_out = out_cotangent.reshape(-1, width).astype(jnp.float32)
    grad_two, ffn_gain_grad, ffn_shift_grad = norm_backward(grad_out, normed_two, inv_two, ffn_gain)
    grad_ffn = grad_two.astype(jnp.bfloat16)
    down_bias_grad = jnp.sum(grad_ffn, axis=0, dtype=jnp.float32)
    down_part = contract_rows(acts_low, grad_ffn)
    grad_acts = contract_last(grad_ffn, full_down)
    _, gelu_back = jax.vjp(partial(jax.nn.gelu, approximate=False), pre_act)
    grad_pre = gelu_back(grad_acts)[0].astype(jnp.bfloat16)
    up_bias_grad = jnp.sum(grad_pre, axis=0, dtype=jnp.float32)
    up_part = contract_rows(hidden_low, grad_pre)
    grad_hidden = grad_two + lax.psum(
        contract_last(grad_pre, full_up).astype(jnp.bfloat16), "tp"
    ).astype(jnp.float32)
    grad_one, attn_gain_grad, attn_shift_grad = norm_backward(
        grad_hidden, normed_one, inv_one, attn_gain
    )
    grad_attn = grad_one.astype(jnp.bfloat16)
    out_bias_grad = jnp.sum(grad_attn, axis=0, dtype=jnp.float32)
    out_part = contract_rows(mixed_rows, grad_attn)
    grad_mixed = contract_last(grad_attn, full_out).astype(jnp.bfloat16).reshape(shaped)
    keys_back, values_back = (
        lax.all_gather(keys_mine, "ctx", axis=1, tiled=True),
        lax.all_gather(values_mine, "ctx", axis=1, tiled=True),
    )
    grad_queries, grad_keys_all, grad_values_all = lax.map(
        attend_backward,
        (queries, keys_back, values_back, query_docs, segment_ids, grad_mixed, log_total),
    )
    grad_keys, grad_values = (
        lax.psum_scatter(
            grad_keys_all.astype(jnp.bfloat16), "ctx", scatter_dimension=1, tiled=True
        ).astype(jnp.float32),
        lax.psum_scatter(
            grad_values_all.astype(jnp.bfloat16), "ctx", scatter_dimension=1, tiled=True
        ).astype(jnp.float32),
    )
    grad_keys = grad_keys.astype(jnp.bfloat16).reshape(-1, local_width)
    grad_values = grad_values.astype(jnp.bfloat16).reshape(-1, local_width)
    grad_scaled = grad_queries.reshape(-1, local_width) * jnp.bfloat16(scale)
    grad_joined = jnp.concatenate([grad_scaled, grad_keys, grad_values], axis=1)
    joined_part = contract_rows(rows_in, grad_joined)
    query_part = joined_part[:, :local_width]
    key_part = joined_part[:, local_width : 2 * local_width]
    value_part = joined_part[:, 2 * local_width :]
    query_bias_grad = jnp.sum(grad_scaled, axis=0, dtype=jnp.float32)
    value_bias_grad = jnp.sum(grad_values, axis=0, dtype=jnp.float32)
    back_terms = contract_last(grad_joined, joined_proj)
    input_grad = (
        grad_one + lax.psum(back_terms.astype(jnp.bfloat16), "tp").astype(jnp.float32)
    ).reshape(layer_input.shape)
    sliced = (
        lax.psum_scatter(
            query_part.astype(jnp.bfloat16), "shard", scatter_dimension=0, tiled=True
        ).astype(jnp.float32),
        lax.psum_scatter(
            key_part.astype(jnp.bfloat16), "shard", scatter_dimension=0, tiled=True
        ).astype(jnp.float32),
        lax.psum_scatter(
            value_part.astype(jnp.bfloat16), "shard", scatter_dimension=0, tiled=True
        ).astype(jnp.float32),
        lax.psum_scatter(
            out_part.astype(jnp.bfloat16), "shard", scatter_dimension=1, tiled=True
        ).astype(jnp.float32),
        lax.psum_scatter(
            up_part.astype(jnp.bfloat16), "shard", scatter_dimension=0, tiled=True
        ).astype(jnp.float32),
        lax.psum_scatter(
            down_part.astype(jnp.bfloat16), "shard", scatter_dimension=1, tiled=True
        ).astype(jnp.float32),
    )
    reduced = (
        lax.psum(sliced[0].astype(jnp.bfloat16), "ctx").astype(jnp.float32),
        lax.psum(sliced[1].astype(jnp.bfloat16), "ctx").astype(jnp.float32),
        lax.psum(sliced[2].astype(jnp.bfloat16), "ctx").astype(jnp.float32),
        lax.psum(sliced[3].astype(jnp.bfloat16), "ctx").astype(jnp.float32),
        lax.psum(sliced[4].astype(jnp.bfloat16), "ctx").astype(jnp.float32),
        lax.psum(sliced[5].astype(jnp.bfloat16), "ctx").astype(jnp.float32),
    )
    small = lax.psum(
        (
            query_bias_grad,
            value_bias_grad,
            out_bias_grad,
            attn_gain_grad,
            attn_shift_grad,
            up_bias_grad,
            down_bias_grad,
            ffn_gain_grad,
            ffn_shift_grad,
        ),
        ("shard", "ctx"),
    )
    return (
        layer_output,
        input_grad,
        reduced[0],
        small[0],
        reduced[1],
        reduced[2],
        small[1],
        reduced[3],
        small[2],
        small[3],
        small[4],
        reduced[4],
        small[5],
        reduced[5],
        small[6],
        small[7],
        small[8],
    )


PAIR = 2 * HEAD_DIM
QBLOCK = 128


def dot32(left, right):
    return jnp.dot(left, right, preferred_element_type=jnp.float32)


def stack_heads(rows):
    lane = lax.broadcasted_iota(jnp.int32, rows.shape, 1)
    nought = jnp.zeros_like(rows)
    return jnp.concatenate(
        [jnp.where(lane < HEAD_DIM, rows, nought), jnp.where(lane >= HEAD_DIM, rows, nought)], axis=0
    )


def unstack_heads(wide):
    return jnp.concatenate([wide[:HEAD_DIM, :QBLOCK], wide[HEAD_DIM:, QBLOCK:]], axis=0).T


def masked_scores(span, queries, keys, key_docs, query_docs):
    scores = contract_last(keys, queries)
    same = key_docs == query_docs
    return jnp.where(jnp.concatenate([same, same], axis=1), scores, jnp.float32(far_below))


def attend_kernel(span, q_ref, k_ref, v_ref, kd_ref, qd_ref, *refs):
    o_ref, l_ref = refs[-2:]
    first = pl.multiple_of(pl.program_id(1) * QBLOCK, QBLOCK)
    keys = k_ref[pl.ds(first, span), :]
    values = v_ref[pl.ds(first, span), :]
    scores = masked_scores(
        span, stack_heads(q_ref[...]), keys, kd_ref[pl.ds(first, span), :], qd_ref[0]
    )
    top = jnp.max(scores, axis=0, keepdims=True)
    expo = jnp.exp(scores - top)
    total = jnp.sum(expo, axis=0, keepdims=True)
    probs = (expo * (1.0 / total)).astype(jnp.bfloat16)
    o_ref[...] = unstack_heads(contract_rows(values, probs)).astype(jnp.bfloat16)
    l_ref[0, 0] = top + jnp.log(total)


def attend_back_kernel(span, q_ref, k_ref, v_ref, kd_ref, qd_ref, do_ref, l_ref, *refs):
    dq_ref, dk_ref, dv_ref, dk_acc, dv_acc = refs[-5:]
    step = pl.program_id(1)

    @pl.when(step == 0)
    def _():
        dk_acc[...] = jnp.zeros_like(dk_acc)
        dv_acc[...] = jnp.zeros_like(dv_acc)

    first = pl.multiple_of(step * QBLOCK, QBLOCK)
    here = pl.ds(first, span)
    keys = k_ref[here, :]
    values = v_ref[here, :]
    queries = stack_heads(q_ref[...])
    grads = stack_heads(do_ref[...])
    scores = masked_scores(span, queries, keys, kd_ref[here, :], qd_ref[0])
    probs = jnp.exp(scores - l_ref[0, 0])
    grad_probs = contract_last(values, grads)
    inner = jnp.sum(grad_probs * probs, axis=0, keepdims=True)
    grad_scores = (probs * (grad_probs - inner)).astype(jnp.bfloat16)
    grad_queries = unstack_heads(contract_rows(keys, grad_scores))
    grad_queries = (grad_queries * (1.0 / math.sqrt(HEAD_DIM))).astype(jnp.bfloat16)
    dq_ref[...] = grad_queries
    dk_acc[here, :] += dot32(grad_scores, queries)
    dv_acc[here, :] += dot32(probs.astype(jnp.bfloat16), grads)

    @pl.when(step == pl.num_programs(1) - 1)
    def _():
        dk_ref[...] = dk_acc[...].astype(jnp.bfloat16)
        dv_ref[...] = dv_acc[...].astype(jnp.bfloat16)


def attention_specs(window, at=0):
    rows = pl.BlockSpec((QBLOCK, PAIR), lambda h, i: (i, at + h))
    keys = pl.BlockSpec((window, PAIR), lambda h, i: (0, at + h))
    key_docs = pl.BlockSpec((window, QBLOCK), lambda h, i: (0, 0))
    query_docs = pl.BlockSpec((1, 1, QBLOCK), lambda h, i: (i, 0, 0))
    logs = pl.BlockSpec((1, 1, 1, 2 * QBLOCK), lambda h, i: (at + h, i, 0, 0))
    return rows, keys, key_docs, query_docs, logs


def attend(queries, keys, values, key_docs, query_docs, reach, at, pairs, prior=()):
    count, width = queries.shape
    window = keys.shape[0]
    blocks, span = count // QBLOCK, QBLOCK + 2 * reach
    rows, key_spec, kd_spec, qd_spec, logs = attention_specs(window, at)
    return pl.pallas_call(
        partial(attend_kernel, span),
        grid=(pairs, blocks),
        in_specs=[rows, key_spec, key_spec, kd_spec, qd_spec]
        + [pl.BlockSpec(memory_space=pl.ANY)] * len(prior),
        out_specs=[rows, logs],
        out_shape=[
            jax.ShapeDtypeStruct((count, width), jnp.bfloat16),
            jax.ShapeDtypeStruct((width // PAIR, blocks, 1, 2 * QBLOCK), jnp.float32),
        ],
        input_output_aliases={5 + i: i for i in range(len(prior))},
        compiler_params=pltpu.CompilerParams(vmem_limit_bytes=12 << 20),
        cost_estimate=pl.CostEstimate(
            flops=16 * count * span * PAIR * pairs, bytes_accessed=4 << 20, transcendentals=0
        ),
        name="attend",
    )(queries, keys, values, key_docs, query_docs, *prior)


def attend_back(
    queries, keys, values, key_docs, query_docs, grads, logs_in, reach, at, pairs, prior=()
):
    count, width = queries.shape
    window = keys.shape[0]
    blocks, span = count // QBLOCK, QBLOCK + 2 * reach
    rows, key_spec, kd_spec, qd_spec, logs = attention_specs(window, at)
    return pl.pallas_call(
        partial(attend_back_kernel, span),
        grid=(pairs, blocks),
        in_specs=[rows, key_spec, key_spec, kd_spec, qd_spec, rows, logs]
        + [pl.BlockSpec(memory_space=pl.ANY)] * len(prior),
        out_specs=[rows, key_spec, key_spec],
        out_shape=[
            jax.ShapeDtypeStruct((count, width), jnp.bfloat16),
            jax.ShapeDtypeStruct((window, width), jnp.bfloat16),
            jax.ShapeDtypeStruct((window, width), jnp.bfloat16),
        ],
        scratch_shapes=[
            pltpu.VMEM((window, PAIR), jnp.float32),
            pltpu.VMEM((window, PAIR), jnp.float32),
        ],
        input_output_aliases={7 + i: i for i in range(len(prior))},
        compiler_params=pltpu.CompilerParams(vmem_limit_bytes=16 << 20),
        cost_estimate=pl.CostEstimate(
            flops=40 * count * span * PAIR * pairs, bytes_accessed=6 << 20, transcendentals=0
        ),
        name="attend_back",
    )(queries, keys, values, key_docs, query_docs, grads, logs_in, *prior)


def half_cols(position, half):
    return pl.ds(pl.multiple_of(position * half, half), half)


def add_or_set(first, ref, index, terms):
    @pl.when(first)
    def _():
        ref[index] = terms

    @pl.when(jnp.logical_not(first))
    def _():
        ref[index] += terms


def ffn_kernel(place_ref, hb_ref, up_ref, down_ref, bias_ref, *refs):
    half = up_ref.shape[3]
    near, far = half_cols(place_ref[1], half), half_cols(1 - place_ref[1], half)
    last = len(refs) > 3
    if last:
        base_ref, _, _, acts_ref, slope_ref, own_ref, other_ref = refs
    else:
        acts_ref, slope_ref, total = refs

        @pl.when(pl.program_id(0) == 0)
        def _():
            total[...] = jnp.zeros_like(total)

    def chunk(rows):
        pre_act = dot32(hb_ref[rows, near], up_ref[0, 0]) + dot32(hb_ref[rows, far], up_ref[0, 1])
        pre_act += bias_ref[0]
        cdf = 0.5 * (1.0 + lax.erf(pre_act * math.sqrt(0.5)))
        bell = jnp.exp(-0.5 * pre_act * pre_act) * (1.0 / math.sqrt(2 * math.pi))
        acts = (pre_act * cdf).astype(jnp.bfloat16)
        acts_ref[rows] = acts
        slope_ref[rows] = (cdf + pre_act * bell).astype(jnp.bfloat16)
        return dot32(acts, down_ref[0, 0]), dot32(acts, down_ref[0, 1])

    count = hb_ref.shape[0] // 2
    if last:
        for part, to in enumerate((own_ref, other_ref)):
            rows = slice(part * count, (part + 1) * count)
            for cols, terms in zip((near, far), chunk(rows)):
                to[:, cols] = (base_ref[rows, cols] + terms).astype(to.dtype)
    else:

        @pl.loop(0, 2)
        def _(part):
            rows = pl.ds(pl.multiple_of(part * count, count), count)
            for cols, terms in zip((near, far), chunk(rows)):
                total[rows, cols] += terms


def ffn_back_kernel(
    place_ref,
    dz_ref,
    hb_ref,
    acts_ref,
    slope_ref,
    up_ref,
    down_ref,
    own_ref,
    other_ref,
    up_keep,
    up_give,
    down_keep,
    down_give,
    sums_ref,
    total,
    grad_pre,
):
    step = pl.program_id(0)
    half = up_ref.shape[3]
    quarter = half // 2
    count = own_ref.shape[0]
    near, far = half_cols(place_ref[1], half), half_cols(1 - place_ref[1], half)
    @pl.when(step == 0)
    def _():
        total[...] = jnp.zeros_like(total)

    sums_ref[...] = jnp.zeros_like(sums_ref)

    @pl.loop(0, 2)
    def _(part):
        rows = pl.ds(pl.multiple_of(part * count, count), count)
        grad_acts = contract_last(dz_ref[rows, near], down_ref[0, 0])
        grad_acts += contract_last(dz_ref[rows, far], down_ref[0, 1])
        low = (slope_ref[rows].astype(jnp.float32) * grad_acts).astype(jnp.bfloat16)
        grad_pre[rows] = low
        sums_ref[0] += row_sum(low.astype(jnp.float32))
        total[rows, near] += contract_last(low, up_ref[0, 0])
        total[rows, far] += contract_last(low, up_ref[0, 1])

    for side, cols in enumerate((near, far)):
        up_grad = contract_rows(hb_ref[:, cols], grad_pre[...]).astype(jnp.bfloat16)
        down_grad = contract_rows(acts_ref[...], dz_ref[:, cols]).astype(jnp.bfloat16)
        down_to = down_give if side else down_keep
        for across in (0, 1):
            mine = slice(across * quarter, (across + 1) * quarter)
            theirs = slice((1 - across) * quarter, (2 - across) * quarter)

            @pl.when(place_ref[3] == across)
            def _():
                up_keep[side, 0] = up_grad[mine]
                up_give[side, 0] = up_grad[theirs]
                down_to[0, 0] = down_grad[mine]
                down_to[1, 0] = down_grad[theirs]

    @pl.when(step == pl.num_programs(0) - 1)
    def _():
        own_ref[...] = total[:count]
        other_ref[...] = total[count:].astype(jnp.bfloat16)


def whole(shape):
    return pl.BlockSpec(shape, lambda *_: (0,) * len(shape))


def ffn(place, rows, weights, bias, steps, prior=()):
    both, width = rows.shape
    tps, shards, _, half = weights.shape
    count = both // 2
    at = tps - steps if prior else 0
    matrix = (1, shards, half, half)
    block = pl.BlockSpec((both, half), lambda i, _: (0, at + i))
    hidden = jax.ShapeDtypeStruct((both, tps * half), jnp.bfloat16)
    if prior:
        last_specs = [whole((count, width)), whole((count, width))]
        last_shapes = [
            jax.ShapeDtypeStruct((count, width), jnp.float32),
            jax.ShapeDtypeStruct((count, width), jnp.bfloat16),
        ]
        prior_specs = [whole((both, width))] + [pl.BlockSpec(memory_space=pl.ANY)] * 2
    else:
        last_specs = [whole((both, width))]
        last_shapes = [jax.ShapeDtypeStruct((both, width), jnp.float32)]
        prior_specs = []
    return pl.pallas_call(
        ffn_kernel,
        grid_spec=pltpu.PrefetchScalarGridSpec(
            num_scalar_prefetch=1,
            grid=(steps,),
            in_specs=[
                whole((both, width)),
                pl.BlockSpec(matrix, lambda i, _: (at + i, 0, 0, 0)),
                pl.BlockSpec(matrix, lambda i, _: (at + i, 0, 1, 0)),
                pl.BlockSpec((1, 1, half), lambda i, _: (at + i, 0, 0)),
            ]
            + prior_specs,
            out_specs=[block, block] + last_specs,
        ),
        out_shape=[hidden, hidden] + last_shapes,
        input_output_aliases={6: 0, 7: 1} if prior else {},
        compiler_params=pltpu.CompilerParams(vmem_limit_bytes=20 << 20),
        cost_estimate=pl.CostEstimate(
            flops=12 * both * width * steps * half, bytes_accessed=3 * steps << 20, transcendentals=0
        ),
        name="ffn",
    )(place, rows, weights, weights, bias, *prior)


def ffn_back(place, grads, rows, acts, slope, weights):
    both, width = rows.shape
    tps, shards, _, half = weights.shape
    count = both // 2
    matrix = (1, shards, half, half)
    block = pl.BlockSpec((both, half), lambda i, _: (0, i))

    def source(i, place_ref):
        return (place_ref[2] + tps - jnp.where(i < 2, i, 5 - i)) % tps

    parts = pl.BlockSpec(
        (2, 1, half // 2, half), lambda i, at: (0, source(i, at), 0, 0)
    )
    return pl.pallas_call(
        ffn_back_kernel,
        grid_spec=pltpu.PrefetchScalarGridSpec(
            num_scalar_prefetch=1,
            grid=(tps,),
            in_specs=[
                whole((both, width)),
                whole((both, width)),
                block,
                block,
                pl.BlockSpec(matrix, lambda i, _: (i, 0, 0, 0)),
                pl.BlockSpec(matrix, lambda i, _: (i, 0, 1, 0)),
            ],
            out_specs=[
                whole((count, width)),
                whole((count, width)),
                parts,
                parts,
                parts,
                parts,
                pl.BlockSpec((1, 1, half), lambda i, at: (source(i, at), 0, 0)),
            ],
            scratch_shapes=[
                pltpu.VMEM((both, width), jnp.float32),
                pltpu.VMEM((both, half), jnp.bfloat16),
            ],
        ),
        out_shape=[
            jax.ShapeDtypeStruct((count, width), jnp.float32),
            jax.ShapeDtypeStruct((count, width), jnp.bfloat16),
            *[jax.ShapeDtypeStruct((2, tps, half // 2, half), jnp.bfloat16)] * 4,
            jax.ShapeDtypeStruct((tps, 1, half), jnp.float32),
        ],
        compiler_params=pltpu.CompilerParams(vmem_limit_bytes=26 << 20),
        cost_estimate=pl.CostEstimate(
            flops=12 * both * width * tps * half, bytes_accessed=20 << 20, transcendentals=0
        ),
        name="ffn_back",
    )(place, grads, rows, acts, slope, weights, weights)


def project_kernel(
    place_ref, w_mine, w_other, x_mine, x_other, bias_ref, q_ref, k_ref, v_ref, x_ref, wt
):
    core, shard, tp, across, start = (place_ref[i] for i in range(5))
    depth = w_mine.shape[3]
    width = x_ref.shape[1]
    part = width // 8
    length = 4 * x_mine.shape[2]
    reach = length // 2
    for c, source in enumerate((w_mine, w_other)):
        for y in (0, 1):
            cols = half_cols(shard + y - 2 * shard * y, depth)
            for k in range(4):
                row = ((tp + 4 - k) & 3) * 2 + core + c - 2 * core * c
                rows = pl.ds(pl.multiple_of(row * part, part), part)
                for m in range(3):
                    wt[m, rows, cols] = source[y, k, m * part : (m + 1) * part]
    for i in range(x_ref.shape[0] // QBLOCK):
        row = start - reach + i * QBLOCK
        inside = jnp.logical_and(row >= 0, row < 2 * length)
        at = jnp.where(inside, row, 0) // QBLOCK
        seq, block, piece = at // 8, (at // 2) & 3, at & 1
        here = jnp.where((block >> 1) == across, 0, 1)
        rows = pl.ds(pl.multiple_of(piece * QBLOCK, QBLOCK), QBLOCK)
        mine, other = x_mine[here, seq, rows], x_other[here, seq, rows]
        found = jnp.where((block & 1) == core, mine, other)
        x_ref[i * QBLOCK : (i + 1) * QBLOCK] = jnp.where(inside, found, jnp.zeros_like(found))
    count = q_ref.shape[0]
    scaled = contract_last(x_ref[reach : reach + count], wt[0]) + bias_ref[0:1]
    q_ref[...] = (scaled * (1.0 / math.sqrt(HEAD_DIM))).astype(jnp.bfloat16)
    chunk = x_ref.shape[0] // 4

    @pl.loop(0, 4)
    def _(step):
        rows = pl.ds(pl.multiple_of(step * chunk, 32), chunk)
        k_ref[rows] = contract_last(x_ref[rows], wt[1]).astype(jnp.bfloat16)
        v_ref[rows] = (contract_last(x_ref[rows], wt[2]) + bias_ref[1:2]).astype(jnp.bfloat16)


def project(place, w_mine, w_other, x_mine, x_other, biases, count, window):
    width = x_mine.shape[-1]
    return pl.pallas_call(
        project_kernel,
        in_specs=[pl.BlockSpec(memory_space=pltpu.SMEM)]
        + [pl.BlockSpec(memory_space=pltpu.VMEM)] * 5,
        out_specs=[pl.BlockSpec(memory_space=pltpu.VMEM)] * 5,
        out_shape=[
            jax.ShapeDtypeStruct((count, width), jnp.bfloat16),
            jax.ShapeDtypeStruct((window, width), jnp.bfloat16),
            jax.ShapeDtypeStruct((window, width), jnp.bfloat16),
            jax.ShapeDtypeStruct((window, width), jnp.bfloat16),
            jax.ShapeDtypeStruct((3, width, width), jnp.bfloat16),
        ],
        compiler_params=pltpu.CompilerParams(vmem_limit_bytes=24 << 20),
        cost_estimate=pl.CostEstimate(
            flops=4 * window * width * width, bytes_accessed=16 << 20, transcendentals=0
        ),
        name="project",
    )(place, w_mine, w_other, x_mine, x_other, biases)


def norm_pieces(resid):
    center = resid - jnp.mean(resid, axis=-1, keepdims=True)
    inv_std = lax.rsqrt(jnp.mean(center * center, axis=-1, keepdims=True) + eps_norm)
    return center * inv_std, inv_std


def norm_pull(grad_out, normed, inv_std, gain):
    grad_normed = grad_out * gain
    return inv_std * (
        grad_normed
        - jnp.mean(grad_normed, axis=-1, keepdims=True)
        - normed * jnp.mean(grad_normed * normed, axis=-1, keepdims=True)
    )


def row_sum(rows):
    return jnp.sum(rows, axis=0, keepdims=True)


def attend_out_kernel(
    place_ref, o_ref, x_ref, w_mine, w_other, vec_ref, h_ref, hb_ref, n_ref, i_ref, wo_ref
):
    core, shard, tp = (place_ref[i] for i in range(3))
    part, depth = w_mine.shape[2:]
    for c, source in enumerate((w_mine, w_other)):
        for y in (0, 1):
            cols = half_cols(shard + y - 2 * shard * y, depth)
            for k in range(4):
                row = ((tp + 4 - k) & 3) * 2 + core + c - 2 * core * c
                rows = pl.ds(pl.multiple_of(row * part, part), part)
                wo_ref[rows, cols] = source[k, y]
    resid = x_ref[...].astype(jnp.float32) + dot32(o_ref[...], wo_ref[...]) + vec_ref[0:1]
    normed, inv_std = norm_pieces(resid)
    hidden = normed * vec_ref[1:2] + vec_ref[2:3]
    h_ref[...] = hidden
    hb_ref[...] = hidden.astype(jnp.bfloat16)
    n_ref[...] = normed
    i_ref[...] = jnp.broadcast_to(inv_std, i_ref.shape)


def attend_out(place, mixed, rows, w_mine, w_other, vectors):
    count, width = mixed.shape
    vmem = pl.BlockSpec(memory_space=pltpu.VMEM)
    return pl.pallas_call(
        attend_out_kernel,
        in_specs=[pl.BlockSpec(memory_space=pltpu.SMEM)] + [vmem] * 5,
        out_specs=[vmem] * 5,
        out_shape=[
            jax.ShapeDtypeStruct((count, width), jnp.float32),
            jax.ShapeDtypeStruct((count, width), jnp.bfloat16),
            jax.ShapeDtypeStruct((count, width), jnp.float32),
            jax.ShapeDtypeStruct((count, QBLOCK), jnp.float32),
            jax.ShapeDtypeStruct((width, width), jnp.bfloat16),
        ],
        compiler_params=pltpu.CompilerParams(vmem_limit_bytes=10 << 20),
        cost_estimate=pl.CostEstimate(
            flops=2 * count * width * width, bytes_accessed=8 << 20, transcendentals=0
        ),
        name="attend_out",
    )(place, mixed, rows, w_mine, w_other, vectors)


def ffn_norm_kernel(h_ref, own_ref, got_ref, g_ref, vec_ref, y_ref, dr_ref, dz_ref, sums_ref):
    resid = h_ref[...] + own_ref[...] + got_ref[...].astype(jnp.float32) + vec_ref[0:1]
    normed, inv_std = norm_pieces(resid)
    y_ref[...] = (normed * vec_ref[1:2] + vec_ref[2:3]).astype(jnp.bfloat16)
    grad_out = g_ref[...].astype(jnp.float32)
    grad = norm_pull(grad_out, normed, inv_std, vec_ref[1:2])
    low = grad.astype(jnp.bfloat16)
    dr_ref[...] = grad
    dz_ref[...] = low
    sums_ref[0:1] = row_sum(low.astype(jnp.float32))
    sums_ref[1:2] = row_sum(grad_out * normed)
    sums_ref[2:3] = row_sum(grad_out)


def ffn_norm(hidden, own, got, cots, vectors):
    count, width = hidden.shape
    vmem = pl.BlockSpec(memory_space=pltpu.VMEM)
    return pl.pallas_call(
        ffn_norm_kernel,
        in_specs=[vmem] * 5,
        out_specs=[vmem] * 4,
        out_shape=[
            jax.ShapeDtypeStruct((count, width), jnp.bfloat16),
            jax.ShapeDtypeStruct((count, width), jnp.float32),
            jax.ShapeDtypeStruct((count, width), jnp.bfloat16),
            jax.ShapeDtypeStruct((3, width), jnp.float32),
        ],
        compiler_params=pltpu.CompilerParams(vmem_limit_bytes=12 << 20),
        cost_estimate=pl.CostEstimate(
            flops=30 * count * width, bytes_accessed=7 << 20, transcendentals=0
        ),
        name="ffn_norm",
    )(hidden, own, got, cots, vectors)


def attend_norm_kernel(
    dr_ref, own_ref, got_ref, n_ref, i_ref, vec_ref, wo_ref, out_ref, da_ref, do_ref, sums_ref
):
    grad_out = dr_ref[...] + own_ref[...] + got_ref[...].astype(jnp.float32)
    normed = n_ref[...]
    grad = norm_pull(grad_out, normed, i_ref[:, :1], vec_ref[1:2])
    low = grad.astype(jnp.bfloat16)
    out_ref[...] = grad
    da_ref[...] = low
    do_ref[...] = contract_last(low, wo_ref[...]).astype(jnp.bfloat16)
    sums_ref[0:1] = row_sum(low.astype(jnp.float32))
    sums_ref[1:2] = row_sum(grad_out * normed)
    sums_ref[2:3] = row_sum(grad_out)


def attend_norm(grads, own, got, normed, inv_std, vectors, weights):
    count, width = grads.shape
    vmem = pl.BlockSpec(memory_space=pltpu.VMEM)
    return pl.pallas_call(
        attend_norm_kernel,
        in_specs=[vmem] * 7,
        out_specs=[vmem] * 4,
        out_shape=[
            jax.ShapeDtypeStruct((count, width), jnp.float32),
            jax.ShapeDtypeStruct((count, width), jnp.bfloat16),
            jax.ShapeDtypeStruct((count, width), jnp.bfloat16),
            jax.ShapeDtypeStruct((3, width), jnp.float32),
        ],
        compiler_params=pltpu.CompilerParams(vmem_limit_bytes=12 << 20),
        cost_estimate=pl.CostEstimate(
            flops=2 * count * width * width, bytes_accessed=9 << 20, transcendentals=0
        ),
        name="attend_norm",
    )(grads, own, got, normed, inv_std, vectors, weights)


def attn_grads_kernel(
    place_ref, dq_ref, dk_ref, dv_ref, o_ref, da_ref, x_ref, w_ref, sums_ref, *parts
):
    core, shard, across = place_ref[0], place_ref[1], place_ref[3]
    grad_ref = parts[2]
    depth = x_ref.shape[1] // 2
    part = depth // 4
    sides = (
        (dq_ref, x_ref),
        (dk_ref, w_ref),
        (dv_ref, w_ref),
        (o_ref, da_ref),
    )
    for m, (left, right) in enumerate(sides):
        grad_ref[...] = contract_rows(left[...], right[...]).astype(jnp.bfloat16)
        group = across if m < 2 else 1 - across
        rows = slice((m % 2) * part, (m % 2 + 1) * part)
        for z in (0, 1):
            for c in (0, 1):
                at = pl.ds(pl.multiple_of((2 * z + c + core - 2 * c * core) * part, part), part)
                parts[c][shard, group, z, rows] = grad_ref[at, :depth]
                parts[c][1 - shard, group, z, rows] = grad_ref[at, depth:]
    for c in (0, 1):
        for y in (0, 1):
            parts[c][y, across, :, 2 * part :] = sums_ref[c, 0]
            parts[c][y, 1 - across, :, 2 * part :] = sums_ref[c, 1]


def attn_grads(place, grad_queries, grad_keys, grad_values, mixed, grad_attn, rows, near, sums):
    count, width = rows.shape
    window = near.shape[0]
    depth = width // 2
    extra = sums.shape[3]
    high = depth // 2 + extra
    cols = pl.BlockSpec((count, depth), lambda i, _: (0, i))
    near_cols = pl.BlockSpec((window, depth), lambda i, _: (0, i))
    return pl.pallas_call(
        attn_grads_kernel,
        grid_spec=pltpu.PrefetchScalarGridSpec(
            num_scalar_prefetch=1,
            grid=(2,),
            in_specs=[
                cols,
                near_cols,
                near_cols,
                cols,
                whole((count, width)),
                whole((count, width)),
                whole((window, width)),
                pl.BlockSpec((2, 2, 2, extra, depth), lambda i, _: (0, 0, i, 0, 0)),
            ],
            out_specs=[pl.BlockSpec((2, 2, 2, high, depth), lambda i, _: (0, 0, i, 0, 0))] * 2,
            scratch_shapes=[pltpu.VMEM((depth, width), jnp.bfloat16)],
        ),
        out_shape=[jax.ShapeDtypeStruct((2, 2, 4, high, depth), jnp.bfloat16)] * 2,
        compiler_params=pltpu.CompilerParams(vmem_limit_bytes=24 << 20),
        cost_estimate=pl.CostEstimate(
            flops=4 * (window + count) * width * width, bytes_accessed=16 << 20, transcendentals=0
        ),
        name="attn_grads",
    )(place, grad_queries, grad_keys, grad_values, mixed, grad_attn, rows, near, sums)


def span_grads_kernel(
    place_ref,
    dq_ref,
    dk_ref,
    dv_ref,
    w_ref,
    base_ref,
    own_ref,
    first_ref,
    second_ref,
    give_ref,
    near,
):
    core = place_ref[0]
    count, reach = own_ref.shape[0], give_ref.shape[0]
    far = count + reach
    size = near.shape[0] // 4

    @pl.loop(0, 4)
    def _(step):
        rows = pl.ds(pl.multiple_of(step * size, 32), size)
        near[rows] = dot32(dk_ref[rows], w_ref[1]) + dot32(dv_ref[rows], w_ref[2])

    def rows_at(start, size):
        return near[pl.ds(pl.multiple_of(start, QBLOCK), size)].astype(jnp.bfloat16)

    give_ref[...] = rows_at((1 - core) * far, reach)
    first_ref[...] = rows_at(jnp.where(core == 0, reach - count, far), count)
    second_ref[...] = rows_at(jnp.where(core == 0, 0, far + count), reach - count)
    own_ref[...] = base_ref[...] + dot32(dq_ref[...], w_ref[0]) + near[reach:far]


def span_grads(place, grad_queries, grad_keys, grad_values, weights, base):
    count, width = base.shape
    reach = (grad_keys.shape[0] - count) // 2
    vmem = pl.BlockSpec(memory_space=pltpu.VMEM)
    return pl.pallas_call(
        span_grads_kernel,
        in_specs=[pl.BlockSpec(memory_space=pltpu.SMEM)] + [vmem] * 5,
        out_specs=[vmem] * 4,
        out_shape=[
            jax.ShapeDtypeStruct((count, width), jnp.float32),
            jax.ShapeDtypeStruct((count, width), jnp.bfloat16),
            jax.ShapeDtypeStruct((reach - count, width), jnp.bfloat16),
            jax.ShapeDtypeStruct((reach, width), jnp.bfloat16),
        ],
        scratch_shapes=[pltpu.VMEM(grad_keys.shape, jnp.float32)],
        compiler_params=pltpu.CompilerParams(vmem_limit_bytes=16 << 20),
        cost_estimate=pl.CostEstimate(
            flops=4 * (count + 2 * reach) * width * width,
            bytes_accessed=12 << 20,
            transcendentals=0,
        ),
        name="span_grads",
    )(place, grad_queries, grad_keys, grad_values, weights, base)


def assemble_kernel(place_ref, one, two, three, four, halves, out_ref):
    core, tp, across = place_ref[0], place_ref[2], place_ref[3]
    block = out_ref.shape[1]
    part = block // 2
    mine = pl.ds(pl.multiple_of(core * part, part), part)
    other = pl.ds(pl.multiple_of((1 - core) * part, part), part)
    for k, source in enumerate((one, two, three, four)):
        z = (tp + 4 - k) & 3
        group, side = 3 * (z >> 1), z & 1
        out_ref[group + jnp.where(side == 1, 1, 2 * across)] = source[:block].astype(out_ref.dtype)
        foreign = group + 2 - 2 * across

        @pl.when(((side + across + core) & 1) == 1)
        def _():
            out_ref[foreign, mine] = source[block:].astype(out_ref.dtype)
            out_ref[foreign, other] = halves[k].astype(out_ref.dtype)


def assemble_late_kernel(place_ref, one, two, three, four, middle, foreign, out_ref):
    core, tp, across = place_ref[0], place_ref[2], place_ref[3]
    block = out_ref.shape[1]
    part = block // 2
    for k, source in enumerate((one, two, three, four)):
        z = (tp + 4 - k) & 3
        group, side = 3 * (z >> 1), z & 1
        at = group + jnp.where(side == 1, 1, 2 * across)
        odd = (across + side) & 1

        @pl.when(jnp.logical_and(odd == 0, core == 0))
        def _():
            out_ref[at] = source[:block]

        @pl.when(jnp.logical_and(odd == 0, core == 1))
        def _():
            out_ref[at, :part] = middle[k]
            out_ref[at, part:] = source[:part]

        @pl.when(jnp.logical_and(odd == 1, core == 0))
        def _():
            out_ref[at, :part] = source[block:]
            out_ref[at, part:] = middle[k]

        @pl.when(jnp.logical_and(odd == 1, core == 1))
        def _():
            out_ref[at] = source[part:]

        @pl.when(((side + across + core) & 1) == 1)
        def _():
            out_ref[group + 2 - 2 * across] = foreign[k // 2]


def assemble(kernel, place, pieces, others, seqs, dtype):
    rows, width = pieces[0].shape
    vmem = pl.BlockSpec(memory_space=pltpu.VMEM)
    return pl.pallas_call(
        kernel,
        in_specs=[pl.BlockSpec(memory_space=pltpu.SMEM)] + [vmem] * (4 + len(others)),
        out_specs=vmem,
        out_shape=jax.ShapeDtypeStruct((seqs, rows * 2 // 3, width), dtype),
        compiler_params=pltpu.CompilerParams(vmem_limit_bytes=10 << 20),
        cost_estimate=pl.CostEstimate(flops=1 << 20, bytes_accessed=8 << 20, transcendentals=0),
        name="assemble",
    )(place, *pieces, *others)


def finish_ffn_kernel(place_ref, mine, across_got, core_got, both_got, up_ref, down_ref):
    core, across = place_ref[0], place_ref[3]
    depth = mine.shape[1]
    part = depth // 2
    for c, x, source in (
        (core, across, mine),
        (core, 1 - across, across_got),
        (1 - core, across, core_got),
        (1 - core, 1 - across, both_got),
    ):
        rows = pl.ds(pl.multiple_of(x * part, part), part)
        up_ref[rows, half_cols(c, depth)] = source[:part].astype(jnp.float32)
        rows = pl.ds(pl.multiple_of(c * depth + x * part, part), part)
        down_ref[rows] = source[part:].astype(jnp.float32)


def finish_attn_kernel(
    place_ref, mine, across_got, core_got, both_got, q_ref, k_ref, v_ref, o_ref, sums_ref
):
    core, across = place_ref[0], place_ref[3]
    part = q_ref.shape[0] // 2
    for c, x, source in (
        (core, across, mine),
        (core, 1 - across, across_got),
        (1 - core, across, core_got),
        (1 - core, 1 - across, both_got),
    ):
        rows = pl.ds(pl.multiple_of(c * part, part), part)
        one = source[:part].astype(jnp.float32)
        two = source[part : 2 * part].astype(jnp.float32)
        sums_ref[c, x] = source[2 * part :].astype(jnp.float32)

        @pl.when(x == 0)
        def _():
            q_ref[rows], k_ref[rows] = one, two

        @pl.when(x == 1)
        def _():
            v_ref[rows], o_ref[rows] = one, two


def finish(kernel, place, pieces, shapes, name):
    vmem = pl.BlockSpec(memory_space=pltpu.VMEM)
    return pl.pallas_call(
        kernel,
        in_specs=[pl.BlockSpec(memory_space=pltpu.SMEM)] + [vmem] * 4,
        out_specs=[vmem] * len(shapes),
        out_shape=[jax.ShapeDtypeStruct(shape, jnp.float32) for shape in shapes],
        compiler_params=pltpu.CompilerParams(vmem_limit_bytes=8 << 20),
        cost_estimate=pl.CostEstimate(flops=1 << 20, bytes_accessed=4 << 20, transcendentals=0),
        name=name,
    )(place, *pieces)


def ctx_swap(array, bit):
    return lax.ppermute(array, "ctx", [(i, i ^ bit) for i in range(4)])


def core_swap(array):
    return ctx_swap(array, 1)


def tie(*arrays):
    return lax.optimization_barrier(arrays)


def across_swap(array):
    return ctx_swap(array, 2)


def in_order(flag, mine, other):
    return jnp.where(flag == 0, mine, other), jnp.where(flag == 0, other, mine)


def at(across, core, tp):
    return (2 * across + core) * 4 + tp


def across_pairs():
    pairs = []
    for tp in range(4):
        for across in (0, 1):
            core = across ^ (tp & 1)
            pairs.append((at(1 - across, core, tp), at(across, core, tp)))
    return pairs


def tp_shifts(array, cuts=(slice(None), slice(None), slice(None))):
    return [
        lax.ppermute(array[cut], "tp", [(i, (i + shift) % 4) for i in range(4)])
        for shift, cut in zip((1, 2, 3), cuts)
        if cut is not None
    ]


def by_tp(array, shifted):
    one, two, three = shifted
    line = jnp.stack([three, two, one, array, three, two, one])
    return lax.dynamic_slice_in_dim(line, 3 - lax.axis_index("tp"), 4, 0)


def shard_swap(array):
    return lax.ppermute(array, "shard", [(0, 1), (1, 0)])


def low_sum(left, right):
    return (left.astype(jnp.float32) + right.astype(jnp.float32)).astype(jnp.bfloat16)


def scatter_tp_start(parts):
    tp = lax.axis_index("tp")
    moved = [lax.dynamic_index_in_dim(parts, tp, 0, keepdims=False)]
    for shift in (1, 2, 3):
        sent = lax.dynamic_index_in_dim(parts, (tp + shift) & 3, 0, keepdims=False)
        moved.append(lax.ppermute(sent, "tp", [(i, (i + shift) % 4) for i in range(4)]))
    return moved


def scatter_tp_end(moved):
    return sum(part.astype(jnp.float32) for part in moved).astype(jnp.bfloat16)


def chain_pairs(turn):
    pairs = []
    for group in (0, 2):
        path = [(0, group), (0, group + 1), (1, group + 1), (1, group)]
        for (across, tp), (next_across, next_tp) in zip(path[:-1], path[1:]):
            pairs.append((at(across, 1, tp), at(next_across, 1 ^ turn, next_tp)))
            pairs.append((at(next_across, 0, next_tp), at(across, turn, tp)))
    return pairs


def block_pairs(core):
    pairs = []
    for tp in range(4):
        for across in (0, 1):
            source = 1 ^ across ^ (tp & 1)
            pairs.append((at(across, source, tp), at(1 - across, core, tp)))
    return pairs


def span_shards(
    layer_input,
    segment_ids,
    query_proj,
    query_bias,
    key_proj,
    value_proj,
    value_bias,
    out_proj,
    out_bias,
    attn_gain,
    attn_shift,
    up_proj,
    up_bias,
    down_proj,
    down_bias,
    ffn_gain,
    ffn_shift,
    out_cotangent,
):
    seqs, block, width = layer_input.shape
    length = segment_ids.shape[1]
    reach = length // 2
    count = seqs * block // 4
    window = count + 2 * reach
    bf16, f32 = jnp.bfloat16, jnp.float32
    ctx, tp = lax.axis_index("ctx"), lax.axis_index("tp")
    shard = lax.axis_index("shard")
    core, across, side = ctx & 1, ctx >> 1, tp & 1
    place = 2 * across + (side ^ across)
    odd = across ^ side

    heads = query_proj.shape[1]
    half = heads // 2
    depth = query_proj.shape[0]
    cut = up_proj.shape[1] // 2
    own_in = lax.dynamic_slice_in_dim(
        jnp.stack([query_proj.T, key_proj.T, value_proj.T]), core * half, half, 1
    ).reshape(3 * half, depth)
    own_biases = jnp.stack(
        [
            jnp.concatenate([query_bias, value_bias]),
            lax.dynamic_slice_in_dim(up_bias, core * cut, cut, 0),
        ]
    )
    own_in = jnp.concatenate([own_in, own_biases, jnp.zeros((14, depth), bf16)], axis=0)
    out_half = out_proj.shape[0] // 2
    own_rest = jnp.concatenate(
        [
            lax.dynamic_slice_in_dim(up_proj, core * cut, cut, 1),
            lax.dynamic_slice_in_dim(down_proj, core * cut, cut, 0),
            lax.dynamic_slice_in_dim(out_proj, core * out_half, out_half, 0),
        ],
        axis=0,
    )
    first_seq = 3 * (tp >> 1)
    mine = lax.dynamic_slice_in_dim(layer_input, first_seq + across, 2, 0)
    theirs = across_swap(lax.dynamic_slice_in_dim(layer_input, first_seq + 1 - across, 2, 0))
    in_shifted = tp_shifts(own_in)
    far_rest = shard_swap(own_rest)
    *in_shifted, theirs, far_rest = tie(*in_shifted, theirs, far_rest)
    in_near = jnp.stack([own_in] + in_shifted)
    (rest_one,) = tp_shifts(tie(own_rest, in_near)[0], (slice(None), None, None))
    own_pair = jnp.stack([own_rest[: 2 * cut], far_rest[: 2 * cut]])
    in_far, rest_one, own_pair = tie(shard_swap(in_near), rest_one, own_pair)
    in_mine = jnp.stack([in_near, in_far])
    own_late = tie(own_rest, in_far)[0]
    (rest_three,) = tp_shifts(own_late, (None, None, slice(None)))
    (some_two,) = tp_shifts(own_late, (None, slice(cut, None), None))
    (up_two,) = tp_shifts(own_late, (None, slice(cut), None))
    in_other = core_swap(in_mine)
    bias_rows = in_mine[0, :, 3 * half]
    in_biases = by_tp(bias_rows[0], [bias_rows[1], bias_rows[2], bias_rows[3]]).astype(f32)
    in_biases = jnp.stack([in_biases[:, :heads].reshape(-1), in_biases[:, heads:].reshape(-1)])
    up_bias_here = in_mine[0, :, 3 * half + 1].reshape(4, 1, cut).astype(f32)

    pair = jnp.stack([mine, theirs])
    pair_other = core_swap(pair)
    start = 2 * count * place + count * core - length * across
    ids = lax.dynamic_slice_in_dim(segment_ids, first_seq + across, 2, 0)
    ids = (ids + jnp.array([[0], [1 << 16]], jnp.int32)).reshape(-1)
    no_doc = jnp.full((reach,), -1, jnp.int32)
    window_docs = lax.dynamic_slice_in_dim(
        jnp.concatenate([no_doc, ids, no_doc]), start, window, 0
    )
    key_docs = jnp.broadcast_to(window_docs[:, None], (window, QBLOCK))
    query_docs = window_docs[reach : reach + count].reshape(-1, 1, QBLOCK)

    place = jnp.stack([core, shard, tp, across, start])
    far_one = shard_swap(rest_one)
    queries, keys, values, in_window, weights_t = project(
        place, in_mine, in_other, pair, pair_other, in_biases, count, window
    )
    rows_in = in_window[reach : reach + count]
    queries, far_one, out_cotangent = tie(queries, far_one, out_cotangent)
    split = width // PAIR // 2
    attention = queries, keys, values, key_docs, query_docs, reach
    mixed, logs = attend(*attention, 0, split)
    mixed, rest_three, some_two = tie(mixed, rest_three, some_two)
    far_three, far_some_two = shard_swap(rest_three), shard_swap(some_two)
    mixed, logs = attend(*attention, split, width // PAIR - split, (mixed, logs))
    mixed, far_three, far_some_two, up_two = tie(mixed, far_three, far_some_two, up_two)
    far_up_two = shard_swap(up_two)
    out_mine = jnp.stack(
        [
            jnp.stack([one[-out_half:], two[-out_half:]])
            for one, two in (
                (own_rest, far_rest),
                (rest_one, far_one),
                (some_two, far_some_two),
                (rest_three, far_three),
            )
        ]
    )
    attn_vectors = jnp.stack([out_bias, attn_gain, attn_shift]).astype(f32)
    hidden, hidden_low, normed_one, inv_one, full_out = attend_out(
        place, mixed, rows_in, out_mine, core_swap(out_mine), attn_vectors
    )
    hidden_other = core_swap(hidden_low)
    hidden_both = jnp.concatenate([hidden_low, hidden_other], axis=0)
    ffn_weights = jnp.stack(
        [
            own_pair,
            jnp.stack([rest_one[: 2 * cut], far_one[: 2 * cut]]),
            jnp.stack([rest_three[: 2 * cut], far_three[: 2 * cut]]),
            own_pair,
        ]
    )
    ffn_bias = jnp.stack([up_bias_here[k] for k in (0, 1, 3, 2)])
    acts, slope, ffn_sum = ffn(place, hidden_both, ffn_weights, ffn_bias, 3)
    ffn_sum, far_up_two = tie(ffn_sum, far_up_two)
    rest = ffn_weights.at[3].set(
        jnp.stack(
            [
                jnp.concatenate([up_two, some_two[:cut]], axis=0),
                jnp.concatenate([far_up_two, far_some_two[:cut]], axis=0),
            ]
        )
    )
    acts, slope, ffn_own, ffn_other = ffn(
        place, hidden_both, rest, ffn_bias, 1, (ffn_sum, acts, slope)
    )

    half_block = block // 2

    def deliver_start(rows):
        far_rows = jnp.where(odd == 0, rows[-block:], rows[:block])
        return (
            core_swap(jnp.where(odd == 0, rows[block:], rows[:half_block])),
            lax.ppermute(far_rows[:half_block], ("ctx", "tp"), block_pairs(0)),
            lax.ppermute(far_rows[half_block:], ("ctx", "tp"), block_pairs(1)),
        )

    def deliver_pack(rows, middle, low, high):
        where_kept = [
            rows[:block],
            jnp.concatenate([middle, rows[:half_block]], axis=0),
            jnp.concatenate([rows[block:], middle], axis=0),
            rows[half_block:],
        ]
        kept = jnp.where(
            odd == 0,
            jnp.where(core == 0, where_kept[0], where_kept[1]),
            jnp.where(core == 0, where_kept[2], where_kept[3]),
        )
        return jnp.concatenate([kept, low + high], axis=0)

    near_cot = lax.dynamic_index_in_dim(
        out_cotangent, first_seq + odd + across, 0, keepdims=False
    )
    far_cot = lax.ppermute(
        lax.dynamic_index_in_dim(out_cotangent, first_seq + 2 - 2 * across, 0, keepdims=False),
        ("ctx", "tp"),
        across_pairs(),
    )
    cot_pair = jnp.stack([near_cot, far_cot])
    cot_swapped = core_swap(cot_pair)
    low_cot, high_cot = in_order(core, near_cot, cot_swapped[0])
    far_cot = jnp.where(core == odd, far_cot, cot_swapped[1])
    chip_cot = jnp.where(
        odd == 0,
        jnp.concatenate([low_cot, high_cot, far_cot], axis=0),
        jnp.concatenate([far_cot, low_cot, high_cot], axis=0),
    )
    cot_rows = lax.dynamic_slice_in_dim(chip_cot, core * count, count, 0)


    ffn_vectors = jnp.stack([down_bias, ffn_gain, ffn_shift]).astype(f32)
    output_rows, grad_two, grad_ffn, ffn_sums = ffn_norm(
        hidden, ffn_own, core_swap(ffn_other), cot_rows, ffn_vectors
    )
    grad_other = core_swap(grad_ffn)
    grad_ffn_both = jnp.concatenate([grad_ffn, grad_other], axis=0)
    out_pieces = [output_rows] + tp_shifts(output_rows)
    back_own, back_other, up_keep, up_give, down_keep, down_give, up_sums = ffn_back(
        place, grad_ffn_both, hidden_both, acts, slope, rest
    )
    back_own, out_pieces[1] = tie(back_own, out_pieces[1])
    grad_one, grad_attn, grad_mixed, attn_sums = attend_norm(
        grad_two, back_own, core_swap(back_other), normed_one, inv_one, attn_vectors, full_out
    )
    up_got = across_swap(up_give)
    down_got = shard_swap(down_give)
    attention = queries, keys, values, key_docs, query_docs, grad_mixed, logs, reach
    back = attend_back(*attention, 0, split)
    *back, up_got, down_got, out_pieces[3] = tie(*back, up_got, down_got, out_pieces[3])
    up_parts, down_parts = low_sum(up_keep, up_got), low_sum(down_keep, down_got)
    up_got, down_got = shard_swap(up_parts[1]), across_swap(down_parts[1])
    grad_scaled, grad_keys, grad_values = attend_back(
        *attention, split, width // PAIR - split, back
    )
    grad_keys, up_got, down_got, out_pieces[2] = tie(grad_keys, up_got, down_got, out_pieces[2])
    ffn_parts = jnp.concatenate(
        [low_sum(up_parts[0], up_got), low_sum(down_parts[0], down_got)], axis=1
    )
    ffn_near = scatter_tp_start(ffn_parts)
    own_sum, first, second, give = span_grads(
        place, grad_scaled, grad_keys, grad_values, weights_t, grad_one
    )
    got = core_swap(give)
    shared = reach - count
    to_own = lax.dynamic_slice_in_dim(got, (1 - core) * shared, count, 0)
    to_next = lax.dynamic_slice_in_dim(got, core * count, shared, 0)
    no_rows = jnp.zeros((count - shared, width), bf16)
    first = low_sum(
        first,
        jnp.where(
            core == 0,
            jnp.concatenate([no_rows, to_next], axis=0),
            jnp.concatenate([to_next, no_rows], axis=0),
        ),
    )
    first_got = lax.ppermute(first, ("ctx", "tp"), chain_pairs(1))
    second_got = lax.ppermute(second, ("ctx", "tp"), chain_pairs(0))
    head_sums = jnp.concatenate(
        [
            jnp.sum(grad_scaled, axis=0, dtype=f32).reshape(4, 1, heads),
            jnp.sum(grad_values, axis=0, dtype=f32).reshape(4, 1, heads),
        ],
        axis=2,
    )
    row_sums = jnp.concatenate([attn_sums, ffn_sums], axis=0).reshape(12, depth)
    sums = jnp.concatenate(
        [head_sums, jnp.broadcast_to(row_sums, (4, 12, depth))], axis=1
    ).astype(bf16)
    up_sums = up_sums.astype(bf16)
    no_sum = jnp.zeros_like(up_sums)
    sums = jnp.stack(
        [
            jnp.concatenate([sums, up_sums, no_sum, no_sum], axis=1),
            jnp.concatenate([sums, no_sum, no_sum, no_sum], axis=1),
        ]
    )
    sums = sums.reshape(2, 4, 2, 8, depth).transpose(0, 2, 1, 3, 4)
    grad_keys, first_now = tie(grad_keys, first)
    attn_parts = attn_grads(
        place,
        grad_scaled,
        grad_keys,
        grad_values,
        mixed,
        grad_attn,
        rows_in,
        in_window,
        sums,
    )
    first_got, second_got, attn_keep, attn_give, ffn_near[1] = tie(
        first_got, second_got, *attn_parts, ffn_near[1]
    )
    attn_core = core_swap(attn_give)
    own_sum += to_own.astype(f32) + first_got.astype(f32)
    own_sum += jnp.where(
        core == 0,
        jnp.concatenate([no_rows, second_got], axis=0),
        jnp.concatenate([second_got, no_rows], axis=0),
    ).astype(f32)
    own_low = own_sum.astype(bf16)
    in_moves = deliver_start(own_low)
    *in_moves, attn_core, ffn_near[3] = tie(*in_moves, attn_core, ffn_near[3])
    in_packed = deliver_pack(own_low, *in_moves)
    in_pieces = [in_packed] + tp_shifts(in_packed)
    attn_parts = low_sum(attn_keep, attn_core)
    attn_got = shard_swap(attn_parts[1])
    parity = (tp + 1 + across + core) & 1
    out_sent = [
        jnp.where(
            core == 0,
            jnp.where(parity == 0, even[:block], odd_one[:block]),
            jnp.where(parity == 0, even[-block:], odd_one[-block:]),
        )
        for even, odd_one in (out_pieces[:2], out_pieces[2:])
    ]
    out_foreign = lax.ppermute(jnp.stack(out_sent), "ctx", [(i, 3 - i) for i in range(4)])
    out_middle = core_swap(
        jnp.stack(
            [
                jnp.where(((across + tp + k) & 1) == 0, piece[block:], piece[:half_block])
                for k, piece in enumerate(out_pieces)
            ]
        )
    )
    attn_got, in_pieces[1], ffn_near[2] = tie(attn_got, in_pieces[1], ffn_near[2])
    ffn_low = scatter_tp_end(ffn_near)
    ffn_got = across_swap(ffn_low)
    attn_mid = low_sum(attn_parts[0], attn_got)
    attn_got = across_swap(attn_mid[1])
    attn_got, in_pieces[3], ffn_got, out_middle, out_foreign = tie(
        attn_got, in_pieces[3], ffn_got, out_middle, out_foreign
    )
    attn_near = scatter_tp_start(low_sum(attn_mid[0], attn_got))
    layer_output = assemble(
        assemble_late_kernel, place, out_pieces, (out_middle, out_foreign), seqs, bf16
    )
    layer_output, in_pieces[2] = tie(layer_output, in_pieces[2])
    in_halves = core_swap(jnp.stack([piece[block:] for piece in in_pieces]))
    input_grad = assemble(assemble_kernel, place, in_pieces, (in_halves,), seqs, f32)
    up_grad, down_grad = finish(
        finish_ffn_kernel,
        place,
        (ffn_low, ffn_got, core_swap(ffn_low), core_swap(ffn_got)),
        ((cut, 2 * cut), (2 * cut, cut)),
        "finish_ffn",
    )
    attn_low = scatter_tp_end(attn_near)
    attn_got, input_grad = tie(across_swap(attn_low), input_grad)
    *weight_grads, sums = finish(
        finish_attn_kernel,
        place,
        (attn_low, attn_got, core_swap(attn_low), core_swap(attn_got)),
        ((heads, depth),) * 4 + ((2, 2, 8, depth),),
        "finish_attn",
    )
    up_bias_grad = sums[:, 1, 5].reshape(-1)
    sums = sums[0].reshape(16, depth)
    row_sums = sums[1:13].reshape(6, width)
    return (
        layer_output,
        input_grad,
        weight_grads[0].T,
        sums[0, :heads],
        weight_grads[1].T,
        weight_grads[2].T,
        sums[0, heads:],
        weight_grads[3],
        row_sums[0],
        row_sums[1],
        row_sums[2],
        up_grad,
        up_bias_grad,
        down_grad,
        row_sums[3],
        row_sums[4],
        row_sums[5],
    )


def pick_plan(mesh):
    shape = dict(mesh.shape)

    def plan(layer_input, segment_ids, *others):
        seqs, block, _ = layer_input.shape
        fits = (
            (shape["shard"], shape["ctx"], shape["tp"]) == (2, 4, 4)
            and seqs == 6
            and segment_ids.shape[1] == 4 * block
            and block == 2 * QBLOCK
        )
        chosen = span_shards if fits else general_shards
        return chosen(layer_input, segment_ids, *others)

    return plan


def solution(mesh):
    return jax.shard_map(
        pick_plan(mesh),
        mesh=mesh,
        in_specs=(
            P("shard", "ctx", None),
            P("shard", None),
            P("shard", "tp"),
            P("tp"),
            P("shard", "tp"),
            P("shard", "tp"),
            P("tp"),
            P("tp", "shard"),
            P(),
            P(),
            P(),
            P("shard", "tp"),
            P("tp"),
            P("tp", "shard"),
            P(),
            P(),
            P(),
            P("shard", "ctx", None),
        ),
        out_specs=(
            P("shard", "ctx", None),
            P("shard", "ctx", None),
            P("shard", "tp"),
            P("tp"),
            P("shard", "tp"),
            P("shard", "tp"),
            P("tp"),
            P("tp", "shard"),
            P(),
            P(),
            P(),
            P("shard", "tp"),
            P("tp"),
            P("tp", "shard"),
            P(),
            P(),
            P(),
        ),
        check_vma=False,
    )
```

```python
from functools import partial
import math

import jax
import jax.numpy as jnp
from jax import lax
from jax.experimental import pallas as pl
from jax.experimental.pallas import tpu as pltpu
from jax.sharding import PartitionSpec as P

HEAD_DIM = 64


eps_norm = 1e-12
far_below = -1e30


def contract_rows(left, right):
    return lax.dot_general(
        left, right, (((0,), (0,)), ((), ())), preferred_element_type=jnp.float32
    )


def contract_last(left, right):
    return lax.dot_general(
        left, right, (((1,), (1,)), ((), ())), preferred_element_type=jnp.float32
    )


def norm_forward(resid, norm_gain, norm_shift):
    center = resid - jnp.mean(resid, axis=-1, keepdims=True)
    inv_std = lax.rsqrt(jnp.mean(center * center, axis=-1, keepdims=True) + eps_norm)
    normed = center * inv_std
    return (normed * norm_gain + norm_shift, normed, inv_std)


def norm_backward(grad_out, normed, inv_std, norm_gain):
    grad_normed = grad_out * norm_gain
    grad_in = inv_std * (
        grad_normed
        - jnp.mean(grad_normed, axis=-1, keepdims=True)
        - normed * jnp.mean(grad_normed * normed, axis=-1, keepdims=True)
    )
    return (grad_in, jnp.sum(grad_out * normed, axis=0), jnp.sum(grad_out, axis=0))


def split_heads(matrix):
    return matrix.reshape(matrix.shape[0], matrix.shape[1] // HEAD_DIM, HEAD_DIM)


def scores_of(queries, keys_all, query_docs, key_docs):
    scores = jnp.einsum(
        "qhd,khd->hqk",
        split_heads(queries),
        split_heads(keys_all),
        preferred_element_type=jnp.float32,
    )
    same_doc = (query_docs[:, None] == key_docs[None, :])[None]
    return jnp.where(same_doc, scores, jnp.float32(far_below))


def attend_forward(item):
    queries, keys_all, values_all, query_docs, key_docs = item
    scores = scores_of(queries, keys_all, query_docs, key_docs)
    top_score = jnp.max(scores, axis=-1, keepdims=True)
    expo = jnp.exp(scores - top_score)
    total = jnp.sum(expo, axis=-1, keepdims=True)
    probs = (expo / total).astype(jnp.bfloat16)
    mixed = jnp.einsum(
        "hqk,khd->qhd", probs, split_heads(values_all), preferred_element_type=jnp.float32
    )
    return (
        mixed.reshape(queries.shape).astype(jnp.bfloat16),
        (top_score + jnp.log(total))[:, :, 0],
    )


def score_grads(queries, keys_all, values_all, query_docs, key_docs, grad_mixed, log_total):
    scores = scores_of(queries, keys_all, query_docs, key_docs)
    probs = jnp.exp(scores - log_total[:, :, None])
    grad_probs = jnp.einsum(
        "qhd,khd->hqk",
        split_heads(grad_mixed),
        split_heads(values_all),
        preferred_element_type=jnp.float32,
    )
    inner = jnp.sum(grad_probs * probs, axis=-1)
    grad_scores = (probs * (grad_probs - inner[:, :, None])).astype(jnp.bfloat16)
    return (probs, grad_scores, inner)


def attend_backward(item):
    queries, keys_all, values_all, query_docs, key_docs, grad_mixed, log_total = item
    probs, grad_scores, inner = score_grads(
        queries, keys_all, values_all, query_docs, key_docs, grad_mixed, log_total
    )
    grad_heads = split_heads(grad_mixed)
    grad_queries = jnp.einsum(
        "hqk,khd->qhd", grad_scores, split_heads(keys_all), preferred_element_type=jnp.float32
    )
    grad_keys = jnp.einsum(
        "hqk,qhd->khd", grad_scores, split_heads(queries), preferred_element_type=jnp.float32
    )
    grad_values = jnp.einsum(
        "hqk,qhd->khd", probs.astype(jnp.bfloat16), grad_heads, preferred_element_type=jnp.float32
    )
    return (
        grad_queries.reshape(queries.shape).astype(jnp.bfloat16),
        grad_keys.reshape(keys_all.shape),
        grad_values.reshape(values_all.shape),
    )


def general_shards(
    layer_input,
    segment_ids,
    query_proj,
    query_bias,
    key_proj,
    value_proj,
    value_bias,
    out_proj,
    out_bias,
    attn_gain,
    attn_shift,
    up_proj,
    up_bias,
    down_proj,
    down_bias,
    ffn_gain,
    ffn_shift,
    out_cotangent,
):
    seq_here, ctx_rows, width = layer_input.shape
    scale = 1.0 / math.sqrt(HEAD_DIM)
    full_query, full_key, full_value, full_out, full_up, full_down = (
        lax.all_gather(query_proj, "shard", axis=0, tiled=True),
        lax.all_gather(key_proj, "shard", axis=0, tiled=True),
        lax.all_gather(value_proj, "shard", axis=0, tiled=True),
        lax.all_gather(out_proj, "shard", axis=1, tiled=True),
        lax.all_gather(up_proj, "shard", axis=0, tiled=True),
        lax.all_gather(down_proj, "shard", axis=1, tiled=True),
    )
    local_width = full_query.shape[1]
    joined_proj = jnp.concatenate([full_query, full_key, full_value], axis=1)
    rows_in = layer_input.reshape(seq_here * ctx_rows, width)
    projected = jnp.dot(rows_in, joined_proj, preferred_element_type=jnp.float32)
    shaped = (seq_here, ctx_rows, local_width)
    queries = (
        ((projected[:, :local_width] + query_bias) * scale).astype(jnp.bfloat16).reshape(shaped)
    )
    keys_mine = projected[:, local_width : 2 * local_width].astype(jnp.bfloat16).reshape(shaped)
    values_mine = (
        (projected[:, 2 * local_width :] + value_bias).astype(jnp.bfloat16).reshape(shaped)
    )
    keys_all, values_all = (
        lax.all_gather(keys_mine, "ctx", axis=1, tiled=True),
        lax.all_gather(values_mine, "ctx", axis=1, tiled=True),
    )
    query_docs = lax.dynamic_slice_in_dim(
        segment_ids, lax.axis_index("ctx") * ctx_rows, ctx_rows, 1
    )
    mixed, log_total = lax.map(
        attend_forward, (queries, keys_all, values_all, query_docs, segment_ids)
    )
    mixed_rows = mixed.reshape(-1, local_width)
    attended = (
        lax.psum(
            jnp.dot(mixed_rows, full_out, preferred_element_type=jnp.float32).astype(jnp.bfloat16),
            "tp",
        ).astype(jnp.float32)
        + out_bias
    )
    hidden, normed_one, inv_one = norm_forward(
        rows_in.astype(jnp.float32) + attended, attn_gain, attn_shift
    )
    hidden_low = hidden.astype(jnp.bfloat16)
    pre_act = jnp.dot(hidden_low, full_up, preferred_element_type=jnp.float32) + up_bias
    acts_low = jax.nn.gelu(pre_act, approximate=False).astype(jnp.bfloat16)
    ffn_out = (
        lax.psum(
            jnp.dot(acts_low, full_down, preferred_element_type=jnp.float32).astype(jnp.bfloat16),
            "tp",
        ).astype(jnp.float32)
        + down_bias
    )
    output_rows, normed_two, inv_two = norm_forward(hidden + ffn_out, ffn_gain, ffn_shift)
    layer_output = output_rows.astype(jnp.bfloat16).reshape(layer_input.shape)
    grad_out = out_cotangent.reshape(-1, width).astype(jnp.float32)
    grad_two, ffn_gain_grad, ffn_shift_grad = norm_backward(grad_out, normed_two, inv_two, ffn_gain)
    grad_ffn = grad_two.astype(jnp.bfloat16)
    down_bias_grad = jnp.sum(grad_ffn, axis=0, dtype=jnp.float32)
    down_part = contract_rows(acts_low, grad_ffn)
    grad_acts = contract_last(grad_ffn, full_down)
    _, gelu_back = jax.vjp(partial(jax.nn.gelu, approximate=False), pre_act)
    grad_pre = gelu_back(grad_acts)[0].astype(jnp.bfloat16)
    up_bias_grad = jnp.sum(grad_pre, axis=0, dtype=jnp.float32)
    up_part = contract_rows(hidden_low, grad_pre)
    grad_hidden = grad_two + lax.psum(
        contract_last(grad_pre, full_up).astype(jnp.bfloat16), "tp"
    ).astype(jnp.float32)
    grad_one, attn_gain_grad, attn_shift_grad = norm_backward(
        grad_hidden, normed_one, inv_one, attn_gain
    )
    grad_attn = grad_one.astype(jnp.bfloat16)
    out_bias_grad = jnp.sum(grad_attn, axis=0, dtype=jnp.float32)
    out_part = contract_rows(mixed_rows, grad_attn)
    grad_mixed = contract_last(grad_attn, full_out).astype(jnp.bfloat16).reshape(shaped)
    keys_back, values_back = (
        lax.all_gather(keys_mine, "ctx", axis=1, tiled=True),
        lax.all_gather(values_mine, "ctx", axis=1, tiled=True),
    )
    grad_queries, grad_keys_all, grad_values_all = lax.map(
        attend_backward,
        (queries, keys_back, values_back, query_docs, segment_ids, grad_mixed, log_total),
    )
    grad_keys, grad_values = (
        lax.psum_scatter(
            grad_keys_all.astype(jnp.bfloat16), "ctx", scatter_dimension=1, tiled=True
        ).astype(jnp.float32),
        lax.psum_scatter(
            grad_values_all.astype(jnp.bfloat16), "ctx", scatter_dimension=1, tiled=True
        ).astype(jnp.float32),
    )
    grad_keys = grad_keys.astype(jnp.bfloat16).reshape(-1, local_width)
    grad_values = grad_values.astype(jnp.bfloat16).reshape(-1, local_width)
    grad_scaled = grad_queries.reshape(-1, local_width) * jnp.bfloat16(scale)
    grad_joined = jnp.concatenate([grad_scaled, grad_keys, grad_values], axis=1)
    joined_part = contract_rows(rows_in, grad_joined)
    query_part = joined_part[:, :local_width]
    key_part = joined_part[:, local_width : 2 * local_width]
    value_part = joined_part[:, 2 * local_width :]
    query_bias_grad = jnp.sum(grad_scaled, axis=0, dtype=jnp.float32)
    value_bias_grad = jnp.sum(grad_values, axis=0, dtype=jnp.float32)
    back_terms = contract_last(grad_joined, joined_proj)
    input_grad = (
        grad_one + lax.psum(back_terms.astype(jnp.bfloat16), "tp").astype(jnp.float32)
    ).reshape(layer_input.shape)
    sliced = (
        lax.psum_scatter(
            query_part.astype(jnp.bfloat16), "shard", scatter_dimension=0, tiled=True
        ).astype(jnp.float32),
        lax.psum_scatter(
            key_part.astype(jnp.bfloat16), "shard", scatter_dimension=0, tiled=True
        ).astype(jnp.float32),
        lax.psum_scatter(
            value_part.astype(jnp.bfloat16), "shard", scatter_dimension=0, tiled=True
        ).astype(jnp.float32),
        lax.psum_scatter(
            out_part.astype(jnp.bfloat16), "shard", scatter_dimension=1, tiled=True
        ).astype(jnp.float32),
        lax.psum_scatter(
            up_part.astype(jnp.bfloat16), "shard", scatter_dimension=0, tiled=True
        ).astype(jnp.float32),
        lax.psum_scatter(
            down_part.astype(jnp.bfloat16), "shard", scatter_dimension=1, tiled=True
        ).astype(jnp.float32),
    )
    reduced = (
        lax.psum(sliced[0].astype(jnp.bfloat16), "ctx").astype(jnp.float32),
        lax.psum(sliced[1].astype(jnp.bfloat16), "ctx").astype(jnp.float32),
        lax.psum(sliced[2].astype(jnp.bfloat16), "ctx").astype(jnp.float32),
        lax.psum(sliced[3].astype(jnp.bfloat16), "ctx").astype(jnp.float32),
        lax.psum(sliced[4].astype(jnp.bfloat16), "ctx").astype(jnp.float32),
        lax.psum(sliced[5].astype(jnp.bfloat16), "ctx").astype(jnp.float32),
    )
    small = lax.psum(
        (
            query_bias_grad,
            value_bias_grad,
            out_bias_grad,
            attn_gain_grad,
            attn_shift_grad,
            up_bias_grad,
            down_bias_grad,
            ffn_gain_grad,
            ffn_shift_grad,
        ),
        ("shard", "ctx"),
    )
    return (
        layer_output,
        input_grad,
        reduced[0],
        small[0],
        reduced[1],
        reduced[2],
        small[1],
        reduced[3],
        small[2],
        small[3],
        small[4],
        reduced[4],
        small[5],
        reduced[5],
        small[6],
        small[7],
        small[8],
    )


PAIR = 2 * HEAD_DIM
QBLOCK = 128


def dot32(left, right):
    return jnp.dot(left, right, preferred_element_type=jnp.float32)


def stack_heads(rows):
    lane = lax.broadcasted_iota(jnp.int32, rows.shape, 1)
    nought = jnp.zeros_like(rows)
    return jnp.concatenate(
        [jnp.where(lane < HEAD_DIM, rows, nought), jnp.where(lane >= HEAD_DIM, rows, nought)], axis=0
    )


def unstack_heads(tall):
    count = tall.shape[0] // 2
    lane = lax.broadcasted_iota(jnp.int32, (count, tall.shape[1]), 1)
    return jnp.where(lane < HEAD_DIM, tall[:count], tall[count:])


def masked_scores(queries, keys, same):
    scores = contract_last(queries, keys)
    return jnp.where(jnp.concatenate([same, same], axis=0), scores, jnp.float32(far_below))


def attend_kernel(span, q_ref, k_ref, v_ref, kd_ref, qd_ref, *refs):
    o_ref, l_ref = refs[-2:]
    here = pl.ds(pl.multiple_of(pl.program_id(1) * QBLOCK, QBLOCK), span)
    same = qd_ref[:, :1] == kd_ref[:, here]
    logs = []
    for pair in range(q_ref.shape[1] // PAIR):
        cols = slice(pair * PAIR, (pair + 1) * PAIR)
        scores = masked_scores(stack_heads(q_ref[:, cols]), k_ref[here, cols], same)
        top = jnp.max(scores, axis=1, keepdims=True)
        expo = jnp.exp(scores - top)
        total = jnp.sum(expo, axis=1, keepdims=True)
        mixed = dot32(expo.astype(jnp.bfloat16), v_ref[here, cols]) * (1.0 / total)
        o_ref[:, cols] = unstack_heads(mixed).astype(jnp.bfloat16)
        log = top + jnp.log(total)
        logs += [log[:QBLOCK], log[QBLOCK:]]
    l_ref[0] = jnp.concatenate(logs, axis=1)


def attend_back_kernel(span, q_ref, k_ref, v_ref, kd_ref, qd_ref, do_ref, l_ref, *refs):
    dq_ref, dk_ref, dv_ref, dk_acc, dv_acc = refs[-5:]
    step = pl.program_id(1)

    @pl.when(step == 0)
    def _():
        dk_acc[...] = jnp.zeros_like(dk_acc)
        dv_acc[...] = jnp.zeros_like(dv_acc)

    here = pl.ds(pl.multiple_of(step * QBLOCK, QBLOCK), span)
    same = qd_ref[:, :1] == kd_ref[:, here]
    logs = l_ref[0]
    for pair in range(q_ref.shape[1] // PAIR):
        cols = slice(pair * PAIR, (pair + 1) * PAIR)
        keys = k_ref[here, cols]
        queries, grads = stack_heads(q_ref[:, cols]), stack_heads(do_ref[:, cols])
        log = jnp.concatenate([logs[:, 2 * pair + i : 2 * pair + i + 1] for i in (0, 1)], axis=0)
        probs = jnp.exp(masked_scores(queries, keys, same) - log)
        grad_probs = contract_last(grads, v_ref[here, cols])
        inner = jnp.sum(grad_probs * probs, axis=1, keepdims=True)
        grad_scores = (probs * (grad_probs - inner)).astype(jnp.bfloat16)
        grad_queries = unstack_heads(dot32(grad_scores, keys))
        dq_ref[:, cols] = (grad_queries * (1.0 / math.sqrt(HEAD_DIM))).astype(jnp.bfloat16)
        dk_acc[here, cols] += contract_rows(grad_scores, queries)
        dv_acc[here, cols] += contract_rows(probs.astype(jnp.bfloat16), grads)

    @pl.when(step == pl.num_programs(1) - 1)
    def _():
        dk_ref[...] = dk_acc[...].astype(jnp.bfloat16)
        dv_ref[...] = dv_acc[...].astype(jnp.bfloat16)


def attention_specs(window, cols, at):
    rows = pl.BlockSpec((QBLOCK, cols), lambda h, i: (i, at + h))
    keys = pl.BlockSpec((window, cols), lambda h, i: (0, at + h))
    key_docs = pl.BlockSpec((1, window), lambda h, i: (0, 0))
    query_docs = pl.BlockSpec((QBLOCK, QBLOCK), lambda h, i: (i, 0))
    logs = pl.BlockSpec((1, QBLOCK, cols // HEAD_DIM), lambda h, i: (at + h, i, 0))
    return rows, keys, key_docs, query_docs, logs


def attend(queries, keys, values, key_docs, query_docs, reach, half, prior=()):
    count, width = queries.shape
    window, cols = keys.shape[0], width // 2
    span = QBLOCK + 2 * reach
    rows, key_spec, kd_spec, qd_spec, logs = attention_specs(window, cols, half)
    return pl.pallas_call(
        partial(attend_kernel, span),
        grid=(1, count // QBLOCK),
        in_specs=[rows, key_spec, key_spec, kd_spec, qd_spec]
        + [pl.BlockSpec(memory_space=pl.ANY)] * len(prior),
        out_specs=[rows, logs],
        out_shape=[
            jax.ShapeDtypeStruct((count, width), jnp.bfloat16),
            jax.ShapeDtypeStruct((2, count, cols // HEAD_DIM), jnp.float32),
        ],
        input_output_aliases={5 + i: i for i in range(len(prior))},
        compiler_params=pltpu.CompilerParams(vmem_limit_bytes=16 << 20),
        cost_estimate=pl.CostEstimate(
            flops=16 * count * span * cols, bytes_accessed=4 << 20, transcendentals=0
        ),
        name="attend",
    )(queries, keys, values, key_docs, query_docs, *prior)


def attend_back(
    queries, keys, values, key_docs, query_docs, grads, logs_in, reach, half, prior=()
):
    count, width = queries.shape
    window, cols = keys.shape[0], width // 2
    span = QBLOCK + 2 * reach
    rows, key_spec, kd_spec, qd_spec, logs = attention_specs(window, cols, half)
    return pl.pallas_call(
        partial(attend_back_kernel, span),
        grid=(1, count // QBLOCK),
        in_specs=[rows, key_spec, key_spec, kd_spec, qd_spec, rows, logs]
        + [pl.BlockSpec(memory_space=pl.ANY)] * len(prior),
        out_specs=[rows, key_spec, key_spec],
        out_shape=[
            jax.ShapeDtypeStruct((count, width), jnp.bfloat16),
            jax.ShapeDtypeStruct((window, width), jnp.bfloat16),
            jax.ShapeDtypeStruct((window, width), jnp.bfloat16),
        ],
        scratch_shapes=[pltpu.VMEM((window, cols), jnp.float32)] * 2,
        input_output_aliases={7 + i: i for i in range(len(prior))},
        compiler_params=pltpu.CompilerParams(vmem_limit_bytes=24 << 20),
        cost_estimate=pl.CostEstimate(
            flops=40 * count * span * cols, bytes_accessed=6 << 20, transcendentals=0
        ),
        name="attend_back",
    )(queries, keys, values, key_docs, query_docs, grads, logs_in, *prior)


def half_cols(position, half):
    return pl.ds(pl.multiple_of(position * half, half), half)


def add_or_set(first, ref, index, terms):
    @pl.when(first)
    def _():
        ref[index] = terms

    @pl.when(jnp.logical_not(first))
    def _():
        ref[index] += terms


def ffn_kernel(place_ref, hb_ref, up_ref, down_ref, bias_ref, *refs):
    half = up_ref.shape[3]
    near, far = half_cols(place_ref[1], half), half_cols(1 - place_ref[1], half)
    last = len(refs) > 3
    if last:
        base_ref, _, _, acts_ref, slope_ref, own_ref, other_ref = refs
    else:
        acts_ref, slope_ref, total = refs

        @pl.when(pl.program_id(0) == 0)
        def _():
            total[...] = jnp.zeros_like(total)

    def chunk(rows):
        pre_act = dot32(hb_ref[rows, near], up_ref[0, 0]) + dot32(hb_ref[rows, far], up_ref[0, 1])
        pre_act += bias_ref[0]
        cdf = 0.5 * (1.0 + lax.erf(pre_act * math.sqrt(0.5)))
        bell = jnp.exp(-0.5 * pre_act * pre_act) * (1.0 / math.sqrt(2 * math.pi))
        acts = (pre_act * cdf).astype(jnp.bfloat16)
        acts_ref[rows] = acts
        slope_ref[rows] = (cdf + pre_act * bell).astype(jnp.bfloat16)
        return dot32(acts, down_ref[0, 0]), dot32(acts, down_ref[0, 1])

    count = hb_ref.shape[0] // 2
    if last:
        for part, to in enumerate((own_ref, other_ref)):
            rows = slice(part * count, (part + 1) * count)
            for cols, terms in zip((near, far), chunk(rows)):
                to[:, cols] = (base_ref[rows, cols] + terms).astype(to.dtype)
    else:

        @pl.loop(0, 2)
        def _(part):
            rows = pl.ds(pl.multiple_of(part * count, count), count)
            for cols, terms in zip((near, far), chunk(rows)):
                total[rows, cols] += terms


def ffn_back_kernel(
    place_ref,
    dz_ref,
    hb_ref,
    acts_ref,
    slope_ref,
    up_ref,
    down_ref,
    own_ref,
    other_ref,
    up_keep,
    up_give,
    down_keep,
    down_give,
    sums_ref,
    total,
    grad_pre,
    rows_t,
):
    step = pl.program_id(0)
    half = up_ref.shape[3]
    quarter = half // 2
    count = own_ref.shape[0]
    near, far = half_cols(place_ref[1], half), half_cols(1 - place_ref[1], half)
    @pl.when(step == 0)
    def _():
        total[...] = jnp.zeros_like(total)

    sums_ref[...] = jnp.zeros_like(sums_ref)

    @pl.loop(0, 2)
    def _(part):
        rows = pl.ds(pl.multiple_of(part * count, count), count)
        grad_acts = contract_last(dz_ref[rows, near], down_ref[0, 0])
        grad_acts += contract_last(dz_ref[rows, far], down_ref[0, 1])
        low = (slope_ref[rows].astype(jnp.float32) * grad_acts).astype(jnp.bfloat16)
        grad_pre[rows] = low
        sums_ref[0] += row_sum(low.astype(jnp.float32))
        total[rows, near] += contract_last(low, up_ref[0, 0])
        total[rows, far] += contract_last(low, up_ref[0, 1])

    @pl.when(step == 0)
    def _():
        rows_t[...] = hb_ref[...].T

    acts_t = acts_ref[...].T
    for side, cols in enumerate((near, far)):
        up_grad = dot32(rows_t[cols], grad_pre[...]).astype(jnp.bfloat16)
        down_grad = dot32(acts_t, dz_ref[:, cols]).astype(jnp.bfloat16)
        down_to = down_give if side else down_keep
        for across in (0, 1):
            mine = slice(across * quarter, (across + 1) * quarter)
            theirs = slice((1 - across) * quarter, (2 - across) * quarter)

            @pl.when(place_ref[3] == across)
            def _():
                up_keep[side, 0] = up_grad[mine]
                up_give[side, 0] = up_grad[theirs]
                down_to[0, 0] = down_grad[mine]
                down_to[1, 0] = down_grad[theirs]

    @pl.when(step == pl.num_programs(0) - 1)
    def _():
        own_ref[...] = total[:count].astype(jnp.bfloat16)
        other_ref[...] = total[count:].astype(jnp.bfloat16)


def whole(shape):
    return pl.BlockSpec(shape, lambda *_: (0,) * len(shape))


def ffn(place, rows, weights, bias, steps, prior=()):
    both, width = rows.shape
    tps, shards, _, half = weights.shape
    count = both // 2
    at = tps - steps if prior else 0
    matrix = (1, shards, half, half)
    block = pl.BlockSpec((both, half), lambda i, _: (0, at + i))
    hidden = jax.ShapeDtypeStruct((both, tps * half), jnp.bfloat16)
    if prior:
        last_specs = [whole((count, width)), whole((count, width))]
        last_shapes = [
            jax.ShapeDtypeStruct((count, width), jnp.bfloat16),
            jax.ShapeDtypeStruct((count, width), jnp.bfloat16),
        ]
        prior_specs = [whole((both, width))] + [pl.BlockSpec(memory_space=pl.ANY)] * 2
    else:
        last_specs = [whole((both, width))]
        last_shapes = [jax.ShapeDtypeStruct((both, width), jnp.float32)]
        prior_specs = []
    return pl.pallas_call(
        ffn_kernel,
        grid_spec=pltpu.PrefetchScalarGridSpec(
            num_scalar_prefetch=1,
            grid=(steps,),
            in_specs=[
                whole((both, width)),
                pl.BlockSpec(matrix, lambda i, _: (at + i, 0, 0, 0)),
                pl.BlockSpec(matrix, lambda i, _: (at + i, 0, 1, 0)),
                pl.BlockSpec((1, 1, half), lambda i, _: (at + i, 0, 0)),
            ]
            + prior_specs,
            out_specs=[block, block] + last_specs,
        ),
        out_shape=[hidden, hidden] + last_shapes,
        input_output_aliases={6: 0, 7: 1} if prior else {},
        compiler_params=pltpu.CompilerParams(vmem_limit_bytes=20 << 20),
        cost_estimate=pl.CostEstimate(
            flops=12 * both * width * steps * half, bytes_accessed=3 * steps << 20, transcendentals=0
        ),
        name="ffn",
    )(place, rows, weights, weights, bias, *prior)


def ffn_back(place, grads, rows, acts, slope, weights):
    both, width = rows.shape
    tps, shards, _, half = weights.shape
    count = both // 2
    matrix = (1, shards, half, half)
    block = pl.BlockSpec((both, half), lambda i, _: (0, i))

    def source(i, place_ref):
        return (place_ref[2] + tps - jnp.where(i < 2, i, 5 - i)) % tps

    parts = pl.BlockSpec(
        (2, 1, half // 2, half), lambda i, at: (0, source(i, at), 0, 0)
    )
    return pl.pallas_call(
        ffn_back_kernel,
        grid_spec=pltpu.PrefetchScalarGridSpec(
            num_scalar_prefetch=1,
            grid=(tps,),
            in_specs=[
                whole((both, width)),
                whole((both, width)),
                block,
                block,
                pl.BlockSpec(matrix, lambda i, _: (i, 0, 0, 0)),
                pl.BlockSpec(matrix, lambda i, _: (i, 0, 1, 0)),
            ],
            out_specs=[
                whole((count, width)),
                whole((count, width)),
                parts,
                parts,
                parts,
                parts,
                pl.BlockSpec((1, 1, half), lambda i, at: (source(i, at), 0, 0)),
            ],
            scratch_shapes=[
                pltpu.VMEM((both, width), jnp.float32),
                pltpu.VMEM((both, half), jnp.bfloat16),
                pltpu.VMEM((width, both), jnp.bfloat16),
            ],
        ),
        out_shape=[
            jax.ShapeDtypeStruct((count, width), jnp.bfloat16),
            jax.ShapeDtypeStruct((count, width), jnp.bfloat16),
            *[jax.ShapeDtypeStruct((2, tps, half // 2, half), jnp.bfloat16)] * 4,
            jax.ShapeDtypeStruct((tps, 1, half), jnp.float32),
        ],
        compiler_params=pltpu.CompilerParams(vmem_limit_bytes=26 << 20),
        cost_estimate=pl.CostEstimate(
            flops=12 * both * width * tps * half, bytes_accessed=20 << 20, transcendentals=0
        ),
        name="ffn_back",
    )(place, grads, rows, acts, slope, weights, weights)


def project_kernel(
    place_ref, w_mine, w_other, x_mine, x_other, bias_ref, q_ref, k_ref, v_ref, x_ref, wt
):
    core, shard, tp, across, start = (place_ref[i] for i in range(5))
    depth = w_mine.shape[3]
    width = x_ref.shape[1]
    part = width // 8
    length = 4 * x_mine.shape[2]
    reach = length // 2
    for c, source in enumerate((w_mine, w_other)):
        for y in (0, 1):
            cols = half_cols(shard + y - 2 * shard * y, depth)
            for k in range(4):
                row = ((tp + 4 - k) & 3) * 2 + core + c - 2 * core * c
                rows = pl.ds(pl.multiple_of(row * part, part), part)
                for m in range(3):
                    wt[m, rows, cols] = source[y, k, m * part : (m + 1) * part]
    for i in range(x_ref.shape[0] // QBLOCK):
        row = start - reach + i * QBLOCK
        inside = jnp.logical_and(row >= 0, row < 2 * length)
        at = jnp.where(inside, row, 0) // QBLOCK
        seq, block, piece = at // 8, (at // 2) & 3, at & 1
        here = jnp.where((block >> 1) == across, 0, 1)
        rows = pl.ds(pl.multiple_of(piece * QBLOCK, QBLOCK), QBLOCK)
        mine, other = x_mine[here, seq, rows], x_other[here, seq, rows]
        found = jnp.where((block & 1) == core, mine, other)
        x_ref[i * QBLOCK : (i + 1) * QBLOCK] = jnp.where(inside, found, jnp.zeros_like(found))
    count = q_ref.shape[0]
    scaled = contract_last(x_ref[reach : reach + count], wt[0]) + bias_ref[0:1]
    q_ref[...] = (scaled * (1.0 / math.sqrt(HEAD_DIM))).astype(jnp.bfloat16)
    chunk = x_ref.shape[0] // 4

    @pl.loop(0, 4)
    def _(step):
        rows = pl.ds(pl.multiple_of(step * chunk, 32), chunk)
        k_ref[rows] = contract_last(x_ref[rows], wt[1]).astype(jnp.bfloat16)
        v_ref[rows] = (contract_last(x_ref[rows], wt[2]) + bias_ref[1:2]).astype(jnp.bfloat16)


def project(place, w_mine, w_other, x_mine, x_other, biases, count, window):
    width = x_mine.shape[-1]
    return pl.pallas_call(
        project_kernel,
        in_specs=[pl.BlockSpec(memory_space=pltpu.SMEM)]
        + [pl.BlockSpec(memory_space=pltpu.VMEM)] * 5,
        out_specs=[pl.BlockSpec(memory_space=pltpu.VMEM)] * 5,
        out_shape=[
            jax.ShapeDtypeStruct((count, width), jnp.bfloat16),
            jax.ShapeDtypeStruct((window, width), jnp.bfloat16),
            jax.ShapeDtypeStruct((window, width), jnp.bfloat16),
            jax.ShapeDtypeStruct((window, width), jnp.bfloat16),
            jax.ShapeDtypeStruct((3, width, width), jnp.bfloat16),
        ],
        compiler_params=pltpu.CompilerParams(vmem_limit_bytes=24 << 20),
        cost_estimate=pl.CostEstimate(
            flops=4 * window * width * width, bytes_accessed=16 << 20, transcendentals=0
        ),
        name="project",
    )(place, w_mine, w_other, x_mine, x_other, biases)


def norm_pieces(resid):
    center = resid - jnp.mean(resid, axis=-1, keepdims=True)
    inv_std = lax.rsqrt(jnp.mean(center * center, axis=-1, keepdims=True) + eps_norm)
    return center * inv_std, inv_std


def norm_pull(grad_out, normed, inv_std, gain):
    grad_normed = grad_out * gain
    return inv_std * (
        grad_normed
        - jnp.mean(grad_normed, axis=-1, keepdims=True)
        - normed * jnp.mean(grad_normed * normed, axis=-1, keepdims=True)
    )


def row_sum(rows):
    return jnp.sum(rows, axis=0, keepdims=True)


def attend_out_kernel(
    place_ref, o_ref, x_ref, w_mine, w_other, vec_ref, hb_ref, n_ref, i_ref, wo_ref
):
    core, shard, tp = (place_ref[i] for i in range(3))
    part, depth = w_mine.shape[2:]

    @pl.when(pl.program_id(0) == 0)
    def _():
        for c, source in enumerate((w_mine, w_other)):
            for y in (0, 1):
                cols = half_cols(shard + y - 2 * shard * y, depth)
                for k in range(4):
                    row = ((tp + 4 - k) & 3) * 2 + core + c - 2 * core * c
                    rows = pl.ds(pl.multiple_of(row * part, part), part)
                    wo_ref[rows, cols] = source[k, y]

    resid = x_ref[...].astype(jnp.float32) + dot32(o_ref[...], wo_ref[...]) + vec_ref[0:1]
    normed, inv_std = norm_pieces(resid)
    hb_ref[...] = (normed * vec_ref[1:2] + vec_ref[2:3]).astype(jnp.bfloat16)
    n_ref[...] = normed.astype(jnp.bfloat16)
    i_ref[...] = jnp.broadcast_to(inv_std, i_ref.shape)


def row_blocks(width):
    return pl.BlockSpec((QBLOCK, width), lambda i, *_: (i, 0))


def on_rows(kernel, count, in_specs, out_specs, out_shape, name, scalars=0):
    return pl.pallas_call(
        kernel,
        grid_spec=pltpu.PrefetchScalarGridSpec(
            num_scalar_prefetch=scalars,
            grid=(count // QBLOCK,),
            in_specs=in_specs,
            out_specs=out_specs,
        ),
        out_shape=out_shape,
        compiler_params=pltpu.CompilerParams(vmem_limit_bytes=12 << 20),
        cost_estimate=pl.CostEstimate(flops=1 << 28, bytes_accessed=6 << 20, transcendentals=0),
        name=name,
    )


def attend_out(place, mixed, window_rows, reach, w_mine, w_other, vectors):
    count, width = mixed.shape
    rows = row_blocks(width)
    low = jax.ShapeDtypeStruct((count, width), jnp.bfloat16)
    return on_rows(
        attend_out_kernel,
        count,
        [
            rows,
            pl.BlockSpec((QBLOCK, width), lambda i, *_: (i + reach // QBLOCK, 0)),
            whole(w_mine.shape),
            whole(w_other.shape),
            whole(vectors.shape),
        ],
        [rows, rows, row_blocks(QBLOCK), whole((width, width))],
        [
            low,
            low,
            jax.ShapeDtypeStruct((count, QBLOCK), jnp.float32),
            jax.ShapeDtypeStruct((width, width), jnp.bfloat16),
        ],
        "attend_out",
        1,
    )(place, mixed, window_rows, w_mine, w_other, vectors)


def norm_sums(sums_ref, rows):
    sums = jnp.concatenate([row_sum(row) for row in rows], axis=0)
    add_or_set(pl.program_id(0) == 0, sums_ref, slice(None), sums)


def ffn_norm_kernel(h_ref, own_ref, got_ref, g_ref, vec_ref, y_ref, dz_ref, sums_ref):
    resid = h_ref[...].astype(jnp.float32) + own_ref[...].astype(jnp.float32)
    resid += got_ref[...].astype(jnp.float32) + vec_ref[0:1]
    normed, inv_std = norm_pieces(resid)
    y_ref[...] = (normed * vec_ref[1:2] + vec_ref[2:3]).astype(jnp.bfloat16)
    grad_out = g_ref[...].astype(jnp.float32)
    low = norm_pull(grad_out, normed, inv_std, vec_ref[1:2]).astype(jnp.bfloat16)
    dz_ref[...] = low
    norm_sums(sums_ref, (low.astype(jnp.float32), grad_out * normed, grad_out))


def ffn_norm(hidden, own, got, cots, vectors):
    count, width = hidden.shape
    rows = row_blocks(width)
    low = jax.ShapeDtypeStruct((count, width), jnp.bfloat16)
    return on_rows(
        ffn_norm_kernel,
        count,
        [rows, rows, rows, rows, whole(vectors.shape)],
        [rows, rows, whole((3, width))],
        [low, low, jax.ShapeDtypeStruct((3, width), jnp.float32)],
        "ffn_norm",
    )(hidden, own, got, cots, vectors)


def attend_norm_kernel(
    dz_ref, own_ref, got_ref, n_ref, i_ref, vec_ref, wo_ref, out_ref, da_ref, do_ref, sums_ref
):
    grad_out = dz_ref[...].astype(jnp.float32) + own_ref[...].astype(jnp.float32)
    grad_out += got_ref[...].astype(jnp.float32)
    normed = n_ref[...].astype(jnp.float32)
    grad = norm_pull(grad_out, normed, i_ref[:, :1], vec_ref[1:2])
    low = grad.astype(jnp.bfloat16)
    out_ref[...] = grad
    da_ref[...] = low
    do_ref[...] = contract_last(low, wo_ref[...]).astype(jnp.bfloat16)
    norm_sums(sums_ref, (low.astype(jnp.float32), grad_out * normed, grad_out))


def attend_norm(grads, own, got, normed, inv_std, vectors, weights):
    count, width = grads.shape
    rows = row_blocks(width)
    low = jax.ShapeDtypeStruct((count, width), jnp.bfloat16)
    return on_rows(
        attend_norm_kernel,
        count,
        [rows, rows, rows, rows, row_blocks(QBLOCK), whole(vectors.shape), whole(weights.shape)],
        [rows, rows, rows, whole((3, width))],
        [
            jax.ShapeDtypeStruct((count, width), jnp.float32),
            low,
            low,
            jax.ShapeDtypeStruct((3, width), jnp.float32),
        ],
        "attend_norm",
    )(grads, own, got, normed, inv_std, vectors, weights)


def attn_grads_kernel(
    place_ref, dq_ref, dk_ref, dv_ref, o_ref, da_ref, w_ref, attn_ref, ffn_ref, up_ref, *parts
):
    core, shard, across = place_ref[0], place_ref[1], place_ref[3]
    grad_ref = parts[2]
    depth = w_ref.shape[1] // 2
    part = depth // 4
    count = dq_ref.shape[0]
    reach = (w_ref.shape[0] - count) // 2
    sides = (
        (dq_ref, w_ref.at[reach : reach + count]),
        (dk_ref, w_ref),
        (dv_ref, w_ref),
        (o_ref, da_ref),
    )
    for m, (left, right) in enumerate(sides):
        grad_ref[...] = contract_rows(left[...], right[...]).astype(jnp.bfloat16)
        group = across if m < 2 else 1 - across
        rows = slice((m % 2) * part, (m % 2 + 1) * part)
        for z in (0, 1):
            for c in (0, 1):
                at = pl.ds(pl.multiple_of((2 * z + c + core - 2 * c * core) * part, part), part)
                parts[c][shard, group, z, rows] = grad_ref[at, :depth]
                parts[c][1 - shard, group, z, rows] = grad_ref[at, depth:]
    query_sum = row_sum(dq_ref[...].astype(jnp.float32))
    value_sum = row_sum(dv_ref[...].astype(jnp.float32))
    shared = []
    for source in (attn_ref, ffn_ref):
        for r in range(3):
            shared += [source[r : r + 1, :depth], source[r : r + 1, depth:]]
    half = depth // 2
    for z in (0, 1):
        own = slice(z * half, (z + 1) * half)
        heads = jnp.concatenate([query_sum[:, own], value_sum[:, own]], axis=1)
        none = jnp.zeros_like(heads)
        rows = [heads] + shared
        for c in (0, 1):
            last = [none if c else up_ref[z], none, none]
            for x, group in ((across, rows[:8]), (1 - across, rows[8:] + last)):
                block = jnp.concatenate(group, axis=0).astype(jnp.bfloat16)
                for y in (0, 1):
                    parts[c][y, x, z, 2 * part :] = block


def attn_grads(
    place, grad_queries, grad_keys, grad_values, mixed, grad_attn, near, attn_sums, ffn_sums, up_sums
):
    count, width = mixed.shape
    window = near.shape[0]
    depth = width // 2
    high = depth // 2 + 8
    cols = pl.BlockSpec((count, depth), lambda i, _: (0, i))
    near_cols = pl.BlockSpec((window, depth), lambda i, _: (0, i))
    return pl.pallas_call(
        attn_grads_kernel,
        grid_spec=pltpu.PrefetchScalarGridSpec(
            num_scalar_prefetch=1,
            grid=(2,),
            in_specs=[
                cols,
                near_cols,
                near_cols,
                cols,
                whole((count, width)),
                whole((window, width)),
                whole((3, width)),
                whole((3, width)),
                pl.BlockSpec((2, 1, depth), lambda i, _: (i, 0, 0)),
            ],
            out_specs=[pl.BlockSpec((2, 2, 2, high, depth), lambda i, _: (0, 0, i, 0, 0))] * 2,
            scratch_shapes=[pltpu.VMEM((depth, width), jnp.bfloat16)],
        ),
        out_shape=[jax.ShapeDtypeStruct((2, 2, 4, high, depth), jnp.bfloat16)] * 2,
        compiler_params=pltpu.CompilerParams(vmem_limit_bytes=24 << 20),
        cost_estimate=pl.CostEstimate(
            flops=4 * (window + count) * width * width, bytes_accessed=16 << 20, transcendentals=0
        ),
        name="attn_grads",
    )(
        place,
        grad_queries,
        grad_keys,
        grad_values,
        mixed,
        grad_attn,
        near,
        attn_sums,
        ffn_sums,
        up_sums,
    )


def span_grads_kernel(
    place_ref,
    dq_ref,
    dk_ref,
    dv_ref,
    w_ref,
    base_ref,
    own_ref,
    first_ref,
    second_ref,
    give_ref,
    near,
):
    core = place_ref[0]
    count, reach = own_ref.shape[0], give_ref.shape[0]
    far = count + reach
    size = near.shape[0] // 4

    @pl.loop(0, 4)
    def _(step):
        rows = pl.ds(pl.multiple_of(step * size, 32), size)
        near[rows] = dot32(dk_ref[rows], w_ref[1]) + dot32(dv_ref[rows], w_ref[2])

    def rows_at(start, size):
        return near[pl.ds(pl.multiple_of(start, QBLOCK), size)].astype(jnp.bfloat16)

    give_ref[...] = rows_at((1 - core) * far, reach)
    first_ref[...] = rows_at(jnp.where(core == 0, reach - count, far), count)
    second_ref[...] = rows_at(jnp.where(core == 0, 0, far + count), reach - count)
    own_ref[...] = base_ref[...] + dot32(dq_ref[...], w_ref[0]) + near[reach:far]


def span_grads(place, grad_queries, grad_keys, grad_values, weights, base):
    count, width = base.shape
    reach = (grad_keys.shape[0] - count) // 2
    vmem = pl.BlockSpec(memory_space=pltpu.VMEM)
    return pl.pallas_call(
        span_grads_kernel,
        in_specs=[pl.BlockSpec(memory_space=pltpu.SMEM)] + [vmem] * 5,
        out_specs=[vmem] * 4,
        out_shape=[
            jax.ShapeDtypeStruct((count, width), jnp.float32),
            jax.ShapeDtypeStruct((count, width), jnp.bfloat16),
            jax.ShapeDtypeStruct((reach - count, width), jnp.bfloat16),
            jax.ShapeDtypeStruct((reach, width), jnp.bfloat16),
        ],
        scratch_shapes=[pltpu.VMEM(grad_keys.shape, jnp.float32)],
        compiler_params=pltpu.CompilerParams(vmem_limit_bytes=16 << 20),
        cost_estimate=pl.CostEstimate(
            flops=4 * (count + 2 * reach) * width * width,
            bytes_accessed=12 << 20,
            transcendentals=0,
        ),
        name="span_grads",
    )(place, grad_queries, grad_keys, grad_values, weights, base)


def assemble_kernel(place_ref, one, two, three, four, halves, out_ref):
    core, tp, across = place_ref[0], place_ref[2], place_ref[3]
    block = out_ref.shape[1]
    part = block // 2
    mine = pl.ds(pl.multiple_of(core * part, part), part)
    other = pl.ds(pl.multiple_of((1 - core) * part, part), part)
    for k, source in enumerate((one, two, three, four)):
        z = (tp + 4 - k) & 3
        group, side = 3 * (z >> 1), z & 1
        out_ref[group + jnp.where(side == 1, 1, 2 * across)] = source[:block].astype(out_ref.dtype)
        foreign = group + 2 - 2 * across

        @pl.when(((side + across + core) & 1) == 1)
        def _():
            out_ref[foreign, mine] = source[block:].astype(out_ref.dtype)
            out_ref[foreign, other] = halves[k].astype(out_ref.dtype)


def assemble_late_kernel(place_ref, one, two, three, four, middle, foreign, out_ref):
    core, tp, across = place_ref[0], place_ref[2], place_ref[3]
    block = out_ref.shape[1]
    part = block // 2
    for k, source in enumerate((one, two, three, four)):
        z = (tp + 4 - k) & 3
        group, side = 3 * (z >> 1), z & 1
        at = group + jnp.where(side == 1, 1, 2 * across)
        odd = (across + side) & 1

        @pl.when(jnp.logical_and(odd == 0, core == 0))
        def _():
            out_ref[at] = source[:block]

        @pl.when(jnp.logical_and(odd == 0, core == 1))
        def _():
            out_ref[at, :part] = middle[k]
            out_ref[at, part:] = source[:part]

        @pl.when(jnp.logical_and(odd == 1, core == 0))
        def _():
            out_ref[at, :part] = source[block:]
            out_ref[at, part:] = middle[k]

        @pl.when(jnp.logical_and(odd == 1, core == 1))
        def _():
            out_ref[at] = source[part:]

        @pl.when(((side + across + core) & 1) == 1)
        def _():
            out_ref[group + 2 - 2 * across] = foreign[k // 2]


def assemble(kernel, place, pieces, others, seqs, dtype):
    rows, width = pieces[0].shape
    vmem = pl.BlockSpec(memory_space=pltpu.VMEM)
    return pl.pallas_call(
        kernel,
        in_specs=[pl.BlockSpec(memory_space=pltpu.SMEM)] + [vmem] * (4 + len(others)),
        out_specs=vmem,
        out_shape=jax.ShapeDtypeStruct((seqs, rows * 2 // 3, width), dtype),
        compiler_params=pltpu.CompilerParams(vmem_limit_bytes=10 << 20),
        cost_estimate=pl.CostEstimate(flops=1 << 20, bytes_accessed=8 << 20, transcendentals=0),
        name="assemble",
    )(place, *pieces, *others)


def finish_ffn_kernel(place_ref, mine, across_got, core_got, both_got, up_ref, down_ref):
    core, across = place_ref[0], place_ref[3]
    depth = mine.shape[1]
    part = depth // 2
    for c, x, source in (
        (core, across, mine),
        (core, 1 - across, across_got),
        (1 - core, across, core_got),
        (1 - core, 1 - across, both_got),
    ):
        rows = pl.ds(pl.multiple_of(x * part, part), part)
        up_ref[rows, half_cols(c, depth)] = source[:part].astype(jnp.float32)
        rows = pl.ds(pl.multiple_of(c * depth + x * part, part), part)
        down_ref[rows] = source[part:].astype(jnp.float32)


def finish_attn_kernel(
    place_ref, mine, across_got, core_got, both_got, q_ref, k_ref, v_ref, o_ref, sums_ref
):
    core, across = place_ref[0], place_ref[3]
    part = q_ref.shape[0] // 2
    for c, x, source in (
        (core, across, mine),
        (core, 1 - across, across_got),
        (1 - core, across, core_got),
        (1 - core, 1 - across, both_got),
    ):
        rows = pl.ds(pl.multiple_of(c * part, part), part)
        one = source[:part].astype(jnp.float32)
        two = source[part : 2 * part].astype(jnp.float32)
        sums_ref[c, x] = source[2 * part :].astype(jnp.float32)

        @pl.when(x == 0)
        def _():
            q_ref[rows], k_ref[rows] = one, two

        @pl.when(x == 1)
        def _():
            v_ref[rows], o_ref[rows] = one, two


def finish(kernel, place, pieces, shapes, name):
    vmem = pl.BlockSpec(memory_space=pltpu.VMEM)
    return pl.pallas_call(
        kernel,
        in_specs=[pl.BlockSpec(memory_space=pltpu.SMEM)] + [vmem] * 4,
        out_specs=[vmem] * len(shapes),
        out_shape=[jax.ShapeDtypeStruct(shape, jnp.float32) for shape in shapes],
        compiler_params=pltpu.CompilerParams(vmem_limit_bytes=8 << 20),
        cost_estimate=pl.CostEstimate(flops=1 << 20, bytes_accessed=4 << 20, transcendentals=0),
        name=name,
    )(place, *pieces)


def ctx_swap(array, bit):
    return lax.ppermute(array, "ctx", [(i, i ^ bit) for i in range(4)])


def core_swap(array):
    return ctx_swap(array, 1)


def tie(*arrays):
    return lax.optimization_barrier(arrays)


def across_swap(array):
    return ctx_swap(array, 2)


def in_order(flag, mine, other):
    return jnp.where(flag == 0, mine, other), jnp.where(flag == 0, other, mine)


def at(across, core, tp):
    return (2 * across + core) * 4 + tp


def across_pairs():
    pairs = []
    for tp in range(4):
        for across in (0, 1):
            core = across ^ (tp & 1)
            pairs.append((at(1 - across, core, tp), at(across, core, tp)))
    return pairs


def tp_shifts(array, cuts=(slice(None), slice(None), slice(None))):
    return [
        lax.ppermute(array[cut], "tp", [(i, (i + shift) % 4) for i in range(4)])
        for shift, cut in zip((1, 2, 3), cuts)
        if cut is not None
    ]


def by_tp(array, shifted):
    one, two, three = shifted
    line = jnp.stack([three, two, one, array, three, two, one])
    return lax.dynamic_slice_in_dim(line, 3 - lax.axis_index("tp"), 4, 0)


def shard_swap(array):
    return lax.ppermute(array, "shard", [(0, 1), (1, 0)])


def low_sum(left, right):
    return (left.astype(jnp.float32) + right.astype(jnp.float32)).astype(jnp.bfloat16)


def scatter_tp_start(parts):
    tp = lax.axis_index("tp")
    moved = [lax.dynamic_index_in_dim(parts, tp, 0, keepdims=False)]
    for shift in (1, 2, 3):
        sent = lax.dynamic_index_in_dim(parts, (tp + shift) & 3, 0, keepdims=False)
        moved.append(lax.ppermute(sent, "tp", [(i, (i + shift) % 4) for i in range(4)]))
    return moved


def scatter_tp_end(moved):
    return sum(part.astype(jnp.float32) for part in moved).astype(jnp.bfloat16)


def chain_pairs(turn):
    pairs = []
    for group in (0, 2):
        path = [(0, group), (0, group + 1), (1, group + 1), (1, group)]
        for (across, tp), (next_across, next_tp) in zip(path[:-1], path[1:]):
            pairs.append((at(across, 1, tp), at(next_across, 1 ^ turn, next_tp)))
            pairs.append((at(next_across, 0, next_tp), at(across, turn, tp)))
    return pairs


def block_pairs(core):
    pairs = []
    for tp in range(4):
        for across in (0, 1):
            source = 1 ^ across ^ (tp & 1)
            pairs.append((at(across, source, tp), at(1 - across, core, tp)))
    return pairs


def span_shards(
    layer_input,
    segment_ids,
    query_proj,
    query_bias,
    key_proj,
    value_proj,
    value_bias,
    out_proj,
    out_bias,
    attn_gain,
    attn_shift,
    up_proj,
    up_bias,
    down_proj,
    down_bias,
    ffn_gain,
    ffn_shift,
    out_cotangent,
):
    seqs, block, width = layer_input.shape
    length = segment_ids.shape[1]
    reach = length // 2
    count = seqs * block // 4
    window = count + 2 * reach
    bf16, f32 = jnp.bfloat16, jnp.float32
    ctx, tp = lax.axis_index("ctx"), lax.axis_index("tp")
    shard = lax.axis_index("shard")
    core, across, side = ctx & 1, ctx >> 1, tp & 1
    place = 2 * across + (side ^ across)
    odd = across ^ side

    heads = query_proj.shape[1]
    half = heads // 2
    depth = query_proj.shape[0]
    cut = up_proj.shape[1] // 2
    own_in = lax.dynamic_slice_in_dim(
        jnp.stack([query_proj.T, key_proj.T, value_proj.T]), core * half, half, 1
    ).reshape(3 * half, depth)
    own_biases = jnp.stack(
        [
            jnp.concatenate([query_bias, value_bias]),
            lax.dynamic_slice_in_dim(up_bias, core * cut, cut, 0),
        ]
    )
    own_in = jnp.concatenate([own_in, own_biases, jnp.zeros((14, depth), bf16)], axis=0)
    out_half = out_proj.shape[0] // 2
    own_rest = jnp.concatenate(
        [
            lax.dynamic_slice_in_dim(up_proj, core * cut, cut, 1),
            lax.dynamic_slice_in_dim(down_proj, core * cut, cut, 0),
            lax.dynamic_slice_in_dim(out_proj, core * out_half, out_half, 0),
        ],
        axis=0,
    )
    first_seq = 3 * (tp >> 1)
    mine = lax.dynamic_slice_in_dim(layer_input, first_seq + across, 2, 0)
    theirs = across_swap(lax.dynamic_slice_in_dim(layer_input, first_seq + 1 - across, 2, 0))
    in_shifted = tp_shifts(own_in)
    far_rest = shard_swap(own_rest)
    *in_shifted, theirs, far_rest = tie(*in_shifted, theirs, far_rest)
    in_near = jnp.stack([own_in] + in_shifted)
    (rest_one,) = tp_shifts(tie(own_rest, in_near)[0], (slice(None), None, None))
    own_pair = jnp.stack([own_rest[: 2 * cut], far_rest[: 2 * cut]])
    near_cot = lax.dynamic_index_in_dim(
        out_cotangent, first_seq + odd + across, 0, keepdims=False
    )
    far_cot = lax.ppermute(
        lax.dynamic_index_in_dim(
            tie(out_cotangent, theirs)[0], first_seq + 2 - 2 * across, 0, keepdims=False
        ),
        ("ctx", "tp"),
        across_pairs(),
    )
    in_far, rest_one, own_pair, far_cot = tie(shard_swap(in_near), rest_one, own_pair, far_cot)
    in_mine = jnp.stack([in_near, in_far])
    (rest_three,) = tp_shifts(tie(own_rest, in_near)[0], (None, None, slice(None)))
    in_other, rest_three = tie(core_swap(in_mine), rest_three)
    own_late = tie(own_rest, rest_three)[0]
    (some_two,) = tp_shifts(own_late, (None, slice(cut, None), None))
    (up_two,) = tp_shifts(own_late, (None, slice(cut), None))
    far_three = shard_swap(rest_three)
    bias_rows = in_mine[0, :, 3 * half]
    in_biases = by_tp(bias_rows[0], [bias_rows[1], bias_rows[2], bias_rows[3]]).astype(f32)
    in_biases = jnp.stack([in_biases[:, :heads].reshape(-1), in_biases[:, heads:].reshape(-1)])
    up_bias_here = in_mine[0, :, 3 * half + 1].reshape(4, 1, cut).astype(f32)

    pair = jnp.stack([mine, theirs])
    pair_other = core_swap(pair)
    start = 2 * count * place + count * core - length * across
    ids = lax.dynamic_slice_in_dim(segment_ids, first_seq + across, 2, 0)
    ids = (ids + jnp.array([[0], [1 << 16]], jnp.int32)).reshape(-1)
    no_doc = jnp.full((reach,), -1, jnp.int32)
    window_docs = lax.dynamic_slice_in_dim(
        jnp.concatenate([no_doc, ids, no_doc]), start, window, 0
    )
    key_docs = window_docs[None]
    query_docs = jnp.broadcast_to(window_docs[reach : reach + count, None], (count, QBLOCK))

    place = jnp.stack([core, shard, tp, across, start])
    far_one = shard_swap(rest_one)
    queries, keys, values, in_window, weights_t = project(
        place, in_mine, in_other, pair, pair_other, in_biases, count, window
    )
    attention = queries, keys, values, key_docs, query_docs, reach
    mixed, logs = attend(*attention, 0)
    mixed, far_one, far_three, some_two = tie(mixed, far_one, far_three, some_two)
    far_some_two = shard_swap(some_two)
    mixed, logs = attend(*attention, 1, (mixed, logs))
    mixed, far_some_two, up_two = tie(mixed, far_some_two, up_two)
    far_up_two = shard_swap(up_two)
    out_mine = jnp.stack(
        [
            jnp.stack([one[-out_half:], two[-out_half:]])
            for one, two in (
                (own_rest, far_rest),
                (rest_one, far_one),
                (some_two, far_some_two),
                (rest_three, far_three),
            )
        ]
    )
    attn_vectors = jnp.stack([out_bias, attn_gain, attn_shift]).astype(f32)
    hidden_low, normed_one, inv_one, full_out = attend_out(
        place, mixed, in_window, reach, out_mine, core_swap(out_mine), attn_vectors
    )
    hidden_other = core_swap(hidden_low)
    hidden_both = jnp.concatenate([hidden_low, hidden_other], axis=0)
    ffn_weights = jnp.stack(
        [
            own_pair,
            jnp.stack([rest_one[: 2 * cut], far_one[: 2 * cut]]),
            jnp.stack([rest_three[: 2 * cut], far_three[: 2 * cut]]),
            own_pair,
        ]
    )
    ffn_bias = jnp.stack([up_bias_here[k] for k in (0, 1, 3, 2)])
    acts, slope, ffn_sum = ffn(place, hidden_both, ffn_weights, ffn_bias, 3)
    ffn_sum, far_up_two = tie(ffn_sum, far_up_two)
    rest = ffn_weights.at[3].set(
        jnp.stack(
            [
                jnp.concatenate([up_two, some_two[:cut]], axis=0),
                jnp.concatenate([far_up_two, far_some_two[:cut]], axis=0),
            ]
        )
    )
    acts, slope, ffn_own, ffn_other = ffn(
        place, hidden_both, rest, ffn_bias, 1, (ffn_sum, acts, slope)
    )

    half_block = block // 2

    def deliver_start(rows):
        far_rows = jnp.where(odd == 0, rows[-block:], rows[:block])
        return (
            core_swap(jnp.where(odd == 0, rows[block:], rows[:half_block])),
            lax.ppermute(far_rows[:half_block], ("ctx", "tp"), block_pairs(0)),
            lax.ppermute(far_rows[half_block:], ("ctx", "tp"), block_pairs(1)),
        )

    def deliver_pack(rows, middle, low, high):
        where_kept = [
            rows[:block],
            jnp.concatenate([middle, rows[:half_block]], axis=0),
            jnp.concatenate([rows[block:], middle], axis=0),
            rows[half_block:],
        ]
        kept = jnp.where(
            odd == 0,
            jnp.where(core == 0, where_kept[0], where_kept[1]),
            jnp.where(core == 0, where_kept[2], where_kept[3]),
        )
        return jnp.concatenate([kept, low + high], axis=0)

    cot_pair = tie(jnp.stack([near_cot, far_cot]), queries)[0]
    cot_swapped = core_swap(cot_pair)
    low_cot, high_cot = in_order(core, near_cot, cot_swapped[0])
    far_cot = jnp.where(core == odd, far_cot, cot_swapped[1])
    chip_cot = jnp.where(
        odd == 0,
        jnp.concatenate([low_cot, high_cot, far_cot], axis=0),
        jnp.concatenate([far_cot, low_cot, high_cot], axis=0),
    )
    cot_rows = lax.dynamic_slice_in_dim(chip_cot, core * count, count, 0)


    ffn_vectors = jnp.stack([down_bias, ffn_gain, ffn_shift]).astype(f32)
    output_rows, grad_ffn, ffn_sums = ffn_norm(
        hidden_low, ffn_own, core_swap(ffn_other), cot_rows, ffn_vectors
    )
    grad_other = core_swap(grad_ffn)
    grad_ffn_both = jnp.concatenate([grad_ffn, grad_other], axis=0)
    out_pieces = [output_rows] + tp_shifts(output_rows)
    back_own, back_other, up_keep, up_give, down_keep, down_give, up_sums = ffn_back(
        place, grad_ffn_both, hidden_both, acts, slope, rest
    )
    back_own, out_pieces[1] = tie(back_own, out_pieces[1])
    grad_one, grad_attn, grad_mixed, attn_sums = attend_norm(
        grad_ffn, back_own, core_swap(back_other), normed_one, inv_one, attn_vectors, full_out
    )
    up_got = across_swap(up_give)
    down_got = shard_swap(down_give)
    attention = queries, keys, values, key_docs, query_docs, grad_mixed, logs, reach
    back = attend_back(*attention, 0)
    *back, out_pieces[3] = tie(*back, out_pieces[3])
    grad_scaled, grad_keys, grad_values = attend_back(*attention, 1, back)
    grad_keys, up_got, down_got = tie(grad_keys, up_got, down_got)
    up_parts, down_parts = low_sum(up_keep, up_got), low_sum(down_keep, down_got)
    up_got, down_got = shard_swap(up_parts[1]), across_swap(down_parts[1])
    own_sum, first, second, give = span_grads(
        place, grad_scaled, grad_keys, grad_values, weights_t, grad_one
    )
    got = core_swap(give)
    shared = reach - count
    to_own = lax.dynamic_slice_in_dim(got, (1 - core) * shared, count, 0)
    to_next = lax.dynamic_slice_in_dim(got, core * count, shared, 0)
    no_rows = jnp.zeros((count - shared, width), bf16)
    first = low_sum(
        first,
        jnp.where(
            core == 0,
            jnp.concatenate([no_rows, to_next], axis=0),
            jnp.concatenate([to_next, no_rows], axis=0),
        ),
    )
    first_now, up_got, down_got, out_pieces[2] = tie(first, up_got, down_got, out_pieces[2])
    ffn_parts = jnp.concatenate(
        [low_sum(up_parts[0], up_got), low_sum(down_parts[0], down_got)], axis=1
    )
    ffn_near = scatter_tp_start(ffn_parts)
    first_got = lax.ppermute(first, ("ctx", "tp"), chain_pairs(1))
    second_got = lax.ppermute(second, ("ctx", "tp"), chain_pairs(0))
    grad_keys, first_now = tie(grad_keys, first)
    attn_parts = attn_grads(
        place,
        grad_scaled,
        grad_keys,
        grad_values,
        mixed,
        grad_attn,
        in_window,
        attn_sums,
        ffn_sums,
        up_sums,
    )
    first_got, second_got, attn_keep, attn_give, ffn_near[1], ffn_near[3] = tie(
        first_got, second_got, *attn_parts, ffn_near[1], ffn_near[3]
    )
    attn_core = core_swap(attn_give)
    own_sum += to_own.astype(f32) + first_got.astype(f32)
    own_sum += jnp.where(
        core == 0,
        jnp.concatenate([no_rows, second_got], axis=0),
        jnp.concatenate([second_got, no_rows], axis=0),
    ).astype(f32)
    own_low = own_sum.astype(bf16)
    in_moves = deliver_start(own_low)
    *in_moves, attn_core, ffn_near[2] = tie(*in_moves, attn_core, ffn_near[2])
    in_packed = deliver_pack(own_low, *in_moves)
    in_pieces = [in_packed] + tp_shifts(in_packed)
    attn_parts = low_sum(attn_keep, attn_core)
    attn_got = shard_swap(attn_parts[1])
    parity = (tp + 1 + across + core) & 1
    out_sent = [
        jnp.where(
            core == 0,
            jnp.where(parity == 0, even[:block], odd_one[:block]),
            jnp.where(parity == 0, even[-block:], odd_one[-block:]),
        )
        for even, odd_one in (out_pieces[:2], out_pieces[2:])
    ]
    out_foreign = lax.ppermute(jnp.stack(out_sent), "ctx", [(i, 3 - i) for i in range(4)])
    out_middle = core_swap(
        jnp.stack(
            [
                jnp.where(((across + tp + k) & 1) == 0, piece[block:], piece[:half_block])
                for k, piece in enumerate(out_pieces)
            ]
        )
    )
    attn_got, in_pieces[1], in_pieces[3] = tie(attn_got, in_pieces[1], in_pieces[3])
    attn_mid = low_sum(attn_parts[0], attn_got)
    attn_got = across_swap(attn_mid[1])
    ffn_low = scatter_tp_end(ffn_near)
    ffn_got = across_swap(ffn_low)
    attn_got, out_foreign, out_middle = tie(attn_got, out_foreign, out_middle)
    attn_near = scatter_tp_start(low_sum(attn_mid[0], attn_got))
    layer_output = assemble(
        assemble_late_kernel, place, out_pieces, (out_middle, out_foreign), seqs, bf16
    )
    layer_output, in_pieces[2], attn_near[3], ffn_got = tie(
        layer_output, in_pieces[2], attn_near[3], ffn_got
    )
    in_halves = core_swap(jnp.stack([piece[block:] for piece in in_pieces]))
    input_grad = assemble(assemble_kernel, place, in_pieces, (in_halves,), seqs, f32)
    up_grad, down_grad = finish(
        finish_ffn_kernel,
        place,
        (ffn_low, ffn_got, core_swap(ffn_low), core_swap(ffn_got)),
        ((cut, 2 * cut), (2 * cut, cut)),
        "finish_ffn",
    )
    attn_low = scatter_tp_end(attn_near)
    attn_got, input_grad = tie(across_swap(attn_low), input_grad)
    *weight_grads, sums = finish(
        finish_attn_kernel,
        place,
        (attn_low, attn_got, core_swap(attn_low), core_swap(attn_got)),
        ((heads, depth),) * 4 + ((2, 2, 8, depth),),
        "finish_attn",
    )
    up_bias_grad = sums[:, 1, 5].reshape(-1)
    sums = sums[0].reshape(16, depth)
    row_sums = sums[1:13].reshape(6, width)
    return (
        layer_output,
        input_grad,
        weight_grads[0].T,
        sums[0, :heads],
        weight_grads[1].T,
        weight_grads[2].T,
        sums[0, heads:],
        weight_grads[3],
        row_sums[0],
        row_sums[1],
        row_sums[2],
        up_grad,
        up_bias_grad,
        down_grad,
        row_sums[3],
        row_sums[4],
        row_sums[5],
    )


def pick_plan(mesh):
    shape = dict(mesh.shape)

    def plan(layer_input, segment_ids, *others):
        seqs, block, _ = layer_input.shape
        fits = (
            (shape["shard"], shape["ctx"], shape["tp"]) == (2, 4, 4)
            and seqs == 6
            and segment_ids.shape[1] == 4 * block
            and block == 2 * QBLOCK
        )
        chosen = span_shards if fits else general_shards
        return chosen(layer_input, segment_ids, *others)

    return plan


def solution(mesh):
    return jax.shard_map(
        pick_plan(mesh),
        mesh=mesh,
        in_specs=(
            P("shard", "ctx", None),
            P("shard", None),
            P("shard", "tp"),
            P("tp"),
            P("shard", "tp"),
            P("shard", "tp"),
            P("tp"),
            P("tp", "shard"),
            P(),
            P(),
            P(),
            P("shard", "tp"),
            P("tp"),
            P("tp", "shard"),
            P(),
            P(),
            P(),
            P("shard", "ctx", None),
        ),
        out_specs=(
            P("shard", "ctx", None),
            P("shard", "ctx", None),
            P("shard", "tp"),
            P("tp"),
            P("shard", "tp"),
            P("shard", "tp"),
            P("tp"),
            P("tp", "shard"),
            P(),
            P(),
            P(),
            P("shard", "tp"),
            P("tp"),
            P("tp", "shard"),
            P(),
            P(),
            P(),
        ),
        check_vma=False,
    )
```

```python
from functools import partial
import math

import jax
import jax.numpy as jnp
from jax import lax
from jax.experimental import pallas as pl
from jax.experimental.pallas import tpu as pltpu
from jax.sharding import PartitionSpec as P

HEAD_DIM = 64


eps_norm = 1e-12
far_below = -1e30


def contract_rows(left, right):
    return lax.dot_general(
        left, right, (((0,), (0,)), ((), ())), preferred_element_type=jnp.float32
    )


def contract_last(left, right):
    return lax.dot_general(
        left, right, (((1,), (1,)), ((), ())), preferred_element_type=jnp.float32
    )


def norm_forward(resid, norm_gain, norm_shift):
    center = resid - jnp.mean(resid, axis=-1, keepdims=True)
    inv_std = lax.rsqrt(jnp.mean(center * center, axis=-1, keepdims=True) + eps_norm)
    normed = center * inv_std
    return (normed * norm_gain + norm_shift, normed, inv_std)


def norm_backward(grad_out, normed, inv_std, norm_gain):
    grad_normed = grad_out * norm_gain
    grad_in = inv_std * (
        grad_normed
        - jnp.mean(grad_normed, axis=-1, keepdims=True)
        - normed * jnp.mean(grad_normed * normed, axis=-1, keepdims=True)
    )
    return (grad_in, jnp.sum(grad_out * normed, axis=0), jnp.sum(grad_out, axis=0))


def split_heads(matrix):
    return matrix.reshape(matrix.shape[0], matrix.shape[1] // HEAD_DIM, HEAD_DIM)


def scores_of(queries, keys_all, query_docs, key_docs):
    scores = jnp.einsum(
        "qhd,khd->hqk",
        split_heads(queries),
        split_heads(keys_all),
        preferred_element_type=jnp.float32,
    )
    same_doc = (query_docs[:, None] == key_docs[None, :])[None]
    return jnp.where(same_doc, scores, jnp.float32(far_below))


def attend_forward(item):
    queries, keys_all, values_all, query_docs, key_docs = item
    scores = scores_of(queries, keys_all, query_docs, key_docs)
    top_score = jnp.max(scores, axis=-1, keepdims=True)
    expo = jnp.exp(scores - top_score)
    total = jnp.sum(expo, axis=-1, keepdims=True)
    probs = (expo / total).astype(jnp.bfloat16)
    mixed = jnp.einsum(
        "hqk,khd->qhd", probs, split_heads(values_all), preferred_element_type=jnp.float32
    )
    return (
        mixed.reshape(queries.shape).astype(jnp.bfloat16),
        (top_score + jnp.log(total))[:, :, 0],
    )


def score_grads(queries, keys_all, values_all, query_docs, key_docs, grad_mixed, log_total):
    scores = scores_of(queries, keys_all, query_docs, key_docs)
    probs = jnp.exp(scores - log_total[:, :, None])
    grad_probs = jnp.einsum(
        "qhd,khd->hqk",
        split_heads(grad_mixed),
        split_heads(values_all),
        preferred_element_type=jnp.float32,
    )
    inner = jnp.sum(grad_probs * probs, axis=-1)
    grad_scores = (probs * (grad_probs - inner[:, :, None])).astype(jnp.bfloat16)
    return (probs, grad_scores, inner)


def attend_backward(item):
    queries, keys_all, values_all, query_docs, key_docs, grad_mixed, log_total = item
    probs, grad_scores, inner = score_grads(
        queries, keys_all, values_all, query_docs, key_docs, grad_mixed, log_total
    )
    grad_heads = split_heads(grad_mixed)
    grad_queries = jnp.einsum(
        "hqk,khd->qhd", grad_scores, split_heads(keys_all), preferred_element_type=jnp.float32
    )
    grad_keys = jnp.einsum(
        "hqk,qhd->khd", grad_scores, split_heads(queries), preferred_element_type=jnp.float32
    )
    grad_values = jnp.einsum(
        "hqk,qhd->khd", probs.astype(jnp.bfloat16), grad_heads, preferred_element_type=jnp.float32
    )
    return (
        grad_queries.reshape(queries.shape).astype(jnp.bfloat16),
        grad_keys.reshape(keys_all.shape),
        grad_values.reshape(values_all.shape),
    )


def general_shards(
    layer_input,
    segment_ids,
    query_proj,
    query_bias,
    key_proj,
    value_proj,
    value_bias,
    out_proj,
    out_bias,
    attn_gain,
    attn_shift,
    up_proj,
    up_bias,
    down_proj,
    down_bias,
    ffn_gain,
    ffn_shift,
    out_cotangent,
):
    seq_here, ctx_rows, width = layer_input.shape
    scale = 1.0 / math.sqrt(HEAD_DIM)
    full_query, full_key, full_value, full_out, full_up, full_down = (
        lax.all_gather(query_proj, "shard", axis=0, tiled=True),
        lax.all_gather(key_proj, "shard", axis=0, tiled=True),
        lax.all_gather(value_proj, "shard", axis=0, tiled=True),
        lax.all_gather(out_proj, "shard", axis=1, tiled=True),
        lax.all_gather(up_proj, "shard", axis=0, tiled=True),
        lax.all_gather(down_proj, "shard", axis=1, tiled=True),
    )
    local_width = full_query.shape[1]
    joined_proj = jnp.concatenate([full_query, full_key, full_value], axis=1)
    rows_in = layer_input.reshape(seq_here * ctx_rows, width)
    projected = jnp.dot(rows_in, joined_proj, preferred_element_type=jnp.float32)
    shaped = (seq_here, ctx_rows, local_width)
    queries = (
        ((projected[:, :local_width] + query_bias) * scale).astype(jnp.bfloat16).reshape(shaped)
    )
    keys_mine = projected[:, local_width : 2 * local_width].astype(jnp.bfloat16).reshape(shaped)
    values_mine = (
        (projected[:, 2 * local_width :] + value_bias).astype(jnp.bfloat16).reshape(shaped)
    )
    keys_all, values_all = (
        lax.all_gather(keys_mine, "ctx", axis=1, tiled=True),
        lax.all_gather(values_mine, "ctx", axis=1, tiled=True),
    )
    query_docs = lax.dynamic_slice_in_dim(
        segment_ids, lax.axis_index("ctx") * ctx_rows, ctx_rows, 1
    )
    mixed, log_total = lax.map(
        attend_forward, (queries, keys_all, values_all, query_docs, segment_ids)
    )
    mixed_rows = mixed.reshape(-1, local_width)
    attended = (
        lax.psum(
            jnp.dot(mixed_rows, full_out, preferred_element_type=jnp.float32).astype(jnp.bfloat16),
            "tp",
        ).astype(jnp.float32)
        + out_bias
    )
    hidden, normed_one, inv_one = norm_forward(
        rows_in.astype(jnp.float32) + attended, attn_gain, attn_shift
    )
    hidden_low = hidden.astype(jnp.bfloat16)
    pre_act = jnp.dot(hidden_low, full_up, preferred_element_type=jnp.float32) + up_bias
    acts_low = jax.nn.gelu(pre_act, approximate=False).astype(jnp.bfloat16)
    ffn_out = (
        lax.psum(
            jnp.dot(acts_low, full_down, preferred_element_type=jnp.float32).astype(jnp.bfloat16),
            "tp",
        ).astype(jnp.float32)
        + down_bias
    )
    output_rows, normed_two, inv_two = norm_forward(hidden + ffn_out, ffn_gain, ffn_shift)
    layer_output = output_rows.astype(jnp.bfloat16).reshape(layer_input.shape)
    grad_out = out_cotangent.reshape(-1, width).astype(jnp.float32)
    grad_two, ffn_gain_grad, ffn_shift_grad = norm_backward(grad_out, normed_two, inv_two, ffn_gain)
    grad_ffn = grad_two.astype(jnp.bfloat16)
    down_bias_grad = jnp.sum(grad_ffn, axis=0, dtype=jnp.float32)
    down_part = contract_rows(acts_low, grad_ffn)
    grad_acts = contract_last(grad_ffn, full_down)
    _, gelu_back = jax.vjp(partial(jax.nn.gelu, approximate=False), pre_act)
    grad_pre = gelu_back(grad_acts)[0].astype(jnp.bfloat16)
    up_bias_grad = jnp.sum(grad_pre, axis=0, dtype=jnp.float32)
    up_part = contract_rows(hidden_low, grad_pre)
    grad_hidden = grad_two + lax.psum(
        contract_last(grad_pre, full_up).astype(jnp.bfloat16), "tp"
    ).astype(jnp.float32)
    grad_one, attn_gain_grad, attn_shift_grad = norm_backward(
        grad_hidden, normed_one, inv_one, attn_gain
    )
    grad_attn = grad_one.astype(jnp.bfloat16)
    out_bias_grad = jnp.sum(grad_attn, axis=0, dtype=jnp.float32)
    out_part = contract_rows(mixed_rows, grad_attn)
    grad_mixed = contract_last(grad_attn, full_out).astype(jnp.bfloat16).reshape(shaped)
    keys_back, values_back = (
        lax.all_gather(keys_mine, "ctx", axis=1, tiled=True),
        lax.all_gather(values_mine, "ctx", axis=1, tiled=True),
    )
    grad_queries, grad_keys_all, grad_values_all = lax.map(
        attend_backward,
        (queries, keys_back, values_back, query_docs, segment_ids, grad_mixed, log_total),
    )
    grad_keys, grad_values = (
        lax.psum_scatter(
            grad_keys_all.astype(jnp.bfloat16), "ctx", scatter_dimension=1, tiled=True
        ).astype(jnp.float32),
        lax.psum_scatter(
            grad_values_all.astype(jnp.bfloat16), "ctx", scatter_dimension=1, tiled=True
        ).astype(jnp.float32),
    )
    grad_keys = grad_keys.astype(jnp.bfloat16).reshape(-1, local_width)
    grad_values = grad_values.astype(jnp.bfloat16).reshape(-1, local_width)
    grad_scaled = grad_queries.reshape(-1, local_width) * jnp.bfloat16(scale)
    grad_joined = jnp.concatenate([grad_scaled, grad_keys, grad_values], axis=1)
    joined_part = contract_rows(rows_in, grad_joined)
    query_part = joined_part[:, :local_width]
    key_part = joined_part[:, local_width : 2 * local_width]
    value_part = joined_part[:, 2 * local_width :]
    query_bias_grad = jnp.sum(grad_scaled, axis=0, dtype=jnp.float32)
    value_bias_grad = jnp.sum(grad_values, axis=0, dtype=jnp.float32)
    back_terms = contract_last(grad_joined, joined_proj)
    input_grad = (
        grad_one + lax.psum(back_terms.astype(jnp.bfloat16), "tp").astype(jnp.float32)
    ).reshape(layer_input.shape)
    sliced = (
        lax.psum_scatter(
            query_part.astype(jnp.bfloat16), "shard", scatter_dimension=0, tiled=True
        ).astype(jnp.float32),
        lax.psum_scatter(
            key_part.astype(jnp.bfloat16), "shard", scatter_dimension=0, tiled=True
        ).astype(jnp.float32),
        lax.psum_scatter(
            value_part.astype(jnp.bfloat16), "shard", scatter_dimension=0, tiled=True
        ).astype(jnp.float32),
        lax.psum_scatter(
            out_part.astype(jnp.bfloat16), "shard", scatter_dimension=1, tiled=True
        ).astype(jnp.float32),
        lax.psum_scatter(
            up_part.astype(jnp.bfloat16), "shard", scatter_dimension=0, tiled=True
        ).astype(jnp.float32),
        lax.psum_scatter(
            down_part.astype(jnp.bfloat16), "shard", scatter_dimension=1, tiled=True
        ).astype(jnp.float32),
    )
    reduced = (
        lax.psum(sliced[0].astype(jnp.bfloat16), "ctx").astype(jnp.float32),
        lax.psum(sliced[1].astype(jnp.bfloat16), "ctx").astype(jnp.float32),
        lax.psum(sliced[2].astype(jnp.bfloat16), "ctx").astype(jnp.float32),
        lax.psum(sliced[3].astype(jnp.bfloat16), "ctx").astype(jnp.float32),
        lax.psum(sliced[4].astype(jnp.bfloat16), "ctx").astype(jnp.float32),
        lax.psum(sliced[5].astype(jnp.bfloat16), "ctx").astype(jnp.float32),
    )
    small = lax.psum(
        (
            query_bias_grad,
            value_bias_grad,
            out_bias_grad,
            attn_gain_grad,
            attn_shift_grad,
            up_bias_grad,
            down_bias_grad,
            ffn_gain_grad,
            ffn_shift_grad,
        ),
        ("shard", "ctx"),
    )
    return (
        layer_output,
        input_grad,
        reduced[0],
        small[0],
        reduced[1],
        reduced[2],
        small[1],
        reduced[3],
        small[2],
        small[3],
        small[4],
        reduced[4],
        small[5],
        reduced[5],
        small[6],
        small[7],
        small[8],
    )


PAIR = 2 * HEAD_DIM
QBLOCK = 128


def dot32(left, right):
    return jnp.dot(left, right, preferred_element_type=jnp.float32)


def stack_heads(rows):
    lane = lax.broadcasted_iota(jnp.int32, rows.shape, 1)
    nought = jnp.zeros_like(rows)
    return jnp.concatenate(
        [jnp.where(lane < HEAD_DIM, rows, nought), jnp.where(lane >= HEAD_DIM, rows, nought)], axis=0
    )


def unstack_heads(tall):
    count = tall.shape[0] // 2
    lane = lax.broadcasted_iota(jnp.int32, (count, tall.shape[1]), 1)
    return jnp.where(lane < HEAD_DIM, tall[:count], tall[count:])


def masked_scores(queries, keys, same):
    scores = contract_last(queries, keys)
    return jnp.where(jnp.concatenate([same, same], axis=0), scores, jnp.float32(far_below))


def attend_kernel(span, q_ref, k_ref, v_ref, kd_ref, qd_ref, *refs):
    o_ref, l_ref = refs[-2:]
    here = pl.ds(pl.multiple_of(pl.program_id(1) * QBLOCK, QBLOCK), span)
    same = qd_ref[:, :1] == kd_ref[:, here]
    logs = []
    for pair in range(q_ref.shape[1] // PAIR):
        cols = slice(pair * PAIR, (pair + 1) * PAIR)
        scores = masked_scores(stack_heads(q_ref[:, cols]), k_ref[here, cols], same)
        top = jnp.max(scores, axis=1, keepdims=True)
        expo = jnp.exp(scores - top)
        total = jnp.sum(expo, axis=1, keepdims=True)
        mixed = dot32(expo.astype(jnp.bfloat16), v_ref[here, cols]) * (1.0 / total)
        o_ref[:, cols] = unstack_heads(mixed).astype(jnp.bfloat16)
        log = top + jnp.log(total)
        logs += [log[:QBLOCK], log[QBLOCK:]]
    l_ref[0] = jnp.concatenate(logs, axis=1)


def attend_back_kernel(span, q_ref, k_ref, v_ref, kd_ref, qd_ref, do_ref, l_ref, *refs):
    dq_ref, dk_ref, dv_ref, dk_acc, dv_acc = refs[-5:]
    step = pl.program_id(1)

    @pl.when(step == 0)
    def _():
        dk_acc[...] = jnp.zeros_like(dk_acc)
        dv_acc[...] = jnp.zeros_like(dv_acc)

    here = pl.ds(pl.multiple_of(step * QBLOCK, QBLOCK), span)
    same = qd_ref[:, :1] == kd_ref[:, here]
    logs = l_ref[0]
    for pair in range(q_ref.shape[1] // PAIR):
        cols = slice(pair * PAIR, (pair + 1) * PAIR)
        keys = k_ref[here, cols]
        queries, grads = stack_heads(q_ref[:, cols]), stack_heads(do_ref[:, cols])
        log = jnp.concatenate([logs[:, 2 * pair + i : 2 * pair + i + 1] for i in (0, 1)], axis=0)
        probs = jnp.exp(masked_scores(queries, keys, same) - log)
        grad_probs = contract_last(grads, v_ref[here, cols])
        inner = jnp.sum(grad_probs * probs, axis=1, keepdims=True)
        grad_scores = (probs * (grad_probs - inner)).astype(jnp.bfloat16)
        grad_queries = unstack_heads(dot32(grad_scores, keys))
        dq_ref[:, cols] = (grad_queries * (1.0 / math.sqrt(HEAD_DIM))).astype(jnp.bfloat16)
        dk_acc[here, cols] += contract_rows(grad_scores, queries)
        dv_acc[here, cols] += contract_rows(probs.astype(jnp.bfloat16), grads)

    @pl.when(step == pl.num_programs(1) - 1)
    def _():
        dk_ref[...] = dk_acc[...].astype(jnp.bfloat16)
        dv_ref[...] = dv_acc[...].astype(jnp.bfloat16)


def attention_specs(window, cols, at):
    rows = pl.BlockSpec((QBLOCK, cols), lambda h, i: (i, at + h))
    keys = pl.BlockSpec((window, cols), lambda h, i: (0, at + h))
    key_docs = pl.BlockSpec((1, window), lambda h, i: (0, 0))
    query_docs = pl.BlockSpec((QBLOCK, QBLOCK), lambda h, i: (i, 0))
    logs = pl.BlockSpec((1, QBLOCK, cols // HEAD_DIM), lambda h, i: (at + h, i, 0))
    return rows, keys, key_docs, query_docs, logs


def attend(queries, keys, values, key_docs, query_docs, reach, half, prior=()):
    count, width = queries.shape
    window, cols = keys.shape[0], width // 2
    span = QBLOCK + 2 * reach
    rows, key_spec, kd_spec, qd_spec, logs = attention_specs(window, cols, half)
    return pl.pallas_call(
        partial(attend_kernel, span),
        grid=(1, count // QBLOCK),
        in_specs=[rows, key_spec, key_spec, kd_spec, qd_spec]
        + [pl.BlockSpec(memory_space=pl.ANY)] * len(prior),
        out_specs=[rows, logs],
        out_shape=[
            jax.ShapeDtypeStruct((count, width), jnp.bfloat16),
            jax.ShapeDtypeStruct((2, count, cols // HEAD_DIM), jnp.float32),
        ],
        input_output_aliases={5 + i: i for i in range(len(prior))},
        compiler_params=pltpu.CompilerParams(vmem_limit_bytes=16 << 20),
        cost_estimate=pl.CostEstimate(
            flops=16 * count * span * cols, bytes_accessed=4 << 20, transcendentals=0
        ),
        name="attend",
    )(queries, keys, values, key_docs, query_docs, *prior)


def attend_back(queries, keys, values, key_docs, query_docs, reach, grads, logs_in):
    count, width = queries.shape
    window, cols = keys.shape[0], width // 2
    span = QBLOCK + 2 * reach
    rows, key_spec, kd_spec, qd_spec, logs = attention_specs(window, cols, 0)
    return pl.pallas_call(
        partial(attend_back_kernel, span),
        grid=(2, count // QBLOCK),
        in_specs=[rows, key_spec, key_spec, kd_spec, qd_spec, rows, logs],
        out_specs=[rows, key_spec, key_spec],
        out_shape=[
            jax.ShapeDtypeStruct((count, width), jnp.bfloat16),
            jax.ShapeDtypeStruct((window, width), jnp.bfloat16),
            jax.ShapeDtypeStruct((window, width), jnp.bfloat16),
        ],
        scratch_shapes=[pltpu.VMEM((window, cols), jnp.float32)] * 2,
        compiler_params=pltpu.CompilerParams(vmem_limit_bytes=24 << 20),
        cost_estimate=pl.CostEstimate(
            flops=40 * count * span * width, bytes_accessed=12 << 20, transcendentals=0
        ),
        name="attend_back",
    )(queries, keys, values, key_docs, query_docs, grads, logs_in)


def half_cols(position, half):
    return pl.ds(pl.multiple_of(position * half, half), half)


def add_or_set(first, ref, index, terms):
    @pl.when(first)
    def _():
        ref[index] = terms

    @pl.when(jnp.logical_not(first))
    def _():
        ref[index] += terms


def ffn_kernel(first_block, place_ref, hb_ref, w_ref, bias_ref, *refs):
    half = w_ref.shape[3]
    count = hb_ref.shape[0] // 2
    near, far = half_cols(place_ref[1], half), half_cols(1 - place_ref[1], half)
    hb_near = refs[-1]
    hb_near[:, :half] = hb_ref[:, near]
    hb_near[:, half:] = hb_ref[:, far]

    def chunk(block, rows, acts_ref, slope_ref):
        up = w_ref[block, :, :half].reshape(2 * half, half)
        pre_act = dot32(hb_near[rows], up) + bias_ref[block]
        cdf = 0.5 * (1.0 + lax.erf(pre_act * math.sqrt(0.5)))
        bell = jnp.exp(-0.5 * pre_act * pre_act) * (1.0 / math.sqrt(2 * math.pi))
        acts = (pre_act * cdf).astype(jnp.bfloat16)
        cols = pl.ds(pl.multiple_of(block * half, half), half)
        acts_ref[rows, cols] = acts
        slope_ref[rows, cols] = (cdf + pre_act * bell).astype(jnp.bfloat16)
        return dot32(acts, w_ref[block, 0, half:]), dot32(acts, w_ref[block, 1, half:])

    blocks = w_ref.shape[0]
    if first_block:
        base_ref, _, _, acts_ref, slope_ref, own_ref, other_ref = refs[:-1]
        for part, to in enumerate((own_ref, other_ref)):
            rows = slice(part * count, (part + 1) * count)
            terms = chunk(blocks - 1, rows, acts_ref, slope_ref)
            for y, cols in enumerate((near, far)):
                base = base_ref[rows, y * half : (y + 1) * half]
                to[:, cols] = (base + terms[y]).astype(to.dtype)
    else:
        acts_ref, slope_ref, total = refs[:-1]
        total[...] = jnp.zeros_like(total)

        @pl.loop(0, 2 * (blocks - 1))
        def _(i):
            rows = pl.ds(pl.multiple_of((i & 1) * count, count), count)
            one, two = chunk(i >> 1, rows, acts_ref, slope_ref)
            total[rows, :half] += one
            total[rows, half:] += two


def ffn_back_kernel(
    place_ref,
    dz_ref,
    hb_ref,
    acts_ref,
    slope_ref,
    w_ref,
    own_ref,
    other_ref,
    up_keep,
    up_give,
    down_keep,
    down_give,
    sums_ref,
    total,
    grad_pre,
    dz_near,
    rows_t,
    up_both,
    down_both,
    sums,
):
    step = pl.program_id(0)
    half = w_ref.shape[3]
    quarter = half // 2
    count = own_ref.shape[0]
    near, far = half_cols(place_ref[1], half), half_cols(1 - place_ref[1], half)
    first, second = slice(0, half), slice(half, 2 * half)

    @pl.when(step == 0)
    def _():
        total[...] = jnp.zeros_like(total)
        for to, cols in ((first, near), (second, far)):
            dz_near[:, to] = dz_ref[:, cols]
            rows_t[to] = hb_ref[:, cols].T

    for k, hid in enumerate((first, second)):
        for y, to in enumerate((first, second)):
            up_both[to, hid] = w_ref[k, y, :half]
            down_both[hid, to] = w_ref[k, y, half:]
    sums[...] = jnp.zeros_like(sums)

    @pl.loop(0, 2)
    def _(part):
        rows = pl.ds(pl.multiple_of(part * count, count), count)
        grad_acts = contract_last(dz_near[rows], down_both[...])
        low = (slope_ref[rows].astype(jnp.float32) * grad_acts).astype(jnp.bfloat16)
        grad_pre[rows] = low
        sums[...] += row_sum(low.astype(jnp.float32))
        total[rows] += contract_last(low, up_both[...])

    tps = [(place_ref[2] + 4 - jnp.where(step == 0, k, 3 - k)) & 3 for k in (0, 1)]
    for tp, hid in zip(tps, (first, second)):
        sums_ref[tp] = sums[:, hid]
    acts_t = acts_ref[...].T
    for side, cols in enumerate((first, second)):
        up_grad = dot32(rows_t[cols], grad_pre[...]).astype(jnp.bfloat16)
        down_grad = dot32(acts_t, dz_near[:, cols]).astype(jnp.bfloat16)
        down_to = down_give if side else down_keep
        for across in (0, 1):

            @pl.when(place_ref[3] == across)
            def _():
                for k in (0, 1):
                    tp = tps[k]
                    hid = slice(k * half, (k + 1) * half)
                    for x in (0, 1):
                        part = slice((x ^ across) * quarter, (x ^ across) * quarter + quarter)
                        down_rows = slice(k * half + part.start, k * half + part.stop)
                        (up_give if x else up_keep)[side, tp] = up_grad[part, hid]
                        down_to[x, tp] = down_grad[down_rows]

    @pl.when(step == pl.num_programs(0) - 1)
    def _():
        own_ref[:, near] = total[:count, first].astype(jnp.bfloat16)
        own_ref[:, far] = total[:count, second].astype(jnp.bfloat16)
        other_ref[:, near] = total[count:, first].astype(jnp.bfloat16)
        other_ref[:, far] = total[count:, second].astype(jnp.bfloat16)


def once(shape):
    return pl.BlockSpec(
        shape, lambda *_: (0,) * len(shape), pipeline_mode=pl.Buffered(buffer_count=1)
    )


def whole(shape):
    return pl.BlockSpec(shape, lambda *_: (0,) * len(shape))


def ffn(place, rows, weights, bias, prior=()):
    both, width = rows.shape
    tps, shards, _, half = weights.shape
    count = both // 2
    vmem = pl.BlockSpec(memory_space=pltpu.VMEM)
    low = jax.ShapeDtypeStruct((count, width), jnp.bfloat16)
    hidden = jax.ShapeDtypeStruct((both, tps * half), jnp.bfloat16)
    last = [low, low] if prior else [jax.ShapeDtypeStruct((both, width), jnp.float32)]
    steps = 1 if prior else tps - 1
    return pl.pallas_call(
        partial(ffn_kernel, bool(prior)),
        in_specs=[pl.BlockSpec(memory_space=pltpu.SMEM)] + [vmem] * (3 + len(prior)),
        out_specs=[vmem] * (2 + len(last)),
        out_shape=[hidden, hidden] + last,
        scratch_shapes=[pltpu.VMEM((both, width), jnp.bfloat16)],
        input_output_aliases={5: 0, 6: 1} if prior else {},
        compiler_params=pltpu.CompilerParams(vmem_limit_bytes=16 << 20),
        cost_estimate=pl.CostEstimate(
            flops=12 * both * width * steps * half, bytes_accessed=3 * steps << 20, transcendentals=0
        ),
        name="ffn",
    )(place, rows, weights, bias, *prior)


def ffn_back(place, grads, rows, acts, slope, weights):
    both, width = rows.shape
    tps, shards, _, half = weights.shape
    count = both // 2
    block = pl.BlockSpec((both, 2 * half), lambda i, _: (0, i))
    parts = (2, tps, half // 2, half)
    low = jax.ShapeDtypeStruct((count, width), jnp.bfloat16)
    return pl.pallas_call(
        ffn_back_kernel,
        grid_spec=pltpu.PrefetchScalarGridSpec(
            num_scalar_prefetch=1,
            grid=(tps // 2,),
            in_specs=[
                once((both, width)),
                once((both, width)),
                block,
                block,
                pl.BlockSpec((2, shards, 2 * half, half), lambda i, _: (i, 0, 0, 0)),
            ],
            out_specs=[
                whole((count, width)),
                whole((count, width)),
                *[whole(parts)] * 4,
                whole((tps, 1, half)),
            ],
            scratch_shapes=[
                pltpu.VMEM((both, width), jnp.float32),
                pltpu.VMEM((both, 2 * half), jnp.bfloat16),
                pltpu.VMEM((both, width), jnp.bfloat16),
                pltpu.VMEM((width, both), jnp.bfloat16),
                pltpu.VMEM((width, 2 * half), jnp.bfloat16),
                pltpu.VMEM((2 * half, width), jnp.bfloat16),
                pltpu.VMEM((1, 2 * half), jnp.float32),
            ],
        ),
        out_shape=[
            low,
            low,
            *[jax.ShapeDtypeStruct(parts, jnp.bfloat16)] * 4,
            jax.ShapeDtypeStruct((tps, 1, half), jnp.float32),
        ],
        compiler_params=pltpu.CompilerParams(vmem_limit_bytes=30 << 20),
        cost_estimate=pl.CostEstimate(
            flops=12 * both * width * tps * half, bytes_accessed=20 << 20, transcendentals=0
        ),
        name="ffn_back",
    )(place, grads, rows, acts, slope, weights)


def project_kernel(
    place_ref, w_mine, w_other, x_mine, x_other, bias_ref, q_ref, k_ref, v_ref, x_ref, wt
):
    core, shard, tp, across, start = (place_ref[i] for i in range(5))
    depth = w_mine.shape[3]
    width = x_ref.shape[1]
    part = width // 8
    length = 4 * x_mine.shape[2]
    reach = length // 2
    for c, source in enumerate((w_mine, w_other)):
        for y in (0, 1):
            cols = half_cols(shard + y - 2 * shard * y, depth)
            for k in range(4):
                row = ((tp + 4 - k) & 3) * 2 + core + c - 2 * core * c
                rows = pl.ds(pl.multiple_of(row * part, part), part)
                for m in range(3):
                    wt[m, rows, cols] = source[y, k, m * part : (m + 1) * part]
    for i in range(x_ref.shape[0] // QBLOCK):
        row = start - reach + i * QBLOCK
        inside = jnp.logical_and(row >= 0, row < 2 * length)
        at = jnp.where(inside, row, 0) // QBLOCK
        seq, block, piece = at // 8, (at // 2) & 3, at & 1
        here = jnp.where((block >> 1) == across, 0, 1)
        rows = pl.ds(pl.multiple_of(piece * QBLOCK, QBLOCK), QBLOCK)
        mine, other = x_mine[here, seq, rows], x_other[here, seq, rows]
        found = jnp.where((block & 1) == core, mine, other)
        x_ref[i * QBLOCK : (i + 1) * QBLOCK] = jnp.where(inside, found, jnp.zeros_like(found))
    count = q_ref.shape[0]
    scaled = contract_last(x_ref[reach : reach + count], wt[0]) + bias_ref[0:1]
    q_ref[...] = (scaled * (1.0 / math.sqrt(HEAD_DIM))).astype(jnp.bfloat16)
    chunk = x_ref.shape[0] // 4

    @pl.loop(0, 4)
    def _(step):
        rows = pl.ds(pl.multiple_of(step * chunk, 32), chunk)
        k_ref[rows] = contract_last(x_ref[rows], wt[1]).astype(jnp.bfloat16)
        v_ref[rows] = (contract_last(x_ref[rows], wt[2]) + bias_ref[1:2]).astype(jnp.bfloat16)


def project(place, w_mine, w_other, x_mine, x_other, biases, count, window):
    width = x_mine.shape[-1]
    return pl.pallas_call(
        project_kernel,
        in_specs=[pl.BlockSpec(memory_space=pltpu.SMEM)]
        + [pl.BlockSpec(memory_space=pltpu.VMEM)] * 5,
        out_specs=[pl.BlockSpec(memory_space=pltpu.VMEM)] * 5,
        out_shape=[
            jax.ShapeDtypeStruct((count, width), jnp.bfloat16),
            jax.ShapeDtypeStruct((window, width), jnp.bfloat16),
            jax.ShapeDtypeStruct((window, width), jnp.bfloat16),
            jax.ShapeDtypeStruct((window, width), jnp.bfloat16),
            jax.ShapeDtypeStruct((3, width, width), jnp.bfloat16),
        ],
        compiler_params=pltpu.CompilerParams(vmem_limit_bytes=24 << 20),
        cost_estimate=pl.CostEstimate(
            flops=4 * window * width * width, bytes_accessed=16 << 20, transcendentals=0
        ),
        name="project",
    )(place, w_mine, w_other, x_mine, x_other, biases)


def norm_pieces(resid):
    center = resid - jnp.mean(resid, axis=-1, keepdims=True)
    inv_std = lax.rsqrt(jnp.mean(center * center, axis=-1, keepdims=True) + eps_norm)
    return center * inv_std, inv_std


def norm_pull(grad_out, normed, inv_std, gain):
    grad_normed = grad_out * gain
    return inv_std * (
        grad_normed
        - jnp.mean(grad_normed, axis=-1, keepdims=True)
        - normed * jnp.mean(grad_normed * normed, axis=-1, keepdims=True)
    )


def row_sum(rows):
    return jnp.sum(rows, axis=0, keepdims=True)


def attend_out_kernel(
    place_ref, o_ref, x_ref, w_mine, w_other, vec_ref, hb_ref, n_ref, i_ref, wo_ref
):
    core, shard, tp = (place_ref[i] for i in range(3))
    part, depth = w_mine.shape[2:]

    @pl.when(pl.program_id(0) == 0)
    def _():
        for c, source in enumerate((w_mine, w_other)):
            for y in (0, 1):
                cols = half_cols(shard + y - 2 * shard * y, depth)
                for k in range(4):
                    row = ((tp + 4 - k) & 3) * 2 + core + c - 2 * core * c
                    rows = pl.ds(pl.multiple_of(row * part, part), part)
                    wo_ref[rows, cols] = source[k, y]

    resid = x_ref[...].astype(jnp.float32) + dot32(o_ref[...], wo_ref[...]) + vec_ref[0:1]
    normed, inv_std = norm_pieces(resid)
    hb_ref[...] = (normed * vec_ref[1:2] + vec_ref[2:3]).astype(jnp.bfloat16)
    n_ref[...] = normed.astype(jnp.bfloat16)
    i_ref[...] = jnp.broadcast_to(inv_std, i_ref.shape)


def row_blocks(width):
    return pl.BlockSpec((QBLOCK, width), lambda i, *_: (i, 0))


def on_rows(kernel, count, in_specs, out_specs, out_shape, name, scalars=0):
    return pl.pallas_call(
        kernel,
        grid_spec=pltpu.PrefetchScalarGridSpec(
            num_scalar_prefetch=scalars,
            grid=(count // QBLOCK,),
            in_specs=in_specs,
            out_specs=out_specs,
        ),
        out_shape=out_shape,
        compiler_params=pltpu.CompilerParams(vmem_limit_bytes=12 << 20),
        cost_estimate=pl.CostEstimate(flops=1 << 28, bytes_accessed=6 << 20, transcendentals=0),
        name=name,
    )


def attend_out(place, mixed, window_rows, reach, w_mine, w_other, vectors):
    count, width = mixed.shape
    rows = row_blocks(width)
    low = jax.ShapeDtypeStruct((count, width), jnp.bfloat16)
    return on_rows(
        attend_out_kernel,
        count,
        [
            rows,
            pl.BlockSpec((QBLOCK, width), lambda i, *_: (i + reach // QBLOCK, 0)),
            whole(w_mine.shape),
            whole(w_other.shape),
            whole(vectors.shape),
        ],
        [rows, rows, row_blocks(QBLOCK), whole((width, width))],
        [
            low,
            low,
            jax.ShapeDtypeStruct((count, QBLOCK), jnp.float32),
            jax.ShapeDtypeStruct((width, width), jnp.bfloat16),
        ],
        "attend_out",
        1,
    )(place, mixed, window_rows, w_mine, w_other, vectors)


def norm_sums(sums_ref, rows):
    sums = jnp.concatenate([row_sum(row) for row in rows], axis=0)
    add_or_set(pl.program_id(0) == 0, sums_ref, slice(None), sums)


def ffn_norm_kernel(h_ref, own_ref, got_ref, g_ref, vec_ref, y_ref, dz_ref, sums_ref):
    resid = h_ref[...].astype(jnp.float32) + own_ref[...].astype(jnp.float32)
    resid += got_ref[...].astype(jnp.float32) + vec_ref[0:1]
    normed, inv_std = norm_pieces(resid)
    y_ref[...] = (normed * vec_ref[1:2] + vec_ref[2:3]).astype(jnp.bfloat16)
    grad_out = g_ref[...].astype(jnp.float32)
    low = norm_pull(grad_out, normed, inv_std, vec_ref[1:2]).astype(jnp.bfloat16)
    dz_ref[...] = low
    norm_sums(sums_ref, (low.astype(jnp.float32), grad_out * normed, grad_out))


def ffn_norm(hidden, own, got, cots, vectors):
    count, width = hidden.shape
    rows = row_blocks(width)
    low = jax.ShapeDtypeStruct((count, width), jnp.bfloat16)
    return on_rows(
        ffn_norm_kernel,
        count,
        [rows, rows, rows, rows, whole(vectors.shape)],
        [rows, rows, whole((3, width))],
        [low, low, jax.ShapeDtypeStruct((3, width), jnp.float32)],
        "ffn_norm",
    )(hidden, own, got, cots, vectors)


def attend_norm_kernel(
    dz_ref, own_ref, got_ref, n_ref, i_ref, vec_ref, wo_ref, out_ref, da_ref, do_ref, sums_ref
):
    grad_out = dz_ref[...].astype(jnp.float32) + own_ref[...].astype(jnp.float32)
    grad_out += got_ref[...].astype(jnp.float32)
    normed = n_ref[...].astype(jnp.float32)
    grad = norm_pull(grad_out, normed, i_ref[:, :1], vec_ref[1:2])
    low = grad.astype(jnp.bfloat16)
    out_ref[...] = grad
    da_ref[...] = low
    do_ref[...] = contract_last(low, wo_ref[...]).astype(jnp.bfloat16)
    norm_sums(sums_ref, (low.astype(jnp.float32), grad_out * normed, grad_out))


def attend_norm(grads, own, got, normed, inv_std, vectors, weights):
    count, width = grads.shape
    rows = row_blocks(width)
    low = jax.ShapeDtypeStruct((count, width), jnp.bfloat16)
    return on_rows(
        attend_norm_kernel,
        count,
        [rows, rows, rows, rows, row_blocks(QBLOCK), whole(vectors.shape), whole(weights.shape)],
        [rows, rows, rows, whole((3, width))],
        [
            jax.ShapeDtypeStruct((count, width), jnp.float32),
            low,
            low,
            jax.ShapeDtypeStruct((3, width), jnp.float32),
        ],
        "attend_norm",
    )(grads, own, got, normed, inv_std, vectors, weights)


def attn_grads_kernel(
    place_ref, dq_ref, dk_ref, dv_ref, o_ref, da_ref, w_ref, attn_ref, ffn_ref, up_ref, *parts
):
    core, shard, across = place_ref[0], place_ref[1], place_ref[3]
    grad_ref = parts[2]
    depth = w_ref.shape[1] // 2
    part = depth // 4
    count = dq_ref.shape[0]
    reach = (w_ref.shape[0] - count) // 2
    sides = (
        (dq_ref, w_ref.at[reach : reach + count]),
        (dk_ref, w_ref),
        (dv_ref, w_ref),
        (o_ref, da_ref),
    )
    for m, (left, right) in enumerate(sides):
        grad_ref[...] = contract_rows(left[...], right[...]).astype(jnp.bfloat16)
        group = across if m < 2 else 1 - across
        rows = slice((m % 2) * part, (m % 2 + 1) * part)
        for z in (0, 1):
            for c in (0, 1):
                at = pl.ds(pl.multiple_of((2 * z + c + core - 2 * c * core) * part, part), part)
                parts[c][shard, group, z, rows] = grad_ref[at, :depth]
                parts[c][1 - shard, group, z, rows] = grad_ref[at, depth:]
    query_sum = row_sum(dq_ref[...].astype(jnp.float32))
    value_sum = row_sum(dv_ref[...].astype(jnp.float32))
    shared = []
    for source in (attn_ref, ffn_ref):
        for r in range(3):
            shared += [source[r : r + 1, :depth], source[r : r + 1, depth:]]
    half = depth // 2
    for z in (0, 1):
        own = slice(z * half, (z + 1) * half)
        heads = jnp.concatenate([query_sum[:, own], value_sum[:, own]], axis=1)
        none = jnp.zeros_like(heads)
        rows = [heads] + shared
        for c in (0, 1):
            last = [none if c else up_ref[z], none, none]
            for x, group in ((across, rows[:8]), (1 - across, rows[8:] + last)):
                block = jnp.concatenate(group, axis=0).astype(jnp.bfloat16)
                for y in (0, 1):
                    parts[c][y, x, z, 2 * part :] = block


def attn_grads(
    place, grad_queries, grad_keys, grad_values, mixed, grad_attn, near, attn_sums, ffn_sums, up_sums
):
    count, width = mixed.shape
    window = near.shape[0]
    depth = width // 2
    high = depth // 2 + 8
    cols = pl.BlockSpec((count, depth), lambda i, _: (0, i))
    near_cols = pl.BlockSpec((window, depth), lambda i, _: (0, i))
    return pl.pallas_call(
        attn_grads_kernel,
        grid_spec=pltpu.PrefetchScalarGridSpec(
            num_scalar_prefetch=1,
            grid=(2,),
            in_specs=[
                cols,
                near_cols,
                near_cols,
                cols,
                whole((count, width)),
                whole((window, width)),
                whole((3, width)),
                whole((3, width)),
                pl.BlockSpec((2, 1, depth), lambda i, _: (i, 0, 0)),
            ],
            out_specs=[pl.BlockSpec((2, 2, 2, high, depth), lambda i, _: (0, 0, i, 0, 0))] * 2,
            scratch_shapes=[pltpu.VMEM((depth, width), jnp.bfloat16)],
        ),
        out_shape=[jax.ShapeDtypeStruct((2, 2, 4, high, depth), jnp.bfloat16)] * 2,
        compiler_params=pltpu.CompilerParams(vmem_limit_bytes=24 << 20),
        cost_estimate=pl.CostEstimate(
            flops=4 * (window + count) * width * width, bytes_accessed=16 << 20, transcendentals=0
        ),
        name="attn_grads",
    )(
        place,
        grad_queries,
        grad_keys,
        grad_values,
        mixed,
        grad_attn,
        near,
        attn_sums,
        ffn_sums,
        up_sums,
    )


def span_grads_kernel(
    place_ref,
    dq_ref,
    dk_ref,
    dv_ref,
    w_ref,
    base_ref,
    own_ref,
    first_ref,
    second_ref,
    give_ref,
    near,
):
    core = place_ref[0]
    count, reach = own_ref.shape[0], give_ref.shape[0]
    far = count + reach
    size = near.shape[0] // 4

    @pl.loop(0, 4)
    def _(step):
        rows = pl.ds(pl.multiple_of(step * size, 32), size)
        near[rows] = dot32(dk_ref[rows], w_ref[1]) + dot32(dv_ref[rows], w_ref[2])

    def rows_at(start, size):
        return near[pl.ds(pl.multiple_of(start, QBLOCK), size)].astype(jnp.bfloat16)

    give_ref[...] = rows_at((1 - core) * far, reach)
    first_ref[...] = rows_at(jnp.where(core == 0, reach - count, far), count)
    second_ref[...] = rows_at(jnp.where(core == 0, 0, far + count), reach - count)
    own_ref[...] = base_ref[...] + dot32(dq_ref[...], w_ref[0]) + near[reach:far]


def span_grads(place, grad_queries, grad_keys, grad_values, weights, base):
    count, width = base.shape
    reach = (grad_keys.shape[0] - count) // 2
    vmem = pl.BlockSpec(memory_space=pltpu.VMEM)
    return pl.pallas_call(
        span_grads_kernel,
        in_specs=[pl.BlockSpec(memory_space=pltpu.SMEM)] + [vmem] * 5,
        out_specs=[vmem] * 4,
        out_shape=[
            jax.ShapeDtypeStruct((count, width), jnp.float32),
            jax.ShapeDtypeStruct((count, width), jnp.bfloat16),
            jax.ShapeDtypeStruct((reach - count, width), jnp.bfloat16),
            jax.ShapeDtypeStruct((reach, width), jnp.bfloat16),
        ],
        scratch_shapes=[pltpu.VMEM(grad_keys.shape, jnp.float32)],
        compiler_params=pltpu.CompilerParams(vmem_limit_bytes=16 << 20),
        cost_estimate=pl.CostEstimate(
            flops=4 * (count + 2 * reach) * width * width,
            bytes_accessed=12 << 20,
            transcendentals=0,
        ),
        name="span_grads",
    )(place, grad_queries, grad_keys, grad_values, weights, base)


def assemble_kernel(place_ref, one, two, three, four, halves, out_ref):
    core, tp, across = place_ref[0], place_ref[2], place_ref[3]
    block = out_ref.shape[1]
    part = block // 2
    mine = pl.ds(pl.multiple_of(core * part, part), part)
    other = pl.ds(pl.multiple_of((1 - core) * part, part), part)
    for k, source in enumerate((one, two, three, four)):
        z = (tp + 4 - k) & 3
        group, side = 3 * (z >> 1), z & 1
        out_ref[group + jnp.where(side == 1, 1, 2 * across)] = source[:block].astype(out_ref.dtype)
        foreign = group + 2 - 2 * across

        @pl.when(((side + across + core) & 1) == 1)
        def _():
            out_ref[foreign, mine] = source[block:].astype(out_ref.dtype)
            out_ref[foreign, other] = halves[k].astype(out_ref.dtype)


def assemble_late_kernel(place_ref, one, two, three, four, middle, foreign, out_ref):
    core, tp, across = place_ref[0], place_ref[2], place_ref[3]
    block = out_ref.shape[1]
    part = block // 2
    for k, source in enumerate((one, two, three, four)):
        z = (tp + 4 - k) & 3
        group, side = 3 * (z >> 1), z & 1
        at = group + jnp.where(side == 1, 1, 2 * across)
        odd = (across + side) & 1

        @pl.when(jnp.logical_and(odd == 0, core == 0))
        def _():
            out_ref[at] = source[:block]

        @pl.when(jnp.logical_and(odd == 0, core == 1))
        def _():
            out_ref[at, :part] = middle[k]
            out_ref[at, part:] = source[:part]

        @pl.when(jnp.logical_and(odd == 1, core == 0))
        def _():
            out_ref[at, :part] = source[block:]
            out_ref[at, part:] = middle[k]

        @pl.when(jnp.logical_and(odd == 1, core == 1))
        def _():
            out_ref[at] = source[part:]

        @pl.when(((side + across + core) & 1) == 1)
        def _():
            out_ref[group + 2 - 2 * across] = foreign[k // 2]


def assemble(kernel, place, pieces, others, seqs, dtype):
    rows, width = pieces[0].shape
    vmem = pl.BlockSpec(memory_space=pltpu.VMEM)
    return pl.pallas_call(
        kernel,
        in_specs=[pl.BlockSpec(memory_space=pltpu.SMEM)] + [vmem] * (4 + len(others)),
        out_specs=vmem,
        out_shape=jax.ShapeDtypeStruct((seqs, rows * 2 // 3, width), dtype),
        compiler_params=pltpu.CompilerParams(vmem_limit_bytes=10 << 20),
        cost_estimate=pl.CostEstimate(flops=1 << 20, bytes_accessed=8 << 20, transcendentals=0),
        name="assemble",
    )(place, *pieces, *others)


def finish_ffn_kernel(place_ref, mine, across_got, core_got, both_got, up_ref, down_ref):
    core, across = place_ref[0], place_ref[3]
    depth = mine.shape[1]
    part = depth // 2
    for c, x, source in (
        (core, across, mine),
        (core, 1 - across, across_got),
        (1 - core, across, core_got),
        (1 - core, 1 - across, both_got),
    ):
        rows = pl.ds(pl.multiple_of(x * part, part), part)
        up_ref[rows, half_cols(c, depth)] = source[:part].astype(jnp.float32)
        rows = pl.ds(pl.multiple_of(c * depth + x * part, part), part)
        down_ref[rows] = source[part:].astype(jnp.float32)


def finish_attn_kernel(
    place_ref, mine, across_got, core_got, both_got, q_ref, k_ref, v_ref, o_ref, sums_ref
):
    core, across = place_ref[0], place_ref[3]
    part = q_ref.shape[0] // 2
    for c, x, source in (
        (core, across, mine),
        (core, 1 - across, across_got),
        (1 - core, across, core_got),
        (1 - core, 1 - across, both_got),
    ):
        rows = pl.ds(pl.multiple_of(c * part, part), part)
        one = source[:part].astype(jnp.float32)
        two = source[part : 2 * part].astype(jnp.float32)
        sums_ref[c, x] = source[2 * part :].astype(jnp.float32)

        @pl.when(x == 0)
        def _():
            q_ref[rows], k_ref[rows] = one, two

        @pl.when(x == 1)
        def _():
            v_ref[rows], o_ref[rows] = one, two


def finish(kernel, place, pieces, shapes, name):
    vmem = pl.BlockSpec(memory_space=pltpu.VMEM)
    return pl.pallas_call(
        kernel,
        in_specs=[pl.BlockSpec(memory_space=pltpu.SMEM)] + [vmem] * 4,
        out_specs=[vmem] * len(shapes),
        out_shape=[jax.ShapeDtypeStruct(shape, jnp.float32) for shape in shapes],
        compiler_params=pltpu.CompilerParams(vmem_limit_bytes=8 << 20),
        cost_estimate=pl.CostEstimate(flops=1 << 20, bytes_accessed=4 << 20, transcendentals=0),
        name=name,
    )(place, *pieces)


def ctx_swap(array, bit):
    return lax.ppermute(array, "ctx", [(i, i ^ bit) for i in range(4)])


def core_swap(array):
    return ctx_swap(array, 1)


def tie(*arrays):
    return lax.optimization_barrier(arrays)


def across_swap(array):
    return ctx_swap(array, 2)


def in_order(flag, mine, other):
    return jnp.where(flag == 0, mine, other), jnp.where(flag == 0, other, mine)


def at(across, core, tp):
    return (2 * across + core) * 4 + tp


def across_pairs():
    pairs = []
    for tp in range(4):
        for across in (0, 1):
            core = across ^ (tp & 1)
            pairs.append((at(1 - across, core, tp), at(across, core, tp)))
    return pairs


def tp_shifts(array, cuts=(slice(None), slice(None), slice(None))):
    return [
        lax.ppermute(array[cut], "tp", [(i, (i + shift) % 4) for i in range(4)])
        for shift, cut in zip((1, 2, 3), cuts)
        if cut is not None
    ]


def by_tp(array, shifted):
    one, two, three = shifted
    line = jnp.stack([three, two, one, array, three, two, one])
    return lax.dynamic_slice_in_dim(line, 3 - lax.axis_index("tp"), 4, 0)


def shard_swap(array):
    return lax.ppermute(array, "shard", [(0, 1), (1, 0)])


def low_sum(left, right):
    return (left.astype(jnp.float32) + right.astype(jnp.float32)).astype(jnp.bfloat16)


def scatter_tp_start(parts):
    tp = lax.axis_index("tp")
    moved = [lax.dynamic_index_in_dim(parts, tp, 0, keepdims=False)]
    for shift in (1, 2, 3):
        sent = lax.dynamic_index_in_dim(parts, (tp + shift) & 3, 0, keepdims=False)
        moved.append(lax.ppermute(sent, "tp", [(i, (i + shift) % 4) for i in range(4)]))
    return moved


def scatter_tp_end(moved):
    return sum(part.astype(jnp.float32) for part in moved).astype(jnp.bfloat16)


def chain_pairs(turn):
    pairs = []
    for group in (0, 2):
        path = [(0, group), (0, group + 1), (1, group + 1), (1, group)]
        for (across, tp), (next_across, next_tp) in zip(path[:-1], path[1:]):
            pairs.append((at(across, 1, tp), at(next_across, 1 ^ turn, next_tp)))
            pairs.append((at(next_across, 0, next_tp), at(across, turn, tp)))
    return pairs


def block_pairs(core):
    pairs = []
    for tp in range(4):
        for across in (0, 1):
            source = 1 ^ across ^ (tp & 1)
            pairs.append((at(across, source, tp), at(1 - across, core, tp)))
    return pairs


def span_shards(
    layer_input,
    segment_ids,
    query_proj,
    query_bias,
    key_proj,
    value_proj,
    value_bias,
    out_proj,
    out_bias,
    attn_gain,
    attn_shift,
    up_proj,
    up_bias,
    down_proj,
    down_bias,
    ffn_gain,
    ffn_shift,
    out_cotangent,
):
    seqs, block, width = layer_input.shape
    length = segment_ids.shape[1]
    reach = length // 2
    count = seqs * block // 4
    window = count + 2 * reach
    bf16, f32 = jnp.bfloat16, jnp.float32
    ctx, tp = lax.axis_index("ctx"), lax.axis_index("tp")
    shard = lax.axis_index("shard")
    core, across, side = ctx & 1, ctx >> 1, tp & 1
    place = 2 * across + (side ^ across)
    odd = across ^ side

    heads = query_proj.shape[1]
    half = heads // 2
    depth = query_proj.shape[0]
    cut = up_proj.shape[1] // 2
    own_in = lax.dynamic_slice_in_dim(
        jnp.stack([query_proj.T, key_proj.T, value_proj.T]), core * half, half, 1
    ).reshape(3 * half, depth)
    own_biases = jnp.stack(
        [
            jnp.concatenate([query_bias, value_bias]),
            lax.dynamic_slice_in_dim(up_bias, core * cut, cut, 0),
        ]
    )
    own_in = jnp.concatenate([own_in, own_biases, jnp.zeros((14, depth), bf16)], axis=0)
    out_half = out_proj.shape[0] // 2
    own_rest = jnp.concatenate(
        [
            lax.dynamic_slice_in_dim(up_proj, core * cut, cut, 1),
            lax.dynamic_slice_in_dim(down_proj, core * cut, cut, 0),
            lax.dynamic_slice_in_dim(out_proj, core * out_half, out_half, 0),
        ],
        axis=0,
    )
    first_seq = 3 * (tp >> 1)
    mine = lax.dynamic_slice_in_dim(layer_input, first_seq + across, 2, 0)
    theirs = across_swap(lax.dynamic_slice_in_dim(layer_input, first_seq + 1 - across, 2, 0))
    in_shifted = tp_shifts(own_in)
    far_rest = shard_swap(own_rest)
    *in_shifted, theirs, far_rest = tie(*in_shifted, theirs, far_rest)
    in_near = jnp.stack([own_in] + in_shifted)
    (rest_one,) = tp_shifts(tie(own_rest, in_near)[0], (slice(None), None, None))
    own_pair = jnp.stack([own_rest[: 2 * cut], far_rest[: 2 * cut]])
    near_cot = lax.dynamic_index_in_dim(
        out_cotangent, first_seq + odd + across, 0, keepdims=False
    )
    far_cot = lax.ppermute(
        lax.dynamic_index_in_dim(
            tie(out_cotangent, theirs)[0], first_seq + 2 - 2 * across, 0, keepdims=False
        ),
        ("ctx", "tp"),
        across_pairs(),
    )
    in_far, rest_one, own_pair, far_cot = tie(shard_swap(in_near), rest_one, own_pair, far_cot)
    in_mine = jnp.stack([in_near, in_far])
    (rest_three,) = tp_shifts(tie(own_rest, in_near)[0], (None, None, slice(None)))
    in_other, rest_three = tie(core_swap(in_mine), rest_three)
    own_late = tie(own_rest, rest_three)[0]
    (some_two,) = tp_shifts(own_late, (None, slice(cut, None), None))
    (up_two,) = tp_shifts(own_late, (None, slice(cut), None))
    far_three = shard_swap(rest_three)
    bias_rows = in_mine[0, :, 3 * half]
    in_biases = by_tp(bias_rows[0], [bias_rows[1], bias_rows[2], bias_rows[3]]).astype(f32)
    in_biases = jnp.stack([in_biases[:, :heads].reshape(-1), in_biases[:, heads:].reshape(-1)])
    up_bias_here = in_mine[0, :, 3 * half + 1].reshape(4, 1, cut).astype(f32)

    pair = jnp.stack([mine, theirs])
    pair_other = core_swap(pair)
    start = 2 * count * place + count * core - length * across
    ids = lax.dynamic_slice_in_dim(segment_ids, first_seq + across, 2, 0)
    ids = (ids + jnp.array([[0], [1 << 16]], jnp.int32)).reshape(-1)
    no_doc = jnp.full((reach,), -1, jnp.int32)
    window_docs = lax.dynamic_slice_in_dim(
        jnp.concatenate([no_doc, ids, no_doc]), start, window, 0
    )
    key_docs = window_docs[None]
    query_docs = jnp.broadcast_to(window_docs[reach : reach + count, None], (count, QBLOCK))

    place = jnp.stack([core, shard, tp, across, start])
    far_one = shard_swap(rest_one)
    queries, keys, values, in_window, weights_t = project(
        place, in_mine, in_other, pair, pair_other, in_biases, count, window
    )
    attention = queries, keys, values, key_docs, query_docs, reach
    mixed, logs = attend(*attention, 0)
    mixed, far_one, far_three, some_two = tie(mixed, far_one, far_three, some_two)
    far_some_two = shard_swap(some_two)
    mixed, logs = attend(*attention, 1, (mixed, logs))
    mixed, far_some_two, up_two = tie(mixed, far_some_two, up_two)
    far_up_two = shard_swap(up_two)
    out_mine = jnp.stack(
        [
            jnp.stack([one[-out_half:], two[-out_half:]])
            for one, two in (
                (own_rest, far_rest),
                (rest_one, far_one),
                (some_two, far_some_two),
                (rest_three, far_three),
            )
        ]
    )
    attn_vectors = jnp.stack([out_bias, attn_gain, attn_shift]).astype(f32)
    hidden_low, normed_one, inv_one, full_out = attend_out(
        place, mixed, in_window, reach, out_mine, core_swap(out_mine), attn_vectors
    )
    hidden_other = core_swap(hidden_low)
    hidden_both = jnp.concatenate([hidden_low, hidden_other], axis=0)
    ffn_weights = jnp.stack(
        [
            own_pair,
            jnp.stack([rest_one[: 2 * cut], far_one[: 2 * cut]]),
            jnp.stack([rest_three[: 2 * cut], far_three[: 2 * cut]]),
            own_pair,
        ]
    )
    ffn_bias = jnp.stack([up_bias_here[k] for k in (0, 1, 3, 2)])
    acts, slope, ffn_sum = ffn(place, hidden_both, ffn_weights, ffn_bias)
    ffn_sum, far_up_two = tie(ffn_sum, far_up_two)
    rest = ffn_weights.at[3].set(
        jnp.stack(
            [
                jnp.concatenate([up_two, some_two[:cut]], axis=0),
                jnp.concatenate([far_up_two, far_some_two[:cut]], axis=0),
            ]
        )
    )
    acts, slope, ffn_own, ffn_other = ffn(
        place, hidden_both, rest, ffn_bias, (ffn_sum, acts, slope)
    )

    half_block = block // 2

    def deliver_start(rows):
        far_rows = jnp.where(odd == 0, rows[-block:], rows[:block])
        return (
            core_swap(jnp.where(odd == 0, rows[block:], rows[:half_block])),
            lax.ppermute(far_rows[:half_block], ("ctx", "tp"), block_pairs(0)),
            lax.ppermute(far_rows[half_block:], ("ctx", "tp"), block_pairs(1)),
        )

    def deliver_pack(rows, middle, low, high):
        where_kept = [
            rows[:block],
            jnp.concatenate([middle, rows[:half_block]], axis=0),
            jnp.concatenate([rows[block:], middle], axis=0),
            rows[half_block:],
        ]
        kept = jnp.where(
            odd == 0,
            jnp.where(core == 0, where_kept[0], where_kept[1]),
            jnp.where(core == 0, where_kept[2], where_kept[3]),
        )
        return jnp.concatenate([kept, low + high], axis=0)

    cot_pair = tie(jnp.stack([near_cot, far_cot]), queries)[0]
    cot_swapped = core_swap(cot_pair)
    low_cot, high_cot = in_order(core, near_cot, cot_swapped[0])
    far_cot = jnp.where(core == odd, far_cot, cot_swapped[1])
    chip_cot = jnp.where(
        odd == 0,
        jnp.concatenate([low_cot, high_cot, far_cot], axis=0),
        jnp.concatenate([far_cot, low_cot, high_cot], axis=0),
    )
    cot_rows = lax.dynamic_slice_in_dim(chip_cot, core * count, count, 0)


    ffn_vectors = jnp.stack([down_bias, ffn_gain, ffn_shift]).astype(f32)
    output_rows, grad_ffn, ffn_sums = ffn_norm(
        hidden_low, ffn_own, core_swap(ffn_other), cot_rows, ffn_vectors
    )
    grad_other = core_swap(grad_ffn)
    grad_ffn_both = jnp.concatenate([grad_ffn, grad_other], axis=0)
    out_pieces = [output_rows] + tp_shifts(output_rows)
    back_own, back_other, up_keep, up_give, down_keep, down_give, up_sums = ffn_back(
        place, grad_ffn_both, hidden_both, acts, slope, rest
    )
    back_own, out_pieces[1] = tie(back_own, out_pieces[1])
    grad_one, grad_attn, grad_mixed, attn_sums = attend_norm(
        grad_ffn, back_own, core_swap(back_other), normed_one, inv_one, attn_vectors, full_out
    )
    up_got = across_swap(up_give)
    down_got = shard_swap(down_give)
    grad_scaled, grad_keys, grad_values = attend_back(*attention, grad_mixed, logs)
    grad_keys, up_got, down_got, out_pieces[2] = tie(grad_keys, up_got, down_got, out_pieces[2])
    up_parts = [low_sum(up_keep[i], up_got[i]) for i in (0, 1)]
    down_parts = [low_sum(down_keep[i], down_got[i]) for i in (0, 1)]
    up_got, down_got = shard_swap(up_parts[1]), across_swap(down_parts[1])
    own_sum, first, second, give = span_grads(
        place, grad_scaled, grad_keys, grad_values, weights_t, grad_one
    )
    got = core_swap(give)
    shared = reach - count
    to_own = lax.dynamic_slice_in_dim(got, (1 - core) * shared, count, 0)
    to_next = lax.dynamic_slice_in_dim(got, core * count, shared, 0)
    no_rows = jnp.zeros((count - shared, width), bf16)
    first = low_sum(
        first,
        jnp.where(
            core == 0,
            jnp.concatenate([no_rows, to_next], axis=0),
            jnp.concatenate([to_next, no_rows], axis=0),
        ),
    )
    first_now, up_got, down_got, out_pieces[3] = tie(first, up_got, down_got, out_pieces[3])
    ffn_parts = jnp.concatenate(
        [low_sum(up_parts[0], up_got), low_sum(down_parts[0], down_got)], axis=1
    )
    ffn_near = scatter_tp_start(ffn_parts)
    first_got = lax.ppermute(first, ("ctx", "tp"), chain_pairs(1))
    second_got = lax.ppermute(second, ("ctx", "tp"), chain_pairs(0))
    grad_keys, first_now = tie(grad_keys, first)
    attn_parts = attn_grads(
        place,
        grad_scaled,
        grad_keys,
        grad_values,
        mixed,
        grad_attn,
        in_window,
        attn_sums,
        ffn_sums,
        up_sums,
    )
    first_got, second_got, attn_keep, attn_give, ffn_near[1], ffn_near[3] = tie(
        first_got, second_got, *attn_parts, ffn_near[1], ffn_near[3]
    )
    attn_core = core_swap(attn_give)
    own_sum += to_own.astype(f32) + first_got.astype(f32)
    own_sum += jnp.where(
        core == 0,
        jnp.concatenate([no_rows, second_got], axis=0),
        jnp.concatenate([second_got, no_rows], axis=0),
    ).astype(f32)
    own_low = own_sum.astype(bf16)
    in_moves = deliver_start(own_low)
    *in_moves, attn_core, ffn_near[2] = tie(*in_moves, attn_core, ffn_near[2])
    in_packed = deliver_pack(own_low, *in_moves)
    in_pieces = [in_packed] + tp_shifts(in_packed)
    attn_parts = [low_sum(attn_keep[i], attn_core[i]) for i in (0, 1)]
    attn_got = shard_swap(attn_parts[1])
    parity = (tp + 1 + across + core) & 1
    out_sent = [
        jnp.where(
            core == 0,
            jnp.where(parity == 0, even[:block], odd_one[:block]),
            jnp.where(parity == 0, even[-block:], odd_one[-block:]),
        )
        for even, odd_one in (out_pieces[:2], out_pieces[2:])
    ]
    out_foreign = lax.ppermute(jnp.stack(out_sent), "ctx", [(i, 3 - i) for i in range(4)])
    out_middle = core_swap(
        jnp.stack(
            [
                jnp.where(((across + tp + k) & 1) == 0, piece[block:], piece[:half_block])
                for k, piece in enumerate(out_pieces)
            ]
        )
    )
    attn_got, in_pieces[1], in_pieces[3] = tie(attn_got, in_pieces[1], in_pieces[3])
    attn_mid = [low_sum(attn_parts[0][i], attn_got[i]) for i in (0, 1)]
    attn_got = across_swap(attn_mid[1])
    ffn_low = scatter_tp_end(ffn_near)
    ffn_got = across_swap(ffn_low)
    attn_got, out_foreign, out_middle = tie(attn_got, out_foreign, out_middle)
    attn_near = scatter_tp_start(low_sum(attn_mid[0], attn_got))
    layer_output = assemble(
        assemble_late_kernel, place, out_pieces, (out_middle, out_foreign), seqs, bf16
    )
    layer_output, in_pieces[2], attn_near[3], ffn_got = tie(
        layer_output, in_pieces[2], attn_near[3], ffn_got
    )
    in_halves = core_swap(jnp.stack([piece[block:] for piece in in_pieces]))
    input_grad = assemble(assemble_kernel, place, in_pieces, (in_halves,), seqs, f32)
    up_grad, down_grad = finish(
        finish_ffn_kernel,
        place,
        (ffn_low, ffn_got, core_swap(ffn_low), core_swap(ffn_got)),
        ((cut, 2 * cut), (2 * cut, cut)),
        "finish_ffn",
    )
    attn_low = scatter_tp_end(attn_near)
    attn_got, input_grad = tie(across_swap(attn_low), input_grad)
    *weight_grads, sums = finish(
        finish_attn_kernel,
        place,
        (attn_low, attn_got, core_swap(attn_low), core_swap(attn_got)),
        ((heads, depth),) * 4 + ((2, 2, 8, depth),),
        "finish_attn",
    )
    up_bias_grad = sums[:, 1, 5].reshape(-1)
    sums = sums[0].reshape(16, depth)
    row_sums = sums[1:13].reshape(6, width)
    return (
        layer_output,
        input_grad,
        weight_grads[0].T,
        sums[0, :heads],
        weight_grads[1].T,
        weight_grads[2].T,
        sums[0, heads:],
        weight_grads[3],
        row_sums[0],
        row_sums[1],
        row_sums[2],
        up_grad,
        up_bias_grad,
        down_grad,
        row_sums[3],
        row_sums[4],
        row_sums[5],
    )


def pick_plan(mesh):
    shape = dict(mesh.shape)

    def plan(layer_input, segment_ids, *others):
        seqs, block, _ = layer_input.shape
        fits = (
            (shape["shard"], shape["ctx"], shape["tp"]) == (2, 4, 4)
            and seqs == 6
            and segment_ids.shape[1] == 4 * block
            and block == 2 * QBLOCK
        )
        chosen = span_shards if fits else general_shards
        return chosen(layer_input, segment_ids, *others)

    return plan


def solution(mesh):
    return jax.shard_map(
        pick_plan(mesh),
        mesh=mesh,
        in_specs=(
            P("shard", "ctx", None),
            P("shard", None),
            P("shard", "tp"),
            P("tp"),
            P("shard", "tp"),
            P("shard", "tp"),
            P("tp"),
            P("tp", "shard"),
            P(),
            P(),
            P(),
            P("shard", "tp"),
            P("tp"),
            P("tp", "shard"),
            P(),
            P(),
            P(),
            P("shard", "ctx", None),
        ),
        out_specs=(
            P("shard", "ctx", None),
            P("shard", "ctx", None),
            P("shard", "tp"),
            P("tp"),
            P("shard", "tp"),
            P("shard", "tp"),
            P("tp"),
            P("tp", "shard"),
            P(),
            P(),
            P(),
            P("shard", "tp"),
            P("tp"),
            P("tp", "shard"),
            P(),
            P(),
            P(),
        ),
        check_vma=False,
    )
```

```python
from functools import partial
import math

import jax
import jax.numpy as jnp
from jax import lax
from jax.experimental import pallas as pl
from jax.experimental.pallas import tpu as pltpu
from jax.sharding import PartitionSpec as P

HEAD_DIM = 64


eps_norm = 1e-12
far_below = -1e30


def contract_rows(left, right):
    return lax.dot_general(
        left, right, (((0,), (0,)), ((), ())), preferred_element_type=jnp.float32
    )


def contract_last(left, right):
    return lax.dot_general(
        left, right, (((1,), (1,)), ((), ())), preferred_element_type=jnp.float32
    )


def norm_forward(resid, norm_gain, norm_shift):
    center = resid - jnp.mean(resid, axis=-1, keepdims=True)
    inv_std = lax.rsqrt(jnp.mean(center * center, axis=-1, keepdims=True) + eps_norm)
    normed = center * inv_std
    return (normed * norm_gain + norm_shift, normed, inv_std)


def norm_backward(grad_out, normed, inv_std, norm_gain):
    grad_normed = grad_out * norm_gain
    grad_in = inv_std * (
        grad_normed
        - jnp.mean(grad_normed, axis=-1, keepdims=True)
        - normed * jnp.mean(grad_normed * normed, axis=-1, keepdims=True)
    )
    return (grad_in, jnp.sum(grad_out * normed, axis=0), jnp.sum(grad_out, axis=0))


def split_heads(matrix):
    return matrix.reshape(matrix.shape[0], matrix.shape[1] // HEAD_DIM, HEAD_DIM)


def scores_of(queries, keys_all, query_docs, key_docs):
    scores = jnp.einsum(
        "qhd,khd->hqk",
        split_heads(queries),
        split_heads(keys_all),
        preferred_element_type=jnp.float32,
    )
    same_doc = (query_docs[:, None] == key_docs[None, :])[None]
    return jnp.where(same_doc, scores, jnp.float32(far_below))


def attend_forward(item):
    queries, keys_all, values_all, query_docs, key_docs = item
    scores = scores_of(queries, keys_all, query_docs, key_docs)
    top_score = jnp.max(scores, axis=-1, keepdims=True)
    expo = jnp.exp(scores - top_score)
    total = jnp.sum(expo, axis=-1, keepdims=True)
    probs = (expo / total).astype(jnp.bfloat16)
    mixed = jnp.einsum(
        "hqk,khd->qhd", probs, split_heads(values_all), preferred_element_type=jnp.float32
    )
    return (
        mixed.reshape(queries.shape).astype(jnp.bfloat16),
        (top_score + jnp.log(total))[:, :, 0],
    )


def score_grads(queries, keys_all, values_all, query_docs, key_docs, grad_mixed, log_total):
    scores = scores_of(queries, keys_all, query_docs, key_docs)
    probs = jnp.exp(scores - log_total[:, :, None])
    grad_probs = jnp.einsum(
        "qhd,khd->hqk",
        split_heads(grad_mixed),
        split_heads(values_all),
        preferred_element_type=jnp.float32,
    )
    inner = jnp.sum(grad_probs * probs, axis=-1)
    grad_scores = (probs * (grad_probs - inner[:, :, None])).astype(jnp.bfloat16)
    return (probs, grad_scores, inner)


def attend_backward(item):
    queries, keys_all, values_all, query_docs, key_docs, grad_mixed, log_total = item
    probs, grad_scores, inner = score_grads(
        queries, keys_all, values_all, query_docs, key_docs, grad_mixed, log_total
    )
    grad_heads = split_heads(grad_mixed)
    grad_queries = jnp.einsum(
        "hqk,khd->qhd", grad_scores, split_heads(keys_all), preferred_element_type=jnp.float32
    )
    grad_keys = jnp.einsum(
        "hqk,qhd->khd", grad_scores, split_heads(queries), preferred_element_type=jnp.float32
    )
    grad_values = jnp.einsum(
        "hqk,qhd->khd", probs.astype(jnp.bfloat16), grad_heads, preferred_element_type=jnp.float32
    )
    return (
        grad_queries.reshape(queries.shape).astype(jnp.bfloat16),
        grad_keys.reshape(keys_all.shape),
        grad_values.reshape(values_all.shape),
    )


def general_shards(
    layer_input,
    segment_ids,
    query_proj,
    query_bias,
    key_proj,
    value_proj,
    value_bias,
    out_proj,
    out_bias,
    attn_gain,
    attn_shift,
    up_proj,
    up_bias,
    down_proj,
    down_bias,
    ffn_gain,
    ffn_shift,
    out_cotangent,
):
    seq_here, ctx_rows, width = layer_input.shape
    scale = 1.0 / math.sqrt(HEAD_DIM)
    full_query, full_key, full_value, full_out, full_up, full_down = (
        lax.all_gather(query_proj, "shard", axis=0, tiled=True),
        lax.all_gather(key_proj, "shard", axis=0, tiled=True),
        lax.all_gather(value_proj, "shard", axis=0, tiled=True),
        lax.all_gather(out_proj, "shard", axis=1, tiled=True),
        lax.all_gather(up_proj, "shard", axis=0, tiled=True),
        lax.all_gather(down_proj, "shard", axis=1, tiled=True),
    )
    local_width = full_query.shape[1]
    joined_proj = jnp.concatenate([full_query, full_key, full_value], axis=1)
    rows_in = layer_input.reshape(seq_here * ctx_rows, width)
    projected = jnp.dot(rows_in, joined_proj, preferred_element_type=jnp.float32)
    shaped = (seq_here, ctx_rows, local_width)
    queries = (
        ((projected[:, :local_width] + query_bias) * scale).astype(jnp.bfloat16).reshape(shaped)
    )
    keys_mine = projected[:, local_width : 2 * local_width].astype(jnp.bfloat16).reshape(shaped)
    values_mine = (
        (projected[:, 2 * local_width :] + value_bias).astype(jnp.bfloat16).reshape(shaped)
    )
    keys_all, values_all = (
        lax.all_gather(keys_mine, "ctx", axis=1, tiled=True),
        lax.all_gather(values_mine, "ctx", axis=1, tiled=True),
    )
    query_docs = lax.dynamic_slice_in_dim(
        segment_ids, lax.axis_index("ctx") * ctx_rows, ctx_rows, 1
    )
    mixed, log_total = lax.map(
        attend_forward, (queries, keys_all, values_all, query_docs, segment_ids)
    )
    mixed_rows = mixed.reshape(-1, local_width)
    attended = (
        lax.psum(
            jnp.dot(mixed_rows, full_out, preferred_element_type=jnp.float32).astype(jnp.bfloat16),
            "tp",
        ).astype(jnp.float32)
        + out_bias
    )
    hidden, normed_one, inv_one = norm_forward(
        rows_in.astype(jnp.float32) + attended, attn_gain, attn_shift
    )
    hidden_low = hidden.astype(jnp.bfloat16)
    pre_act = jnp.dot(hidden_low, full_up, preferred_element_type=jnp.float32) + up_bias
    acts_low = jax.nn.gelu(pre_act, approximate=False).astype(jnp.bfloat16)
    ffn_out = (
        lax.psum(
            jnp.dot(acts_low, full_down, preferred_element_type=jnp.float32).astype(jnp.bfloat16),
            "tp",
        ).astype(jnp.float32)
        + down_bias
    )
    output_rows, normed_two, inv_two = norm_forward(hidden + ffn_out, ffn_gain, ffn_shift)
    layer_output = output_rows.astype(jnp.bfloat16).reshape(layer_input.shape)
    grad_out = out_cotangent.reshape(-1, width).astype(jnp.float32)
    grad_two, ffn_gain_grad, ffn_shift_grad = norm_backward(grad_out, normed_two, inv_two, ffn_gain)
    grad_ffn = grad_two.astype(jnp.bfloat16)
    down_bias_grad = jnp.sum(grad_ffn, axis=0, dtype=jnp.float32)
    down_part = contract_rows(acts_low, grad_ffn)
    grad_acts = contract_last(grad_ffn, full_down)
    _, gelu_back = jax.vjp(partial(jax.nn.gelu, approximate=False), pre_act)
    grad_pre = gelu_back(grad_acts)[0].astype(jnp.bfloat16)
    up_bias_grad = jnp.sum(grad_pre, axis=0, dtype=jnp.float32)
    up_part = contract_rows(hidden_low, grad_pre)
    grad_hidden = grad_two + lax.psum(
        contract_last(grad_pre, full_up).astype(jnp.bfloat16), "tp"
    ).astype(jnp.float32)
    grad_one, attn_gain_grad, attn_shift_grad = norm_backward(
        grad_hidden, normed_one, inv_one, attn_gain
    )
    grad_attn = grad_one.astype(jnp.bfloat16)
    out_bias_grad = jnp.sum(grad_attn, axis=0, dtype=jnp.float32)
    out_part = contract_rows(mixed_rows, grad_attn)
    grad_mixed = contract_last(grad_attn, full_out).astype(jnp.bfloat16).reshape(shaped)
    keys_back, values_back = (
        lax.all_gather(keys_mine, "ctx", axis=1, tiled=True),
        lax.all_gather(values_mine, "ctx", axis=1, tiled=True),
    )
    grad_queries, grad_keys_all, grad_values_all = lax.map(
        attend_backward,
        (queries, keys_back, values_back, query_docs, segment_ids, grad_mixed, log_total),
    )
    grad_keys, grad_values = (
        lax.psum_scatter(
            grad_keys_all.astype(jnp.bfloat16), "ctx", scatter_dimension=1, tiled=True
        ).astype(jnp.float32),
        lax.psum_scatter(
            grad_values_all.astype(jnp.bfloat16), "ctx", scatter_dimension=1, tiled=True
        ).astype(jnp.float32),
    )
    grad_keys = grad_keys.astype(jnp.bfloat16).reshape(-1, local_width)
    grad_values = grad_values.astype(jnp.bfloat16).reshape(-1, local_width)
    grad_scaled = grad_queries.reshape(-1, local_width) * jnp.bfloat16(scale)
    grad_joined = jnp.concatenate([grad_scaled, grad_keys, grad_values], axis=1)
    joined_part = contract_rows(rows_in, grad_joined)
    query_part = joined_part[:, :local_width]
    key_part = joined_part[:, local_width : 2 * local_width]
    value_part = joined_part[:, 2 * local_width :]
    query_bias_grad = jnp.sum(grad_scaled, axis=0, dtype=jnp.float32)
    value_bias_grad = jnp.sum(grad_values, axis=0, dtype=jnp.float32)
    back_terms = contract_last(grad_joined, joined_proj)
    input_grad = (
        grad_one + lax.psum(back_terms.astype(jnp.bfloat16), "tp").astype(jnp.float32)
    ).reshape(layer_input.shape)
    sliced = (
        lax.psum_scatter(
            query_part.astype(jnp.bfloat16), "shard", scatter_dimension=0, tiled=True
        ).astype(jnp.float32),
        lax.psum_scatter(
            key_part.astype(jnp.bfloat16), "shard", scatter_dimension=0, tiled=True
        ).astype(jnp.float32),
        lax.psum_scatter(
            value_part.astype(jnp.bfloat16), "shard", scatter_dimension=0, tiled=True
        ).astype(jnp.float32),
        lax.psum_scatter(
            out_part.astype(jnp.bfloat16), "shard", scatter_dimension=1, tiled=True
        ).astype(jnp.float32),
        lax.psum_scatter(
            up_part.astype(jnp.bfloat16), "shard", scatter_dimension=0, tiled=True
        ).astype(jnp.float32),
        lax.psum_scatter(
            down_part.astype(jnp.bfloat16), "shard", scatter_dimension=1, tiled=True
        ).astype(jnp.float32),
    )
    reduced = (
        lax.psum(sliced[0].astype(jnp.bfloat16), "ctx").astype(jnp.float32),
        lax.psum(sliced[1].astype(jnp.bfloat16), "ctx").astype(jnp.float32),
        lax.psum(sliced[2].astype(jnp.bfloat16), "ctx").astype(jnp.float32),
        lax.psum(sliced[3].astype(jnp.bfloat16), "ctx").astype(jnp.float32),
        lax.psum(sliced[4].astype(jnp.bfloat16), "ctx").astype(jnp.float32),
        lax.psum(sliced[5].astype(jnp.bfloat16), "ctx").astype(jnp.float32),
    )
    small = lax.psum(
        (
            query_bias_grad,
            value_bias_grad,
            out_bias_grad,
            attn_gain_grad,
            attn_shift_grad,
            up_bias_grad,
            down_bias_grad,
            ffn_gain_grad,
            ffn_shift_grad,
        ),
        ("shard", "ctx"),
    )
    return (
        layer_output,
        input_grad,
        reduced[0],
        small[0],
        reduced[1],
        reduced[2],
        small[1],
        reduced[3],
        small[2],
        small[3],
        small[4],
        reduced[4],
        small[5],
        reduced[5],
        small[6],
        small[7],
        small[8],
    )


PAIR = 2 * HEAD_DIM
QBLOCK = 128


def dot32(left, right):
    return jnp.dot(left, right, preferred_element_type=jnp.float32)


def stack_heads(rows):
    lane = lax.broadcasted_iota(jnp.int32, rows.shape, 1)
    nought = jnp.zeros_like(rows)
    return jnp.concatenate(
        [jnp.where(lane < HEAD_DIM, rows, nought), jnp.where(lane >= HEAD_DIM, rows, nought)], axis=0
    )


def unstack_heads(tall):
    count = tall.shape[0] // 2
    lane = lax.broadcasted_iota(jnp.int32, (count, tall.shape[1]), 1)
    return jnp.where(lane < HEAD_DIM, tall[:count], tall[count:])


def masked_scores(queries, keys, same):
    scores = contract_last(queries, keys)
    return jnp.where(jnp.concatenate([same, same], axis=0), scores, jnp.float32(far_below))


def attend_kernel(span, q_ref, k_ref, v_ref, kd_ref, qd_ref, *refs):
    o_ref, l_ref = refs[-2:]
    here = pl.ds(pl.multiple_of(pl.program_id(1) * QBLOCK, QBLOCK), span)
    same = qd_ref[:, :1] == kd_ref[:, here]
    logs = []
    for pair in range(q_ref.shape[1] // PAIR):
        cols = slice(pair * PAIR, (pair + 1) * PAIR)
        scores = masked_scores(stack_heads(q_ref[:, cols]), k_ref[here, cols], same)
        top = jnp.max(scores, axis=1, keepdims=True)
        expo = jnp.exp(scores - top)
        total = jnp.sum(expo, axis=1, keepdims=True)
        mixed = dot32(expo.astype(jnp.bfloat16), v_ref[here, cols]) * (1.0 / total)
        o_ref[:, cols] = unstack_heads(mixed).astype(jnp.bfloat16)
        log = top + jnp.log(total)
        logs += [log[:QBLOCK], log[QBLOCK:]]
    l_ref[0] = jnp.concatenate(logs, axis=1)


def attend_back_kernel(span, q_ref, k_ref, v_ref, kd_ref, qd_ref, do_ref, l_ref, *refs):
    dq_ref, dk_ref, dv_ref, dk_acc, dv_acc = refs[-5:]
    step = pl.program_id(1)

    @pl.when(step == 0)
    def _():
        dk_acc[...] = jnp.zeros_like(dk_acc)
        dv_acc[...] = jnp.zeros_like(dv_acc)

    here = pl.ds(pl.multiple_of(step * QBLOCK, QBLOCK), span)
    same = qd_ref[:, :1] == kd_ref[:, here]
    logs = l_ref[0]
    for pair in range(q_ref.shape[1] // PAIR):
        cols = slice(pair * PAIR, (pair + 1) * PAIR)
        keys = k_ref[here, cols]
        queries, grads = stack_heads(q_ref[:, cols]), stack_heads(do_ref[:, cols])
        log = jnp.concatenate([logs[:, 2 * pair + i : 2 * pair + i + 1] for i in (0, 1)], axis=0)
        probs = jnp.exp(masked_scores(queries, keys, same) - log)
        grad_probs = contract_last(grads, v_ref[here, cols])
        inner = jnp.sum(grad_probs * probs, axis=1, keepdims=True)
        grad_scores = (probs * (grad_probs - inner)).astype(jnp.bfloat16)
        grad_queries = unstack_heads(dot32(grad_scores, keys))
        dq_ref[:, cols] = (grad_queries * (1.0 / math.sqrt(HEAD_DIM))).astype(jnp.bfloat16)
        dk_acc[here, cols] += contract_rows(grad_scores, queries)
        dv_acc[here, cols] += contract_rows(probs.astype(jnp.bfloat16), grads)

    @pl.when(step == pl.num_programs(1) - 1)
    def _():
        dk_ref[...] = dk_acc[...].astype(jnp.bfloat16)
        dv_ref[...] = dv_acc[...].astype(jnp.bfloat16)


def attention_specs(window, cols, at):
    rows = pl.BlockSpec((QBLOCK, cols), lambda h, i: (i, at + h))
    keys = pl.BlockSpec((window, cols), lambda h, i: (0, at + h))
    key_docs = pl.BlockSpec((1, window), lambda h, i: (0, 0))
    query_docs = pl.BlockSpec((QBLOCK, QBLOCK), lambda h, i: (i, 0))
    logs = pl.BlockSpec((1, QBLOCK, cols // HEAD_DIM), lambda h, i: (at + h, i, 0))
    return rows, keys, key_docs, query_docs, logs


def attend(queries, keys, values, key_docs, query_docs, reach, half, prior=()):
    count, width = queries.shape
    window, cols = keys.shape[0], width // 2
    span = QBLOCK + 2 * reach
    rows, key_spec, kd_spec, qd_spec, logs = attention_specs(window, cols, half)
    return pl.pallas_call(
        partial(attend_kernel, span),
        grid=(1, count // QBLOCK),
        in_specs=[rows, key_spec, key_spec, kd_spec, qd_spec]
        + [pl.BlockSpec(memory_space=pl.ANY)] * len(prior),
        out_specs=[rows, logs],
        out_shape=[
            jax.ShapeDtypeStruct((count, width), jnp.bfloat16),
            jax.ShapeDtypeStruct((2, count, cols // HEAD_DIM), jnp.float32),
        ],
        input_output_aliases={5 + i: i for i in range(len(prior))},
        compiler_params=pltpu.CompilerParams(vmem_limit_bytes=16 << 20),
        cost_estimate=pl.CostEstimate(
            flops=16 * count * span * cols, bytes_accessed=4 << 20, transcendentals=0
        ),
        name="attend",
    )(queries, keys, values, key_docs, query_docs, *prior)


def attend_back(queries, keys, values, key_docs, query_docs, reach, grads, logs_in):
    count, width = queries.shape
    window, cols = keys.shape[0], width // 2
    span = QBLOCK + 2 * reach
    rows, key_spec, kd_spec, qd_spec, logs = attention_specs(window, cols, 0)
    return pl.pallas_call(
        partial(attend_back_kernel, span),
        grid=(2, count // QBLOCK),
        in_specs=[rows, key_spec, key_spec, kd_spec, qd_spec, rows, logs],
        out_specs=[rows, key_spec, key_spec],
        out_shape=[
            jax.ShapeDtypeStruct((count, width), jnp.bfloat16),
            jax.ShapeDtypeStruct((window, width), jnp.bfloat16),
            jax.ShapeDtypeStruct((window, width), jnp.bfloat16),
        ],
        scratch_shapes=[pltpu.VMEM((window, cols), jnp.float32)] * 2,
        compiler_params=pltpu.CompilerParams(vmem_limit_bytes=24 << 20),
        cost_estimate=pl.CostEstimate(
            flops=40 * count * span * width, bytes_accessed=12 << 20, transcendentals=0
        ),
        name="attend_back",
    )(queries, keys, values, key_docs, query_docs, grads, logs_in)


def half_cols(position, half):
    return pl.ds(pl.multiple_of(position * half, half), half)


def add_or_set(first, ref, index, terms):
    @pl.when(first)
    def _():
        ref[index] = terms

    @pl.when(jnp.logical_not(first))
    def _():
        ref[index] += terms


def ffn_kernel(first_block, place_ref, h_ref, other_h_ref, w_ref, bias_ref, *refs):
    half = w_ref.shape[3]
    count = h_ref.shape[0]
    near, far = half_cols(place_ref[1], half), half_cols(1 - place_ref[1], half)
    hb_near = refs[-1]
    for part, source in enumerate((h_ref, other_h_ref)):
        rows = slice(part * count, (part + 1) * count)
        hb_near[rows, :half] = source[:, near]
        hb_near[rows, half:] = source[:, far]

    def chunk(block, rows, acts_ref, slope_ref):
        up = w_ref[block, :, :half].reshape(2 * half, half)
        pre_act = dot32(hb_near[rows], up) + bias_ref[block]
        cdf = 0.5 * (1.0 + lax.erf(pre_act * math.sqrt(0.5)))
        bell = jnp.exp(-0.5 * pre_act * pre_act) * (1.0 / math.sqrt(2 * math.pi))
        acts = (pre_act * cdf).astype(jnp.bfloat16)
        cols = pl.ds(pl.multiple_of(block * half, half), half)
        acts_ref[rows, cols] = acts
        slope_ref[rows, cols] = (cdf + pre_act * bell).astype(jnp.bfloat16)
        return dot32(acts, w_ref[block, 0, half:]), dot32(acts, w_ref[block, 1, half:])

    blocks = w_ref.shape[0]
    if first_block:
        base_ref, _, _, acts_ref, slope_ref, own_ref, other_ref = refs[:-1]
        for part, to in enumerate((own_ref, other_ref)):
            rows = slice(part * count, (part + 1) * count)
            terms = chunk(blocks - 1, rows, acts_ref, slope_ref)
            for y, cols in enumerate((near, far)):
                base = base_ref[rows, y * half : (y + 1) * half]
                to[:, cols] = (base + terms[y]).astype(to.dtype)
    else:
        acts_ref, slope_ref, total = refs[:-1]
        total[...] = jnp.zeros_like(total)

        @pl.loop(0, 2 * (blocks - 1))
        def _(i):
            rows = pl.ds(pl.multiple_of((i & 1) * count, count), count)
            one, two = chunk(i >> 1, rows, acts_ref, slope_ref)
            total[rows, :half] += one
            total[rows, half:] += two


def ffn_back_kernel(
    place_ref,
    dz_ref,
    other_dz_ref,
    h_ref,
    other_h_ref,
    acts_ref,
    slope_ref,
    w_ref,
    own_ref,
    other_ref,
    up_keep,
    up_give,
    down_keep,
    down_give,
    sums_ref,
    total,
    grad_pre,
    dz_near,
    rows_t,
    up_both,
    down_both,
    sums,
):
    step = pl.program_id(0)
    half = w_ref.shape[3]
    quarter = half // 2
    count = own_ref.shape[0]
    near, far = half_cols(place_ref[1], half), half_cols(1 - place_ref[1], half)
    first, second = slice(0, half), slice(half, 2 * half)

    @pl.when(step == 0)
    def _():
        total[...] = jnp.zeros_like(total)
        for to, cols in ((first, near), (second, far)):
            dz_near[:count, to] = dz_ref[:, cols]
            dz_near[count:, to] = other_dz_ref[:, cols]
            rows_t[to, :count] = h_ref[:, cols].T
            rows_t[to, count:] = other_h_ref[:, cols].T

    for k, hid in enumerate((first, second)):
        for y, to in enumerate((first, second)):
            up_both[to, hid] = w_ref[k, y, :half]
            down_both[hid, to] = w_ref[k, y, half:]
    sums[...] = jnp.zeros_like(sums)

    @pl.loop(0, 2)
    def _(part):
        rows = pl.ds(pl.multiple_of(part * count, count), count)
        grad_acts = contract_last(dz_near[rows], down_both[...])
        low = (slope_ref[rows].astype(jnp.float32) * grad_acts).astype(jnp.bfloat16)
        grad_pre[rows] = low
        sums[...] += row_sum(low.astype(jnp.float32))
        total[rows] += contract_last(low, up_both[...])

    tps = [(place_ref[2] + 4 - jnp.where(step == 0, k, 3 - k)) & 3 for k in (0, 1)]
    for tp, hid in zip(tps, (first, second)):
        sums_ref[tp] = sums[:, hid]
    acts_t = acts_ref[...].T
    for side, cols in enumerate((first, second)):
        up_grad = dot32(rows_t[cols], grad_pre[...]).astype(jnp.bfloat16)
        down_grad = dot32(acts_t, dz_near[:, cols]).astype(jnp.bfloat16)
        down_to = down_give if side else down_keep
        for across in (0, 1):

            @pl.when(place_ref[3] == across)
            def _():
                for k in (0, 1):
                    tp = tps[k]
                    hid = slice(k * half, (k + 1) * half)
                    for x in (0, 1):
                        part = slice((x ^ across) * quarter, (x ^ across) * quarter + quarter)
                        down_rows = slice(k * half + part.start, k * half + part.stop)
                        (up_give if x else up_keep)[side, tp] = up_grad[part, hid]
                        down_to[x, tp] = down_grad[down_rows]

    @pl.when(step == pl.num_programs(0) - 1)
    def _():
        own_ref[:, near] = total[:count, first].astype(jnp.bfloat16)
        own_ref[:, far] = total[:count, second].astype(jnp.bfloat16)
        other_ref[:, near] = total[count:, first].astype(jnp.bfloat16)
        other_ref[:, far] = total[count:, second].astype(jnp.bfloat16)


def once(shape):
    return pl.BlockSpec(
        shape, lambda *_: (0,) * len(shape), pipeline_mode=pl.Buffered(buffer_count=1)
    )


def whole(shape):
    return pl.BlockSpec(shape, lambda *_: (0,) * len(shape))


def ffn(place, rows, other_rows, weights, bias, prior=()):
    count, width = rows.shape
    both = 2 * count
    tps, shards, _, half = weights.shape
    vmem = pl.BlockSpec(memory_space=pltpu.VMEM)
    low = jax.ShapeDtypeStruct((count, width), jnp.bfloat16)
    hidden = jax.ShapeDtypeStruct((both, tps * half), jnp.bfloat16)
    last = [low, low] if prior else [jax.ShapeDtypeStruct((both, width), jnp.float32)]
    steps = 1 if prior else tps - 1
    return pl.pallas_call(
        partial(ffn_kernel, bool(prior)),
        in_specs=[pl.BlockSpec(memory_space=pltpu.SMEM)] + [vmem] * (4 + len(prior)),
        out_specs=[vmem] * (2 + len(last)),
        out_shape=[hidden, hidden] + last,
        scratch_shapes=[pltpu.VMEM((both, width), jnp.bfloat16)],
        input_output_aliases={6: 0, 7: 1} if prior else {},
        compiler_params=pltpu.CompilerParams(vmem_limit_bytes=16 << 20),
        cost_estimate=pl.CostEstimate(
            flops=12 * both * width * steps * half, bytes_accessed=3 * steps << 20, transcendentals=0
        ),
        name="ffn",
    )(place, rows, other_rows, weights, bias, *prior)


def ffn_back(place, grads, other_grads, rows, other_rows, acts, slope, weights):
    count, width = rows.shape
    both = 2 * count
    tps, shards, _, half = weights.shape
    block = pl.BlockSpec((both, 2 * half), lambda i, _: (0, i))
    parts = (2, tps, half // 2, half)
    low = jax.ShapeDtypeStruct((count, width), jnp.bfloat16)
    return pl.pallas_call(
        ffn_back_kernel,
        grid_spec=pltpu.PrefetchScalarGridSpec(
            num_scalar_prefetch=1,
            grid=(tps // 2,),
            in_specs=[
                *[once((count, width))] * 4,
                block,
                block,
                pl.BlockSpec((2, shards, 2 * half, half), lambda i, _: (i, 0, 0, 0)),
            ],
            out_specs=[
                whole((count, width)),
                whole((count, width)),
                *[whole(parts)] * 4,
                whole((tps, 1, half)),
            ],
            scratch_shapes=[
                pltpu.VMEM((both, width), jnp.float32),
                pltpu.VMEM((both, 2 * half), jnp.bfloat16),
                pltpu.VMEM((both, width), jnp.bfloat16),
                pltpu.VMEM((width, both), jnp.bfloat16),
                pltpu.VMEM((width, 2 * half), jnp.bfloat16),
                pltpu.VMEM((2 * half, width), jnp.bfloat16),
                pltpu.VMEM((1, 2 * half), jnp.float32),
            ],
        ),
        out_shape=[
            low,
            low,
            *[jax.ShapeDtypeStruct(parts, jnp.bfloat16)] * 4,
            jax.ShapeDtypeStruct((tps, 1, half), jnp.float32),
        ],
        compiler_params=pltpu.CompilerParams(vmem_limit_bytes=30 << 20),
        cost_estimate=pl.CostEstimate(
            flops=12 * both * width * tps * half, bytes_accessed=20 << 20, transcendentals=0
        ),
        name="ffn_back",
    )(place, grads, other_grads, rows, other_rows, acts, slope, weights)


def project_kernel(
    place_ref, w_mine, w_other, x_mine, x_other, bias_ref, q_ref, k_ref, v_ref, x_ref, wt
):
    core, shard, tp, across, start = (place_ref[i] for i in range(5))
    depth = w_mine.shape[3]
    width = x_ref.shape[1]
    part = width // 8
    length = 4 * x_mine.shape[2]
    reach = length // 2
    for c, source in enumerate((w_mine, w_other)):
        for y in (0, 1):
            cols = half_cols(shard + y - 2 * shard * y, depth)
            for k in range(4):
                row = ((tp + 4 - k) & 3) * 2 + core + c - 2 * core * c
                rows = pl.ds(pl.multiple_of(row * part, part), part)
                for m in range(3):
                    wt[m, rows, cols] = source[y, k, m * part : (m + 1) * part]
    for i in range(x_ref.shape[0] // QBLOCK):
        row = start - reach + i * QBLOCK
        inside = jnp.logical_and(row >= 0, row < 2 * length)
        at = jnp.where(inside, row, 0) // QBLOCK
        seq, block, piece = at // 8, (at // 2) & 3, at & 1
        here = jnp.where((block >> 1) == across, 0, 1)
        rows = pl.ds(pl.multiple_of(piece * QBLOCK, QBLOCK), QBLOCK)
        mine, other = x_mine[here, seq, rows], x_other[here, seq, rows]
        found = jnp.where((block & 1) == core, mine, other)
        x_ref[i * QBLOCK : (i + 1) * QBLOCK] = jnp.where(inside, found, jnp.zeros_like(found))
    count = q_ref.shape[0]
    scaled = contract_last(x_ref[reach : reach + count], wt[0]) + bias_ref[0:1]
    q_ref[...] = (scaled * (1.0 / math.sqrt(HEAD_DIM))).astype(jnp.bfloat16)
    chunk = x_ref.shape[0] // 4

    @pl.loop(0, 4)
    def _(step):
        rows = pl.ds(pl.multiple_of(step * chunk, 32), chunk)
        k_ref[rows] = contract_last(x_ref[rows], wt[1]).astype(jnp.bfloat16)
        v_ref[rows] = (contract_last(x_ref[rows], wt[2]) + bias_ref[1:2]).astype(jnp.bfloat16)


def project(place, w_mine, w_other, x_mine, x_other, biases, count, window):
    width = x_mine.shape[-1]
    return pl.pallas_call(
        project_kernel,
        in_specs=[pl.BlockSpec(memory_space=pltpu.SMEM)]
        + [pl.BlockSpec(memory_space=pltpu.VMEM)] * 5,
        out_specs=[pl.BlockSpec(memory_space=pltpu.VMEM)] * 5,
        out_shape=[
            jax.ShapeDtypeStruct((count, width), jnp.bfloat16),
            jax.ShapeDtypeStruct((window, width), jnp.bfloat16),
            jax.ShapeDtypeStruct((window, width), jnp.bfloat16),
            jax.ShapeDtypeStruct((window, width), jnp.bfloat16),
            jax.ShapeDtypeStruct((3, width, width), jnp.bfloat16),
        ],
        compiler_params=pltpu.CompilerParams(vmem_limit_bytes=24 << 20),
        cost_estimate=pl.CostEstimate(
            flops=4 * window * width * width, bytes_accessed=16 << 20, transcendentals=0
        ),
        name="project",
    )(place, w_mine, w_other, x_mine, x_other, biases)


def norm_pieces(resid):
    center = resid - jnp.mean(resid, axis=-1, keepdims=True)
    inv_std = lax.rsqrt(jnp.mean(center * center, axis=-1, keepdims=True) + eps_norm)
    return center * inv_std, inv_std


def norm_pull(grad_out, normed, inv_std, gain):
    grad_normed = grad_out * gain
    return inv_std * (
        grad_normed
        - jnp.mean(grad_normed, axis=-1, keepdims=True)
        - normed * jnp.mean(grad_normed * normed, axis=-1, keepdims=True)
    )


def row_sum(rows):
    return jnp.sum(rows, axis=0, keepdims=True)


def attend_out_kernel(
    place_ref, o_ref, x_ref, w_mine, w_other, vec_ref, hb_ref, n_ref, i_ref, wo_ref
):
    core, shard, tp = (place_ref[i] for i in range(3))
    part, depth = w_mine.shape[2:]

    @pl.when(pl.program_id(0) == 0)
    def _():
        for c, source in enumerate((w_mine, w_other)):
            for y in (0, 1):
                cols = half_cols(shard + y - 2 * shard * y, depth)
                for k in range(4):
                    row = ((tp + 4 - k) & 3) * 2 + core + c - 2 * core * c
                    rows = pl.ds(pl.multiple_of(row * part, part), part)
                    wo_ref[rows, cols] = source[k, y]

    resid = x_ref[...].astype(jnp.float32) + dot32(o_ref[...], wo_ref[...]) + vec_ref[0:1]
    normed, inv_std = norm_pieces(resid)
    hb_ref[...] = (normed * vec_ref[1:2] + vec_ref[2:3]).astype(jnp.bfloat16)
    n_ref[...] = normed.astype(jnp.bfloat16)
    i_ref[...] = jnp.broadcast_to(inv_std, i_ref.shape)


def row_blocks(width):
    return pl.BlockSpec((QBLOCK, width), lambda i, *_: (i, 0))


def on_rows(kernel, count, in_specs, out_specs, out_shape, name, scalars=0):
    return pl.pallas_call(
        kernel,
        grid_spec=pltpu.PrefetchScalarGridSpec(
            num_scalar_prefetch=scalars,
            grid=(count // QBLOCK,),
            in_specs=in_specs,
            out_specs=out_specs,
        ),
        out_shape=out_shape,
        compiler_params=pltpu.CompilerParams(vmem_limit_bytes=12 << 20),
        cost_estimate=pl.CostEstimate(flops=1 << 28, bytes_accessed=6 << 20, transcendentals=0),
        name=name,
    )


def attend_out(place, mixed, window_rows, reach, w_mine, w_other, vectors):
    count, width = mixed.shape
    rows = row_blocks(width)
    low = jax.ShapeDtypeStruct((count, width), jnp.bfloat16)
    return on_rows(
        attend_out_kernel,
        count,
        [
            rows,
            pl.BlockSpec((QBLOCK, width), lambda i, *_: (i + reach // QBLOCK, 0)),
            whole(w_mine.shape),
            whole(w_other.shape),
            whole(vectors.shape),
        ],
        [rows, rows, row_blocks(QBLOCK), whole((width, width))],
        [
            low,
            low,
            jax.ShapeDtypeStruct((count, QBLOCK), jnp.float32),
            jax.ShapeDtypeStruct((width, width), jnp.bfloat16),
        ],
        "attend_out",
        1,
    )(place, mixed, window_rows, w_mine, w_other, vectors)


def norm_sums(sums_ref, rows):
    sums = jnp.concatenate([row_sum(row) for row in rows], axis=0)
    add_or_set(pl.program_id(0) == 0, sums_ref, slice(None), sums)


def cot_source(i, place_ref):
    core, tp, across = place_ref[0], place_ref[2], place_ref[3]
    odd = (across + tp) & 1
    block = 3 * core + i - 2 * odd
    block = jnp.where(block < 0, block + 6, block)
    far = block >> 1 == 2
    held = jnp.where(far, core == odd, core == (block >> 1))
    return jnp.where(far, 1, 0), block & 1, jnp.where(held, 1, 0)


def ffn_norm_kernel(
    place_ref, h_ref, own_ref, got_ref, g_ref, g_other_ref, vec_ref, y_ref, dz_ref, sums_ref
):
    resid = h_ref[...].astype(jnp.float32) + own_ref[...].astype(jnp.float32)
    resid += got_ref[...].astype(jnp.float32) + vec_ref[0:1]
    normed, inv_std = norm_pieces(resid)
    y_ref[...] = (normed * vec_ref[1:2] + vec_ref[2:3]).astype(jnp.bfloat16)
    held = cot_source(pl.program_id(0), place_ref)[2]
    grad_out = jnp.where(held == 1, g_ref[0], g_other_ref[0]).astype(jnp.float32)
    low = norm_pull(grad_out, normed, inv_std, vec_ref[1:2]).astype(jnp.bfloat16)
    dz_ref[...] = low
    norm_sums(sums_ref, (low.astype(jnp.float32), grad_out * normed, grad_out))


def ffn_norm(place, hidden, own, got, cots, other_cots, vectors):
    count, width = hidden.shape
    rows = row_blocks(width)
    cot = pl.BlockSpec((1, QBLOCK, width), lambda i, at: (*cot_source(i, at)[:2], 0))
    low = jax.ShapeDtypeStruct((count, width), jnp.bfloat16)
    return on_rows(
        ffn_norm_kernel,
        count,
        [rows, rows, rows, cot, cot, whole(vectors.shape)],
        [rows, rows, whole((3, width))],
        [low, low, jax.ShapeDtypeStruct((3, width), jnp.float32)],
        "ffn_norm",
        1,
    )(place, hidden, own, got, cots, other_cots, vectors)


def attend_norm_kernel(
    dz_ref, own_ref, got_ref, n_ref, i_ref, vec_ref, wo_ref, out_ref, da_ref, do_ref, sums_ref
):
    grad_out = dz_ref[...].astype(jnp.float32) + own_ref[...].astype(jnp.float32)
    grad_out += got_ref[...].astype(jnp.float32)
    normed = n_ref[...].astype(jnp.float32)
    grad = norm_pull(grad_out, normed, i_ref[:, :1], vec_ref[1:2])
    low = grad.astype(jnp.bfloat16)
    out_ref[...] = grad
    da_ref[...] = low
    do_ref[...] = contract_last(low, wo_ref[...]).astype(jnp.bfloat16)
    norm_sums(sums_ref, (low.astype(jnp.float32), grad_out * normed, grad_out))


def attend_norm(grads, own, got, normed, inv_std, vectors, weights):
    count, width = grads.shape
    rows = row_blocks(width)
    low = jax.ShapeDtypeStruct((count, width), jnp.bfloat16)
    return on_rows(
        attend_norm_kernel,
        count,
        [rows, rows, rows, rows, row_blocks(QBLOCK), whole(vectors.shape), whole(weights.shape)],
        [rows, rows, rows, whole((3, width))],
        [
            jax.ShapeDtypeStruct((count, width), jnp.float32),
            low,
            low,
            jax.ShapeDtypeStruct((3, width), jnp.float32),
        ],
        "attend_norm",
    )(grads, own, got, normed, inv_std, vectors, weights)


def attn_grads_kernel(
    place_ref, dq_ref, dk_ref, dv_ref, o_ref, da_ref, w_ref, attn_ref, ffn_ref, up_ref, *parts
):
    core, shard, across = place_ref[0], place_ref[1], place_ref[3]
    grad_ref = parts[2]
    depth = w_ref.shape[1] // 2
    part = depth // 4
    count = dq_ref.shape[0]
    reach = (w_ref.shape[0] - count) // 2
    sides = (
        (dq_ref, w_ref.at[reach : reach + count]),
        (dk_ref, w_ref),
        (dv_ref, w_ref),
        (o_ref, da_ref),
    )
    for m, (left, right) in enumerate(sides):
        grad_ref[...] = contract_rows(left[...], right[...]).astype(jnp.bfloat16)
        group = across if m < 2 else 1 - across
        rows = slice((m % 2) * part, (m % 2 + 1) * part)
        for z in (0, 1):
            for c in (0, 1):
                at = pl.ds(pl.multiple_of((2 * z + c + core - 2 * c * core) * part, part), part)
                parts[c][shard, group, z, rows] = grad_ref[at, :depth]
                parts[c][1 - shard, group, z, rows] = grad_ref[at, depth:]
    query_sum = row_sum(dq_ref[...].astype(jnp.float32))
    value_sum = row_sum(dv_ref[...].astype(jnp.float32))
    shared = []
    for source in (attn_ref, ffn_ref):
        for r in range(3):
            shared += [source[r : r + 1, :depth], source[r : r + 1, depth:]]
    half = depth // 2
    for z in (0, 1):
        own = slice(z * half, (z + 1) * half)
        heads = jnp.concatenate([query_sum[:, own], value_sum[:, own]], axis=1)
        none = jnp.zeros_like(heads)
        rows = [heads] + shared
        for c in (0, 1):
            last = [none if c else up_ref[z], none, none]
            for x, group in ((across, rows[:8]), (1 - across, rows[8:] + last)):
                block = jnp.concatenate(group, axis=0).astype(jnp.bfloat16)
                for y in (0, 1):
                    parts[c][y, x, z, 2 * part :] = block


def attn_grads(
    place, grad_queries, grad_keys, grad_values, mixed, grad_attn, near, attn_sums, ffn_sums, up_sums
):
    count, width = mixed.shape
    window = near.shape[0]
    depth = width // 2
    high = depth // 2 + 8
    cols = pl.BlockSpec((count, depth), lambda i, _: (0, i))
    near_cols = pl.BlockSpec((window, depth), lambda i, _: (0, i))
    return pl.pallas_call(
        attn_grads_kernel,
        grid_spec=pltpu.PrefetchScalarGridSpec(
            num_scalar_prefetch=1,
            grid=(2,),
            in_specs=[
                cols,
                near_cols,
                near_cols,
                cols,
                whole((count, width)),
                whole((window, width)),
                whole((3, width)),
                whole((3, width)),
                pl.BlockSpec((2, 1, depth), lambda i, _: (i, 0, 0)),
            ],
            out_specs=[pl.BlockSpec((2, 2, 2, high, depth), lambda i, _: (0, 0, i, 0, 0))] * 2,
            scratch_shapes=[pltpu.VMEM((depth, width), jnp.bfloat16)],
        ),
        out_shape=[jax.ShapeDtypeStruct((2, 2, 4, high, depth), jnp.bfloat16)] * 2,
        compiler_params=pltpu.CompilerParams(vmem_limit_bytes=24 << 20),
        cost_estimate=pl.CostEstimate(
            flops=4 * (window + count) * width * width, bytes_accessed=16 << 20, transcendentals=0
        ),
        name="attn_grads",
    )(
        place,
        grad_queries,
        grad_keys,
        grad_values,
        mixed,
        grad_attn,
        near,
        attn_sums,
        ffn_sums,
        up_sums,
    )


def span_grads_kernel(
    place_ref,
    dq_ref,
    dk_ref,
    dv_ref,
    w_ref,
    base_ref,
    own_ref,
    first_ref,
    second_ref,
    give_ref,
    near,
):
    core = place_ref[0]
    count, reach = own_ref.shape[0], give_ref.shape[0]
    far = count + reach
    size = near.shape[0] // 4

    @pl.loop(0, 4)
    def _(step):
        rows = pl.ds(pl.multiple_of(step * size, 32), size)
        near[rows] = dot32(dk_ref[rows], w_ref[1]) + dot32(dv_ref[rows], w_ref[2])

    def rows_at(start, size):
        return near[pl.ds(pl.multiple_of(start, QBLOCK), size)].astype(jnp.bfloat16)

    give_ref[...] = rows_at((1 - core) * far, reach)
    first_ref[...] = rows_at(jnp.where(core == 0, reach - count, far), count)
    second_ref[...] = rows_at(jnp.where(core == 0, 0, far + count), reach - count)
    own_ref[...] = base_ref[...] + dot32(dq_ref[...], w_ref[0]) + near[reach:far]


def span_grads(place, grad_queries, grad_keys, grad_values, weights, base):
    count, width = base.shape
    reach = (grad_keys.shape[0] - count) // 2
    vmem = pl.BlockSpec(memory_space=pltpu.VMEM)
    return pl.pallas_call(
        span_grads_kernel,
        in_specs=[pl.BlockSpec(memory_space=pltpu.SMEM)] + [vmem] * 5,
        out_specs=[vmem] * 4,
        out_shape=[
            jax.ShapeDtypeStruct((count, width), jnp.float32),
            jax.ShapeDtypeStruct((count, width), jnp.bfloat16),
            jax.ShapeDtypeStruct((reach - count, width), jnp.bfloat16),
            jax.ShapeDtypeStruct((reach, width), jnp.bfloat16),
        ],
        scratch_shapes=[pltpu.VMEM(grad_keys.shape, jnp.float32)],
        compiler_params=pltpu.CompilerParams(vmem_limit_bytes=16 << 20),
        cost_estimate=pl.CostEstimate(
            flops=4 * (count + 2 * reach) * width * width,
            bytes_accessed=12 << 20,
            transcendentals=0,
        ),
        name="span_grads",
    )(place, grad_queries, grad_keys, grad_values, weights, base)


def assemble_kernel(place_ref, one, two, three, four, halves, out_ref):
    core, tp, across = place_ref[0], place_ref[2], place_ref[3]
    block = out_ref.shape[1]
    part = block // 2
    mine = pl.ds(pl.multiple_of(core * part, part), part)
    other = pl.ds(pl.multiple_of((1 - core) * part, part), part)
    for k, source in enumerate((one, two, three, four)):
        z = (tp + 4 - k) & 3
        group, side = 3 * (z >> 1), z & 1
        out_ref[group + jnp.where(side == 1, 1, 2 * across)] = source[:block].astype(out_ref.dtype)
        foreign = group + 2 - 2 * across

        @pl.when(((side + across + core) & 1) == 1)
        def _():
            out_ref[foreign, mine] = source[block:].astype(out_ref.dtype)
            out_ref[foreign, other] = halves[k].astype(out_ref.dtype)


def assemble_late_kernel(place_ref, one, two, three, four, middle, foreign, out_ref):
    core, tp, across = place_ref[0], place_ref[2], place_ref[3]
    block = out_ref.shape[1]
    part = block // 2
    for k, source in enumerate((one, two, three, four)):
        z = (tp + 4 - k) & 3
        group, side = 3 * (z >> 1), z & 1
        at = group + jnp.where(side == 1, 1, 2 * across)
        odd = (across + side) & 1

        @pl.when(jnp.logical_and(odd == 0, core == 0))
        def _():
            out_ref[at] = source[:block]

        @pl.when(jnp.logical_and(odd == 0, core == 1))
        def _():
            out_ref[at, :part] = middle[k]
            out_ref[at, part:] = source[:part]

        @pl.when(jnp.logical_and(odd == 1, core == 0))
        def _():
            out_ref[at, :part] = source[block:]
            out_ref[at, part:] = middle[k]

        @pl.when(jnp.logical_and(odd == 1, core == 1))
        def _():
            out_ref[at] = source[part:]

        @pl.when(((side + across + core) & 1) == 1)
        def _():
            out_ref[group + 2 - 2 * across] = foreign[k // 2]


def assemble(kernel, place, pieces, others, seqs, dtype):
    rows, width = pieces[0].shape
    vmem = pl.BlockSpec(memory_space=pltpu.VMEM)
    return pl.pallas_call(
        kernel,
        in_specs=[pl.BlockSpec(memory_space=pltpu.SMEM)] + [vmem] * (4 + len(others)),
        out_specs=vmem,
        out_shape=jax.ShapeDtypeStruct((seqs, rows * 2 // 3, width), dtype),
        compiler_params=pltpu.CompilerParams(vmem_limit_bytes=10 << 20),
        cost_estimate=pl.CostEstimate(flops=1 << 20, bytes_accessed=8 << 20, transcendentals=0),
        name="assemble",
    )(place, *pieces, *others)


def finish_ffn_kernel(place_ref, mine, across_got, core_got, both_got, up_ref, down_ref):
    core, across = place_ref[0], place_ref[3]
    depth = mine.shape[1]
    part = depth // 2
    for c, x, source in (
        (core, across, mine),
        (core, 1 - across, across_got),
        (1 - core, across, core_got),
        (1 - core, 1 - across, both_got),
    ):
        rows = pl.ds(pl.multiple_of(x * part, part), part)
        up_ref[rows, half_cols(c, depth)] = source[:part].astype(jnp.float32)
        rows = pl.ds(pl.multiple_of(c * depth + x * part, part), part)
        down_ref[rows] = source[part:].astype(jnp.float32)


def finish_attn_kernel(
    place_ref, mine, across_got, core_got, both_got, q_ref, k_ref, v_ref, o_ref, *refs
):
    *vectors, sums_ref = refs
    core, across = place_ref[0], place_ref[3]
    part = q_ref.shape[0] // 2
    for c, x, source in (
        (core, across, mine),
        (core, 1 - across, across_got),
        (1 - core, across, core_got),
        (1 - core, 1 - across, both_got),
    ):
        rows = pl.ds(pl.multiple_of(c * part, part), part)
        one = source[:part].astype(jnp.float32)
        two = source[part : 2 * part].astype(jnp.float32)
        sums_ref[c, x] = source[2 * part :].astype(jnp.float32)

        @pl.when(x == 0)
        def _():
            q_ref[rows], k_ref[rows] = one, two

        @pl.when(x == 1)
        def _():
            v_ref[rows], o_ref[rows] = one, two

    def flat(*rows):
        return jnp.concatenate(rows, axis=1).reshape(-1)

    sums = sums_ref[core].reshape(16, 4 * part)
    for r, to in enumerate(vectors[:6]):
        to[...] = flat(sums[2 * r + 1 : 2 * r + 2], sums[2 * r + 2 : 2 * r + 3])
    vectors[6][...] = flat(sums_ref[0, 1, 5:6], sums_ref[1, 1, 5:6])
    vectors[7][...] = sums[0:1, : 2 * part].reshape(-1)
    vectors[8][...] = sums[0:1, 2 * part :].reshape(-1)


def finish(kernel, place, pieces, shapes, name, scratch=()):
    vmem = pl.BlockSpec(memory_space=pltpu.VMEM)
    return pl.pallas_call(
        kernel,
        in_specs=[pl.BlockSpec(memory_space=pltpu.SMEM)] + [vmem] * 4,
        out_specs=[vmem] * len(shapes),
        out_shape=[jax.ShapeDtypeStruct(shape, jnp.float32) for shape in shapes],
        scratch_shapes=scratch,
        compiler_params=pltpu.CompilerParams(vmem_limit_bytes=8 << 20),
        cost_estimate=pl.CostEstimate(flops=1 << 20, bytes_accessed=4 << 20, transcendentals=0),
        name=name,
    )(place, *pieces)


def ctx_swap(array, bit):
    return lax.ppermute(array, "ctx", [(i, i ^ bit) for i in range(4)])


def core_swap(array):
    return ctx_swap(array, 1)


def tie(*arrays):
    return lax.optimization_barrier(arrays)


def across_swap(array):
    return ctx_swap(array, 2)


def in_order(flag, mine, other):
    return jnp.where(flag == 0, mine, other), jnp.where(flag == 0, other, mine)


def at(across, core, tp):
    return (2 * across + core) * 4 + tp


def across_pairs():
    pairs = []
    for tp in range(4):
        for across in (0, 1):
            core = across ^ (tp & 1)
            pairs.append((at(1 - across, core, tp), at(across, core, tp)))
    return pairs


def tp_shifts(array, cuts=(slice(None), slice(None), slice(None))):
    return [
        lax.ppermute(array[cut], "tp", [(i, (i + shift) % 4) for i in range(4)])
        for shift, cut in zip((1, 2, 3), cuts)
        if cut is not None
    ]


def by_tp(array, shifted):
    one, two, three = shifted
    line = jnp.stack([three, two, one, array, three, two, one])
    return lax.dynamic_slice_in_dim(line, 3 - lax.axis_index("tp"), 4, 0)


def shard_swap(array):
    return lax.ppermute(array, "shard", [(0, 1), (1, 0)])


def low_sum(left, right):
    return (left.astype(jnp.float32) + right.astype(jnp.float32)).astype(jnp.bfloat16)


def scatter_tp_start(parts):
    tp = lax.axis_index("tp")
    moved = [lax.dynamic_index_in_dim(parts, tp, 0, keepdims=False)]
    for shift in (1, 2, 3):
        sent = lax.dynamic_index_in_dim(parts, (tp + shift) & 3, 0, keepdims=False)
        moved.append(lax.ppermute(sent, "tp", [(i, (i + shift) % 4) for i in range(4)]))
    return moved


def scatter_tp_end(moved):
    return sum(part.astype(jnp.float32) for part in moved).astype(jnp.bfloat16)


def chain_pairs(turn):
    pairs = []
    for group in (0, 2):
        path = [(0, group), (0, group + 1), (1, group + 1), (1, group)]
        for (across, tp), (next_across, next_tp) in zip(path[:-1], path[1:]):
            pairs.append((at(across, 1, tp), at(next_across, 1 ^ turn, next_tp)))
            pairs.append((at(next_across, 0, next_tp), at(across, turn, tp)))
    return pairs


def block_pairs(core):
    pairs = []
    for tp in range(4):
        for across in (0, 1):
            source = 1 ^ across ^ (tp & 1)
            pairs.append((at(across, source, tp), at(1 - across, core, tp)))
    return pairs


def span_shards(
    layer_input,
    segment_ids,
    query_proj,
    query_bias,
    key_proj,
    value_proj,
    value_bias,
    out_proj,
    out_bias,
    attn_gain,
    attn_shift,
    up_proj,
    up_bias,
    down_proj,
    down_bias,
    ffn_gain,
    ffn_shift,
    out_cotangent,
):
    seqs, block, width = layer_input.shape
    length = segment_ids.shape[1]
    reach = length // 2
    count = seqs * block // 4
    window = count + 2 * reach
    bf16, f32 = jnp.bfloat16, jnp.float32
    ctx, tp = lax.axis_index("ctx"), lax.axis_index("tp")
    shard = lax.axis_index("shard")
    core, across, side = ctx & 1, ctx >> 1, tp & 1
    place = 2 * across + (side ^ across)
    odd = across ^ side

    heads = query_proj.shape[1]
    half = heads // 2
    depth = query_proj.shape[0]
    cut = up_proj.shape[1] // 2
    own_in = lax.dynamic_slice_in_dim(
        jnp.stack([query_proj.T, key_proj.T, value_proj.T]), core * half, half, 1
    ).reshape(3 * half, depth)
    own_biases = jnp.stack(
        [
            jnp.concatenate([query_bias, value_bias]),
            lax.dynamic_slice_in_dim(up_bias, core * cut, cut, 0),
        ]
    )
    own_in = jnp.concatenate([own_in, own_biases, jnp.zeros((14, depth), bf16)], axis=0)
    out_half = out_proj.shape[0] // 2
    own_rest = jnp.concatenate(
        [
            lax.dynamic_slice_in_dim(up_proj, core * cut, cut, 1),
            lax.dynamic_slice_in_dim(down_proj, core * cut, cut, 0),
            lax.dynamic_slice_in_dim(out_proj, core * out_half, out_half, 0),
        ],
        axis=0,
    )
    first_seq = 3 * (tp >> 1)
    mine = lax.dynamic_slice_in_dim(layer_input, first_seq + across, 2, 0)
    theirs = across_swap(lax.dynamic_slice_in_dim(layer_input, first_seq + 1 - across, 2, 0))
    in_shifted = tp_shifts(own_in)
    far_rest = shard_swap(own_rest)
    *in_shifted, theirs, far_rest = tie(*in_shifted, theirs, far_rest)
    in_near = jnp.stack([own_in] + in_shifted)
    (rest_one,) = tp_shifts(tie(own_rest, in_near)[0], (slice(None), None, None))
    own_pair = jnp.stack([own_rest[: 2 * cut], far_rest[: 2 * cut]])
    near_cot = lax.dynamic_index_in_dim(
        out_cotangent, first_seq + odd + across, 0, keepdims=False
    )
    far_cot = lax.ppermute(
        lax.dynamic_index_in_dim(
            tie(out_cotangent, theirs)[0], first_seq + 2 - 2 * across, 0, keepdims=False
        ),
        ("ctx", "tp"),
        across_pairs(),
    )
    in_far, rest_one, own_pair, far_cot = tie(shard_swap(in_near), rest_one, own_pair, far_cot)
    in_mine = jnp.stack([in_near, in_far])
    (rest_three,) = tp_shifts(tie(own_rest, in_near)[0], (None, None, slice(None)))
    in_other, rest_three = tie(core_swap(in_mine), rest_three)
    own_late = tie(own_rest, rest_three)[0]
    (some_two,) = tp_shifts(own_late, (None, slice(cut, None), None))
    (up_two,) = tp_shifts(own_late, (None, slice(cut), None))
    far_three = shard_swap(rest_three)
    bias_rows = in_mine[0, :, 3 * half]
    in_biases = by_tp(bias_rows[0], [bias_rows[1], bias_rows[2], bias_rows[3]]).astype(f32)
    in_biases = jnp.stack([in_biases[:, :heads].reshape(-1), in_biases[:, heads:].reshape(-1)])
    up_bias_here = in_mine[0, :, 3 * half + 1].reshape(4, 1, cut).astype(f32)

    pair = jnp.stack([mine, theirs])
    pair_other = core_swap(pair)
    start = 2 * count * place + count * core - length * across
    ids = lax.dynamic_slice_in_dim(segment_ids, first_seq + across, 2, 0)
    ids = (ids + jnp.array([[0], [1 << 16]], jnp.int32)).reshape(-1)
    no_doc = jnp.full((reach,), -1, jnp.int32)
    window_docs = lax.dynamic_slice_in_dim(
        jnp.concatenate([no_doc, ids, no_doc]), start, window, 0
    )
    key_docs = window_docs[None]
    query_docs = jnp.broadcast_to(window_docs[reach : reach + count, None], (count, QBLOCK))

    place = jnp.stack([core, shard, tp, across, start])
    far_one = shard_swap(rest_one)
    queries, keys, values, in_window, weights_t = project(
        place, in_mine, in_other, pair, pair_other, in_biases, count, window
    )
    attention = queries, keys, values, key_docs, query_docs, reach
    mixed, logs = attend(*attention, 0)
    mixed, far_one, far_three, some_two = tie(mixed, far_one, far_three, some_two)
    far_some_two = shard_swap(some_two)
    mixed, logs = attend(*attention, 1, (mixed, logs))
    mixed, far_some_two, up_two = tie(mixed, far_some_two, up_two)
    far_up_two = shard_swap(up_two)
    out_mine = jnp.stack(
        [
            jnp.stack([one[-out_half:], two[-out_half:]])
            for one, two in (
                (own_rest, far_rest),
                (rest_one, far_one),
                (some_two, far_some_two),
                (rest_three, far_three),
            )
        ]
    )
    attn_vectors = jnp.stack([out_bias, attn_gain, attn_shift]).astype(f32)
    hidden_low, normed_one, inv_one, full_out = attend_out(
        place, mixed, in_window, reach, out_mine, core_swap(out_mine), attn_vectors
    )
    hidden_other = core_swap(hidden_low)
    hidden_both = hidden_low, hidden_other
    ffn_weights = jnp.stack(
        [
            own_pair,
            jnp.stack([rest_one[: 2 * cut], far_one[: 2 * cut]]),
            jnp.stack([rest_three[: 2 * cut], far_three[: 2 * cut]]),
            own_pair,
        ]
    )
    ffn_bias = jnp.stack([up_bias_here[k] for k in (0, 1, 3, 2)])
    acts, slope, ffn_sum = ffn(place, *hidden_both, ffn_weights, ffn_bias)
    ffn_sum, far_up_two = tie(ffn_sum, far_up_two)
    rest = ffn_weights.at[3].set(
        jnp.stack(
            [
                jnp.concatenate([up_two, some_two[:cut]], axis=0),
                jnp.concatenate([far_up_two, far_some_two[:cut]], axis=0),
            ]
        )
    )
    acts, slope, ffn_own, ffn_other = ffn(
        place, *hidden_both, rest, ffn_bias, (ffn_sum, acts, slope)
    )

    half_block = block // 2

    def deliver_start(rows):
        far_rows = jnp.where(odd == 0, rows[-block:], rows[:block])
        return (
            core_swap(jnp.where(odd == 0, rows[block:], rows[:half_block])),
            lax.ppermute(far_rows[:half_block], ("ctx", "tp"), block_pairs(0)),
            lax.ppermute(far_rows[half_block:], ("ctx", "tp"), block_pairs(1)),
        )

    def deliver_pack(rows, middle, low, high):
        where_kept = [
            rows[:block],
            jnp.concatenate([middle, rows[:half_block]], axis=0),
            jnp.concatenate([rows[block:], middle], axis=0),
            rows[half_block:],
        ]
        kept = jnp.where(
            odd == 0,
            jnp.where(core == 0, where_kept[0], where_kept[1]),
            jnp.where(core == 0, where_kept[2], where_kept[3]),
        )
        return jnp.concatenate([kept, low + high], axis=0)

    cot_pair = tie(jnp.stack([near_cot, far_cot]), queries)[0]
    cot_swapped = core_swap(cot_pair)

    ffn_vectors = jnp.stack([down_bias, ffn_gain, ffn_shift]).astype(f32)
    output_rows, grad_ffn, ffn_sums = ffn_norm(
        place, hidden_low, ffn_own, core_swap(ffn_other), cot_pair, cot_swapped, ffn_vectors
    )
    grad_other = core_swap(grad_ffn)
    out_pieces = [output_rows] + tp_shifts(output_rows)
    back_own, back_other, up_keep, up_give, down_keep, down_give, up_sums = ffn_back(
        place, grad_ffn, grad_other, *hidden_both, acts, slope, rest
    )
    back_own, out_pieces[1] = tie(back_own, out_pieces[1])
    grad_one, grad_attn, grad_mixed, attn_sums = attend_norm(
        grad_ffn, back_own, core_swap(back_other), normed_one, inv_one, attn_vectors, full_out
    )
    up_got = across_swap(up_give)
    down_got = shard_swap(down_give)
    grad_scaled, grad_keys, grad_values = attend_back(*attention, grad_mixed, logs)
    grad_keys, up_got, down_got, out_pieces[2] = tie(grad_keys, up_got, down_got, out_pieces[2])
    up_parts = [low_sum(up_keep[i], up_got[i]) for i in (0, 1)]
    down_parts = [low_sum(down_keep[i], down_got[i]) for i in (0, 1)]
    up_got, down_got = shard_swap(up_parts[1]), across_swap(down_parts[1])
    own_sum, first, second, give = span_grads(
        place, grad_scaled, grad_keys, grad_values, weights_t, grad_one
    )
    got = core_swap(give)
    shared = reach - count
    to_own = lax.dynamic_slice_in_dim(got, (1 - core) * shared, count, 0)
    to_next = lax.dynamic_slice_in_dim(got, core * count, shared, 0)
    no_rows = jnp.zeros((count - shared, width), bf16)
    first = low_sum(
        first,
        jnp.where(
            core == 0,
            jnp.concatenate([no_rows, to_next], axis=0),
            jnp.concatenate([to_next, no_rows], axis=0),
        ),
    )
    first_now, up_got, down_got, out_pieces[3] = tie(first, up_got, down_got, out_pieces[3])
    ffn_parts = jnp.concatenate(
        [low_sum(up_parts[0], up_got), low_sum(down_parts[0], down_got)], axis=1
    )
    ffn_near = scatter_tp_start(ffn_parts)
    first_got = lax.ppermute(first, ("ctx", "tp"), chain_pairs(1))
    second_got = lax.ppermute(second, ("ctx", "tp"), chain_pairs(0))
    grad_keys, first_now = tie(grad_keys, first)
    attn_parts = attn_grads(
        place,
        grad_scaled,
        grad_keys,
        grad_values,
        mixed,
        grad_attn,
        in_window,
        attn_sums,
        ffn_sums,
        up_sums,
    )
    first_got, second_got, attn_keep, attn_give, ffn_near[1], ffn_near[3] = tie(
        first_got, second_got, *attn_parts, ffn_near[1], ffn_near[3]
    )
    attn_core = core_swap(attn_give)
    own_sum += to_own.astype(f32) + first_got.astype(f32)
    own_sum += jnp.where(
        core == 0,
        jnp.concatenate([no_rows, second_got], axis=0),
        jnp.concatenate([second_got, no_rows], axis=0),
    ).astype(f32)
    own_low = own_sum.astype(bf16)
    in_moves = deliver_start(own_low)
    *in_moves, attn_core, ffn_near[2] = tie(*in_moves, attn_core, ffn_near[2])
    in_packed = deliver_pack(own_low, *in_moves)
    in_pieces = [in_packed] + tp_shifts(in_packed)
    attn_parts = [low_sum(attn_keep[i], attn_core[i]) for i in (0, 1)]
    attn_got = shard_swap(attn_parts[1])
    parity = (tp + 1 + across + core) & 1
    out_sent = [
        jnp.where(
            core == 0,
            jnp.where(parity == 0, even[:block], odd_one[:block]),
            jnp.where(parity == 0, even[-block:], odd_one[-block:]),
        )
        for even, odd_one in (out_pieces[:2], out_pieces[2:])
    ]
    out_foreign = lax.ppermute(jnp.stack(out_sent), "ctx", [(i, 3 - i) for i in range(4)])
    out_middle = core_swap(
        jnp.stack(
            [
                jnp.where(((across + tp + k) & 1) == 0, piece[block:], piece[:half_block])
                for k, piece in enumerate(out_pieces)
            ]
        )
    )
    attn_got, in_pieces[1], in_pieces[3] = tie(attn_got, in_pieces[1], in_pieces[3])
    attn_mid = [low_sum(attn_parts[0][i], attn_got[i]) for i in (0, 1)]
    attn_got = across_swap(attn_mid[1])
    ffn_low = scatter_tp_end(ffn_near)
    ffn_got = across_swap(ffn_low)
    attn_got, out_foreign, out_middle = tie(attn_got, out_foreign, out_middle)
    attn_near = scatter_tp_start(low_sum(attn_mid[0], attn_got))
    layer_output = assemble(
        assemble_late_kernel, place, out_pieces, (out_middle, out_foreign), seqs, bf16
    )
    layer_output, in_pieces[2], attn_near[3], ffn_got = tie(
        layer_output, in_pieces[2], attn_near[3], ffn_got
    )
    in_halves = core_swap(jnp.stack([piece[block:] for piece in in_pieces]))
    input_grad = assemble(assemble_kernel, place, in_pieces, (in_halves,), seqs, f32)
    up_grad, down_grad = finish(
        finish_ffn_kernel,
        place,
        (ffn_low, ffn_got, core_swap(ffn_low), core_swap(ffn_got)),
        ((cut, 2 * cut), (2 * cut, cut)),
        "finish_ffn",
    )
    attn_low = scatter_tp_end(attn_near)
    attn_got, input_grad = tie(across_swap(attn_low), input_grad)
    finished = finish(
        finish_attn_kernel,
        place,
        (attn_low, attn_got, core_swap(attn_low), core_swap(attn_got)),
        ((heads, depth),) * 4 + ((width,),) * 6 + ((2 * cut,), (heads,), (heads,)),
        "finish_attn",
        [pltpu.VMEM((2, 2, 8, depth), f32)],
    )
    weight_grads, row_sums = finished[:4], finished[4:10]
    up_bias_grad, query_bias_grad, value_bias_grad = finished[10:]
    return (
        layer_output,
        input_grad,
        weight_grads[0].T,
        query_bias_grad,
        weight_grads[1].T,
        weight_grads[2].T,
        value_bias_grad,
        weight_grads[3],
        row_sums[0],
        row_sums[1],
        row_sums[2],
        up_grad,
        up_bias_grad,
        down_grad,
        row_sums[3],
        row_sums[4],
        row_sums[5],
    )


def pick_plan(mesh):
    shape = dict(mesh.shape)

    def plan(layer_input, segment_ids, *others):
        seqs, block, _ = layer_input.shape
        fits = (
            (shape["shard"], shape["ctx"], shape["tp"]) == (2, 4, 4)
            and seqs == 6
            and segment_ids.shape[1] == 4 * block
            and block == 2 * QBLOCK
        )
        chosen = span_shards if fits else general_shards
        return chosen(layer_input, segment_ids, *others)

    return plan


def solution(mesh):
    return jax.shard_map(
        pick_plan(mesh),
        mesh=mesh,
        in_specs=(
            P("shard", "ctx", None),
            P("shard", None),
            P("shard", "tp"),
            P("tp"),
            P("shard", "tp"),
            P("shard", "tp"),
            P("tp"),
            P("tp", "shard"),
            P(),
            P(),
            P(),
            P("shard", "tp"),
            P("tp"),
            P("tp", "shard"),
            P(),
            P(),
            P(),
            P("shard", "ctx", None),
        ),
        out_specs=(
            P("shard", "ctx", None),
            P("shard", "ctx", None),
            P("shard", "tp"),
            P("tp"),
            P("shard", "tp"),
            P("shard", "tp"),
            P("tp"),
            P("tp", "shard"),
            P(),
            P(),
            P(),
            P("shard", "tp"),
            P("tp"),
            P("tp", "shard"),
            P(),
            P(),
            P(),
        ),
        check_vma=False,
    )
```

```python
from functools import partial
import math

import jax
import jax.numpy as jnp
from jax import lax
from jax.experimental import pallas as pl
from jax.experimental.pallas import tpu as pltpu
from jax.sharding import PartitionSpec as P

HEAD_DIM = 64


eps_norm = 1e-12
far_below = -1e30


def contract_rows(left, right):
    return lax.dot_general(
        left, right, (((0,), (0,)), ((), ())), preferred_element_type=jnp.float32
    )


def contract_last(left, right):
    return lax.dot_general(
        left, right, (((1,), (1,)), ((), ())), preferred_element_type=jnp.float32
    )


def norm_forward(resid, norm_gain, norm_shift):
    center = resid - jnp.mean(resid, axis=-1, keepdims=True)
    inv_std = lax.rsqrt(jnp.mean(center * center, axis=-1, keepdims=True) + eps_norm)
    normed = center * inv_std
    return (normed * norm_gain + norm_shift, normed, inv_std)


def norm_backward(grad_out, normed, inv_std, norm_gain):
    grad_normed = grad_out * norm_gain
    grad_in = inv_std * (
        grad_normed
        - jnp.mean(grad_normed, axis=-1, keepdims=True)
        - normed * jnp.mean(grad_normed * normed, axis=-1, keepdims=True)
    )
    return (grad_in, jnp.sum(grad_out * normed, axis=0), jnp.sum(grad_out, axis=0))


def split_heads(matrix):
    return matrix.reshape(matrix.shape[0], matrix.shape[1] // HEAD_DIM, HEAD_DIM)


def scores_of(queries, keys_all, query_docs, key_docs):
    scores = jnp.einsum(
        "qhd,khd->hqk",
        split_heads(queries),
        split_heads(keys_all),
        preferred_element_type=jnp.float32,
    )
    same_doc = (query_docs[:, None] == key_docs[None, :])[None]
    return jnp.where(same_doc, scores, jnp.float32(far_below))


def attend_forward(item):
    queries, keys_all, values_all, query_docs, key_docs = item
    scores = scores_of(queries, keys_all, query_docs, key_docs)
    top_score = jnp.max(scores, axis=-1, keepdims=True)
    expo = jnp.exp(scores - top_score)
    total = jnp.sum(expo, axis=-1, keepdims=True)
    probs = (expo / total).astype(jnp.bfloat16)
    mixed = jnp.einsum(
        "hqk,khd->qhd", probs, split_heads(values_all), preferred_element_type=jnp.float32
    )
    return (
        mixed.reshape(queries.shape).astype(jnp.bfloat16),
        (top_score + jnp.log(total))[:, :, 0],
    )


def score_grads(queries, keys_all, values_all, query_docs, key_docs, grad_mixed, log_total):
    scores = scores_of(queries, keys_all, query_docs, key_docs)
    probs = jnp.exp(scores - log_total[:, :, None])
    grad_probs = jnp.einsum(
        "qhd,khd->hqk",
        split_heads(grad_mixed),
        split_heads(values_all),
        preferred_element_type=jnp.float32,
    )
    inner = jnp.sum(grad_probs * probs, axis=-1)
    grad_scores = (probs * (grad_probs - inner[:, :, None])).astype(jnp.bfloat16)
    return (probs, grad_scores, inner)


def attend_backward(item):
    queries, keys_all, values_all, query_docs, key_docs, grad_mixed, log_total = item
    probs, grad_scores, inner = score_grads(
        queries, keys_all, values_all, query_docs, key_docs, grad_mixed, log_total
    )
    grad_heads = split_heads(grad_mixed)
    grad_queries = jnp.einsum(
        "hqk,khd->qhd", grad_scores, split_heads(keys_all), preferred_element_type=jnp.float32
    )
    grad_keys = jnp.einsum(
        "hqk,qhd->khd", grad_scores, split_heads(queries), preferred_element_type=jnp.float32
    )
    grad_values = jnp.einsum(
        "hqk,qhd->khd", probs.astype(jnp.bfloat16), grad_heads, preferred_element_type=jnp.float32
    )
    return (
        grad_queries.reshape(queries.shape).astype(jnp.bfloat16),
        grad_keys.reshape(keys_all.shape),
        grad_values.reshape(values_all.shape),
    )


def general_shards(
    layer_input,
    segment_ids,
    query_proj,
    query_bias,
    key_proj,
    value_proj,
    value_bias,
    out_proj,
    out_bias,
    attn_gain,
    attn_shift,
    up_proj,
    up_bias,
    down_proj,
    down_bias,
    ffn_gain,
    ffn_shift,
    out_cotangent,
):
    seq_here, ctx_rows, width = layer_input.shape
    scale = 1.0 / math.sqrt(HEAD_DIM)
    full_query, full_key, full_value, full_out, full_up, full_down = (
        lax.all_gather(query_proj, "shard", axis=0, tiled=True),
        lax.all_gather(key_proj, "shard", axis=0, tiled=True),
        lax.all_gather(value_proj, "shard", axis=0, tiled=True),
        lax.all_gather(out_proj, "shard", axis=1, tiled=True),
        lax.all_gather(up_proj, "shard", axis=0, tiled=True),
        lax.all_gather(down_proj, "shard", axis=1, tiled=True),
    )
    local_width = full_query.shape[1]
    joined_proj = jnp.concatenate([full_query, full_key, full_value], axis=1)
    rows_in = layer_input.reshape(seq_here * ctx_rows, width)
    projected = jnp.dot(rows_in, joined_proj, preferred_element_type=jnp.float32)
    shaped = (seq_here, ctx_rows, local_width)
    queries = (
        ((projected[:, :local_width] + query_bias) * scale).astype(jnp.bfloat16).reshape(shaped)
    )
    keys_mine = projected[:, local_width : 2 * local_width].astype(jnp.bfloat16).reshape(shaped)
    values_mine = (
        (projected[:, 2 * local_width :] + value_bias).astype(jnp.bfloat16).reshape(shaped)
    )
    keys_all, values_all = (
        lax.all_gather(keys_mine, "ctx", axis=1, tiled=True),
        lax.all_gather(values_mine, "ctx", axis=1, tiled=True),
    )
    query_docs = lax.dynamic_slice_in_dim(
        segment_ids, lax.axis_index("ctx") * ctx_rows, ctx_rows, 1
    )
    mixed, log_total = lax.map(
        attend_forward, (queries, keys_all, values_all, query_docs, segment_ids)
    )
    mixed_rows = mixed.reshape(-1, local_width)
    attended = (
        lax.psum(
            jnp.dot(mixed_rows, full_out, preferred_element_type=jnp.float32).astype(jnp.bfloat16),
            "tp",
        ).astype(jnp.float32)
        + out_bias
    )
    hidden, normed_one, inv_one = norm_forward(
        rows_in.astype(jnp.float32) + attended, attn_gain, attn_shift
    )
    hidden_low = hidden.astype(jnp.bfloat16)
    pre_act = jnp.dot(hidden_low, full_up, preferred_element_type=jnp.float32) + up_bias
    acts_low = jax.nn.gelu(pre_act, approximate=False).astype(jnp.bfloat16)
    ffn_out = (
        lax.psum(
            jnp.dot(acts_low, full_down, preferred_element_type=jnp.float32).astype(jnp.bfloat16),
            "tp",
        ).astype(jnp.float32)
        + down_bias
    )
    output_rows, normed_two, inv_two = norm_forward(hidden + ffn_out, ffn_gain, ffn_shift)
    layer_output = output_rows.astype(jnp.bfloat16).reshape(layer_input.shape)
    grad_out = out_cotangent.reshape(-1, width).astype(jnp.float32)
    grad_two, ffn_gain_grad, ffn_shift_grad = norm_backward(grad_out, normed_two, inv_two, ffn_gain)
    grad_ffn = grad_two.astype(jnp.bfloat16)
    down_bias_grad = jnp.sum(grad_ffn, axis=0, dtype=jnp.float32)
    down_part = contract_rows(acts_low, grad_ffn)
    grad_acts = contract_last(grad_ffn, full_down)
    _, gelu_back = jax.vjp(partial(jax.nn.gelu, approximate=False), pre_act)
    grad_pre = gelu_back(grad_acts)[0].astype(jnp.bfloat16)
    up_bias_grad = jnp.sum(grad_pre, axis=0, dtype=jnp.float32)
    up_part = contract_rows(hidden_low, grad_pre)
    grad_hidden = grad_two + lax.psum(
        contract_last(grad_pre, full_up).astype(jnp.bfloat16), "tp"
    ).astype(jnp.float32)
    grad_one, attn_gain_grad, attn_shift_grad = norm_backward(
        grad_hidden, normed_one, inv_one, attn_gain
    )
    grad_attn = grad_one.astype(jnp.bfloat16)
    out_bias_grad = jnp.sum(grad_attn, axis=0, dtype=jnp.float32)
    out_part = contract_rows(mixed_rows, grad_attn)
    grad_mixed = contract_last(grad_attn, full_out).astype(jnp.bfloat16).reshape(shaped)
    keys_back, values_back = (
        lax.all_gather(keys_mine, "ctx", axis=1, tiled=True),
        lax.all_gather(values_mine, "ctx", axis=1, tiled=True),
    )
    grad_queries, grad_keys_all, grad_values_all = lax.map(
        attend_backward,
        (queries, keys_back, values_back, query_docs, segment_ids, grad_mixed, log_total),
    )
    grad_keys, grad_values = (
        lax.psum_scatter(
            grad_keys_all.astype(jnp.bfloat16), "ctx", scatter_dimension=1, tiled=True
        ).astype(jnp.float32),
        lax.psum_scatter(
            grad_values_all.astype(jnp.bfloat16), "ctx", scatter_dimension=1, tiled=True
        ).astype(jnp.float32),
    )
    grad_keys = grad_keys.astype(jnp.bfloat16).reshape(-1, local_width)
    grad_values = grad_values.astype(jnp.bfloat16).reshape(-1, local_width)
    grad_scaled = grad_queries.reshape(-1, local_width) * jnp.bfloat16(scale)
    grad_joined = jnp.concatenate([grad_scaled, grad_keys, grad_values], axis=1)
    joined_part = contract_rows(rows_in, grad_joined)
    query_part = joined_part[:, :local_width]
    key_part = joined_part[:, local_width : 2 * local_width]
    value_part = joined_part[:, 2 * local_width :]
    query_bias_grad = jnp.sum(grad_scaled, axis=0, dtype=jnp.float32)
    value_bias_grad = jnp.sum(grad_values, axis=0, dtype=jnp.float32)
    back_terms = contract_last(grad_joined, joined_proj)
    input_grad = (
        grad_one + lax.psum(back_terms.astype(jnp.bfloat16), "tp").astype(jnp.float32)
    ).reshape(layer_input.shape)
    sliced = (
        lax.psum_scatter(
            query_part.astype(jnp.bfloat16), "shard", scatter_dimension=0, tiled=True
        ).astype(jnp.float32),
        lax.psum_scatter(
            key_part.astype(jnp.bfloat16), "shard", scatter_dimension=0, tiled=True
        ).astype(jnp.float32),
        lax.psum_scatter(
            value_part.astype(jnp.bfloat16), "shard", scatter_dimension=0, tiled=True
        ).astype(jnp.float32),
        lax.psum_scatter(
            out_part.astype(jnp.bfloat16), "shard", scatter_dimension=1, tiled=True
        ).astype(jnp.float32),
        lax.psum_scatter(
            up_part.astype(jnp.bfloat16), "shard", scatter_dimension=0, tiled=True
        ).astype(jnp.float32),
        lax.psum_scatter(
            down_part.astype(jnp.bfloat16), "shard", scatter_dimension=1, tiled=True
        ).astype(jnp.float32),
    )
    reduced = (
        lax.psum(sliced[0].astype(jnp.bfloat16), "ctx").astype(jnp.float32),
        lax.psum(sliced[1].astype(jnp.bfloat16), "ctx").astype(jnp.float32),
        lax.psum(sliced[2].astype(jnp.bfloat16), "ctx").astype(jnp.float32),
        lax.psum(sliced[3].astype(jnp.bfloat16), "ctx").astype(jnp.float32),
        lax.psum(sliced[4].astype(jnp.bfloat16), "ctx").astype(jnp.float32),
        lax.psum(sliced[5].astype(jnp.bfloat16), "ctx").astype(jnp.float32),
    )
    small = lax.psum(
        (
            query_bias_grad,
            value_bias_grad,
            out_bias_grad,
            attn_gain_grad,
            attn_shift_grad,
            up_bias_grad,
            down_bias_grad,
            ffn_gain_grad,
            ffn_shift_grad,
        ),
        ("shard", "ctx"),
    )
    return (
        layer_output,
        input_grad,
        reduced[0],
        small[0],
        reduced[1],
        reduced[2],
        small[1],
        reduced[3],
        small[2],
        small[3],
        small[4],
        reduced[4],
        small[5],
        reduced[5],
        small[6],
        small[7],
        small[8],
    )


PAIR = 2 * HEAD_DIM
QBLOCK = 128


def dot32(left, right):
    return jnp.dot(left, right, preferred_element_type=jnp.float32)


def stack_heads(rows):
    lane = lax.broadcasted_iota(jnp.int32, rows.shape, 1)
    nought = jnp.zeros_like(rows)
    return jnp.concatenate(
        [jnp.where(lane < HEAD_DIM, rows, nought), jnp.where(lane >= HEAD_DIM, rows, nought)], axis=0
    )


def unstack_heads(tall):
    count = tall.shape[0] // 2
    lane = lax.broadcasted_iota(jnp.int32, (count, tall.shape[1]), 1)
    return jnp.where(lane < HEAD_DIM, tall[:count], tall[count:])


def masked_scores(queries, keys, same):
    scores = contract_last(queries, keys)
    return jnp.where(jnp.concatenate([same, same], axis=0), scores, jnp.float32(far_below))


def attend_kernel(span, q_ref, k_ref, v_ref, kd_ref, qd_ref, *refs):
    o_ref, l_ref = refs[-2:]
    here = pl.ds(pl.multiple_of(pl.program_id(1) * QBLOCK, QBLOCK), span)
    same = qd_ref[:, :1] == kd_ref[:, here]
    logs = []
    for pair in range(q_ref.shape[1] // PAIR):
        cols = slice(pair * PAIR, (pair + 1) * PAIR)
        scores = masked_scores(stack_heads(q_ref[:, cols]), k_ref[here, cols], same)
        top = jnp.max(scores, axis=1, keepdims=True)
        expo = jnp.exp(scores - top)
        total = jnp.sum(expo, axis=1, keepdims=True)
        mixed = dot32(expo.astype(jnp.bfloat16), v_ref[here, cols]) * (1.0 / total)
        o_ref[:, cols] = unstack_heads(mixed).astype(jnp.bfloat16)
        log = top + jnp.log(total)
        logs += [log[:QBLOCK], log[QBLOCK:]]
    l_ref[0] = jnp.concatenate(logs, axis=1)


def attend_back_kernel(
    span, short, plan_ref, q_ref, k_ref, v_ref, kd_ref, qd_ref, do_ref, l_ref, *refs
):
    dq_ref, dk_ref, dv_ref, dk_acc, dv_acc = refs
    step = pl.program_id(1)

    @pl.when(step == 0)
    def _():
        dk_acc[...] = jnp.zeros_like(dk_acc)
        dv_acc[...] = jnp.zeros_like(dv_acc)

    logs = l_ref[0]

    def one_pair(here, same, cols, log):
        keys = k_ref[here, cols]
        queries, grads = stack_heads(q_ref[:, cols]), stack_heads(do_ref[:, cols])
        probs = jnp.exp(masked_scores(queries, keys, same) - log)
        grad_probs = contract_last(grads, v_ref[here, cols])
        inner = jnp.sum(grad_probs * probs, axis=1, keepdims=True)
        grad_scores = (probs * (grad_probs - inner)).astype(jnp.bfloat16)
        grad_queries = unstack_heads(dot32(grad_scores, keys))
        dq_ref[:, cols] = (grad_queries * (1.0 / math.sqrt(HEAD_DIM))).astype(jnp.bfloat16)
        dk_acc[here, cols] += contract_rows(grad_scores, queries)
        dv_acc[here, cols] += contract_rows(probs.astype(jnp.bfloat16), grads)

    pairs = q_ref.shape[1] // PAIR
    fits = plan_ref[1, step] == 1

    @pl.when(fits)
    def _():
        here = pl.ds(pl.multiple_of(plan_ref[0, step], QBLOCK), short)
        same = qd_ref[:, :1] == kd_ref[:, here]
        for pair in range(pairs):
            log = [logs[:, 2 * pair + i : 2 * pair + i + 1] for i in (0, 1)]
            one_pair(
                here, same, slice(pair * PAIR, (pair + 1) * PAIR), jnp.concatenate(log, axis=0)
            )

    @pl.when(jnp.logical_not(fits))
    def _():
        here = pl.ds(pl.multiple_of(step * QBLOCK, QBLOCK), span)
        same = qd_ref[:, :1] == kd_ref[:, here]
        lane = lax.broadcasted_iota(jnp.int32, logs.shape, 1)

        @pl.loop(0, pairs)
        def _(pair):
            log = [
                jnp.sum(jnp.where(lane == 2 * pair + i, logs, 0.0), axis=1, keepdims=True)
                for i in (0, 1)
            ]
            cols = pl.ds(pl.multiple_of(pair * PAIR, PAIR), PAIR)
            one_pair(here, same, cols, jnp.concatenate(log, axis=0))

    @pl.when(step == pl.num_programs(1) - 1)
    def _():
        dk_ref[...] = dk_acc[...].astype(jnp.bfloat16)
        dv_ref[...] = dv_acc[...].astype(jnp.bfloat16)


def attention_specs(window, cols, at):
    rows = pl.BlockSpec((QBLOCK, cols), lambda h, i, *_: (i, at + h))
    keys = pl.BlockSpec((window, cols), lambda h, i, *_: (0, at + h))
    key_docs = pl.BlockSpec((1, window), lambda h, i, *_: (0, 0))
    query_docs = pl.BlockSpec((QBLOCK, QBLOCK), lambda h, i, *_: (i, 0))
    logs = pl.BlockSpec((1, QBLOCK, cols // HEAD_DIM), lambda h, i, *_: (at + h, i, 0))
    return rows, keys, key_docs, query_docs, logs


def attend(queries, keys, values, key_docs, query_docs, reach, half, prior=()):
    count, width = queries.shape
    window, cols = keys.shape[0], width // 2
    span = QBLOCK + 2 * reach
    rows, key_spec, kd_spec, qd_spec, logs = attention_specs(window, cols, half)
    return pl.pallas_call(
        partial(attend_kernel, span),
        grid=(1, count // QBLOCK),
        in_specs=[rows, key_spec, key_spec, kd_spec, qd_spec]
        + [pl.BlockSpec(memory_space=pl.ANY)] * len(prior),
        out_specs=[rows, logs],
        out_shape=[
            jax.ShapeDtypeStruct((count, width), jnp.bfloat16),
            jax.ShapeDtypeStruct((2, count, cols // HEAD_DIM), jnp.float32),
        ],
        input_output_aliases={5 + i: i for i in range(len(prior))},
        compiler_params=pltpu.CompilerParams(vmem_limit_bytes=16 << 20),
        cost_estimate=pl.CostEstimate(
            flops=16 * count * span * cols, bytes_accessed=4 << 20, transcendentals=0
        ),
        name="attend",
    )(queries, keys, values, key_docs, query_docs, *prior)


def attend_back(plan, queries, keys, values, key_docs, query_docs, reach, grads, logs_in):
    count, width = queries.shape
    window, cols = keys.shape[0], width // 2
    span = QBLOCK + 2 * reach
    rows, key_spec, kd_spec, qd_spec, logs = attention_specs(window, cols, 0)
    return pl.pallas_call(
        partial(attend_back_kernel, span, short_span(reach)),
        grid_spec=pltpu.PrefetchScalarGridSpec(
            num_scalar_prefetch=1,
            grid=(2, count // QBLOCK),
            in_specs=[rows, key_spec, key_spec, kd_spec, qd_spec, rows, logs],
            out_specs=[rows, key_spec, key_spec],
            scratch_shapes=[pltpu.VMEM((window, cols), jnp.float32)] * 2,
        ),
        out_shape=[
            jax.ShapeDtypeStruct((count, width), jnp.bfloat16),
            jax.ShapeDtypeStruct((window, width), jnp.bfloat16),
            jax.ShapeDtypeStruct((window, width), jnp.bfloat16),
        ],
        compiler_params=pltpu.CompilerParams(vmem_limit_bytes=24 << 20),
        cost_estimate=pl.CostEstimate(
            flops=40 * count * span * width, bytes_accessed=12 << 20, transcendentals=0
        ),
        name="attend_back",
    )(plan, queries, keys, values, key_docs, query_docs, grads, logs_in)


def short_span(reach):
    return (QBLOCK + 2 * reach) * 2 // 3 // QBLOCK * QBLOCK


def key_plan(docs, reach, count):
    window, short = docs.shape[0], short_span(reach)
    rows = docs[reach : reach + count].reshape(-1, QBLOCK)
    at = jnp.arange(window, dtype=jnp.int32)
    low = jnp.min(jnp.where(docs == rows[:, :1], at, window), axis=1)
    high = jnp.max(jnp.where(docs == rows[:, -1:], at + 1, 0), axis=1)
    start = jnp.minimum(low // QBLOCK * QBLOCK, window - short)
    return jnp.stack([start, (high - start <= short).astype(jnp.int32)])


def half_cols(position, half):
    return pl.ds(pl.multiple_of(position * half, half), half)


def add_or_set(first, ref, index, terms):
    @pl.when(first)
    def _():
        ref[index] = terms

    @pl.when(jnp.logical_not(first))
    def _():
        ref[index] += terms


def ffn_kernel(first_block, place_ref, h_ref, other_h_ref, w_ref, bias_ref, *refs):
    half = w_ref.shape[3]
    count = h_ref.shape[0]
    near, far = half_cols(place_ref[1], half), half_cols(1 - place_ref[1], half)
    hb_near = refs[-1]
    for part, source in enumerate((h_ref, other_h_ref)):
        rows = slice(part * count, (part + 1) * count)
        hb_near[rows, :half] = source[:, near]
        hb_near[rows, half:] = source[:, far]

    def chunk(block, rows, acts_ref, slope_ref):
        up = w_ref[block, :, :half].reshape(2 * half, half)
        pre_act = dot32(hb_near[rows], up) + bias_ref[block]
        cdf = 0.5 * (1.0 + lax.erf(pre_act * math.sqrt(0.5)))
        bell = jnp.exp(-0.5 * pre_act * pre_act) * (1.0 / math.sqrt(2 * math.pi))
        acts = (pre_act * cdf).astype(jnp.bfloat16)
        cols = pl.ds(pl.multiple_of(block * half, half), half)
        acts_ref[rows, cols] = acts
        slope_ref[rows, cols] = (cdf + pre_act * bell).astype(jnp.bfloat16)
        return dot32(acts, w_ref[block, 0, half:]), dot32(acts, w_ref[block, 1, half:])

    blocks = w_ref.shape[0]
    if first_block:
        base_ref, _, _, acts_ref, slope_ref, own_ref, other_ref = refs[:-1]
        for part, to in enumerate((own_ref, other_ref)):
            rows = slice(part * count, (part + 1) * count)
            terms = chunk(blocks - 1, rows, acts_ref, slope_ref)
            for y, cols in enumerate((near, far)):
                base = base_ref[rows, y * half : (y + 1) * half]
                to[:, cols] = (base + terms[y]).astype(to.dtype)
    else:
        acts_ref, slope_ref, total = refs[:-1]
        total[...] = jnp.zeros_like(total)

        @pl.loop(0, 2 * (blocks - 1))
        def _(i):
            rows = pl.ds(pl.multiple_of((i & 1) * count, count), count)
            one, two = chunk(i >> 1, rows, acts_ref, slope_ref)
            total[rows, :half] += one
            total[rows, half:] += two


def ffn_back_kernel(
    place_ref,
    dz_ref,
    other_dz_ref,
    h_ref,
    other_h_ref,
    acts_ref,
    slope_ref,
    w_ref,
    own_ref,
    other_ref,
    up_keep,
    up_give,
    down_keep,
    down_give,
    sums_ref,
    total,
    grad_pre,
    dz_near,
    rows_t,
    up_both,
    down_both,
    sums,
):
    step = pl.program_id(0)
    half = w_ref.shape[3]
    quarter = half // 2
    count = own_ref.shape[0]
    near, far = half_cols(place_ref[1], half), half_cols(1 - place_ref[1], half)
    first, second = slice(0, half), slice(half, 2 * half)

    @pl.when(step == 0)
    def _():
        total[...] = jnp.zeros_like(total)
        for to, cols in ((first, near), (second, far)):
            dz_near[:count, to] = dz_ref[:, cols]
            dz_near[count:, to] = other_dz_ref[:, cols]
            rows_t[to, :count] = h_ref[:, cols].T
            rows_t[to, count:] = other_h_ref[:, cols].T

    for k, hid in enumerate((first, second)):
        for y, to in enumerate((first, second)):
            up_both[to, hid] = w_ref[k, y, :half]
            down_both[hid, to] = w_ref[k, y, half:]
    sums[...] = jnp.zeros_like(sums)

    @pl.loop(0, 2)
    def _(part):
        rows = pl.ds(pl.multiple_of(part * count, count), count)
        grad_acts = contract_last(dz_near[rows], down_both[...])
        low = (slope_ref[rows].astype(jnp.float32) * grad_acts).astype(jnp.bfloat16)
        grad_pre[rows] = low
        sums[...] += row_sum(low.astype(jnp.float32))
        total[rows] += contract_last(low, up_both[...])

    tps = [(place_ref[2] + 4 - jnp.where(step == 0, k, 3 - k)) & 3 for k in (0, 1)]
    for tp, hid in zip(tps, (first, second)):
        sums_ref[tp] = sums[:, hid]
    acts_t = acts_ref[...].T
    for side, cols in enumerate((first, second)):
        up_grad = dot32(rows_t[cols], grad_pre[...]).astype(jnp.bfloat16)
        down_grad = dot32(acts_t, dz_near[:, cols]).astype(jnp.bfloat16)
        down_to = down_give if side else down_keep
        for across in (0, 1):

            @pl.when(place_ref[3] == across)
            def _():
                for k in (0, 1):
                    tp = tps[k]
                    hid = slice(k * half, (k + 1) * half)
                    for x in (0, 1):
                        part = slice((x ^ across) * quarter, (x ^ across) * quarter + quarter)
                        down_rows = slice(k * half + part.start, k * half + part.stop)
                        (up_give if x else up_keep)[side, tp] = up_grad[part, hid]
                        down_to[x, tp] = down_grad[down_rows]

    @pl.when(step == pl.num_programs(0) - 1)
    def _():
        own_ref[:, near] = total[:count, first].astype(jnp.bfloat16)
        own_ref[:, far] = total[:count, second].astype(jnp.bfloat16)
        other_ref[:, near] = total[count:, first].astype(jnp.bfloat16)
        other_ref[:, far] = total[count:, second].astype(jnp.bfloat16)


def once(shape):
    return pl.BlockSpec(
        shape, lambda *_: (0,) * len(shape), pipeline_mode=pl.Buffered(buffer_count=1)
    )


def whole(shape):
    return pl.BlockSpec(shape, lambda *_: (0,) * len(shape))


def ffn(place, rows, other_rows, weights, bias, prior=()):
    count, width = rows.shape
    both = 2 * count
    tps, shards, _, half = weights.shape
    vmem = pl.BlockSpec(memory_space=pltpu.VMEM)
    low = jax.ShapeDtypeStruct((count, width), jnp.bfloat16)
    hidden = jax.ShapeDtypeStruct((both, tps * half), jnp.bfloat16)
    last = [low, low] if prior else [jax.ShapeDtypeStruct((both, width), jnp.float32)]
    steps = 1 if prior else tps - 1
    return pl.pallas_call(
        partial(ffn_kernel, bool(prior)),
        in_specs=[pl.BlockSpec(memory_space=pltpu.SMEM)] + [vmem] * (4 + len(prior)),
        out_specs=[vmem] * (2 + len(last)),
        out_shape=[hidden, hidden] + last,
        scratch_shapes=[pltpu.VMEM((both, width), jnp.bfloat16)],
        input_output_aliases={6: 0, 7: 1} if prior else {},
        compiler_params=pltpu.CompilerParams(vmem_limit_bytes=16 << 20),
        cost_estimate=pl.CostEstimate(
            flops=12 * both * width * steps * half, bytes_accessed=3 * steps << 20, transcendentals=0
        ),
        name="ffn",
    )(place, rows, other_rows, weights, bias, *prior)


def ffn_back(place, grads, other_grads, rows, other_rows, acts, slope, weights):
    count, width = rows.shape
    both = 2 * count
    tps, shards, _, half = weights.shape
    block = pl.BlockSpec((both, 2 * half), lambda i, _: (0, i))
    parts = (2, tps, half // 2, half)
    low = jax.ShapeDtypeStruct((count, width), jnp.bfloat16)
    return pl.pallas_call(
        ffn_back_kernel,
        grid_spec=pltpu.PrefetchScalarGridSpec(
            num_scalar_prefetch=1,
            grid=(tps // 2,),
            in_specs=[
                *[once((count, width))] * 4,
                block,
                block,
                pl.BlockSpec((2, shards, 2 * half, half), lambda i, _: (i, 0, 0, 0)),
            ],
            out_specs=[
                whole((count, width)),
                whole((count, width)),
                *[whole(parts)] * 4,
                whole((tps, 1, half)),
            ],
            scratch_shapes=[
                pltpu.VMEM((both, width), jnp.float32),
                pltpu.VMEM((both, 2 * half), jnp.bfloat16),
                pltpu.VMEM((both, width), jnp.bfloat16),
                pltpu.VMEM((width, both), jnp.bfloat16),
                pltpu.VMEM((width, 2 * half), jnp.bfloat16),
                pltpu.VMEM((2 * half, width), jnp.bfloat16),
                pltpu.VMEM((1, 2 * half), jnp.float32),
            ],
        ),
        out_shape=[
            low,
            low,
            *[jax.ShapeDtypeStruct(parts, jnp.bfloat16)] * 4,
            jax.ShapeDtypeStruct((tps, 1, half), jnp.float32),
        ],
        compiler_params=pltpu.CompilerParams(vmem_limit_bytes=30 << 20),
        cost_estimate=pl.CostEstimate(
            flops=12 * both * width * tps * half, bytes_accessed=20 << 20, transcendentals=0
        ),
        name="ffn_back",
    )(place, grads, other_grads, rows, other_rows, acts, slope, weights)


def project_kernel(
    place_ref, w_mine, w_other, x_mine, x_other, bias_ref, q_ref, k_ref, v_ref, x_ref, wt
):
    core, shard, tp, across, start = (place_ref[i] for i in range(5))
    depth = w_mine.shape[3]
    width = x_ref.shape[1]
    part = width // 8
    length = 4 * x_mine.shape[2]
    reach = length // 2
    for c, source in enumerate((w_mine, w_other)):
        for y in (0, 1):
            cols = half_cols(shard + y - 2 * shard * y, depth)
            for k in range(4):
                row = ((tp + 4 - k) & 3) * 2 + core + c - 2 * core * c
                rows = pl.ds(pl.multiple_of(row * part, part), part)
                for m in range(3):
                    wt[m, rows, cols] = source[y, k, m * part : (m + 1) * part]
    for i in range(x_ref.shape[0] // QBLOCK):
        row = start - reach + i * QBLOCK
        inside = jnp.logical_and(row >= 0, row < 2 * length)
        at = jnp.where(inside, row, 0) // QBLOCK
        seq, block, piece = at // 8, (at // 2) & 3, at & 1
        here = jnp.where((block >> 1) == across, 0, 1)
        rows = pl.ds(pl.multiple_of(piece * QBLOCK, QBLOCK), QBLOCK)
        mine, other = x_mine[here, seq, rows], x_other[here, seq, rows]
        found = jnp.where((block & 1) == core, mine, other)
        x_ref[i * QBLOCK : (i + 1) * QBLOCK] = jnp.where(inside, found, jnp.zeros_like(found))
    count = q_ref.shape[0]
    scaled = contract_last(x_ref[reach : reach + count], wt[0]) + bias_ref[0:1]
    q_ref[...] = (scaled * (1.0 / math.sqrt(HEAD_DIM))).astype(jnp.bfloat16)
    chunk = x_ref.shape[0] // 4

    @pl.loop(0, 4)
    def _(step):
        rows = pl.ds(pl.multiple_of(step * chunk, 32), chunk)
        k_ref[rows] = contract_last(x_ref[rows], wt[1]).astype(jnp.bfloat16)
        v_ref[rows] = (contract_last(x_ref[rows], wt[2]) + bias_ref[1:2]).astype(jnp.bfloat16)


def project(place, w_mine, w_other, x_mine, x_other, biases, count, window):
    width = x_mine.shape[-1]
    return pl.pallas_call(
        project_kernel,
        in_specs=[pl.BlockSpec(memory_space=pltpu.SMEM)]
        + [pl.BlockSpec(memory_space=pltpu.VMEM)] * 5,
        out_specs=[pl.BlockSpec(memory_space=pltpu.VMEM)] * 5,
        out_shape=[
            jax.ShapeDtypeStruct((count, width), jnp.bfloat16),
            jax.ShapeDtypeStruct((window, width), jnp.bfloat16),
            jax.ShapeDtypeStruct((window, width), jnp.bfloat16),
            jax.ShapeDtypeStruct((window, width), jnp.bfloat16),
            jax.ShapeDtypeStruct((3, width, width), jnp.bfloat16),
        ],
        compiler_params=pltpu.CompilerParams(vmem_limit_bytes=24 << 20),
        cost_estimate=pl.CostEstimate(
            flops=4 * window * width * width, bytes_accessed=16 << 20, transcendentals=0
        ),
        name="project",
    )(place, w_mine, w_other, x_mine, x_other, biases)


def norm_pieces(resid):
    center = resid - jnp.mean(resid, axis=-1, keepdims=True)
    inv_std = lax.rsqrt(jnp.mean(center * center, axis=-1, keepdims=True) + eps_norm)
    return center * inv_std, inv_std


def norm_pull(grad_out, normed, inv_std, gain):
    grad_normed = grad_out * gain
    return inv_std * (
        grad_normed
        - jnp.mean(grad_normed, axis=-1, keepdims=True)
        - normed * jnp.mean(grad_normed * normed, axis=-1, keepdims=True)
    )


def row_sum(rows):
    return jnp.sum(rows, axis=0, keepdims=True)


def attend_out_kernel(
    place_ref, o_ref, x_ref, w_mine, w_other, vec_ref, hb_ref, n_ref, i_ref, wo_ref
):
    core, shard, tp = (place_ref[i] for i in range(3))
    part, depth = w_mine.shape[2:]

    @pl.when(pl.program_id(0) == 0)
    def _():
        for c, source in enumerate((w_mine, w_other)):
            for y in (0, 1):
                cols = half_cols(shard + y - 2 * shard * y, depth)
                for k in range(4):
                    row = ((tp + 4 - k) & 3) * 2 + core + c - 2 * core * c
                    rows = pl.ds(pl.multiple_of(row * part, part), part)
                    wo_ref[rows, cols] = source[k, y]

    resid = x_ref[...].astype(jnp.float32) + dot32(o_ref[...], wo_ref[...]) + vec_ref[0:1]
    normed, inv_std = norm_pieces(resid)
    hb_ref[...] = (normed * vec_ref[1:2] + vec_ref[2:3]).astype(jnp.bfloat16)
    n_ref[...] = normed.astype(jnp.bfloat16)
    i_ref[...] = jnp.broadcast_to(inv_std, i_ref.shape)


def row_blocks(width):
    return pl.BlockSpec((QBLOCK, width), lambda i, *_: (i, 0))


def on_rows(kernel, count, in_specs, out_specs, out_shape, name, scalars=0):
    return pl.pallas_call(
        kernel,
        grid_spec=pltpu.PrefetchScalarGridSpec(
            num_scalar_prefetch=scalars,
            grid=(count // QBLOCK,),
            in_specs=in_specs,
            out_specs=out_specs,
        ),
        out_shape=out_shape,
        compiler_params=pltpu.CompilerParams(vmem_limit_bytes=12 << 20),
        cost_estimate=pl.CostEstimate(flops=1 << 28, bytes_accessed=6 << 20, transcendentals=0),
        name=name,
    )


def attend_out(place, mixed, window_rows, reach, w_mine, w_other, vectors):
    count, width = mixed.shape
    rows = row_blocks(width)
    low = jax.ShapeDtypeStruct((count, width), jnp.bfloat16)
    return on_rows(
        attend_out_kernel,
        count,
        [
            rows,
            pl.BlockSpec((QBLOCK, width), lambda i, *_: (i + reach // QBLOCK, 0)),
            whole(w_mine.shape),
            whole(w_other.shape),
            whole(vectors.shape),
        ],
        [rows, rows, row_blocks(QBLOCK), whole((width, width))],
        [
            low,
            low,
            jax.ShapeDtypeStruct((count, QBLOCK), jnp.float32),
            jax.ShapeDtypeStruct((width, width), jnp.bfloat16),
        ],
        "attend_out",
        1,
    )(place, mixed, window_rows, w_mine, w_other, vectors)


def norm_sums(sums_ref, rows):
    sums = jnp.concatenate([row_sum(row) for row in rows], axis=0)
    add_or_set(pl.program_id(0) == 0, sums_ref, slice(None), sums)


def cot_source(i, place_ref):
    core, tp, across = place_ref[0], place_ref[2], place_ref[3]
    odd = (across + tp) & 1
    block = 3 * core + i - 2 * odd
    block = jnp.where(block < 0, block + 6, block)
    far = block >> 1 == 2
    held = jnp.where(far, core == odd, core == (block >> 1))
    return jnp.where(far, 1, 0), block & 1, jnp.where(held, 1, 0)


def ffn_norm_kernel(
    place_ref, h_ref, own_ref, got_ref, g_ref, g_other_ref, vec_ref, y_ref, dz_ref, sums_ref
):
    resid = h_ref[...].astype(jnp.float32) + own_ref[...].astype(jnp.float32)
    resid += got_ref[...].astype(jnp.float32) + vec_ref[0:1]
    normed, inv_std = norm_pieces(resid)
    y_ref[...] = (normed * vec_ref[1:2] + vec_ref[2:3]).astype(jnp.bfloat16)
    held = cot_source(pl.program_id(0), place_ref)[2]
    grad_out = jnp.where(held == 1, g_ref[0], g_other_ref[0]).astype(jnp.float32)
    low = norm_pull(grad_out, normed, inv_std, vec_ref[1:2]).astype(jnp.bfloat16)
    dz_ref[...] = low
    norm_sums(sums_ref, (low.astype(jnp.float32), grad_out * normed, grad_out))


def ffn_norm(place, hidden, own, got, cots, other_cots, vectors):
    count, width = hidden.shape
    rows = row_blocks(width)
    cot = pl.BlockSpec((1, QBLOCK, width), lambda i, at: (*cot_source(i, at)[:2], 0))
    low = jax.ShapeDtypeStruct((count, width), jnp.bfloat16)
    return on_rows(
        ffn_norm_kernel,
        count,
        [rows, rows, rows, cot, cot, whole(vectors.shape)],
        [rows, rows, whole((3, width))],
        [low, low, jax.ShapeDtypeStruct((3, width), jnp.float32)],
        "ffn_norm",
        1,
    )(place, hidden, own, got, cots, other_cots, vectors)


def attend_norm_kernel(
    dz_ref, own_ref, got_ref, n_ref, i_ref, vec_ref, wo_ref, out_ref, da_ref, do_ref, sums_ref
):
    grad_out = dz_ref[...].astype(jnp.float32) + own_ref[...].astype(jnp.float32)
    grad_out += got_ref[...].astype(jnp.float32)
    normed = n_ref[...].astype(jnp.float32)
    grad = norm_pull(grad_out, normed, i_ref[:, :1], vec_ref[1:2])
    low = grad.astype(jnp.bfloat16)
    out_ref[...] = grad
    da_ref[...] = low
    do_ref[...] = contract_last(low, wo_ref[...]).astype(jnp.bfloat16)
    norm_sums(sums_ref, (low.astype(jnp.float32), grad_out * normed, grad_out))


def attend_norm(grads, own, got, normed, inv_std, vectors, weights):
    count, width = grads.shape
    rows = row_blocks(width)
    low = jax.ShapeDtypeStruct((count, width), jnp.bfloat16)
    return on_rows(
        attend_norm_kernel,
        count,
        [rows, rows, rows, rows, row_blocks(QBLOCK), whole(vectors.shape), whole(weights.shape)],
        [rows, rows, rows, whole((3, width))],
        [
            jax.ShapeDtypeStruct((count, width), jnp.float32),
            low,
            low,
            jax.ShapeDtypeStruct((3, width), jnp.float32),
        ],
        "attend_norm",
    )(grads, own, got, normed, inv_std, vectors, weights)


def attn_grads_kernel(
    place_ref, dq_ref, dk_ref, dv_ref, o_ref, da_ref, w_ref, attn_ref, ffn_ref, up_ref, *parts
):
    core, shard, across = place_ref[0], place_ref[1], place_ref[3]
    grad_ref = parts[2]
    depth = w_ref.shape[1] // 2
    part = depth // 4
    count = dq_ref.shape[0]
    reach = (w_ref.shape[0] - count) // 2
    sides = (
        (dq_ref, w_ref.at[reach : reach + count]),
        (dk_ref, w_ref),
        (dv_ref, w_ref),
        (o_ref, da_ref),
    )
    for m, (left, right) in enumerate(sides):
        grad_ref[...] = contract_rows(left[...], right[...]).astype(jnp.bfloat16)
        group = across if m < 2 else 1 - across
        rows = slice((m % 2) * part, (m % 2 + 1) * part)
        for z in (0, 1):
            for c in (0, 1):
                at = pl.ds(pl.multiple_of((2 * z + c + core - 2 * c * core) * part, part), part)
                parts[c][shard, group, z, rows] = grad_ref[at, :depth]
                parts[c][1 - shard, group, z, rows] = grad_ref[at, depth:]
    query_sum = row_sum(dq_ref[...].astype(jnp.float32))
    value_sum = row_sum(dv_ref[...].astype(jnp.float32))
    shared = []
    for source in (attn_ref, ffn_ref):
        for r in range(3):
            shared += [source[r : r + 1, :depth], source[r : r + 1, depth:]]
    half = depth // 2
    for z in (0, 1):
        own = slice(z * half, (z + 1) * half)
        heads = jnp.concatenate([query_sum[:, own], value_sum[:, own]], axis=1)
        none = jnp.zeros_like(heads)
        rows = [heads] + shared
        for c in (0, 1):
            last = [none if c else up_ref[z], none, none]
            for x, group in ((across, rows[:8]), (1 - across, rows[8:] + last)):
                block = jnp.concatenate(group, axis=0).astype(jnp.bfloat16)
                for y in (0, 1):
                    parts[c][y, x, z, 2 * part :] = block


def attn_grads(
    place, grad_queries, grad_keys, grad_values, mixed, grad_attn, near, attn_sums, ffn_sums, up_sums
):
    count, width = mixed.shape
    window = near.shape[0]
    depth = width // 2
    high = depth // 2 + 8
    cols = pl.BlockSpec((count, depth), lambda i, _: (0, i))
    near_cols = pl.BlockSpec((window, depth), lambda i, _: (0, i))
    return pl.pallas_call(
        attn_grads_kernel,
        grid_spec=pltpu.PrefetchScalarGridSpec(
            num_scalar_prefetch=1,
            grid=(2,),
            in_specs=[
                cols,
                near_cols,
                near_cols,
                cols,
                whole((count, width)),
                whole((window, width)),
                whole((3, width)),
                whole((3, width)),
                pl.BlockSpec((2, 1, depth), lambda i, _: (i, 0, 0)),
            ],
            out_specs=[pl.BlockSpec((2, 2, 2, high, depth), lambda i, _: (0, 0, i, 0, 0))] * 2,
            scratch_shapes=[pltpu.VMEM((depth, width), jnp.bfloat16)],
        ),
        out_shape=[jax.ShapeDtypeStruct((2, 2, 4, high, depth), jnp.bfloat16)] * 2,
        compiler_params=pltpu.CompilerParams(vmem_limit_bytes=24 << 20),
        cost_estimate=pl.CostEstimate(
            flops=4 * (window + count) * width * width, bytes_accessed=16 << 20, transcendentals=0
        ),
        name="attn_grads",
    )(
        place,
        grad_queries,
        grad_keys,
        grad_values,
        mixed,
        grad_attn,
        near,
        attn_sums,
        ffn_sums,
        up_sums,
    )


def span_grads_kernel(
    place_ref,
    dq_ref,
    dk_ref,
    dv_ref,
    w_ref,
    base_ref,
    own_ref,
    first_ref,
    second_ref,
    give_ref,
    near,
):
    core = place_ref[0]
    count, reach = own_ref.shape[0], give_ref.shape[0]
    far = count + reach
    size = near.shape[0] // 4

    @pl.loop(0, 4)
    def _(step):
        rows = pl.ds(pl.multiple_of(step * size, 32), size)
        near[rows] = dot32(dk_ref[rows], w_ref[1]) + dot32(dv_ref[rows], w_ref[2])

    def rows_at(start, size):
        return near[pl.ds(pl.multiple_of(start, QBLOCK), size)].astype(jnp.bfloat16)

    give_ref[...] = rows_at((1 - core) * far, reach)
    first_ref[...] = rows_at(jnp.where(core == 0, reach - count, far), count)
    second_ref[...] = rows_at(jnp.where(core == 0, 0, far + count), reach - count)
    own_ref[...] = base_ref[...] + dot32(dq_ref[...], w_ref[0]) + near[reach:far]


def span_grads(place, grad_queries, grad_keys, grad_values, weights, base):
    count, width = base.shape
    reach = (grad_keys.shape[0] - count) // 2
    vmem = pl.BlockSpec(memory_space=pltpu.VMEM)
    return pl.pallas_call(
        span_grads_kernel,
        in_specs=[pl.BlockSpec(memory_space=pltpu.SMEM)] + [vmem] * 5,
        out_specs=[vmem] * 4,
        out_shape=[
            jax.ShapeDtypeStruct((count, width), jnp.float32),
            jax.ShapeDtypeStruct((count, width), jnp.bfloat16),
            jax.ShapeDtypeStruct((reach - count, width), jnp.bfloat16),
            jax.ShapeDtypeStruct((reach, width), jnp.bfloat16),
        ],
        scratch_shapes=[pltpu.VMEM(grad_keys.shape, jnp.float32)],
        compiler_params=pltpu.CompilerParams(vmem_limit_bytes=16 << 20),
        cost_estimate=pl.CostEstimate(
            flops=4 * (count + 2 * reach) * width * width,
            bytes_accessed=12 << 20,
            transcendentals=0,
        ),
        name="span_grads",
    )(place, grad_queries, grad_keys, grad_values, weights, base)


def assemble_kernel(place_ref, one, two, three, four, halves, out_ref):
    core, tp, across = place_ref[0], place_ref[2], place_ref[3]
    block = out_ref.shape[1]
    part = block // 2
    mine = pl.ds(pl.multiple_of(core * part, part), part)
    other = pl.ds(pl.multiple_of((1 - core) * part, part), part)
    for k, source in enumerate((one, two, three, four)):
        z = (tp + 4 - k) & 3
        group, side = 3 * (z >> 1), z & 1
        out_ref[group + jnp.where(side == 1, 1, 2 * across)] = source[:block].astype(out_ref.dtype)
        foreign = group + 2 - 2 * across

        @pl.when(((side + across + core) & 1) == 1)
        def _():
            out_ref[foreign, mine] = source[block:].astype(out_ref.dtype)
            out_ref[foreign, other] = halves[k].astype(out_ref.dtype)


def assemble_late_kernel(place_ref, one, two, three, four, middle, foreign, out_ref):
    core, tp, across = place_ref[0], place_ref[2], place_ref[3]
    block = out_ref.shape[1]
    part = block // 2
    for k, source in enumerate((one, two, three, four)):
        z = (tp + 4 - k) & 3
        group, side = 3 * (z >> 1), z & 1
        at = group + jnp.where(side == 1, 1, 2 * across)
        odd = (across + side) & 1

        @pl.when(jnp.logical_and(odd == 0, core == 0))
        def _():
            out_ref[at] = source[:block]

        @pl.when(jnp.logical_and(odd == 0, core == 1))
        def _():
            out_ref[at, :part] = middle[k]
            out_ref[at, part:] = source[:part]

        @pl.when(jnp.logical_and(odd == 1, core == 0))
        def _():
            out_ref[at, :part] = source[block:]
            out_ref[at, part:] = middle[k]

        @pl.when(jnp.logical_and(odd == 1, core == 1))
        def _():
            out_ref[at] = source[part:]

        @pl.when(((side + across + core) & 1) == 1)
        def _():
            out_ref[group + 2 - 2 * across] = foreign[k // 2]


def assemble(kernel, place, pieces, others, seqs, dtype):
    rows, width = pieces[0].shape
    vmem = pl.BlockSpec(memory_space=pltpu.VMEM)
    return pl.pallas_call(
        kernel,
        in_specs=[pl.BlockSpec(memory_space=pltpu.SMEM)] + [vmem] * (4 + len(others)),
        out_specs=vmem,
        out_shape=jax.ShapeDtypeStruct((seqs, rows * 2 // 3, width), dtype),
        compiler_params=pltpu.CompilerParams(vmem_limit_bytes=10 << 20),
        cost_estimate=pl.CostEstimate(flops=1 << 20, bytes_accessed=8 << 20, transcendentals=0),
        name="assemble",
    )(place, *pieces, *others)


def finish_ffn_kernel(place_ref, mine, across_got, core_got, both_got, up_ref, down_ref):
    core, across = place_ref[0], place_ref[3]
    depth = mine.shape[1]
    part = depth // 2
    for c, x, source in (
        (core, across, mine),
        (core, 1 - across, across_got),
        (1 - core, across, core_got),
        (1 - core, 1 - across, both_got),
    ):
        rows = pl.ds(pl.multiple_of(x * part, part), part)
        up_ref[rows, half_cols(c, depth)] = source[:part].astype(jnp.float32)
        rows = pl.ds(pl.multiple_of(c * depth + x * part, part), part)
        down_ref[rows] = source[part:].astype(jnp.float32)


def finish_attn_kernel(
    place_ref, mine, across_got, core_got, both_got, q_ref, k_ref, v_ref, o_ref, *refs
):
    *vectors, sums_ref = refs
    core, across = place_ref[0], place_ref[3]
    part = q_ref.shape[0] // 2
    for c, x, source in (
        (core, across, mine),
        (core, 1 - across, across_got),
        (1 - core, across, core_got),
        (1 - core, 1 - across, both_got),
    ):
        rows = pl.ds(pl.multiple_of(c * part, part), part)
        one = source[:part].astype(jnp.float32)
        two = source[part : 2 * part].astype(jnp.float32)
        sums_ref[c, x] = source[2 * part :].astype(jnp.float32)

        @pl.when(x == 0)
        def _():
            q_ref[rows], k_ref[rows] = one, two

        @pl.when(x == 1)
        def _():
            v_ref[rows], o_ref[rows] = one, two

    def flat(*rows):
        return jnp.concatenate(rows, axis=1).reshape(-1)

    sums = sums_ref[core].reshape(16, 4 * part)
    for r, to in enumerate(vectors[:6]):
        to[...] = flat(sums[2 * r + 1 : 2 * r + 2], sums[2 * r + 2 : 2 * r + 3])
    vectors[6][...] = flat(sums_ref[0, 1, 5:6], sums_ref[1, 1, 5:6])
    vectors[7][...] = sums[0:1, : 2 * part].reshape(-1)
    vectors[8][...] = sums[0:1, 2 * part :].reshape(-1)


def finish(kernel, place, pieces, shapes, name, scratch=()):
    vmem = pl.BlockSpec(memory_space=pltpu.VMEM)
    return pl.pallas_call(
        kernel,
        in_specs=[pl.BlockSpec(memory_space=pltpu.SMEM)] + [vmem] * 4,
        out_specs=[vmem] * len(shapes),
        out_shape=[jax.ShapeDtypeStruct(shape, jnp.float32) for shape in shapes],
        scratch_shapes=scratch,
        compiler_params=pltpu.CompilerParams(vmem_limit_bytes=8 << 20),
        cost_estimate=pl.CostEstimate(flops=1 << 20, bytes_accessed=4 << 20, transcendentals=0),
        name=name,
    )(place, *pieces)


def ctx_swap(array, bit):
    return lax.ppermute(array, "ctx", [(i, i ^ bit) for i in range(4)])


def core_swap(array):
    return ctx_swap(array, 1)


def tie(*arrays):
    return lax.optimization_barrier(arrays)


def across_swap(array):
    return ctx_swap(array, 2)


def in_order(flag, mine, other):
    return jnp.where(flag == 0, mine, other), jnp.where(flag == 0, other, mine)


def at(across, core, tp):
    return (2 * across + core) * 4 + tp


def across_pairs():
    pairs = []
    for tp in range(4):
        for across in (0, 1):
            core = across ^ (tp & 1)
            pairs.append((at(1 - across, core, tp), at(across, core, tp)))
    return pairs


def tp_shifts(array, cuts=(slice(None), slice(None), slice(None))):
    return [
        lax.ppermute(array[cut], "tp", [(i, (i + shift) % 4) for i in range(4)])
        for shift, cut in zip((1, 2, 3), cuts)
        if cut is not None
    ]


def by_tp(array, shifted):
    one, two, three = shifted
    line = jnp.stack([three, two, one, array, three, two, one])
    return lax.dynamic_slice_in_dim(line, 3 - lax.axis_index("tp"), 4, 0)


def shard_swap(array):
    return lax.ppermute(array, "shard", [(0, 1), (1, 0)])


def low_sum(left, right):
    return (left.astype(jnp.float32) + right.astype(jnp.float32)).astype(jnp.bfloat16)


def scatter_tp_start(parts):
    tp = lax.axis_index("tp")
    moved = [lax.dynamic_index_in_dim(parts, tp, 0, keepdims=False)]
    for shift in (1, 2, 3):
        sent = lax.dynamic_index_in_dim(parts, (tp + shift) & 3, 0, keepdims=False)
        moved.append(lax.ppermute(sent, "tp", [(i, (i + shift) % 4) for i in range(4)]))
    return moved


def scatter_tp_end(moved):
    return sum(part.astype(jnp.float32) for part in moved).astype(jnp.bfloat16)


def chain_pairs(turn):
    pairs = []
    for group in (0, 2):
        path = [(0, group), (0, group + 1), (1, group + 1), (1, group)]
        for (across, tp), (next_across, next_tp) in zip(path[:-1], path[1:]):
            pairs.append((at(across, 1, tp), at(next_across, 1 ^ turn, next_tp)))
            pairs.append((at(next_across, 0, next_tp), at(across, turn, tp)))
    return pairs


def block_pairs(core):
    pairs = []
    for tp in range(4):
        for across in (0, 1):
            source = 1 ^ across ^ (tp & 1)
            pairs.append((at(across, source, tp), at(1 - across, core, tp)))
    return pairs


def span_shards(
    layer_input,
    segment_ids,
    query_proj,
    query_bias,
    key_proj,
    value_proj,
    value_bias,
    out_proj,
    out_bias,
    attn_gain,
    attn_shift,
    up_proj,
    up_bias,
    down_proj,
    down_bias,
    ffn_gain,
    ffn_shift,
    out_cotangent,
):
    seqs, block, width = layer_input.shape
    length = segment_ids.shape[1]
    reach = length // 2
    count = seqs * block // 4
    window = count + 2 * reach
    bf16, f32 = jnp.bfloat16, jnp.float32
    ctx, tp = lax.axis_index("ctx"), lax.axis_index("tp")
    shard = lax.axis_index("shard")
    core, across, side = ctx & 1, ctx >> 1, tp & 1
    place = 2 * across + (side ^ across)
    odd = across ^ side

    heads = query_proj.shape[1]
    half = heads // 2
    depth = query_proj.shape[0]
    cut = up_proj.shape[1] // 2
    own_in = lax.dynamic_slice_in_dim(
        jnp.stack([query_proj.T, key_proj.T, value_proj.T]), core * half, half, 1
    ).reshape(3 * half, depth)
    own_biases = jnp.stack(
        [
            jnp.concatenate([query_bias, value_bias]),
            lax.dynamic_slice_in_dim(up_bias, core * cut, cut, 0),
        ]
    )
    own_in = jnp.concatenate([own_in, own_biases, jnp.zeros((14, depth), bf16)], axis=0)
    out_half = out_proj.shape[0] // 2
    own_rest = jnp.concatenate(
        [
            lax.dynamic_slice_in_dim(up_proj, core * cut, cut, 1),
            lax.dynamic_slice_in_dim(down_proj, core * cut, cut, 0),
            lax.dynamic_slice_in_dim(out_proj, core * out_half, out_half, 0),
        ],
        axis=0,
    )
    first_seq = 3 * (tp >> 1)
    mine = lax.dynamic_slice_in_dim(layer_input, first_seq + across, 2, 0)
    theirs = across_swap(lax.dynamic_slice_in_dim(layer_input, first_seq + 1 - across, 2, 0))
    in_shifted = tp_shifts(own_in)
    far_rest = shard_swap(own_rest)
    *in_shifted, theirs, far_rest = tie(*in_shifted, theirs, far_rest)
    in_near = jnp.stack([own_in] + in_shifted)
    (rest_one,) = tp_shifts(tie(own_rest, in_near)[0], (slice(None), None, None))
    own_pair = jnp.stack([own_rest[: 2 * cut], far_rest[: 2 * cut]])
    near_cot = lax.dynamic_index_in_dim(
        out_cotangent, first_seq + odd + across, 0, keepdims=False
    )
    far_cot = lax.ppermute(
        lax.dynamic_index_in_dim(
            tie(out_cotangent, theirs)[0], first_seq + 2 - 2 * across, 0, keepdims=False
        ),
        ("ctx", "tp"),
        across_pairs(),
    )
    in_far, rest_one, own_pair, far_cot = tie(shard_swap(in_near), rest_one, own_pair, far_cot)
    in_mine = jnp.stack([in_near, in_far])
    (rest_three,) = tp_shifts(tie(own_rest, in_near)[0], (None, None, slice(None)))
    in_other, rest_three = tie(core_swap(in_mine), rest_three)
    own_late = tie(own_rest, rest_three)[0]
    (some_two,) = tp_shifts(own_late, (None, slice(cut, None), None))
    (up_two,) = tp_shifts(own_late, (None, slice(cut), None))
    far_three = shard_swap(rest_three)
    bias_rows = in_mine[0, :, 3 * half]
    in_biases = by_tp(bias_rows[0], [bias_rows[1], bias_rows[2], bias_rows[3]]).astype(f32)
    in_biases = jnp.stack([in_biases[:, :heads].reshape(-1), in_biases[:, heads:].reshape(-1)])
    up_bias_here = in_mine[0, :, 3 * half + 1].reshape(4, 1, cut).astype(f32)

    pair = jnp.stack([mine, theirs])
    pair_other = core_swap(pair)
    start = 2 * count * place + count * core - length * across
    ids = lax.dynamic_slice_in_dim(segment_ids, first_seq + across, 2, 0)
    ids = (ids + jnp.array([[0], [1 << 16]], jnp.int32)).reshape(-1)
    no_doc = jnp.full((reach,), -1, jnp.int32)
    window_docs = lax.dynamic_slice_in_dim(
        jnp.concatenate([no_doc, ids, no_doc]), start, window, 0
    )
    key_docs = window_docs[None]
    query_docs = jnp.broadcast_to(window_docs[reach : reach + count, None], (count, QBLOCK))

    place = jnp.stack([core, shard, tp, across, start])
    far_one = shard_swap(rest_one)
    queries, keys, values, in_window, weights_t = project(
        place, in_mine, in_other, pair, pair_other, in_biases, count, window
    )
    attention = queries, keys, values, key_docs, query_docs, reach
    mixed, logs = attend(*attention, 0)
    mixed, far_one, far_three, some_two = tie(mixed, far_one, far_three, some_two)
    far_some_two = shard_swap(some_two)
    mixed, logs = attend(*attention, 1, (mixed, logs))
    mixed, far_some_two, up_two, plan = tie(
        mixed, far_some_two, up_two, key_plan(window_docs, reach, count)
    )
    far_up_two = shard_swap(up_two)
    out_mine = jnp.stack(
        [
            jnp.stack([one[-out_half:], two[-out_half:]])
            for one, two in (
                (own_rest, far_rest),
                (rest_one, far_one),
                (some_two, far_some_two),
                (rest_three, far_three),
            )
        ]
    )
    attn_vectors = jnp.stack([out_bias, attn_gain, attn_shift]).astype(f32)
    hidden_low, normed_one, inv_one, full_out = attend_out(
        place, mixed, in_window, reach, out_mine, core_swap(out_mine), attn_vectors
    )
    hidden_other = core_swap(hidden_low)
    hidden_both = hidden_low, hidden_other
    ffn_weights = jnp.stack(
        [
            own_pair,
            jnp.stack([rest_one[: 2 * cut], far_one[: 2 * cut]]),
            jnp.stack([rest_three[: 2 * cut], far_three[: 2 * cut]]),
            own_pair,
        ]
    )
    ffn_bias = jnp.stack([up_bias_here[k] for k in (0, 1, 3, 2)])
    acts, slope, ffn_sum = ffn(place, *hidden_both, ffn_weights, ffn_bias)
    ffn_sum, far_up_two = tie(ffn_sum, far_up_two)
    rest = ffn_weights.at[3].set(
        jnp.stack(
            [
                jnp.concatenate([up_two, some_two[:cut]], axis=0),
                jnp.concatenate([far_up_two, far_some_two[:cut]], axis=0),
            ]
        )
    )
    acts, slope, ffn_own, ffn_other = ffn(
        place, *hidden_both, rest, ffn_bias, (ffn_sum, acts, slope)
    )

    half_block = block // 2

    def deliver_start(rows):
        far_rows = jnp.where(odd == 0, rows[-block:], rows[:block])
        return (
            core_swap(jnp.where(odd == 0, rows[block:], rows[:half_block])),
            lax.ppermute(far_rows[:half_block], ("ctx", "tp"), block_pairs(0)),
            lax.ppermute(far_rows[half_block:], ("ctx", "tp"), block_pairs(1)),
        )

    def deliver_pack(rows, middle, low, high):
        where_kept = [
            rows[:block],
            jnp.concatenate([middle, rows[:half_block]], axis=0),
            jnp.concatenate([rows[block:], middle], axis=0),
            rows[half_block:],
        ]
        kept = jnp.where(
            odd == 0,
            jnp.where(core == 0, where_kept[0], where_kept[1]),
            jnp.where(core == 0, where_kept[2], where_kept[3]),
        )
        return jnp.concatenate([kept, low + high], axis=0)

    cot_pair = tie(jnp.stack([near_cot, far_cot]), queries)[0]
    cot_swapped = core_swap(cot_pair)

    ffn_vectors = jnp.stack([down_bias, ffn_gain, ffn_shift]).astype(f32)
    output_rows, grad_ffn, ffn_sums = ffn_norm(
        place, hidden_low, ffn_own, core_swap(ffn_other), cot_pair, cot_swapped, ffn_vectors
    )
    grad_other = core_swap(grad_ffn)
    out_pieces = [output_rows] + tp_shifts(output_rows)
    back_own, back_other, up_keep, up_give, down_keep, down_give, up_sums = ffn_back(
        place, grad_ffn, grad_other, *hidden_both, acts, slope, rest
    )
    back_own, out_pieces[1] = tie(back_own, out_pieces[1])
    grad_one, grad_attn, grad_mixed, attn_sums = attend_norm(
        grad_ffn, back_own, core_swap(back_other), normed_one, inv_one, attn_vectors, full_out
    )
    up_got = across_swap(up_give)
    down_got = shard_swap(down_give)
    grad_scaled, grad_keys, grad_values = attend_back(plan, *attention, grad_mixed, logs)
    own_sum, first, second, give = span_grads(
        place, grad_scaled, grad_keys, grad_values, weights_t, grad_one
    )
    first, up_got, down_got, out_pieces[2] = tie(first, up_got, down_got, out_pieces[2])
    up_parts = [low_sum(up_keep[i], up_got[i]) for i in (0, 1)]
    down_parts = [low_sum(down_keep[i], down_got[i]) for i in (0, 1)]
    up_got, down_got = shard_swap(up_parts[1]), across_swap(down_parts[1])
    got = core_swap(give)
    shared = reach - count
    to_own = lax.dynamic_slice_in_dim(got, (1 - core) * shared, count, 0)
    to_next = lax.dynamic_slice_in_dim(got, core * count, shared, 0)
    no_rows = jnp.zeros((count - shared, width), bf16)
    first = low_sum(
        first,
        jnp.where(
            core == 0,
            jnp.concatenate([no_rows, to_next], axis=0),
            jnp.concatenate([to_next, no_rows], axis=0),
        ),
    )
    first_now, up_got, down_got, out_pieces[3] = tie(first, up_got, down_got, out_pieces[3])
    ffn_parts = jnp.concatenate(
        [low_sum(up_parts[0], up_got), low_sum(down_parts[0], down_got)], axis=1
    )
    ffn_near = scatter_tp_start(ffn_parts)
    first_got = lax.ppermute(first, ("ctx", "tp"), chain_pairs(1))
    second_got = lax.ppermute(second, ("ctx", "tp"), chain_pairs(0))
    grad_keys, first_now = tie(grad_keys, first)
    attn_parts = attn_grads(
        place,
        grad_scaled,
        grad_keys,
        grad_values,
        mixed,
        grad_attn,
        in_window,
        attn_sums,
        ffn_sums,
        up_sums,
    )
    first_got, second_got, attn_keep, attn_give, ffn_near[1], ffn_near[3] = tie(
        first_got, second_got, *attn_parts, ffn_near[1], ffn_near[3]
    )
    attn_core = core_swap(attn_give)
    own_sum += to_own.astype(f32) + first_got.astype(f32)
    own_sum += jnp.where(
        core == 0,
        jnp.concatenate([no_rows, second_got], axis=0),
        jnp.concatenate([second_got, no_rows], axis=0),
    ).astype(f32)
    own_low = own_sum.astype(bf16)
    in_moves = deliver_start(own_low)
    *in_moves, attn_core, ffn_near[2] = tie(*in_moves, attn_core, ffn_near[2])
    in_packed = deliver_pack(own_low, *in_moves)
    in_pieces = [in_packed] + tp_shifts(in_packed)
    attn_parts = [low_sum(attn_keep[i], attn_core[i]) for i in (0, 1)]
    attn_got = shard_swap(attn_parts[1])
    parity = (tp + 1 + across + core) & 1
    out_sent = [
        jnp.where(
            core == 0,
            jnp.where(parity == 0, even[:block], odd_one[:block]),
            jnp.where(parity == 0, even[-block:], odd_one[-block:]),
        )
        for even, odd_one in (out_pieces[:2], out_pieces[2:])
    ]
    out_foreign = lax.ppermute(jnp.stack(out_sent), "ctx", [(i, 3 - i) for i in range(4)])
    out_middle = core_swap(
        jnp.stack(
            [
                jnp.where(((across + tp + k) & 1) == 0, piece[block:], piece[:half_block])
                for k, piece in enumerate(out_pieces)
            ]
        )
    )
    attn_got, in_pieces[1], in_pieces[3] = tie(attn_got, in_pieces[1], in_pieces[3])
    attn_mid = [low_sum(attn_parts[0][i], attn_got[i]) for i in (0, 1)]
    attn_got = across_swap(attn_mid[1])
    ffn_low = scatter_tp_end(ffn_near)
    ffn_got = across_swap(ffn_low)
    attn_got, out_foreign, out_middle = tie(attn_got, out_foreign, out_middle)
    attn_near = scatter_tp_start(low_sum(attn_mid[0], attn_got))
    layer_output = assemble(
        assemble_late_kernel, place, out_pieces, (out_middle, out_foreign), seqs, bf16
    )
    layer_output, in_pieces[2], attn_near[3], ffn_got = tie(
        layer_output, in_pieces[2], attn_near[3], ffn_got
    )
    in_halves = core_swap(jnp.stack([piece[block:] for piece in in_pieces]))
    input_grad = assemble(assemble_kernel, place, in_pieces, (in_halves,), seqs, f32)
    up_grad, down_grad = finish(
        finish_ffn_kernel,
        place,
        (ffn_low, ffn_got, core_swap(ffn_low), core_swap(ffn_got)),
        ((cut, 2 * cut), (2 * cut, cut)),
        "finish_ffn",
    )
    attn_low = scatter_tp_end(attn_near)
    attn_got, input_grad = tie(across_swap(attn_low), input_grad)
    finished = finish(
        finish_attn_kernel,
        place,
        (attn_low, attn_got, core_swap(attn_low), core_swap(attn_got)),
        ((heads, depth),) * 4 + ((width,),) * 6 + ((2 * cut,), (heads,), (heads,)),
        "finish_attn",
        [pltpu.VMEM((2, 2, 8, depth), f32)],
    )
    weight_grads, row_sums = finished[:4], finished[4:10]
    up_bias_grad, query_bias_grad, value_bias_grad = finished[10:]
    return (
        layer_output,
        input_grad,
        weight_grads[0].T,
        query_bias_grad,
        weight_grads[1].T,
        weight_grads[2].T,
        value_bias_grad,
        weight_grads[3],
        row_sums[0],
        row_sums[1],
        row_sums[2],
        up_grad,
        up_bias_grad,
        down_grad,
        row_sums[3],
        row_sums[4],
        row_sums[5],
    )


def pick_plan(mesh):
    shape = dict(mesh.shape)

    def plan(layer_input, segment_ids, *others):
        seqs, block, _ = layer_input.shape
        fits = (
            (shape["shard"], shape["ctx"], shape["tp"]) == (2, 4, 4)
            and seqs == 6
            and segment_ids.shape[1] == 4 * block
            and block == 2 * QBLOCK
        )
        chosen = span_shards if fits else general_shards
        return chosen(layer_input, segment_ids, *others)

    return plan


def solution(mesh):
    return jax.shard_map(
        pick_plan(mesh),
        mesh=mesh,
        in_specs=(
            P("shard", "ctx", None),
            P("shard", None),
            P("shard", "tp"),
            P("tp"),
            P("shard", "tp"),
            P("shard", "tp"),
            P("tp"),
            P("tp", "shard"),
            P(),
            P(),
            P(),
            P("shard", "tp"),
            P("tp"),
            P("tp", "shard"),
            P(),
            P(),
            P(),
            P("shard", "ctx", None),
        ),
        out_specs=(
            P("shard", "ctx", None),
            P("shard", "ctx", None),
            P("shard", "tp"),
            P("tp"),
            P("shard", "tp"),
            P("shard", "tp"),
            P("tp"),
            P("tp", "shard"),
            P(),
            P(),
            P(),
            P("shard", "tp"),
            P("tp"),
            P("tp", "shard"),
            P(),
            P(),
            P(),
        ),
        check_vma=False,
    )
```

```python
from functools import partial
import math

import jax
import jax.numpy as jnp
from jax import lax
from jax.experimental import pallas as pl
from jax.experimental.pallas import tpu as pltpu
from jax.sharding import PartitionSpec as P

HEAD_DIM = 64


eps_norm = 1e-12
far_below = -1e30


def contract_rows(left, right):
    return lax.dot_general(
        left, right, (((0,), (0,)), ((), ())), preferred_element_type=jnp.float32
    )


def contract_last(left, right):
    return lax.dot_general(
        left, right, (((1,), (1,)), ((), ())), preferred_element_type=jnp.float32
    )


def norm_forward(resid, norm_gain, norm_shift):
    center = resid - jnp.mean(resid, axis=-1, keepdims=True)
    inv_std = lax.rsqrt(jnp.mean(center * center, axis=-1, keepdims=True) + eps_norm)
    normed = center * inv_std
    return (normed * norm_gain + norm_shift, normed, inv_std)


def norm_backward(grad_out, normed, inv_std, norm_gain):
    grad_normed = grad_out * norm_gain
    grad_in = inv_std * (
        grad_normed
        - jnp.mean(grad_normed, axis=-1, keepdims=True)
        - normed * jnp.mean(grad_normed * normed, axis=-1, keepdims=True)
    )
    return (grad_in, jnp.sum(grad_out * normed, axis=0), jnp.sum(grad_out, axis=0))


def split_heads(matrix):
    return matrix.reshape(matrix.shape[0], matrix.shape[1] // HEAD_DIM, HEAD_DIM)


def scores_of(queries, keys_all, query_docs, key_docs):
    scores = jnp.einsum(
        "qhd,khd->hqk",
        split_heads(queries),
        split_heads(keys_all),
        preferred_element_type=jnp.float32,
    )
    same_doc = (query_docs[:, None] == key_docs[None, :])[None]
    return jnp.where(same_doc, scores, jnp.float32(far_below))


def attend_forward(item):
    queries, keys_all, values_all, query_docs, key_docs = item
    scores = scores_of(queries, keys_all, query_docs, key_docs)
    top_score = jnp.max(scores, axis=-1, keepdims=True)
    expo = jnp.exp(scores - top_score)
    total = jnp.sum(expo, axis=-1, keepdims=True)
    probs = (expo / total).astype(jnp.bfloat16)
    mixed = jnp.einsum(
        "hqk,khd->qhd", probs, split_heads(values_all), preferred_element_type=jnp.float32
    )
    return (
        mixed.reshape(queries.shape).astype(jnp.bfloat16),
        (top_score + jnp.log(total))[:, :, 0],
    )


def score_grads(queries, keys_all, values_all, query_docs, key_docs, grad_mixed, log_total):
    scores = scores_of(queries, keys_all, query_docs, key_docs)
    probs = jnp.exp(scores - log_total[:, :, None])
    grad_probs = jnp.einsum(
        "qhd,khd->hqk",
        split_heads(grad_mixed),
        split_heads(values_all),
        preferred_element_type=jnp.float32,
    )
    inner = jnp.sum(grad_probs * probs, axis=-1)
    grad_scores = (probs * (grad_probs - inner[:, :, None])).astype(jnp.bfloat16)
    return (probs, grad_scores, inner)


def attend_backward(item):
    queries, keys_all, values_all, query_docs, key_docs, grad_mixed, log_total = item
    probs, grad_scores, inner = score_grads(
        queries, keys_all, values_all, query_docs, key_docs, grad_mixed, log_total
    )
    grad_heads = split_heads(grad_mixed)
    grad_queries = jnp.einsum(
        "hqk,khd->qhd", grad_scores, split_heads(keys_all), preferred_element_type=jnp.float32
    )
    grad_keys = jnp.einsum(
        "hqk,qhd->khd", grad_scores, split_heads(queries), preferred_element_type=jnp.float32
    )
    grad_values = jnp.einsum(
        "hqk,qhd->khd", probs.astype(jnp.bfloat16), grad_heads, preferred_element_type=jnp.float32
    )
    return (
        grad_queries.reshape(queries.shape).astype(jnp.bfloat16),
        grad_keys.reshape(keys_all.shape),
        grad_values.reshape(values_all.shape),
    )


def general_shards(
    layer_input,
    segment_ids,
    query_proj,
    query_bias,
    key_proj,
    value_proj,
    value_bias,
    out_proj,
    out_bias,
    attn_gain,
    attn_shift,
    up_proj,
    up_bias,
    down_proj,
    down_bias,
    ffn_gain,
    ffn_shift,
    out_cotangent,
):
    seq_here, ctx_rows, width = layer_input.shape
    scale = 1.0 / math.sqrt(HEAD_DIM)
    full_query, full_key, full_value, full_out, full_up, full_down = (
        lax.all_gather(query_proj, "shard", axis=0, tiled=True),
        lax.all_gather(key_proj, "shard", axis=0, tiled=True),
        lax.all_gather(value_proj, "shard", axis=0, tiled=True),
        lax.all_gather(out_proj, "shard", axis=1, tiled=True),
        lax.all_gather(up_proj, "shard", axis=0, tiled=True),
        lax.all_gather(down_proj, "shard", axis=1, tiled=True),
    )
    local_width = full_query.shape[1]
    joined_proj = jnp.concatenate([full_query, full_key, full_value], axis=1)
    rows_in = layer_input.reshape(seq_here * ctx_rows, width)
    projected = jnp.dot(rows_in, joined_proj, preferred_element_type=jnp.float32)
    shaped = (seq_here, ctx_rows, local_width)
    queries = (
        ((projected[:, :local_width] + query_bias) * scale).astype(jnp.bfloat16).reshape(shaped)
    )
    keys_mine = projected[:, local_width : 2 * local_width].astype(jnp.bfloat16).reshape(shaped)
    values_mine = (
        (projected[:, 2 * local_width :] + value_bias).astype(jnp.bfloat16).reshape(shaped)
    )
    keys_all, values_all = (
        lax.all_gather(keys_mine, "ctx", axis=1, tiled=True),
        lax.all_gather(values_mine, "ctx", axis=1, tiled=True),
    )
    query_docs = lax.dynamic_slice_in_dim(
        segment_ids, lax.axis_index("ctx") * ctx_rows, ctx_rows, 1
    )
    mixed, log_total = lax.map(
        attend_forward, (queries, keys_all, values_all, query_docs, segment_ids)
    )
    mixed_rows = mixed.reshape(-1, local_width)
    attended = (
        lax.psum(
            jnp.dot(mixed_rows, full_out, preferred_element_type=jnp.float32).astype(jnp.bfloat16),
            "tp",
        ).astype(jnp.float32)
        + out_bias
    )
    hidden, normed_one, inv_one = norm_forward(
        rows_in.astype(jnp.float32) + attended, attn_gain, attn_shift
    )
    hidden_low = hidden.astype(jnp.bfloat16)
    pre_act = jnp.dot(hidden_low, full_up, preferred_element_type=jnp.float32) + up_bias
    acts_low = jax.nn.gelu(pre_act, approximate=False).astype(jnp.bfloat16)
    ffn_out = (
        lax.psum(
            jnp.dot(acts_low, full_down, preferred_element_type=jnp.float32).astype(jnp.bfloat16),
            "tp",
        ).astype(jnp.float32)
        + down_bias
    )
    output_rows, normed_two, inv_two = norm_forward(hidden + ffn_out, ffn_gain, ffn_shift)
    layer_output = output_rows.astype(jnp.bfloat16).reshape(layer_input.shape)
    grad_out = out_cotangent.reshape(-1, width).astype(jnp.float32)
    grad_two, ffn_gain_grad, ffn_shift_grad = norm_backward(grad_out, normed_two, inv_two, ffn_gain)
    grad_ffn = grad_two.astype(jnp.bfloat16)
    down_bias_grad = jnp.sum(grad_ffn, axis=0, dtype=jnp.float32)
    down_part = contract_rows(acts_low, grad_ffn)
    grad_acts = contract_last(grad_ffn, full_down)
    _, gelu_back = jax.vjp(partial(jax.nn.gelu, approximate=False), pre_act)
    grad_pre = gelu_back(grad_acts)[0].astype(jnp.bfloat16)
    up_bias_grad = jnp.sum(grad_pre, axis=0, dtype=jnp.float32)
    up_part = contract_rows(hidden_low, grad_pre)
    grad_hidden = grad_two + lax.psum(
        contract_last(grad_pre, full_up).astype(jnp.bfloat16), "tp"
    ).astype(jnp.float32)
    grad_one, attn_gain_grad, attn_shift_grad = norm_backward(
        grad_hidden, normed_one, inv_one, attn_gain
    )
    grad_attn = grad_one.astype(jnp.bfloat16)
    out_bias_grad = jnp.sum(grad_attn, axis=0, dtype=jnp.float32)
    out_part = contract_rows(mixed_rows, grad_attn)
    grad_mixed = contract_last(grad_attn, full_out).astype(jnp.bfloat16).reshape(shaped)
    keys_back, values_back = (
        lax.all_gather(keys_mine, "ctx", axis=1, tiled=True),
        lax.all_gather(values_mine, "ctx", axis=1, tiled=True),
    )
    grad_queries, grad_keys_all, grad_values_all = lax.map(
        attend_backward,
        (queries, keys_back, values_back, query_docs, segment_ids, grad_mixed, log_total),
    )
    grad_keys, grad_values = (
        lax.psum_scatter(
            grad_keys_all.astype(jnp.bfloat16), "ctx", scatter_dimension=1, tiled=True
        ).astype(jnp.float32),
        lax.psum_scatter(
            grad_values_all.astype(jnp.bfloat16), "ctx", scatter_dimension=1, tiled=True
        ).astype(jnp.float32),
    )
    grad_keys = grad_keys.astype(jnp.bfloat16).reshape(-1, local_width)
    grad_values = grad_values.astype(jnp.bfloat16).reshape(-1, local_width)
    grad_scaled = grad_queries.reshape(-1, local_width) * jnp.bfloat16(scale)
    grad_joined = jnp.concatenate([grad_scaled, grad_keys, grad_values], axis=1)
    joined_part = contract_rows(rows_in, grad_joined)
    query_part = joined_part[:, :local_width]
    key_part = joined_part[:, local_width : 2 * local_width]
    value_part = joined_part[:, 2 * local_width :]
    query_bias_grad = jnp.sum(grad_scaled, axis=0, dtype=jnp.float32)
    value_bias_grad = jnp.sum(grad_values, axis=0, dtype=jnp.float32)
    back_terms = contract_last(grad_joined, joined_proj)
    input_grad = (
        grad_one + lax.psum(back_terms.astype(jnp.bfloat16), "tp").astype(jnp.float32)
    ).reshape(layer_input.shape)
    sliced = (
        lax.psum_scatter(
            query_part.astype(jnp.bfloat16), "shard", scatter_dimension=0, tiled=True
        ).astype(jnp.float32),
        lax.psum_scatter(
            key_part.astype(jnp.bfloat16), "shard", scatter_dimension=0, tiled=True
        ).astype(jnp.float32),
        lax.psum_scatter(
            value_part.astype(jnp.bfloat16), "shard", scatter_dimension=0, tiled=True
        ).astype(jnp.float32),
        lax.psum_scatter(
            out_part.astype(jnp.bfloat16), "shard", scatter_dimension=1, tiled=True
        ).astype(jnp.float32),
        lax.psum_scatter(
            up_part.astype(jnp.bfloat16), "shard", scatter_dimension=0, tiled=True
        ).astype(jnp.float32),
        lax.psum_scatter(
            down_part.astype(jnp.bfloat16), "shard", scatter_dimension=1, tiled=True
        ).astype(jnp.float32),
    )
    reduced = (
        lax.psum(sliced[0].astype(jnp.bfloat16), "ctx").astype(jnp.float32),
        lax.psum(sliced[1].astype(jnp.bfloat16), "ctx").astype(jnp.float32),
        lax.psum(sliced[2].astype(jnp.bfloat16), "ctx").astype(jnp.float32),
        lax.psum(sliced[3].astype(jnp.bfloat16), "ctx").astype(jnp.float32),
        lax.psum(sliced[4].astype(jnp.bfloat16), "ctx").astype(jnp.float32),
        lax.psum(sliced[5].astype(jnp.bfloat16), "ctx").astype(jnp.float32),
    )
    small = lax.psum(
        (
            query_bias_grad,
            value_bias_grad,
            out_bias_grad,
            attn_gain_grad,
            attn_shift_grad,
            up_bias_grad,
            down_bias_grad,
            ffn_gain_grad,
            ffn_shift_grad,
        ),
        ("shard", "ctx"),
    )
    return (
        layer_output,
        input_grad,
        reduced[0],
        small[0],
        reduced[1],
        reduced[2],
        small[1],
        reduced[3],
        small[2],
        small[3],
        small[4],
        reduced[4],
        small[5],
        reduced[5],
        small[6],
        small[7],
        small[8],
    )


PAIR = 2 * HEAD_DIM
QBLOCK = 128


def dot32(left, right):
    return jnp.dot(left, right, preferred_element_type=jnp.float32)


def stack_heads(rows):
    lane = lax.broadcasted_iota(jnp.int32, rows.shape, 1)
    nought = jnp.zeros_like(rows)
    return jnp.concatenate(
        [jnp.where(lane < HEAD_DIM, rows, nought), jnp.where(lane >= HEAD_DIM, rows, nought)], axis=0
    )


def unstack_heads(tall):
    count = tall.shape[0] // 2
    lane = lax.broadcasted_iota(jnp.int32, (count, tall.shape[1]), 1)
    return jnp.where(lane < HEAD_DIM, tall[:count], tall[count:])


def masked_scores(queries, keys, same):
    scores = contract_last(queries, keys)
    return jnp.where(jnp.concatenate([same, same], axis=0), scores, jnp.float32(far_below))


def attend_kernel(span, q_ref, k_ref, v_ref, kd_ref, qd_ref, *refs):
    o_ref, l_ref = refs[-2:]
    here = pl.ds(pl.multiple_of(pl.program_id(1) * QBLOCK, QBLOCK), span)
    same = qd_ref[:, :1] == kd_ref[:, here]

    def one_pair(cols):
        scores = masked_scores(stack_heads(q_ref[:, cols]), k_ref[here, cols], same)
        top = jnp.max(scores, axis=1, keepdims=True)
        expo = jnp.exp(scores - top)
        total = jnp.sum(expo, axis=1, keepdims=True)
        mixed = dot32(expo.astype(jnp.bfloat16), v_ref[here, cols]) * (1.0 / total)
        o_ref[:, cols] = unstack_heads(mixed).astype(jnp.bfloat16)
        log = top + jnp.log(total)
        return log[:QBLOCK], log[QBLOCK:]

    pairs = q_ref.shape[1] // PAIR
    if len(refs) > 2:
        logs = [log for p in range(pairs) for log in one_pair(slice(p * PAIR, (p + 1) * PAIR))]
        l_ref[0] = jnp.concatenate(logs, axis=1)
    else:
        lane = lax.broadcasted_iota(jnp.int32, l_ref.shape[1:], 1)

        @pl.loop(0, pairs)
        def _(pair):
            first, second = one_pair(pl.ds(pl.multiple_of(pair * PAIR, PAIR), PAIR))
            logs = jnp.where(lane == 2 * pair, first, l_ref[0])
            l_ref[0] = jnp.where(lane == 2 * pair + 1, second, logs)


def attend_back_kernel(
    span, short, plan_ref, q_ref, k_ref, v_ref, kd_ref, qd_ref, do_ref, l_ref, *refs
):
    dq_ref, dk_ref, dv_ref, dk_acc, dv_acc = refs
    step = pl.program_id(1)

    @pl.when(step == 0)
    def _():
        dk_acc[...] = jnp.zeros_like(dk_acc)
        dv_acc[...] = jnp.zeros_like(dv_acc)

    logs = l_ref[0]

    def one_pair(here, same, cols, log):
        keys = k_ref[here, cols]
        queries, grads = stack_heads(q_ref[:, cols]), stack_heads(do_ref[:, cols])
        probs = jnp.exp(masked_scores(queries, keys, same) - log)
        grad_probs = contract_last(grads, v_ref[here, cols])
        inner = jnp.sum(grad_probs * probs, axis=1, keepdims=True)
        grad_scores = (probs * (grad_probs - inner)).astype(jnp.bfloat16)
        grad_queries = unstack_heads(dot32(grad_scores, keys))
        dq_ref[:, cols] = (grad_queries * (1.0 / math.sqrt(HEAD_DIM))).astype(jnp.bfloat16)
        dk_acc[here, cols] += contract_rows(grad_scores, queries)
        dv_acc[here, cols] += contract_rows(probs.astype(jnp.bfloat16), grads)

    pairs = q_ref.shape[1] // PAIR
    fits = plan_ref[1, step] == 1

    @pl.when(fits)
    def _():
        here = pl.ds(pl.multiple_of(plan_ref[0, step], QBLOCK), short)
        same = qd_ref[:, :1] == kd_ref[:, here]
        for pair in range(pairs):
            log = [logs[:, 2 * pair + i : 2 * pair + i + 1] for i in (0, 1)]
            one_pair(
                here, same, slice(pair * PAIR, (pair + 1) * PAIR), jnp.concatenate(log, axis=0)
            )

    @pl.when(jnp.logical_not(fits))
    def _():
        here = pl.ds(pl.multiple_of(step * QBLOCK, QBLOCK), span)
        same = qd_ref[:, :1] == kd_ref[:, here]
        lane = lax.broadcasted_iota(jnp.int32, logs.shape, 1)

        @pl.loop(0, pairs)
        def _(pair):
            log = [
                jnp.sum(jnp.where(lane == 2 * pair + i, logs, 0.0), axis=1, keepdims=True)
                for i in (0, 1)
            ]
            cols = pl.ds(pl.multiple_of(pair * PAIR, PAIR), PAIR)
            one_pair(here, same, cols, jnp.concatenate(log, axis=0))

    @pl.when(step == pl.num_programs(1) - 1)
    def _():
        dk_ref[...] = dk_acc[...].astype(jnp.bfloat16)
        dv_ref[...] = dv_acc[...].astype(jnp.bfloat16)


def attention_specs(window, cols, at):
    rows = pl.BlockSpec((QBLOCK, cols), lambda h, i, *_: (i, at + h))
    keys = pl.BlockSpec((window, cols), lambda h, i, *_: (0, at + h))
    key_docs = pl.BlockSpec((1, window), lambda h, i, *_: (0, 0))
    query_docs = pl.BlockSpec((QBLOCK, QBLOCK), lambda h, i, *_: (i, 0))
    logs = pl.BlockSpec((1, QBLOCK, cols // HEAD_DIM), lambda h, i, *_: (at + h, i, 0))
    return rows, keys, key_docs, query_docs, logs


def attend(queries, keys, values, key_docs, query_docs, reach, half, prior=()):
    count, width = queries.shape
    window, cols = keys.shape[0], width // 2
    span = QBLOCK + 2 * reach
    rows, key_spec, kd_spec, qd_spec, logs = attention_specs(window, cols, half)
    return pl.pallas_call(
        partial(attend_kernel, span),
        grid=(1, count // QBLOCK),
        in_specs=[rows, key_spec, key_spec, kd_spec, qd_spec]
        + [pl.BlockSpec(memory_space=pl.ANY)] * len(prior),
        out_specs=[rows, logs],
        out_shape=[
            jax.ShapeDtypeStruct((count, width), jnp.bfloat16),
            jax.ShapeDtypeStruct((2, count, cols // HEAD_DIM), jnp.float32),
        ],
        input_output_aliases={5 + i: i for i in range(len(prior))},
        compiler_params=pltpu.CompilerParams(vmem_limit_bytes=16 << 20),
        cost_estimate=pl.CostEstimate(
            flops=16 * count * span * cols, bytes_accessed=4 << 20, transcendentals=0
        ),
        name="attend",
    )(queries, keys, values, key_docs, query_docs, *prior)


def attend_back(plan, queries, keys, values, key_docs, query_docs, reach, grads, logs_in):
    count, width = queries.shape
    window, cols = keys.shape[0], width // 2
    span = QBLOCK + 2 * reach
    rows, key_spec, kd_spec, qd_spec, logs = attention_specs(window, cols, 0)
    return pl.pallas_call(
        partial(attend_back_kernel, span, short_span(reach)),
        grid_spec=pltpu.PrefetchScalarGridSpec(
            num_scalar_prefetch=1,
            grid=(2, count // QBLOCK),
            in_specs=[rows, key_spec, key_spec, kd_spec, qd_spec, rows, logs],
            out_specs=[rows, key_spec, key_spec],
            scratch_shapes=[pltpu.VMEM((window, cols), jnp.float32)] * 2,
        ),
        out_shape=[
            jax.ShapeDtypeStruct((count, width), jnp.bfloat16),
            jax.ShapeDtypeStruct((window, width), jnp.bfloat16),
            jax.ShapeDtypeStruct((window, width), jnp.bfloat16),
        ],
        compiler_params=pltpu.CompilerParams(vmem_limit_bytes=24 << 20),
        cost_estimate=pl.CostEstimate(
            flops=40 * count * span * width, bytes_accessed=12 << 20, transcendentals=0
        ),
        name="attend_back",
    )(plan, queries, keys, values, key_docs, query_docs, grads, logs_in)


def short_span(reach):
    return (QBLOCK + 2 * reach) * 2 // 3 // QBLOCK * QBLOCK


def key_plan(docs, reach, count):
    window, short = docs.shape[0], short_span(reach)
    rows = docs[reach : reach + count].reshape(-1, QBLOCK)
    at = jnp.arange(window, dtype=jnp.int32)
    low = jnp.min(jnp.where(docs == rows[:, :1], at, window), axis=1)
    high = jnp.max(jnp.where(docs == rows[:, -1:], at + 1, 0), axis=1)
    start = jnp.minimum(low // QBLOCK * QBLOCK, window - short)
    return jnp.stack([start, (high - start <= short).astype(jnp.int32)])


def half_cols(position, half):
    return pl.ds(pl.multiple_of(position * half, half), half)


def add_or_set(first, ref, index, terms):
    @pl.when(first)
    def _():
        ref[index] = terms

    @pl.when(jnp.logical_not(first))
    def _():
        ref[index] += terms


def ffn_kernel(first_block, place_ref, h_ref, other_h_ref, w_ref, bias_ref, *refs):
    half = w_ref.shape[3]
    count = h_ref.shape[0]
    near, far = half_cols(place_ref[1], half), half_cols(1 - place_ref[1], half)
    hb_near = refs[-1]
    for part, source in enumerate((h_ref, other_h_ref)):
        rows = slice(part * count, (part + 1) * count)
        hb_near[rows, :half] = source[:, near]
        hb_near[rows, half:] = source[:, far]

    def chunk(block, rows, acts_ref, slope_ref):
        up = w_ref[block, :, :half].reshape(2 * half, half)
        pre_act = dot32(hb_near[rows], up) + bias_ref[block]
        cdf = 0.5 * (1.0 + lax.erf(pre_act * math.sqrt(0.5)))
        bell = jnp.exp(-0.5 * pre_act * pre_act) * (1.0 / math.sqrt(2 * math.pi))
        acts = (pre_act * cdf).astype(jnp.bfloat16)
        cols = pl.ds(pl.multiple_of(block * half, half), half)
        acts_ref[rows, cols] = acts
        slope_ref[rows, cols] = (cdf + pre_act * bell).astype(jnp.bfloat16)
        return dot32(acts, w_ref[block, 0, half:]), dot32(acts, w_ref[block, 1, half:])

    blocks = w_ref.shape[0]
    if first_block:
        base_ref, _, _, acts_ref, slope_ref, own_ref, other_ref = refs[:-1]
        for part, to in enumerate((own_ref, other_ref)):
            rows = slice(part * count, (part + 1) * count)
            terms = chunk(blocks - 1, rows, acts_ref, slope_ref)
            for y, cols in enumerate((near, far)):
                base = base_ref[rows, y * half : (y + 1) * half]
                to[:, cols] = (base + terms[y]).astype(to.dtype)
    else:
        acts_ref, slope_ref, total = refs[:-1]
        total[...] = jnp.zeros_like(total)

        @pl.loop(0, 2 * (blocks - 1))
        def _(i):
            rows = pl.ds(pl.multiple_of((i & 1) * count, count), count)
            one, two = chunk(i >> 1, rows, acts_ref, slope_ref)
            total[rows, :half] += one
            total[rows, half:] += two


def ffn_back_kernel(
    place_ref,
    dz_ref,
    other_dz_ref,
    h_ref,
    other_h_ref,
    acts_ref,
    slope_ref,
    w_ref,
    own_ref,
    other_ref,
    up_keep,
    up_give,
    down_keep,
    down_give,
    sums_ref,
    total,
    grad_pre,
    dz_near,
    rows_t,
    up_both,
    down_both,
    sums,
):
    step = pl.program_id(0)
    half = w_ref.shape[3]
    quarter = half // 2
    count = own_ref.shape[0]
    near, far = half_cols(place_ref[1], half), half_cols(1 - place_ref[1], half)
    first, second = slice(0, half), slice(half, 2 * half)

    @pl.when(step == 0)
    def _():
        total[...] = jnp.zeros_like(total)
        for to, cols in ((first, near), (second, far)):
            dz_near[:count, to] = dz_ref[:, cols]
            dz_near[count:, to] = other_dz_ref[:, cols]
            rows_t[to, :count] = h_ref[:, cols].T
            rows_t[to, count:] = other_h_ref[:, cols].T

    for k, hid in enumerate((first, second)):
        for y, to in enumerate((first, second)):
            up_both[to, hid] = w_ref[k, y, :half]
            down_both[hid, to] = w_ref[k, y, half:]
    sums[...] = jnp.zeros_like(sums)

    @pl.loop(0, 2)
    def _(part):
        rows = pl.ds(pl.multiple_of(part * count, count), count)
        grad_acts = contract_last(dz_near[rows], down_both[...])
        low = (slope_ref[rows].astype(jnp.float32) * grad_acts).astype(jnp.bfloat16)
        grad_pre[rows] = low
        sums[...] += row_sum(low.astype(jnp.float32))
        total[rows] += contract_last(low, up_both[...])

    tps = [(place_ref[2] + 4 - jnp.where(step == 0, k, 3 - k)) & 3 for k in (0, 1)]
    for tp, hid in zip(tps, (first, second)):
        sums_ref[tp] = sums[:, hid]
    acts_t = acts_ref[...].T
    for side, cols in enumerate((first, second)):
        up_grad = dot32(rows_t[cols], grad_pre[...]).astype(jnp.bfloat16)
        down_grad = dot32(acts_t, dz_near[:, cols]).astype(jnp.bfloat16)
        down_to = down_give if side else down_keep
        for across in (0, 1):

            @pl.when(place_ref[3] == across)
            def _():
                for k in (0, 1):
                    tp = tps[k]
                    hid = slice(k * half, (k + 1) * half)
                    for x in (0, 1):
                        part = slice((x ^ across) * quarter, (x ^ across) * quarter + quarter)
                        down_rows = slice(k * half + part.start, k * half + part.stop)
                        (up_give if x else up_keep)[side, tp] = up_grad[part, hid]
                        down_to[x, tp] = down_grad[down_rows]

    @pl.when(step == pl.num_programs(0) - 1)
    def _():
        own_ref[:, near] = total[:count, first].astype(jnp.bfloat16)
        own_ref[:, far] = total[:count, second].astype(jnp.bfloat16)
        other_ref[:, near] = total[count:, first].astype(jnp.bfloat16)
        other_ref[:, far] = total[count:, second].astype(jnp.bfloat16)


def once(shape):
    return pl.BlockSpec(
        shape, lambda *_: (0,) * len(shape), pipeline_mode=pl.Buffered(buffer_count=1)
    )


def whole(shape):
    return pl.BlockSpec(shape, lambda *_: (0,) * len(shape))


def ffn(place, rows, other_rows, weights, bias, prior=()):
    count, width = rows.shape
    both = 2 * count
    tps, shards, _, half = weights.shape
    vmem = pl.BlockSpec(memory_space=pltpu.VMEM)
    low = jax.ShapeDtypeStruct((count, width), jnp.bfloat16)
    hidden = jax.ShapeDtypeStruct((both, tps * half), jnp.bfloat16)
    last = [low, low] if prior else [jax.ShapeDtypeStruct((both, width), jnp.float32)]
    steps = 1 if prior else tps - 1
    return pl.pallas_call(
        partial(ffn_kernel, bool(prior)),
        in_specs=[pl.BlockSpec(memory_space=pltpu.SMEM)] + [vmem] * (4 + len(prior)),
        out_specs=[vmem] * (2 + len(last)),
        out_shape=[hidden, hidden] + last,
        scratch_shapes=[pltpu.VMEM((both, width), jnp.bfloat16)],
        input_output_aliases={6: 0, 7: 1} if prior else {},
        compiler_params=pltpu.CompilerParams(vmem_limit_bytes=16 << 20),
        cost_estimate=pl.CostEstimate(
            flops=12 * both * width * steps * half, bytes_accessed=3 * steps << 20, transcendentals=0
        ),
        name="ffn",
    )(place, rows, other_rows, weights, bias, *prior)


def ffn_back(place, grads, other_grads, rows, other_rows, acts, slope, weights):
    count, width = rows.shape
    both = 2 * count
    tps, shards, _, half = weights.shape
    block = pl.BlockSpec((both, 2 * half), lambda i, _: (0, i))
    parts = (2, tps, half // 2, half)
    low = jax.ShapeDtypeStruct((count, width), jnp.bfloat16)
    return pl.pallas_call(
        ffn_back_kernel,
        grid_spec=pltpu.PrefetchScalarGridSpec(
            num_scalar_prefetch=1,
            grid=(tps // 2,),
            in_specs=[
                *[once((count, width))] * 4,
                block,
                block,
                pl.BlockSpec((2, shards, 2 * half, half), lambda i, _: (i, 0, 0, 0)),
            ],
            out_specs=[
                whole((count, width)),
                whole((count, width)),
                *[whole(parts)] * 4,
                whole((tps, 1, half)),
            ],
            scratch_shapes=[
                pltpu.VMEM((both, width), jnp.float32),
                pltpu.VMEM((both, 2 * half), jnp.bfloat16),
                pltpu.VMEM((both, width), jnp.bfloat16),
                pltpu.VMEM((width, both), jnp.bfloat16),
                pltpu.VMEM((width, 2 * half), jnp.bfloat16),
                pltpu.VMEM((2 * half, width), jnp.bfloat16),
                pltpu.VMEM((1, 2 * half), jnp.float32),
            ],
        ),
        out_shape=[
            low,
            low,
            *[jax.ShapeDtypeStruct(parts, jnp.bfloat16)] * 4,
            jax.ShapeDtypeStruct((tps, 1, half), jnp.float32),
        ],
        compiler_params=pltpu.CompilerParams(vmem_limit_bytes=30 << 20),
        cost_estimate=pl.CostEstimate(
            flops=12 * both * width * tps * half, bytes_accessed=20 << 20, transcendentals=0
        ),
        name="ffn_back",
    )(place, grads, other_grads, rows, other_rows, acts, slope, weights)


def project_kernel(
    place_ref, w_mine, w_other, x_mine, x_other, bias_ref, q_ref, k_ref, v_ref, x_ref, wt
):
    core, shard, tp, across, start = (place_ref[i] for i in range(5))
    depth = w_mine.shape[3]
    width = x_ref.shape[1]
    part = width // 8
    length = 4 * x_mine.shape[2]
    reach = length // 2
    for c, source in enumerate((w_mine, w_other)):
        for y in (0, 1):
            cols = half_cols(shard + y - 2 * shard * y, depth)
            for k in range(4):
                row = ((tp + 4 - k) & 3) * 2 + core + c - 2 * core * c
                rows = pl.ds(pl.multiple_of(row * part, part), part)
                for m in range(3):
                    wt[m, rows, cols] = source[y, k, m * part : (m + 1) * part]
    for i in range(x_ref.shape[0] // QBLOCK):
        row = start - reach + i * QBLOCK
        inside = jnp.logical_and(row >= 0, row < 2 * length)
        at = jnp.where(inside, row, 0) // QBLOCK
        seq, block, piece = at // 8, (at // 2) & 3, at & 1
        here = jnp.where((block >> 1) == across, 0, 1)
        rows = pl.ds(pl.multiple_of(piece * QBLOCK, QBLOCK), QBLOCK)
        mine, other = x_mine[here, seq, rows], x_other[here, seq, rows]
        found = jnp.where((block & 1) == core, mine, other)
        x_ref[i * QBLOCK : (i + 1) * QBLOCK] = jnp.where(inside, found, jnp.zeros_like(found))
    count = q_ref.shape[0]
    scaled = contract_last(x_ref[reach : reach + count], wt[0]) + bias_ref[0:1]
    q_ref[...] = (scaled * (1.0 / math.sqrt(HEAD_DIM))).astype(jnp.bfloat16)
    chunk = x_ref.shape[0] // 4

    @pl.loop(0, 4)
    def _(step):
        rows = pl.ds(pl.multiple_of(step * chunk, 32), chunk)
        k_ref[rows] = contract_last(x_ref[rows], wt[1]).astype(jnp.bfloat16)
        v_ref[rows] = (contract_last(x_ref[rows], wt[2]) + bias_ref[1:2]).astype(jnp.bfloat16)


def project(place, w_mine, w_other, x_mine, x_other, biases, count, window):
    width = x_mine.shape[-1]
    return pl.pallas_call(
        project_kernel,
        in_specs=[pl.BlockSpec(memory_space=pltpu.SMEM)]
        + [pl.BlockSpec(memory_space=pltpu.VMEM)] * 5,
        out_specs=[pl.BlockSpec(memory_space=pltpu.VMEM)] * 5,
        out_shape=[
            jax.ShapeDtypeStruct((count, width), jnp.bfloat16),
            jax.ShapeDtypeStruct((window, width), jnp.bfloat16),
            jax.ShapeDtypeStruct((window, width), jnp.bfloat16),
            jax.ShapeDtypeStruct((window, width), jnp.bfloat16),
            jax.ShapeDtypeStruct((3, width, width), jnp.bfloat16),
        ],
        compiler_params=pltpu.CompilerParams(vmem_limit_bytes=24 << 20),
        cost_estimate=pl.CostEstimate(
            flops=4 * window * width * width, bytes_accessed=16 << 20, transcendentals=0
        ),
        name="project",
    )(place, w_mine, w_other, x_mine, x_other, biases)


def norm_pieces(resid):
    center = resid - jnp.mean(resid, axis=-1, keepdims=True)
    inv_std = lax.rsqrt(jnp.mean(center * center, axis=-1, keepdims=True) + eps_norm)
    return center * inv_std, inv_std


def norm_pull(grad_out, normed, inv_std, gain):
    grad_normed = grad_out * gain
    return inv_std * (
        grad_normed
        - jnp.mean(grad_normed, axis=-1, keepdims=True)
        - normed * jnp.mean(grad_normed * normed, axis=-1, keepdims=True)
    )


def row_sum(rows):
    return jnp.sum(rows, axis=0, keepdims=True)


def attend_out_kernel(
    place_ref, o_ref, x_ref, w_mine, w_other, vec_ref, hb_ref, n_ref, i_ref, wo_ref
):
    core, shard, tp = (place_ref[i] for i in range(3))
    part, depth = w_mine.shape[2:]

    @pl.when(pl.program_id(0) == 0)
    def _():
        for c, source in enumerate((w_mine, w_other)):
            for y in (0, 1):
                cols = half_cols(shard + y - 2 * shard * y, depth)
                for k in range(4):
                    row = ((tp + 4 - k) & 3) * 2 + core + c - 2 * core * c
                    rows = pl.ds(pl.multiple_of(row * part, part), part)
                    wo_ref[rows, cols] = source[k, y]

    resid = x_ref[...].astype(jnp.float32) + dot32(o_ref[...], wo_ref[...]) + vec_ref[0:1]
    normed, inv_std = norm_pieces(resid)
    hb_ref[...] = (normed * vec_ref[1:2] + vec_ref[2:3]).astype(jnp.bfloat16)
    n_ref[...] = normed.astype(jnp.bfloat16)
    i_ref[...] = jnp.broadcast_to(inv_std, i_ref.shape)


def row_blocks(width):
    return pl.BlockSpec((QBLOCK, width), lambda i, *_: (i, 0))


def on_rows(kernel, count, in_specs, out_specs, out_shape, name, scalars=0):
    return pl.pallas_call(
        kernel,
        grid_spec=pltpu.PrefetchScalarGridSpec(
            num_scalar_prefetch=scalars,
            grid=(count // QBLOCK,),
            in_specs=in_specs,
            out_specs=out_specs,
        ),
        out_shape=out_shape,
        compiler_params=pltpu.CompilerParams(vmem_limit_bytes=12 << 20),
        cost_estimate=pl.CostEstimate(flops=1 << 28, bytes_accessed=6 << 20, transcendentals=0),
        name=name,
    )


def attend_out(place, mixed, window_rows, reach, w_mine, w_other, vectors):
    count, width = mixed.shape
    rows = row_blocks(width)
    low = jax.ShapeDtypeStruct((count, width), jnp.bfloat16)
    return on_rows(
        attend_out_kernel,
        count,
        [
            rows,
            pl.BlockSpec((QBLOCK, width), lambda i, *_: (i + reach // QBLOCK, 0)),
            whole(w_mine.shape),
            whole(w_other.shape),
            whole(vectors.shape),
        ],
        [rows, rows, row_blocks(QBLOCK), whole((width, width))],
        [
            low,
            low,
            jax.ShapeDtypeStruct((count, QBLOCK), jnp.float32),
            jax.ShapeDtypeStruct((width, width), jnp.bfloat16),
        ],
        "attend_out",
        1,
    )(place, mixed, window_rows, w_mine, w_other, vectors)


def norm_sums(sums_ref, rows):
    sums = jnp.concatenate([row_sum(row) for row in rows], axis=0)
    add_or_set(pl.program_id(0) == 0, sums_ref, slice(None), sums)


def cot_source(i, place_ref):
    core, tp, across = place_ref[0], place_ref[2], place_ref[3]
    odd = (across + tp) & 1
    block = 3 * core + i - 2 * odd
    block = jnp.where(block < 0, block + 6, block)
    far = block >> 1 == 2
    held = jnp.where(far, core == odd, core == (block >> 1))
    return jnp.where(far, 1, 0), block & 1, jnp.where(held, 1, 0)


def ffn_norm_kernel(
    place_ref, h_ref, own_ref, got_ref, g_ref, g_other_ref, vec_ref, y_ref, dz_ref, sums_ref
):
    resid = h_ref[...].astype(jnp.float32) + own_ref[...].astype(jnp.float32)
    resid += got_ref[...].astype(jnp.float32) + vec_ref[0:1]
    normed, inv_std = norm_pieces(resid)
    y_ref[...] = (normed * vec_ref[1:2] + vec_ref[2:3]).astype(jnp.bfloat16)
    held = cot_source(pl.program_id(0), place_ref)[2]
    grad_out = jnp.where(held == 1, g_ref[0], g_other_ref[0]).astype(jnp.float32)
    low = norm_pull(grad_out, normed, inv_std, vec_ref[1:2]).astype(jnp.bfloat16)
    dz_ref[...] = low
    norm_sums(sums_ref, (low.astype(jnp.float32), grad_out * normed, grad_out))


def ffn_norm(place, hidden, own, got, cots, other_cots, vectors):
    count, width = hidden.shape
    rows = row_blocks(width)
    cot = pl.BlockSpec((1, QBLOCK, width), lambda i, at: (*cot_source(i, at)[:2], 0))
    low = jax.ShapeDtypeStruct((count, width), jnp.bfloat16)
    return on_rows(
        ffn_norm_kernel,
        count,
        [rows, rows, rows, cot, cot, whole(vectors.shape)],
        [rows, rows, whole((3, width))],
        [low, low, jax.ShapeDtypeStruct((3, width), jnp.float32)],
        "ffn_norm",
        1,
    )(place, hidden, own, got, cots, other_cots, vectors)


def attend_norm_kernel(
    dz_ref, own_ref, got_ref, n_ref, i_ref, vec_ref, wo_ref, out_ref, da_ref, do_ref, sums_ref
):
    grad_out = dz_ref[...].astype(jnp.float32) + own_ref[...].astype(jnp.float32)
    grad_out += got_ref[...].astype(jnp.float32)
    normed = n_ref[...].astype(jnp.float32)
    grad = norm_pull(grad_out, normed, i_ref[:, :1], vec_ref[1:2])
    low = grad.astype(jnp.bfloat16)
    out_ref[...] = grad
    da_ref[...] = low
    do_ref[...] = contract_last(low, wo_ref[...]).astype(jnp.bfloat16)
    norm_sums(sums_ref, (low.astype(jnp.float32), grad_out * normed, grad_out))


def attend_norm(grads, own, got, normed, inv_std, vectors, weights):
    count, width = grads.shape
    rows = row_blocks(width)
    low = jax.ShapeDtypeStruct((count, width), jnp.bfloat16)
    return on_rows(
        attend_norm_kernel,
        count,
        [rows, rows, rows, rows, row_blocks(QBLOCK), whole(vectors.shape), whole(weights.shape)],
        [rows, rows, rows, whole((3, width))],
        [
            jax.ShapeDtypeStruct((count, width), jnp.float32),
            low,
            low,
            jax.ShapeDtypeStruct((3, width), jnp.float32),
        ],
        "attend_norm",
    )(grads, own, got, normed, inv_std, vectors, weights)


def attn_grads_kernel(
    place_ref, dq_ref, dk_ref, dv_ref, o_ref, da_ref, w_ref, attn_ref, ffn_ref, up_ref, *parts
):
    core, shard, across = place_ref[0], place_ref[1], place_ref[3]
    grad_ref = parts[2]
    depth = w_ref.shape[1] // 2
    part = depth // 4
    count = dq_ref.shape[0]
    reach = (w_ref.shape[0] - count) // 2
    sides = (
        (dq_ref, w_ref.at[reach : reach + count]),
        (dk_ref, w_ref),
        (dv_ref, w_ref),
        (o_ref, da_ref),
    )
    for m, (left, right) in enumerate(sides):
        grad_ref[...] = contract_rows(left[...], right[...]).astype(jnp.bfloat16)
        group = across if m < 2 else 1 - across
        rows = slice((m % 2) * part, (m % 2 + 1) * part)
        for z in (0, 1):
            for c in (0, 1):
                at = pl.ds(pl.multiple_of((2 * z + c + core - 2 * c * core) * part, part), part)
                parts[c][shard, group, z, rows] = grad_ref[at, :depth]
                parts[c][1 - shard, group, z, rows] = grad_ref[at, depth:]
    query_sum = row_sum(dq_ref[...].astype(jnp.float32))
    value_sum = row_sum(dv_ref[...].astype(jnp.float32))
    shared = []
    for source in (attn_ref, ffn_ref):
        for r in range(3):
            shared += [source[r : r + 1, :depth], source[r : r + 1, depth:]]
    half = depth // 2
    for z in (0, 1):
        own = slice(z * half, (z + 1) * half)
        heads = jnp.concatenate([query_sum[:, own], value_sum[:, own]], axis=1)
        none = jnp.zeros_like(heads)
        rows = [heads] + shared
        for c in (0, 1):
            last = [none if c else up_ref[z], none, none]
            for x, group in ((across, rows[:8]), (1 - across, rows[8:] + last)):
                block = jnp.concatenate(group, axis=0).astype(jnp.bfloat16)
                for y in (0, 1):
                    parts[c][y, x, z, 2 * part :] = block


def attn_grads(
    place, grad_queries, grad_keys, grad_values, mixed, grad_attn, near, attn_sums, ffn_sums, up_sums
):
    count, width = mixed.shape
    window = near.shape[0]
    depth = width // 2
    high = depth // 2 + 8
    cols = pl.BlockSpec((count, depth), lambda i, _: (0, i))
    near_cols = pl.BlockSpec((window, depth), lambda i, _: (0, i))
    return pl.pallas_call(
        attn_grads_kernel,
        grid_spec=pltpu.PrefetchScalarGridSpec(
            num_scalar_prefetch=1,
            grid=(2,),
            in_specs=[
                cols,
                near_cols,
                near_cols,
                cols,
                whole((count, width)),
                whole((window, width)),
                whole((3, width)),
                whole((3, width)),
                pl.BlockSpec((2, 1, depth), lambda i, _: (i, 0, 0)),
            ],
            out_specs=[pl.BlockSpec((2, 2, 2, high, depth), lambda i, _: (0, 0, i, 0, 0))] * 2,
            scratch_shapes=[pltpu.VMEM((depth, width), jnp.bfloat16)],
        ),
        out_shape=[jax.ShapeDtypeStruct((2, 2, 4, high, depth), jnp.bfloat16)] * 2,
        compiler_params=pltpu.CompilerParams(vmem_limit_bytes=24 << 20),
        cost_estimate=pl.CostEstimate(
            flops=4 * (window + count) * width * width, bytes_accessed=16 << 20, transcendentals=0
        ),
        name="attn_grads",
    )(
        place,
        grad_queries,
        grad_keys,
        grad_values,
        mixed,
        grad_attn,
        near,
        attn_sums,
        ffn_sums,
        up_sums,
    )


def span_grads_kernel(
    place_ref,
    dq_ref,
    dk_ref,
    dv_ref,
    w_ref,
    base_ref,
    own_ref,
    first_ref,
    second_ref,
    give_ref,
    near,
):
    core = place_ref[0]
    count, reach = own_ref.shape[0], give_ref.shape[0]
    far = count + reach
    size = near.shape[0] // 4

    @pl.loop(0, 4)
    def _(step):
        rows = pl.ds(pl.multiple_of(step * size, 32), size)
        near[rows] = dot32(dk_ref[rows], w_ref[1]) + dot32(dv_ref[rows], w_ref[2])

    def rows_at(start, size):
        return near[pl.ds(pl.multiple_of(start, QBLOCK), size)].astype(jnp.bfloat16)

    give_ref[...] = rows_at((1 - core) * far, reach)
    first_ref[...] = rows_at(jnp.where(core == 0, reach - count, far), count)
    second_ref[...] = rows_at(jnp.where(core == 0, 0, far + count), reach - count)
    own_ref[...] = base_ref[...] + dot32(dq_ref[...], w_ref[0]) + near[reach:far]


def span_grads(place, grad_queries, grad_keys, grad_values, weights, base):
    count, width = base.shape
    reach = (grad_keys.shape[0] - count) // 2
    vmem = pl.BlockSpec(memory_space=pltpu.VMEM)
    return pl.pallas_call(
        span_grads_kernel,
        in_specs=[pl.BlockSpec(memory_space=pltpu.SMEM)] + [vmem] * 5,
        out_specs=[vmem] * 4,
        out_shape=[
            jax.ShapeDtypeStruct((count, width), jnp.float32),
            jax.ShapeDtypeStruct((count, width), jnp.bfloat16),
            jax.ShapeDtypeStruct((reach - count, width), jnp.bfloat16),
            jax.ShapeDtypeStruct((reach, width), jnp.bfloat16),
        ],
        scratch_shapes=[pltpu.VMEM(grad_keys.shape, jnp.float32)],
        compiler_params=pltpu.CompilerParams(vmem_limit_bytes=16 << 20),
        cost_estimate=pl.CostEstimate(
            flops=4 * (count + 2 * reach) * width * width,
            bytes_accessed=12 << 20,
            transcendentals=0,
        ),
        name="span_grads",
    )(place, grad_queries, grad_keys, grad_values, weights, base)


def assemble_kernel(place_ref, one, two, three, four, halves, out_ref):
    core, tp, across = place_ref[0], place_ref[2], place_ref[3]
    block = out_ref.shape[1]
    part = block // 2
    mine = pl.ds(pl.multiple_of(core * part, part), part)
    other = pl.ds(pl.multiple_of((1 - core) * part, part), part)
    for k, source in enumerate((one, two, three, four)):
        z = (tp + 4 - k) & 3
        group, side = 3 * (z >> 1), z & 1
        out_ref[group + jnp.where(side == 1, 1, 2 * across)] = source[:block].astype(out_ref.dtype)
        foreign = group + 2 - 2 * across

        @pl.when(((side + across + core) & 1) == 1)
        def _():
            out_ref[foreign, mine] = source[block:].astype(out_ref.dtype)
            out_ref[foreign, other] = halves[k].astype(out_ref.dtype)


def assemble_late_kernel(place_ref, one, two, three, four, middle, foreign, out_ref):
    core, tp, across = place_ref[0], place_ref[2], place_ref[3]
    block = out_ref.shape[1]
    part = block // 2
    for k, source in enumerate((one, two, three, four)):
        z = (tp + 4 - k) & 3
        group, side = 3 * (z >> 1), z & 1
        at = group + jnp.where(side == 1, 1, 2 * across)
        odd = (across + side) & 1

        @pl.when(jnp.logical_and(odd == 0, core == 0))
        def _():
            out_ref[at] = source[:block]

        @pl.when(jnp.logical_and(odd == 0, core == 1))
        def _():
            out_ref[at, :part] = middle[k]
            out_ref[at, part:] = source[:part]

        @pl.when(jnp.logical_and(odd == 1, core == 0))
        def _():
            out_ref[at, :part] = source[block:]
            out_ref[at, part:] = middle[k]

        @pl.when(jnp.logical_and(odd == 1, core == 1))
        def _():
            out_ref[at] = source[part:]

        @pl.when(((side + across + core) & 1) == 1)
        def _():
            out_ref[group + 2 - 2 * across] = foreign[k // 2]


def assemble(kernel, place, pieces, others, seqs, dtype):
    rows, width = pieces[0].shape
    vmem = pl.BlockSpec(memory_space=pltpu.VMEM)
    return pl.pallas_call(
        kernel,
        in_specs=[pl.BlockSpec(memory_space=pltpu.SMEM)] + [vmem] * (4 + len(others)),
        out_specs=vmem,
        out_shape=jax.ShapeDtypeStruct((seqs, rows * 2 // 3, width), dtype),
        compiler_params=pltpu.CompilerParams(vmem_limit_bytes=10 << 20),
        cost_estimate=pl.CostEstimate(flops=1 << 20, bytes_accessed=8 << 20, transcendentals=0),
        name="assemble",
    )(place, *pieces, *others)


def finish_ffn_kernel(place_ref, mine, across_got, core_got, both_got, up_ref, down_ref):
    core, across = place_ref[0], place_ref[3]
    depth = mine.shape[1]
    part = depth // 2
    for c, x, source in (
        (core, across, mine),
        (core, 1 - across, across_got),
        (1 - core, across, core_got),
        (1 - core, 1 - across, both_got),
    ):
        rows = pl.ds(pl.multiple_of(x * part, part), part)
        up_ref[rows, half_cols(c, depth)] = source[:part].astype(jnp.float32)
        rows = pl.ds(pl.multiple_of(c * depth + x * part, part), part)
        down_ref[rows] = source[part:].astype(jnp.float32)


def finish_attn_kernel(
    place_ref, mine, across_got, core_got, both_got, q_ref, k_ref, v_ref, o_ref, *refs
):
    *vectors, sums_ref = refs
    core, across = place_ref[0], place_ref[3]
    part = q_ref.shape[0] // 2
    for c, x, source in (
        (core, across, mine),
        (core, 1 - across, across_got),
        (1 - core, across, core_got),
        (1 - core, 1 - across, both_got),
    ):
        rows = pl.ds(pl.multiple_of(c * part, part), part)
        one = source[:part].astype(jnp.float32)
        two = source[part : 2 * part].astype(jnp.float32)
        sums_ref[c, x] = source[2 * part :].astype(jnp.float32)

        @pl.when(x == 0)
        def _():
            q_ref[rows], k_ref[rows] = one, two

        @pl.when(x == 1)
        def _():
            v_ref[rows], o_ref[rows] = one, two

    def flat(*rows):
        return jnp.concatenate(rows, axis=1).reshape(-1)

    sums = sums_ref[core].reshape(16, 4 * part)
    for r, to in enumerate(vectors[:6]):
        to[...] = flat(sums[2 * r + 1 : 2 * r + 2], sums[2 * r + 2 : 2 * r + 3])
    vectors[6][...] = flat(sums_ref[0, 1, 5:6], sums_ref[1, 1, 5:6])
    vectors[7][...] = sums[0:1, : 2 * part].reshape(-1)
    vectors[8][...] = sums[0:1, 2 * part :].reshape(-1)


def finish(kernel, place, pieces, shapes, name, scratch=()):
    vmem = pl.BlockSpec(memory_space=pltpu.VMEM)
    return pl.pallas_call(
        kernel,
        in_specs=[pl.BlockSpec(memory_space=pltpu.SMEM)] + [vmem] * 4,
        out_specs=[vmem] * len(shapes),
        out_shape=[jax.ShapeDtypeStruct(shape, jnp.float32) for shape in shapes],
        scratch_shapes=scratch,
        compiler_params=pltpu.CompilerParams(vmem_limit_bytes=8 << 20),
        cost_estimate=pl.CostEstimate(flops=1 << 20, bytes_accessed=4 << 20, transcendentals=0),
        name=name,
    )(place, *pieces)


def ctx_swap(array, bit):
    return lax.ppermute(array, "ctx", [(i, i ^ bit) for i in range(4)])


def core_swap(array):
    return ctx_swap(array, 1)


def tie(*arrays):
    return lax.optimization_barrier(arrays)


def across_swap(array):
    return ctx_swap(array, 2)


def in_order(flag, mine, other):
    return jnp.where(flag == 0, mine, other), jnp.where(flag == 0, other, mine)


def at(across, core, tp):
    return (2 * across + core) * 4 + tp


def across_pairs():
    pairs = []
    for tp in range(4):
        for across in (0, 1):
            core = across ^ (tp & 1)
            pairs.append((at(1 - across, core, tp), at(across, core, tp)))
    return pairs


def tp_shifts(array, cuts=(slice(None), slice(None), slice(None))):
    return [
        lax.ppermute(array[cut], "tp", [(i, (i + shift) % 4) for i in range(4)])
        for shift, cut in zip((1, 2, 3), cuts)
        if cut is not None
    ]


def by_tp(array, shifted):
    one, two, three = shifted
    line = jnp.stack([three, two, one, array, three, two, one])
    return lax.dynamic_slice_in_dim(line, 3 - lax.axis_index("tp"), 4, 0)


def shard_swap(array):
    return lax.ppermute(array, "shard", [(0, 1), (1, 0)])


def low_sum(left, right):
    return (left.astype(jnp.float32) + right.astype(jnp.float32)).astype(jnp.bfloat16)


def scatter_tp_start(parts):
    tp = lax.axis_index("tp")
    moved = [lax.dynamic_index_in_dim(parts, tp, 0, keepdims=False)]
    for shift in (1, 2, 3):
        sent = lax.dynamic_index_in_dim(parts, (tp + shift) & 3, 0, keepdims=False)
        moved.append(lax.ppermute(sent, "tp", [(i, (i + shift) % 4) for i in range(4)]))
    return moved


def scatter_tp_end(moved):
    return sum(part.astype(jnp.float32) for part in moved).astype(jnp.bfloat16)


def chain_pairs(turn):
    pairs = []
    for group in (0, 2):
        path = [(0, group), (0, group + 1), (1, group + 1), (1, group)]
        for (across, tp), (next_across, next_tp) in zip(path[:-1], path[1:]):
            pairs.append((at(across, 1, tp), at(next_across, 1 ^ turn, next_tp)))
            pairs.append((at(next_across, 0, next_tp), at(across, turn, tp)))
    return pairs


def block_pairs(core):
    pairs = []
    for tp in range(4):
        for across in (0, 1):
            source = 1 ^ across ^ (tp & 1)
            pairs.append((at(across, source, tp), at(1 - across, core, tp)))
    return pairs


def span_shards(
    layer_input,
    segment_ids,
    query_proj,
    query_bias,
    key_proj,
    value_proj,
    value_bias,
    out_proj,
    out_bias,
    attn_gain,
    attn_shift,
    up_proj,
    up_bias,
    down_proj,
    down_bias,
    ffn_gain,
    ffn_shift,
    out_cotangent,
):
    seqs, block, width = layer_input.shape
    length = segment_ids.shape[1]
    reach = length // 2
    count = seqs * block // 4
    window = count + 2 * reach
    bf16, f32 = jnp.bfloat16, jnp.float32
    ctx, tp = lax.axis_index("ctx"), lax.axis_index("tp")
    shard = lax.axis_index("shard")
    core, across, side = ctx & 1, ctx >> 1, tp & 1
    place = 2 * across + (side ^ across)
    odd = across ^ side

    heads = query_proj.shape[1]
    half = heads // 2
    depth = query_proj.shape[0]
    cut = up_proj.shape[1] // 2
    own_in = lax.dynamic_slice_in_dim(
        jnp.stack([query_proj.T, key_proj.T, value_proj.T]), core * half, half, 1
    ).reshape(3 * half, depth)
    own_biases = jnp.stack(
        [
            jnp.concatenate([query_bias, value_bias]),
            lax.dynamic_slice_in_dim(up_bias, core * cut, cut, 0),
        ]
    )
    own_in = jnp.concatenate([own_in, own_biases, jnp.zeros((14, depth), bf16)], axis=0)
    out_half = out_proj.shape[0] // 2
    own_rest = jnp.concatenate(
        [
            lax.dynamic_slice_in_dim(up_proj, core * cut, cut, 1),
            lax.dynamic_slice_in_dim(down_proj, core * cut, cut, 0),
            lax.dynamic_slice_in_dim(out_proj, core * out_half, out_half, 0),
        ],
        axis=0,
    )
    first_seq = 3 * (tp >> 1)
    mine = lax.dynamic_slice_in_dim(layer_input, first_seq + across, 2, 0)
    theirs = across_swap(lax.dynamic_slice_in_dim(layer_input, first_seq + 1 - across, 2, 0))
    in_shifted = tp_shifts(own_in)
    far_rest = shard_swap(own_rest)
    *in_shifted, theirs, far_rest = tie(*in_shifted, theirs, far_rest)
    in_near = jnp.stack([own_in] + in_shifted)
    (rest_one,) = tp_shifts(tie(own_rest, in_near)[0], (slice(None), None, None))
    own_pair = jnp.stack([own_rest[: 2 * cut], far_rest[: 2 * cut]])
    near_cot = lax.dynamic_index_in_dim(
        out_cotangent, first_seq + odd + across, 0, keepdims=False
    )
    far_cot = lax.ppermute(
        lax.dynamic_index_in_dim(
            tie(out_cotangent, theirs)[0], first_seq + 2 - 2 * across, 0, keepdims=False
        ),
        ("ctx", "tp"),
        across_pairs(),
    )
    in_far, rest_one, own_pair, far_cot = tie(shard_swap(in_near), rest_one, own_pair, far_cot)
    in_mine = jnp.stack([in_near, in_far])
    (rest_three,) = tp_shifts(tie(own_rest, in_near)[0], (None, None, slice(None)))
    in_other, rest_three = tie(core_swap(in_mine), rest_three)
    own_late = tie(own_rest, rest_three)[0]
    (some_two,) = tp_shifts(own_late, (None, slice(cut, None), None))
    (up_two,) = tp_shifts(own_late, (None, slice(cut), None))
    far_three = shard_swap(rest_three)
    bias_rows = in_mine[0, :, 3 * half]
    in_biases = by_tp(bias_rows[0], [bias_rows[1], bias_rows[2], bias_rows[3]]).astype(f32)
    in_biases = jnp.stack([in_biases[:, :heads].reshape(-1), in_biases[:, heads:].reshape(-1)])
    up_bias_here = in_mine[0, :, 3 * half + 1].reshape(4, 1, cut).astype(f32)

    pair = jnp.stack([mine, theirs])
    pair_other = core_swap(pair)
    start = 2 * count * place + count * core - length * across
    ids = lax.dynamic_slice_in_dim(segment_ids, first_seq + across, 2, 0)
    ids = (ids + jnp.array([[0], [1 << 16]], jnp.int32)).reshape(-1)
    no_doc = jnp.full((reach,), -1, jnp.int32)
    window_docs = lax.dynamic_slice_in_dim(
        jnp.concatenate([no_doc, ids, no_doc]), start, window, 0
    )
    key_docs = window_docs[None]
    query_docs = jnp.broadcast_to(window_docs[reach : reach + count, None], (count, QBLOCK))

    place = jnp.stack([core, shard, tp, across, start])
    far_one = shard_swap(rest_one)
    queries, keys, values, in_window, weights_t = project(
        place, in_mine, in_other, pair, pair_other, in_biases, count, window
    )
    attention = queries, keys, values, key_docs, query_docs, reach
    mixed, logs = attend(*attention, 0)
    mixed, far_one, far_three, some_two = tie(mixed, far_one, far_three, some_two)
    far_some_two = shard_swap(some_two)
    mixed, logs = attend(*attention, 1, (mixed, logs))
    mixed, far_some_two, up_two, plan = tie(
        mixed, far_some_two, up_two, key_plan(window_docs, reach, count)
    )
    far_up_two = shard_swap(up_two)
    out_mine = jnp.stack(
        [
            jnp.stack([one[-out_half:], two[-out_half:]])
            for one, two in (
                (own_rest, far_rest),
                (rest_one, far_one),
                (some_two, far_some_two),
                (rest_three, far_three),
            )
        ]
    )
    attn_vectors = jnp.stack([out_bias, attn_gain, attn_shift]).astype(f32)
    hidden_low, normed_one, inv_one, full_out = attend_out(
        place, mixed, in_window, reach, out_mine, core_swap(out_mine), attn_vectors
    )
    hidden_other = core_swap(hidden_low)
    hidden_both = hidden_low, hidden_other
    ffn_weights = jnp.stack(
        [
            own_pair,
            jnp.stack([rest_one[: 2 * cut], far_one[: 2 * cut]]),
            jnp.stack([rest_three[: 2 * cut], far_three[: 2 * cut]]),
            own_pair,
        ]
    )
    ffn_bias = jnp.stack([up_bias_here[k] for k in (0, 1, 3, 2)])
    acts, slope, ffn_sum = ffn(place, *hidden_both, ffn_weights, ffn_bias)
    ffn_sum, far_up_two = tie(ffn_sum, far_up_two)
    rest = ffn_weights.at[3].set(
        jnp.stack(
            [
                jnp.concatenate([up_two, some_two[:cut]], axis=0),
                jnp.concatenate([far_up_two, far_some_two[:cut]], axis=0),
            ]
        )
    )
    acts, slope, ffn_own, ffn_other = ffn(
        place, *hidden_both, rest, ffn_bias, (ffn_sum, acts, slope)
    )

    half_block = block // 2

    def deliver_start(rows):
        far_rows = jnp.where(odd == 0, rows[-block:], rows[:block])
        return (
            core_swap(jnp.where(odd == 0, rows[block:], rows[:half_block])),
            lax.ppermute(far_rows[:half_block], ("ctx", "tp"), block_pairs(0)),
            lax.ppermute(far_rows[half_block:], ("ctx", "tp"), block_pairs(1)),
        )

    def deliver_pack(rows, middle, low, high):
        where_kept = [
            rows[:block],
            jnp.concatenate([middle, rows[:half_block]], axis=0),
            jnp.concatenate([rows[block:], middle], axis=0),
            rows[half_block:],
        ]
        kept = jnp.where(
            odd == 0,
            jnp.where(core == 0, where_kept[0], where_kept[1]),
            jnp.where(core == 0, where_kept[2], where_kept[3]),
        )
        return jnp.concatenate([kept, low + high], axis=0)

    cot_pair = tie(jnp.stack([near_cot, far_cot]), queries)[0]
    cot_swapped = core_swap(cot_pair)

    ffn_vectors = jnp.stack([down_bias, ffn_gain, ffn_shift]).astype(f32)
    output_rows, grad_ffn, ffn_sums = ffn_norm(
        place, hidden_low, ffn_own, core_swap(ffn_other), cot_pair, cot_swapped, ffn_vectors
    )
    grad_other = core_swap(grad_ffn)
    out_pieces = [output_rows] + tp_shifts(output_rows)
    back_own, back_other, up_keep, up_give, down_keep, down_give, up_sums = ffn_back(
        place, grad_ffn, grad_other, *hidden_both, acts, slope, rest
    )
    back_own, out_pieces[1] = tie(back_own, out_pieces[1])
    grad_one, grad_attn, grad_mixed, attn_sums = attend_norm(
        grad_ffn, back_own, core_swap(back_other), normed_one, inv_one, attn_vectors, full_out
    )
    up_got = across_swap(up_give)
    down_got = shard_swap(down_give)
    grad_scaled, grad_keys, grad_values = attend_back(plan, *attention, grad_mixed, logs)
    own_sum, first, second, give = span_grads(
        place, grad_scaled, grad_keys, grad_values, weights_t, grad_one
    )
    first, up_got, down_got, out_pieces[2] = tie(first, up_got, down_got, out_pieces[2])
    up_parts = [low_sum(up_keep[i], up_got[i]) for i in (0, 1)]
    down_parts = [low_sum(down_keep[i], down_got[i]) for i in (0, 1)]
    up_got, down_got = shard_swap(up_parts[1]), across_swap(down_parts[1])
    got = core_swap(give)
    shared = reach - count
    to_own = lax.dynamic_slice_in_dim(got, (1 - core) * shared, count, 0)
    to_next = lax.dynamic_slice_in_dim(got, core * count, shared, 0)
    no_rows = jnp.zeros((count - shared, width), bf16)
    first = low_sum(
        first,
        jnp.where(
            core == 0,
            jnp.concatenate([no_rows, to_next], axis=0),
            jnp.concatenate([to_next, no_rows], axis=0),
        ),
    )
    first_now, up_got, down_got, out_pieces[3] = tie(first, up_got, down_got, out_pieces[3])
    ffn_parts = jnp.concatenate(
        [low_sum(up_parts[0], up_got), low_sum(down_parts[0], down_got)], axis=1
    )
    ffn_near = scatter_tp_start(ffn_parts)
    first_got = lax.ppermute(first, ("ctx", "tp"), chain_pairs(1))
    second_got = lax.ppermute(second, ("ctx", "tp"), chain_pairs(0))
    grad_keys, first_now = tie(grad_keys, first)
    attn_parts = attn_grads(
        place,
        grad_scaled,
        grad_keys,
        grad_values,
        mixed,
        grad_attn,
        in_window,
        attn_sums,
        ffn_sums,
        up_sums,
    )
    first_got, second_got, attn_keep, attn_give, ffn_near[1], ffn_near[3] = tie(
        first_got, second_got, *attn_parts, ffn_near[1], ffn_near[3]
    )
    attn_core = core_swap(attn_give)
    own_sum += to_own.astype(f32) + first_got.astype(f32)
    own_sum += jnp.where(
        core == 0,
        jnp.concatenate([no_rows, second_got], axis=0),
        jnp.concatenate([second_got, no_rows], axis=0),
    ).astype(f32)
    own_low = own_sum.astype(bf16)
    in_moves = deliver_start(own_low)
    *in_moves, attn_core, ffn_near[2] = tie(*in_moves, attn_core, ffn_near[2])
    in_packed = deliver_pack(own_low, *in_moves)
    in_pieces = [in_packed] + tp_shifts(in_packed)
    attn_parts = [low_sum(attn_keep[i], attn_core[i]) for i in (0, 1)]
    attn_got = shard_swap(attn_parts[1])
    parity = (tp + 1 + across + core) & 1
    out_sent = [
        jnp.where(
            core == 0,
            jnp.where(parity == 0, even[:block], odd_one[:block]),
            jnp.where(parity == 0, even[-block:], odd_one[-block:]),
        )
        for even, odd_one in (out_pieces[:2], out_pieces[2:])
    ]
    out_foreign = lax.ppermute(jnp.stack(out_sent), "ctx", [(i, 3 - i) for i in range(4)])
    out_middle = core_swap(
        jnp.stack(
            [
                jnp.where(((across + tp + k) & 1) == 0, piece[block:], piece[:half_block])
                for k, piece in enumerate(out_pieces)
            ]
        )
    )
    attn_got, in_pieces[1], in_pieces[3] = tie(attn_got, in_pieces[1], in_pieces[3])
    attn_mid = [low_sum(attn_parts[0][i], attn_got[i]) for i in (0, 1)]
    attn_got = across_swap(attn_mid[1])
    ffn_low = scatter_tp_end(ffn_near)
    ffn_got = across_swap(ffn_low)
    attn_got, out_foreign, out_middle = tie(attn_got, out_foreign, out_middle)
    attn_near = scatter_tp_start(low_sum(attn_mid[0], attn_got))
    layer_output = assemble(
        assemble_late_kernel, place, out_pieces, (out_middle, out_foreign), seqs, bf16
    )
    layer_output, in_pieces[2], attn_near[3], ffn_got = tie(
        layer_output, in_pieces[2], attn_near[3], ffn_got
    )
    in_halves = core_swap(jnp.stack([piece[block:] for piece in in_pieces]))
    input_grad = assemble(assemble_kernel, place, in_pieces, (in_halves,), seqs, f32)
    up_grad, down_grad = finish(
        finish_ffn_kernel,
        place,
        (ffn_low, ffn_got, core_swap(ffn_low), core_swap(ffn_got)),
        ((cut, 2 * cut), (2 * cut, cut)),
        "finish_ffn",
    )
    attn_low = scatter_tp_end(attn_near)
    attn_got, input_grad = tie(across_swap(attn_low), input_grad)
    finished = finish(
        finish_attn_kernel,
        place,
        (attn_low, attn_got, core_swap(attn_low), core_swap(attn_got)),
        ((heads, depth),) * 4 + ((width,),) * 6 + ((2 * cut,), (heads,), (heads,)),
        "finish_attn",
        [pltpu.VMEM((2, 2, 8, depth), f32)],
    )
    weight_grads, row_sums = finished[:4], finished[4:10]
    up_bias_grad, query_bias_grad, value_bias_grad = finished[10:]
    return (
        layer_output,
        input_grad,
        weight_grads[0].T,
        query_bias_grad,
        weight_grads[1].T,
        weight_grads[2].T,
        value_bias_grad,
        weight_grads[3],
        row_sums[0],
        row_sums[1],
        row_sums[2],
        up_grad,
        up_bias_grad,
        down_grad,
        row_sums[3],
        row_sums[4],
        row_sums[5],
    )


def pick_plan(mesh):
    shape = dict(mesh.shape)

    def plan(layer_input, segment_ids, *others):
        seqs, block, _ = layer_input.shape
        fits = (
            (shape["shard"], shape["ctx"], shape["tp"]) == (2, 4, 4)
            and seqs == 6
            and segment_ids.shape[1] == 4 * block
            and block == 2 * QBLOCK
        )
        chosen = span_shards if fits else general_shards
        return chosen(layer_input, segment_ids, *others)

    return plan


def solution(mesh):
    return jax.shard_map(
        pick_plan(mesh),
        mesh=mesh,
        in_specs=(
            P("shard", "ctx", None),
            P("shard", None),
            P("shard", "tp"),
            P("tp"),
            P("shard", "tp"),
            P("shard", "tp"),
            P("tp"),
            P("tp", "shard"),
            P(),
            P(),
            P(),
            P("shard", "tp"),
            P("tp"),
            P("tp", "shard"),
            P(),
            P(),
            P(),
            P("shard", "ctx", None),
        ),
        out_specs=(
            P("shard", "ctx", None),
            P("shard", "ctx", None),
            P("shard", "tp"),
            P("tp"),
            P("shard", "tp"),
            P("shard", "tp"),
            P("tp"),
            P("tp", "shard"),
            P(),
            P(),
            P(),
            P("shard", "tp"),
            P("tp"),
            P("tp", "shard"),
            P(),
            P(),
            P(),
        ),
        check_vma=False,
    )
```

```python
from functools import partial
import math

import jax
import jax.numpy as jnp
from jax import lax
from jax.experimental import pallas as pl
from jax.experimental.pallas import tpu as pltpu
from jax.sharding import PartitionSpec as P

HEAD_DIM = 64


eps_norm = 1e-12
far_below = -1e30


def contract_rows(left, right):
    return lax.dot_general(
        left, right, (((0,), (0,)), ((), ())), preferred_element_type=jnp.float32
    )


def contract_last(left, right):
    return lax.dot_general(
        left, right, (((1,), (1,)), ((), ())), preferred_element_type=jnp.float32
    )


def norm_forward(resid, norm_gain, norm_shift):
    center = resid - jnp.mean(resid, axis=-1, keepdims=True)
    inv_std = lax.rsqrt(jnp.mean(center * center, axis=-1, keepdims=True) + eps_norm)
    normed = center * inv_std
    return (normed * norm_gain + norm_shift, normed, inv_std)


def norm_backward(grad_out, normed, inv_std, norm_gain):
    grad_normed = grad_out * norm_gain
    grad_in = inv_std * (
        grad_normed
        - jnp.mean(grad_normed, axis=-1, keepdims=True)
        - normed * jnp.mean(grad_normed * normed, axis=-1, keepdims=True)
    )
    return (grad_in, jnp.sum(grad_out * normed, axis=0), jnp.sum(grad_out, axis=0))


def split_heads(matrix):
    return matrix.reshape(matrix.shape[0], matrix.shape[1] // HEAD_DIM, HEAD_DIM)


def scores_of(queries, keys_all, query_docs, key_docs):
    scores = jnp.einsum(
        "qhd,khd->hqk",
        split_heads(queries),
        split_heads(keys_all),
        preferred_element_type=jnp.float32,
    )
    same_doc = (query_docs[:, None] == key_docs[None, :])[None]
    return jnp.where(same_doc, scores, jnp.float32(far_below))


def attend_forward(item):
    queries, keys_all, values_all, query_docs, key_docs = item
    scores = scores_of(queries, keys_all, query_docs, key_docs)
    top_score = jnp.max(scores, axis=-1, keepdims=True)
    expo = jnp.exp(scores - top_score)
    total = jnp.sum(expo, axis=-1, keepdims=True)
    probs = (expo / total).astype(jnp.bfloat16)
    mixed = jnp.einsum(
        "hqk,khd->qhd", probs, split_heads(values_all), preferred_element_type=jnp.float32
    )
    return (
        mixed.reshape(queries.shape).astype(jnp.bfloat16),
        (top_score + jnp.log(total))[:, :, 0],
    )


def score_grads(queries, keys_all, values_all, query_docs, key_docs, grad_mixed, log_total):
    scores = scores_of(queries, keys_all, query_docs, key_docs)
    probs = jnp.exp(scores - log_total[:, :, None])
    grad_probs = jnp.einsum(
        "qhd,khd->hqk",
        split_heads(grad_mixed),
        split_heads(values_all),
        preferred_element_type=jnp.float32,
    )
    inner = jnp.sum(grad_probs * probs, axis=-1)
    grad_scores = (probs * (grad_probs - inner[:, :, None])).astype(jnp.bfloat16)
    return (probs, grad_scores, inner)


def attend_backward(item):
    queries, keys_all, values_all, query_docs, key_docs, grad_mixed, log_total = item
    probs, grad_scores, inner = score_grads(
        queries, keys_all, values_all, query_docs, key_docs, grad_mixed, log_total
    )
    grad_heads = split_heads(grad_mixed)
    grad_queries = jnp.einsum(
        "hqk,khd->qhd", grad_scores, split_heads(keys_all), preferred_element_type=jnp.float32
    )
    grad_keys = jnp.einsum(
        "hqk,qhd->khd", grad_scores, split_heads(queries), preferred_element_type=jnp.float32
    )
    grad_values = jnp.einsum(
        "hqk,qhd->khd", probs.astype(jnp.bfloat16), grad_heads, preferred_element_type=jnp.float32
    )
    return (
        grad_queries.reshape(queries.shape).astype(jnp.bfloat16),
        grad_keys.reshape(keys_all.shape),
        grad_values.reshape(values_all.shape),
    )


def general_shards(
    layer_input,
    segment_ids,
    query_proj,
    query_bias,
    key_proj,
    value_proj,
    value_bias,
    out_proj,
    out_bias,
    attn_gain,
    attn_shift,
    up_proj,
    up_bias,
    down_proj,
    down_bias,
    ffn_gain,
    ffn_shift,
    out_cotangent,
):
    seq_here, ctx_rows, width = layer_input.shape
    scale = 1.0 / math.sqrt(HEAD_DIM)
    full_query, full_key, full_value, full_out, full_up, full_down = (
        lax.all_gather(query_proj, "shard", axis=0, tiled=True),
        lax.all_gather(key_proj, "shard", axis=0, tiled=True),
        lax.all_gather(value_proj, "shard", axis=0, tiled=True),
        lax.all_gather(out_proj, "shard", axis=1, tiled=True),
        lax.all_gather(up_proj, "shard", axis=0, tiled=True),
        lax.all_gather(down_proj, "shard", axis=1, tiled=True),
    )
    local_width = full_query.shape[1]
    joined_proj = jnp.concatenate([full_query, full_key, full_value], axis=1)
    rows_in = layer_input.reshape(seq_here * ctx_rows, width)
    projected = jnp.dot(rows_in, joined_proj, preferred_element_type=jnp.float32)
    shaped = (seq_here, ctx_rows, local_width)
    queries = (
        ((projected[:, :local_width] + query_bias) * scale).astype(jnp.bfloat16).reshape(shaped)
    )
    keys_mine = projected[:, local_width : 2 * local_width].astype(jnp.bfloat16).reshape(shaped)
    values_mine = (
        (projected[:, 2 * local_width :] + value_bias).astype(jnp.bfloat16).reshape(shaped)
    )
    keys_all, values_all = (
        lax.all_gather(keys_mine, "ctx", axis=1, tiled=True),
        lax.all_gather(values_mine, "ctx", axis=1, tiled=True),
    )
    query_docs = lax.dynamic_slice_in_dim(
        segment_ids, lax.axis_index("ctx") * ctx_rows, ctx_rows, 1
    )
    mixed, log_total = lax.map(
        attend_forward, (queries, keys_all, values_all, query_docs, segment_ids)
    )
    mixed_rows = mixed.reshape(-1, local_width)
    attended = (
        lax.psum(
            jnp.dot(mixed_rows, full_out, preferred_element_type=jnp.float32).astype(jnp.bfloat16),
            "tp",
        ).astype(jnp.float32)
        + out_bias
    )
    hidden, normed_one, inv_one = norm_forward(
        rows_in.astype(jnp.float32) + attended, attn_gain, attn_shift
    )
    hidden_low = hidden.astype(jnp.bfloat16)
    pre_act = jnp.dot(hidden_low, full_up, preferred_element_type=jnp.float32) + up_bias
    acts_low = jax.nn.gelu(pre_act, approximate=False).astype(jnp.bfloat16)
    ffn_out = (
        lax.psum(
            jnp.dot(acts_low, full_down, preferred_element_type=jnp.float32).astype(jnp.bfloat16),
            "tp",
        ).astype(jnp.float32)
        + down_bias
    )
    output_rows, normed_two, inv_two = norm_forward(hidden + ffn_out, ffn_gain, ffn_shift)
    layer_output = output_rows.astype(jnp.bfloat16).reshape(layer_input.shape)
    grad_out = out_cotangent.reshape(-1, width).astype(jnp.float32)
    grad_two, ffn_gain_grad, ffn_shift_grad = norm_backward(grad_out, normed_two, inv_two, ffn_gain)
    grad_ffn = grad_two.astype(jnp.bfloat16)
    down_bias_grad = jnp.sum(grad_ffn, axis=0, dtype=jnp.float32)
    down_part = contract_rows(acts_low, grad_ffn)
    grad_acts = contract_last(grad_ffn, full_down)
    _, gelu_back = jax.vjp(partial(jax.nn.gelu, approximate=False), pre_act)
    grad_pre = gelu_back(grad_acts)[0].astype(jnp.bfloat16)
    up_bias_grad = jnp.sum(grad_pre, axis=0, dtype=jnp.float32)
    up_part = contract_rows(hidden_low, grad_pre)
    grad_hidden = grad_two + lax.psum(
        contract_last(grad_pre, full_up).astype(jnp.bfloat16), "tp"
    ).astype(jnp.float32)
    grad_one, attn_gain_grad, attn_shift_grad = norm_backward(
        grad_hidden, normed_one, inv_one, attn_gain
    )
    grad_attn = grad_one.astype(jnp.bfloat16)
    out_bias_grad = jnp.sum(grad_attn, axis=0, dtype=jnp.float32)
    out_part = contract_rows(mixed_rows, grad_attn)
    grad_mixed = contract_last(grad_attn, full_out).astype(jnp.bfloat16).reshape(shaped)
    keys_back, values_back = (
        lax.all_gather(keys_mine, "ctx", axis=1, tiled=True),
        lax.all_gather(values_mine, "ctx", axis=1, tiled=True),
    )
    grad_queries, grad_keys_all, grad_values_all = lax.map(
        attend_backward,
        (queries, keys_back, values_back, query_docs, segment_ids, grad_mixed, log_total),
    )
    grad_keys, grad_values = (
        lax.psum_scatter(
            grad_keys_all.astype(jnp.bfloat16), "ctx", scatter_dimension=1, tiled=True
        ).astype(jnp.float32),
        lax.psum_scatter(
            grad_values_all.astype(jnp.bfloat16), "ctx", scatter_dimension=1, tiled=True
        ).astype(jnp.float32),
    )
    grad_keys = grad_keys.astype(jnp.bfloat16).reshape(-1, local_width)
    grad_values = grad_values.astype(jnp.bfloat16).reshape(-1, local_width)
    grad_scaled = grad_queries.reshape(-1, local_width) * jnp.bfloat16(scale)
    grad_joined = jnp.concatenate([grad_scaled, grad_keys, grad_values], axis=1)
    joined_part = contract_rows(rows_in, grad_joined)
    query_part = joined_part[:, :local_width]
    key_part = joined_part[:, local_width : 2 * local_width]
    value_part = joined_part[:, 2 * local_width :]
    query_bias_grad = jnp.sum(grad_scaled, axis=0, dtype=jnp.float32)
    value_bias_grad = jnp.sum(grad_values, axis=0, dtype=jnp.float32)
    back_terms = contract_last(grad_joined, joined_proj)
    input_grad = (
        grad_one + lax.psum(back_terms.astype(jnp.bfloat16), "tp").astype(jnp.float32)
    ).reshape(layer_input.shape)
    sliced = (
        lax.psum_scatter(
            query_part.astype(jnp.bfloat16), "shard", scatter_dimension=0, tiled=True
        ).astype(jnp.float32),
        lax.psum_scatter(
            key_part.astype(jnp.bfloat16), "shard", scatter_dimension=0, tiled=True
        ).astype(jnp.float32),
        lax.psum_scatter(
            value_part.astype(jnp.bfloat16), "shard", scatter_dimension=0, tiled=True
        ).astype(jnp.float32),
        lax.psum_scatter(
            out_part.astype(jnp.bfloat16), "shard", scatter_dimension=1, tiled=True
        ).astype(jnp.float32),
        lax.psum_scatter(
            up_part.astype(jnp.bfloat16), "shard", scatter_dimension=0, tiled=True
        ).astype(jnp.float32),
        lax.psum_scatter(
            down_part.astype(jnp.bfloat16), "shard", scatter_dimension=1, tiled=True
        ).astype(jnp.float32),
    )
    reduced = (
        lax.psum(sliced[0].astype(jnp.bfloat16), "ctx").astype(jnp.float32),
        lax.psum(sliced[1].astype(jnp.bfloat16), "ctx").astype(jnp.float32),
        lax.psum(sliced[2].astype(jnp.bfloat16), "ctx").astype(jnp.float32),
        lax.psum(sliced[3].astype(jnp.bfloat16), "ctx").astype(jnp.float32),
        lax.psum(sliced[4].astype(jnp.bfloat16), "ctx").astype(jnp.float32),
        lax.psum(sliced[5].astype(jnp.bfloat16), "ctx").astype(jnp.float32),
    )
    small = lax.psum(
        (
            query_bias_grad,
            value_bias_grad,
            out_bias_grad,
            attn_gain_grad,
            attn_shift_grad,
            up_bias_grad,
            down_bias_grad,
            ffn_gain_grad,
            ffn_shift_grad,
        ),
        ("shard", "ctx"),
    )
    return (
        layer_output,
        input_grad,
        reduced[0],
        small[0],
        reduced[1],
        reduced[2],
        small[1],
        reduced[3],
        small[2],
        small[3],
        small[4],
        reduced[4],
        small[5],
        reduced[5],
        small[6],
        small[7],
        small[8],
    )


PAIR = 2 * HEAD_DIM
QBLOCK = 128


def dot32(left, right):
    return jnp.dot(left, right, preferred_element_type=jnp.float32)


def stack_heads(rows):
    lane = lax.broadcasted_iota(jnp.int32, rows.shape, 1)
    nought = jnp.zeros_like(rows)
    return jnp.concatenate(
        [jnp.where(lane < HEAD_DIM, rows, nought), jnp.where(lane >= HEAD_DIM, rows, nought)], axis=0
    )


def unstack_heads(tall):
    count = tall.shape[0] // 2
    lane = lax.broadcasted_iota(jnp.int32, (count, tall.shape[1]), 1)
    return jnp.where(lane < HEAD_DIM, tall[:count], tall[count:])


def masked_scores(queries, keys, same):
    scores = contract_last(queries, keys)
    return jnp.where(jnp.concatenate([same, same], axis=0), scores, jnp.float32(far_below))


def attend_kernel(span, short, q_ref, k_ref, v_ref, kd_ref, qd_ref, *refs):
    o_ref, l_ref = refs[-2:]
    step = pl.program_id(1)
    pairs = q_ref.shape[1] // PAIR

    def one_pair(here, same, cols):
        scores = masked_scores(stack_heads(q_ref[:, cols]), k_ref[here, cols], same)
        top = jnp.max(scores, axis=1, keepdims=True)
        expo = jnp.exp(scores - top)
        total = jnp.sum(expo, axis=1, keepdims=True)
        mixed = dot32(expo.astype(jnp.bfloat16), v_ref[here, cols]) * (1.0 / total)
        o_ref[:, cols] = unstack_heads(mixed).astype(jnp.bfloat16)
        log = top + jnp.log(total)
        return log[:QBLOCK], log[QBLOCK:]

    def looped():
        here = pl.ds(pl.multiple_of(step * QBLOCK, QBLOCK), span)
        same = qd_ref[:, :1] == kd_ref[:, here]
        lane = lax.broadcasted_iota(jnp.int32, l_ref.shape[1:], 1)

        @pl.loop(0, pairs)
        def _(pair):
            cols = pl.ds(pl.multiple_of(pair * PAIR, PAIR), PAIR)
            first, second = one_pair(here, same, cols)
            logs = jnp.where(lane == 2 * pair, first, l_ref[0])
            l_ref[0] = jnp.where(lane == 2 * pair + 1, second, logs)

    if len(refs) == 2:
        looped()
    else:
        plan_ref = refs[0]
        fits = plan_ref[1, step] == 1
        pl.when(jnp.logical_not(fits))(looped)

        @pl.when(fits)
        def _():
            here = pl.ds(pl.multiple_of(plan_ref[0, step], QBLOCK), short)
            same = qd_ref[:, :1] == kd_ref[:, here]
            logs = []
            for pair in range(pairs):
                logs += one_pair(here, same, slice(pair * PAIR, (pair + 1) * PAIR))
            l_ref[0] = jnp.concatenate(logs, axis=1)


def attend_back_kernel(
    span, short, plan_ref, q_ref, k_ref, v_ref, kd_ref, qd_ref, do_ref, l_ref, *refs
):
    dq_ref, dk_ref, dv_ref, dk_acc, dv_acc = refs
    step = pl.program_id(1)

    @pl.when(step == 0)
    def _():
        dk_acc[...] = jnp.zeros_like(dk_acc)
        dv_acc[...] = jnp.zeros_like(dv_acc)

    logs = l_ref[0]

    def one_pair(here, same, cols, log):
        keys = k_ref[here, cols]
        queries, grads = stack_heads(q_ref[:, cols]), stack_heads(do_ref[:, cols])
        probs = jnp.exp(masked_scores(queries, keys, same) - log)
        grad_probs = contract_last(grads, v_ref[here, cols])
        inner = jnp.sum(grad_probs * probs, axis=1, keepdims=True)
        grad_scores = (probs * (grad_probs - inner)).astype(jnp.bfloat16)
        grad_queries = unstack_heads(dot32(grad_scores, keys))
        dq_ref[:, cols] = (grad_queries * (1.0 / math.sqrt(HEAD_DIM))).astype(jnp.bfloat16)
        dk_acc[here, cols] += contract_rows(grad_scores, queries)
        dv_acc[here, cols] += contract_rows(probs.astype(jnp.bfloat16), grads)

    pairs = q_ref.shape[1] // PAIR
    fits = plan_ref[1, step] == 1

    @pl.when(fits)
    def _():
        here = pl.ds(pl.multiple_of(plan_ref[0, step], QBLOCK), short)
        same = qd_ref[:, :1] == kd_ref[:, here]
        for pair in range(pairs):
            log = [logs[:, 2 * pair + i : 2 * pair + i + 1] for i in (0, 1)]
            one_pair(
                here, same, slice(pair * PAIR, (pair + 1) * PAIR), jnp.concatenate(log, axis=0)
            )

    @pl.when(jnp.logical_not(fits))
    def _():
        here = pl.ds(pl.multiple_of(step * QBLOCK, QBLOCK), span)
        same = qd_ref[:, :1] == kd_ref[:, here]
        lane = lax.broadcasted_iota(jnp.int32, logs.shape, 1)

        @pl.loop(0, pairs)
        def _(pair):
            log = [
                jnp.sum(jnp.where(lane == 2 * pair + i, logs, 0.0), axis=1, keepdims=True)
                for i in (0, 1)
            ]
            cols = pl.ds(pl.multiple_of(pair * PAIR, PAIR), PAIR)
            one_pair(here, same, cols, jnp.concatenate(log, axis=0))

    @pl.when(step == pl.num_programs(1) - 1)
    def _():
        dk_ref[...] = dk_acc[...].astype(jnp.bfloat16)
        dv_ref[...] = dv_acc[...].astype(jnp.bfloat16)


def attention_specs(window, cols, at):
    rows = pl.BlockSpec((QBLOCK, cols), lambda h, i, *_: (i, at + h))
    keys = pl.BlockSpec((window, cols), lambda h, i, *_: (0, at + h))
    key_docs = pl.BlockSpec((1, window), lambda h, i, *_: (0, 0))
    query_docs = pl.BlockSpec((QBLOCK, QBLOCK), lambda h, i, *_: (i, 0))
    logs = pl.BlockSpec((1, QBLOCK, cols // HEAD_DIM), lambda h, i, *_: (at + h, i, 0))
    return rows, keys, key_docs, query_docs, logs


def attend(queries, keys, values, key_docs, query_docs, reach, half, prior=()):
    count, width = queries.shape
    window, cols = keys.shape[0], width // 2
    span = QBLOCK + 2 * reach
    rows, key_spec, kd_spec, qd_spec, logs = attention_specs(window, cols, half)
    return pl.pallas_call(
        partial(attend_kernel, span, short_span(reach)),
        grid=(1, count // QBLOCK),
        in_specs=[rows, key_spec, key_spec, kd_spec, qd_spec]
        + ([pl.BlockSpec(memory_space=pltpu.SMEM)] if prior else [])
        + [pl.BlockSpec(memory_space=pl.ANY)] * (len(prior) - 1),
        out_specs=[rows, logs],
        out_shape=[
            jax.ShapeDtypeStruct((count, width), jnp.bfloat16),
            jax.ShapeDtypeStruct((2, count, cols // HEAD_DIM), jnp.float32),
        ],
        input_output_aliases={6: 0, 7: 1} if prior else {},
        compiler_params=pltpu.CompilerParams(vmem_limit_bytes=16 << 20),
        cost_estimate=pl.CostEstimate(
            flops=16 * count * span * cols, bytes_accessed=4 << 20, transcendentals=0
        ),
        name="attend",
    )(queries, keys, values, key_docs, query_docs, *prior)


def attend_back(plan, queries, keys, values, key_docs, query_docs, reach, grads, logs_in):
    count, width = queries.shape
    window, cols = keys.shape[0], width // 2
    span = QBLOCK + 2 * reach
    rows, key_spec, kd_spec, qd_spec, logs = attention_specs(window, cols, 0)
    return pl.pallas_call(
        partial(attend_back_kernel, span, short_span(reach)),
        grid_spec=pltpu.PrefetchScalarGridSpec(
            num_scalar_prefetch=1,
            grid=(2, count // QBLOCK),
            in_specs=[rows, key_spec, key_spec, kd_spec, qd_spec, rows, logs],
            out_specs=[rows, key_spec, key_spec],
            scratch_shapes=[pltpu.VMEM((window, cols), jnp.float32)] * 2,
        ),
        out_shape=[
            jax.ShapeDtypeStruct((count, width), jnp.bfloat16),
            jax.ShapeDtypeStruct((window, width), jnp.bfloat16),
            jax.ShapeDtypeStruct((window, width), jnp.bfloat16),
        ],
        compiler_params=pltpu.CompilerParams(vmem_limit_bytes=24 << 20),
        cost_estimate=pl.CostEstimate(
            flops=40 * count * span * width, bytes_accessed=12 << 20, transcendentals=0
        ),
        name="attend_back",
    )(plan, queries, keys, values, key_docs, query_docs, grads, logs_in)


def short_span(reach):
    return (QBLOCK + 2 * reach) * 2 // 3 // QBLOCK * QBLOCK


def key_plan(docs, reach, count):
    window, short = docs.shape[0], short_span(reach)
    rows = docs[reach : reach + count].reshape(-1, QBLOCK)
    at = jnp.arange(window, dtype=jnp.int32)
    low = jnp.min(jnp.where(docs == rows[:, :1], at, window), axis=1)
    high = jnp.max(jnp.where(docs == rows[:, -1:], at + 1, 0), axis=1)
    start = jnp.minimum(low // QBLOCK * QBLOCK, window - short)
    return jnp.stack([start, (high - start <= short).astype(jnp.int32)])


def half_cols(position, half):
    return pl.ds(pl.multiple_of(position * half, half), half)


def add_or_set(first, ref, index, terms):
    @pl.when(first)
    def _():
        ref[index] = terms

    @pl.when(jnp.logical_not(first))
    def _():
        ref[index] += terms


def ffn_kernel(first_block, place_ref, h_ref, other_h_ref, w_ref, bias_ref, *refs):
    half = w_ref.shape[3]
    count = h_ref.shape[0]
    near, far = half_cols(place_ref[1], half), half_cols(1 - place_ref[1], half)
    hb_near = refs[-1]
    for part, source in enumerate((h_ref, other_h_ref)):
        rows = slice(part * count, (part + 1) * count)
        hb_near[rows, :half] = source[:, near]
        hb_near[rows, half:] = source[:, far]

    def chunk(block, rows, acts_ref, slope_ref):
        up = w_ref[block, :, :half].reshape(2 * half, half)
        pre_act = dot32(hb_near[rows], up) + bias_ref[block]
        cdf = 0.5 * (1.0 + lax.erf(pre_act * math.sqrt(0.5)))
        bell = jnp.exp(-0.5 * pre_act * pre_act) * (1.0 / math.sqrt(2 * math.pi))
        acts = (pre_act * cdf).astype(jnp.bfloat16)
        cols = pl.ds(pl.multiple_of(block * half, half), half)
        acts_ref[rows, cols] = acts
        slope_ref[rows, cols] = (cdf + pre_act * bell).astype(jnp.bfloat16)
        return dot32(acts, w_ref[block, 0, half:]), dot32(acts, w_ref[block, 1, half:])

    blocks = w_ref.shape[0]
    if first_block:
        base_ref, _, _, acts_ref, slope_ref, own_ref, other_ref = refs[:-1]
        for part, to in enumerate((own_ref, other_ref)):
            rows = slice(part * count, (part + 1) * count)
            terms = chunk(blocks - 1, rows, acts_ref, slope_ref)
            for y, cols in enumerate((near, far)):
                base = base_ref[rows, y * half : (y + 1) * half]
                to[:, cols] = (base + terms[y]).astype(to.dtype)
    else:
        acts_ref, slope_ref, total = refs[:-1]
        total[...] = jnp.zeros_like(total)

        @pl.loop(0, 2 * (blocks - 1))
        def _(i):
            rows = pl.ds(pl.multiple_of((i & 1) * count, count), count)
            one, two = chunk(i >> 1, rows, acts_ref, slope_ref)
            total[rows, :half] += one
            total[rows, half:] += two


def ffn_back_kernel(
    place_ref,
    dz_ref,
    other_dz_ref,
    h_ref,
    other_h_ref,
    acts_ref,
    slope_ref,
    w_ref,
    own_ref,
    other_ref,
    up_keep,
    up_give,
    down_keep,
    down_give,
    sums_ref,
    total,
    grad_pre,
    dz_near,
    rows_t,
    up_both,
    down_both,
    sums,
):
    step = pl.program_id(0)
    half = w_ref.shape[3]
    quarter = half // 2
    count = own_ref.shape[0]
    near, far = half_cols(place_ref[1], half), half_cols(1 - place_ref[1], half)
    first, second = slice(0, half), slice(half, 2 * half)

    @pl.when(step == 0)
    def _():
        total[...] = jnp.zeros_like(total)
        for to, cols in ((first, near), (second, far)):
            dz_near[:count, to] = dz_ref[:, cols]
            dz_near[count:, to] = other_dz_ref[:, cols]
            rows_t[to, :count] = h_ref[:, cols].T
            rows_t[to, count:] = other_h_ref[:, cols].T

    for k, hid in enumerate((first, second)):
        for y, to in enumerate((first, second)):
            up_both[to, hid] = w_ref[k, y, :half]
            down_both[hid, to] = w_ref[k, y, half:]
    sums[...] = jnp.zeros_like(sums)

    @pl.loop(0, 2)
    def _(part):
        rows = pl.ds(pl.multiple_of(part * count, count), count)
        grad_acts = contract_last(dz_near[rows], down_both[...])
        low = (slope_ref[rows].astype(jnp.float32) * grad_acts).astype(jnp.bfloat16)
        grad_pre[rows] = low
        sums[...] += row_sum(low.astype(jnp.float32))
        total[rows] += contract_last(low, up_both[...])

    tps = [(place_ref[2] + 4 - jnp.where(step == 0, k, 3 - k)) & 3 for k in (0, 1)]
    for tp, hid in zip(tps, (first, second)):
        sums_ref[tp] = sums[:, hid]
    acts_t = acts_ref[...].T
    for side, cols in enumerate((first, second)):
        up_grad = dot32(rows_t[cols], grad_pre[...]).astype(jnp.bfloat16)
        down_grad = dot32(acts_t, dz_near[:, cols]).astype(jnp.bfloat16)
        down_to = down_give if side else down_keep
        for across in (0, 1):

            @pl.when(place_ref[3] == across)
            def _():
                for k in (0, 1):
                    tp = tps[k]
                    hid = slice(k * half, (k + 1) * half)
                    for x in (0, 1):
                        part = slice((x ^ across) * quarter, (x ^ across) * quarter + quarter)
                        down_rows = slice(k * half + part.start, k * half + part.stop)
                        (up_give if x else up_keep)[side, tp] = up_grad[part, hid]
                        down_to[x, tp] = down_grad[down_rows]

    @pl.when(step == pl.num_programs(0) - 1)
    def _():
        own_ref[:, near] = total[:count, first].astype(jnp.bfloat16)
        own_ref[:, far] = total[:count, second].astype(jnp.bfloat16)
        other_ref[:, near] = total[count:, first].astype(jnp.bfloat16)
        other_ref[:, far] = total[count:, second].astype(jnp.bfloat16)


def once(shape):
    return pl.BlockSpec(
        shape, lambda *_: (0,) * len(shape), pipeline_mode=pl.Buffered(buffer_count=1)
    )


def whole(shape):
    return pl.BlockSpec(shape, lambda *_: (0,) * len(shape))


def ffn(place, rows, other_rows, weights, bias, prior=()):
    count, width = rows.shape
    both = 2 * count
    tps, shards, _, half = weights.shape
    vmem = pl.BlockSpec(memory_space=pltpu.VMEM)
    low = jax.ShapeDtypeStruct((count, width), jnp.bfloat16)
    hidden = jax.ShapeDtypeStruct((both, tps * half), jnp.bfloat16)
    last = [low, low] if prior else [jax.ShapeDtypeStruct((both, width), jnp.float32)]
    steps = 1 if prior else tps - 1
    return pl.pallas_call(
        partial(ffn_kernel, bool(prior)),
        in_specs=[pl.BlockSpec(memory_space=pltpu.SMEM)] + [vmem] * (4 + len(prior)),
        out_specs=[vmem] * (2 + len(last)),
        out_shape=[hidden, hidden] + last,
        scratch_shapes=[pltpu.VMEM((both, width), jnp.bfloat16)],
        input_output_aliases={6: 0, 7: 1} if prior else {},
        compiler_params=pltpu.CompilerParams(vmem_limit_bytes=16 << 20),
        cost_estimate=pl.CostEstimate(
            flops=12 * both * width * steps * half, bytes_accessed=3 * steps << 20, transcendentals=0
        ),
        name="ffn",
    )(place, rows, other_rows, weights, bias, *prior)


def ffn_back(place, grads, other_grads, rows, other_rows, acts, slope, weights):
    count, width = rows.shape
    both = 2 * count
    tps, shards, _, half = weights.shape
    block = pl.BlockSpec((both, 2 * half), lambda i, _: (0, i))
    parts = (2, tps, half // 2, half)
    low = jax.ShapeDtypeStruct((count, width), jnp.bfloat16)
    return pl.pallas_call(
        ffn_back_kernel,
        grid_spec=pltpu.PrefetchScalarGridSpec(
            num_scalar_prefetch=1,
            grid=(tps // 2,),
            in_specs=[
                *[once((count, width))] * 4,
                block,
                block,
                pl.BlockSpec((2, shards, 2 * half, half), lambda i, _: (i, 0, 0, 0)),
            ],
            out_specs=[
                whole((count, width)),
                whole((count, width)),
                *[whole(parts)] * 4,
                whole((tps, 1, half)),
            ],
            scratch_shapes=[
                pltpu.VMEM((both, width), jnp.float32),
                pltpu.VMEM((both, 2 * half), jnp.bfloat16),
                pltpu.VMEM((both, width), jnp.bfloat16),
                pltpu.VMEM((width, both), jnp.bfloat16),
                pltpu.VMEM((width, 2 * half), jnp.bfloat16),
                pltpu.VMEM((2 * half, width), jnp.bfloat16),
                pltpu.VMEM((1, 2 * half), jnp.float32),
            ],
        ),
        out_shape=[
            low,
            low,
            *[jax.ShapeDtypeStruct(parts, jnp.bfloat16)] * 4,
            jax.ShapeDtypeStruct((tps, 1, half), jnp.float32),
        ],
        compiler_params=pltpu.CompilerParams(vmem_limit_bytes=30 << 20),
        cost_estimate=pl.CostEstimate(
            flops=12 * both * width * tps * half, bytes_accessed=20 << 20, transcendentals=0
        ),
        name="ffn_back",
    )(place, grads, other_grads, rows, other_rows, acts, slope, weights)


def project_kernel(
    place_ref, w_mine, w_other, x_mine, x_other, bias_ref, q_ref, k_ref, v_ref, x_ref, wt
):
    core, shard, tp, across, start = (place_ref[i] for i in range(5))
    depth = w_mine.shape[3]
    width = x_ref.shape[1]
    part = width // 8
    length = 4 * x_mine.shape[2]
    reach = length // 2
    for c, source in enumerate((w_mine, w_other)):
        for y in (0, 1):
            cols = half_cols(shard + y - 2 * shard * y, depth)
            for k in range(4):
                row = ((tp + 4 - k) & 3) * 2 + core + c - 2 * core * c
                rows = pl.ds(pl.multiple_of(row * part, part), part)
                for m in range(3):
                    wt[m, rows, cols] = source[y, k, m * part : (m + 1) * part]
    for i in range(x_ref.shape[0] // QBLOCK):
        row = start - reach + i * QBLOCK
        inside = jnp.logical_and(row >= 0, row < 2 * length)
        at = jnp.where(inside, row, 0) // QBLOCK
        seq, block, piece = at // 8, (at // 2) & 3, at & 1
        here = jnp.where((block >> 1) == across, 0, 1)
        rows = pl.ds(pl.multiple_of(piece * QBLOCK, QBLOCK), QBLOCK)
        mine, other = x_mine[here, seq, rows], x_other[here, seq, rows]
        found = jnp.where((block & 1) == core, mine, other)
        x_ref[i * QBLOCK : (i + 1) * QBLOCK] = jnp.where(inside, found, jnp.zeros_like(found))
    count = q_ref.shape[0]
    scaled = contract_last(x_ref[reach : reach + count], wt[0]) + bias_ref[0:1]
    q_ref[...] = (scaled * (1.0 / math.sqrt(HEAD_DIM))).astype(jnp.bfloat16)
    chunk = x_ref.shape[0] // 4

    @pl.loop(0, 4)
    def _(step):
        rows = pl.ds(pl.multiple_of(step * chunk, 32), chunk)
        k_ref[rows] = contract_last(x_ref[rows], wt[1]).astype(jnp.bfloat16)
        v_ref[rows] = (contract_last(x_ref[rows], wt[2]) + bias_ref[1:2]).astype(jnp.bfloat16)


def project(place, w_mine, w_other, x_mine, x_other, biases, count, window):
    width = x_mine.shape[-1]
    return pl.pallas_call(
        project_kernel,
        in_specs=[pl.BlockSpec(memory_space=pltpu.SMEM)]
        + [pl.BlockSpec(memory_space=pltpu.VMEM)] * 5,
        out_specs=[pl.BlockSpec(memory_space=pltpu.VMEM)] * 5,
        out_shape=[
            jax.ShapeDtypeStruct((count, width), jnp.bfloat16),
            jax.ShapeDtypeStruct((window, width), jnp.bfloat16),
            jax.ShapeDtypeStruct((window, width), jnp.bfloat16),
            jax.ShapeDtypeStruct((window, width), jnp.bfloat16),
            jax.ShapeDtypeStruct((3, width, width), jnp.bfloat16),
        ],
        compiler_params=pltpu.CompilerParams(vmem_limit_bytes=24 << 20),
        cost_estimate=pl.CostEstimate(
            flops=4 * window * width * width, bytes_accessed=16 << 20, transcendentals=0
        ),
        name="project",
    )(place, w_mine, w_other, x_mine, x_other, biases)


def norm_pieces(resid):
    center = resid - jnp.mean(resid, axis=-1, keepdims=True)
    inv_std = lax.rsqrt(jnp.mean(center * center, axis=-1, keepdims=True) + eps_norm)
    return center * inv_std, inv_std


def norm_pull(grad_out, normed, inv_std, gain):
    grad_normed = grad_out * gain
    return inv_std * (
        grad_normed
        - jnp.mean(grad_normed, axis=-1, keepdims=True)
        - normed * jnp.mean(grad_normed * normed, axis=-1, keepdims=True)
    )


def row_sum(rows):
    return jnp.sum(rows, axis=0, keepdims=True)


def attend_out_kernel(
    place_ref, o_ref, x_ref, w_mine, w_other, vec_ref, hb_ref, n_ref, i_ref, wo_ref
):
    core, shard, tp = (place_ref[i] for i in range(3))
    part, depth = w_mine.shape[2:]

    @pl.when(pl.program_id(0) == 0)
    def _():
        for c, source in enumerate((w_mine, w_other)):
            for y in (0, 1):
                cols = half_cols(shard + y - 2 * shard * y, depth)
                for k in range(4):
                    row = ((tp + 4 - k) & 3) * 2 + core + c - 2 * core * c
                    rows = pl.ds(pl.multiple_of(row * part, part), part)
                    wo_ref[rows, cols] = source[k, y]

    resid = x_ref[...].astype(jnp.float32) + dot32(o_ref[...], wo_ref[...]) + vec_ref[0:1]
    normed, inv_std = norm_pieces(resid)
    hb_ref[...] = (normed * vec_ref[1:2] + vec_ref[2:3]).astype(jnp.bfloat16)
    n_ref[...] = normed.astype(jnp.bfloat16)
    i_ref[...] = jnp.broadcast_to(inv_std, i_ref.shape)


def row_blocks(width):
    return pl.BlockSpec((QBLOCK, width), lambda i, *_: (i, 0))


def on_rows(kernel, count, in_specs, out_specs, out_shape, name, scalars=0):
    return pl.pallas_call(
        kernel,
        grid_spec=pltpu.PrefetchScalarGridSpec(
            num_scalar_prefetch=scalars,
            grid=(count // QBLOCK,),
            in_specs=in_specs,
            out_specs=out_specs,
        ),
        out_shape=out_shape,
        compiler_params=pltpu.CompilerParams(vmem_limit_bytes=12 << 20),
        cost_estimate=pl.CostEstimate(flops=1 << 28, bytes_accessed=6 << 20, transcendentals=0),
        name=name,
    )


def attend_out(place, mixed, window_rows, reach, w_mine, w_other, vectors):
    count, width = mixed.shape
    rows = row_blocks(width)
    low = jax.ShapeDtypeStruct((count, width), jnp.bfloat16)
    return on_rows(
        attend_out_kernel,
        count,
        [
            rows,
            pl.BlockSpec((QBLOCK, width), lambda i, *_: (i + reach // QBLOCK, 0)),
            whole(w_mine.shape),
            whole(w_other.shape),
            whole(vectors.shape),
        ],
        [rows, rows, row_blocks(QBLOCK), whole((width, width))],
        [
            low,
            low,
            jax.ShapeDtypeStruct((count, QBLOCK), jnp.float32),
            jax.ShapeDtypeStruct((width, width), jnp.bfloat16),
        ],
        "attend_out",
        1,
    )(place, mixed, window_rows, w_mine, w_other, vectors)


def norm_sums(sums_ref, rows):
    sums = jnp.concatenate([row_sum(row) for row in rows], axis=0)
    add_or_set(pl.program_id(0) == 0, sums_ref, slice(None), sums)


def cot_source(i, place_ref):
    core, tp, across = place_ref[0], place_ref[2], place_ref[3]
    odd = (across + tp) & 1
    block = 3 * core + i - 2 * odd
    block = jnp.where(block < 0, block + 6, block)
    far = block >> 1 == 2
    held = jnp.where(far, core == odd, core == (block >> 1))
    return jnp.where(far, 1, 0), block & 1, jnp.where(held, 1, 0)


def ffn_norm_kernel(
    place_ref, h_ref, own_ref, got_ref, g_ref, g_other_ref, vec_ref, y_ref, dz_ref, sums_ref
):
    resid = h_ref[...].astype(jnp.float32) + own_ref[...].astype(jnp.float32)
    resid += got_ref[...].astype(jnp.float32) + vec_ref[0:1]
    normed, inv_std = norm_pieces(resid)
    y_ref[...] = (normed * vec_ref[1:2] + vec_ref[2:3]).astype(jnp.bfloat16)
    held = cot_source(pl.program_id(0), place_ref)[2]
    grad_out = jnp.where(held == 1, g_ref[0], g_other_ref[0]).astype(jnp.float32)
    low = norm_pull(grad_out, normed, inv_std, vec_ref[1:2]).astype(jnp.bfloat16)
    dz_ref[...] = low
    norm_sums(sums_ref, (low.astype(jnp.float32), grad_out * normed, grad_out))


def ffn_norm(place, hidden, own, got, cots, other_cots, vectors):
    count, width = hidden.shape
    rows = row_blocks(width)
    cot = pl.BlockSpec((1, QBLOCK, width), lambda i, at: (*cot_source(i, at)[:2], 0))
    low = jax.ShapeDtypeStruct((count, width), jnp.bfloat16)
    return on_rows(
        ffn_norm_kernel,
        count,
        [rows, rows, rows, cot, cot, whole(vectors.shape)],
        [rows, rows, whole((3, width))],
        [low, low, jax.ShapeDtypeStruct((3, width), jnp.float32)],
        "ffn_norm",
        1,
    )(place, hidden, own, got, cots, other_cots, vectors)


def attend_norm_kernel(
    dz_ref, own_ref, got_ref, n_ref, i_ref, vec_ref, wo_ref, out_ref, da_ref, do_ref, sums_ref
):
    grad_out = dz_ref[...].astype(jnp.float32) + own_ref[...].astype(jnp.float32)
    grad_out += got_ref[...].astype(jnp.float32)
    normed = n_ref[...].astype(jnp.float32)
    grad = norm_pull(grad_out, normed, i_ref[:, :1], vec_ref[1:2])
    low = grad.astype(jnp.bfloat16)
    out_ref[...] = grad
    da_ref[...] = low
    do_ref[...] = contract_last(low, wo_ref[...]).astype(jnp.bfloat16)
    norm_sums(sums_ref, (low.astype(jnp.float32), grad_out * normed, grad_out))


def attend_norm(grads, own, got, normed, inv_std, vectors, weights):
    count, width = grads.shape
    rows = row_blocks(width)
    low = jax.ShapeDtypeStruct((count, width), jnp.bfloat16)
    return on_rows(
        attend_norm_kernel,
        count,
        [rows, rows, rows, rows, row_blocks(QBLOCK), whole(vectors.shape), whole(weights.shape)],
        [rows, rows, rows, whole((3, width))],
        [
            jax.ShapeDtypeStruct((count, width), jnp.float32),
            low,
            low,
            jax.ShapeDtypeStruct((3, width), jnp.float32),
        ],
        "attend_norm",
    )(grads, own, got, normed, inv_std, vectors, weights)


def attn_grads_kernel(
    place_ref, dq_ref, dk_ref, dv_ref, o_ref, da_ref, w_ref, attn_ref, ffn_ref, up_ref, *parts
):
    core, shard, across = place_ref[0], place_ref[1], place_ref[3]
    grad_ref = parts[2]
    depth = w_ref.shape[1] // 2
    part = depth // 4
    count = dq_ref.shape[0]
    reach = (w_ref.shape[0] - count) // 2
    sides = (
        (dq_ref, w_ref.at[reach : reach + count]),
        (dk_ref, w_ref),
        (dv_ref, w_ref),
        (o_ref, da_ref),
    )
    for m, (left, right) in enumerate(sides):
        grad_ref[...] = contract_rows(left[...], right[...]).astype(jnp.bfloat16)
        group = across if m < 2 else 1 - across
        rows = slice((m % 2) * part, (m % 2 + 1) * part)
        for z in (0, 1):
            for c in (0, 1):
                at = pl.ds(pl.multiple_of((2 * z + c + core - 2 * c * core) * part, part), part)
                parts[c][shard, group, z, rows] = grad_ref[at, :depth]
                parts[c][1 - shard, group, z, rows] = grad_ref[at, depth:]
    query_sum = row_sum(dq_ref[...].astype(jnp.float32))
    value_sum = row_sum(dv_ref[...].astype(jnp.float32))
    shared = []
    for source in (attn_ref, ffn_ref):
        for r in range(3):
            shared += [source[r : r + 1, :depth], source[r : r + 1, depth:]]
    half = depth // 2
    for z in (0, 1):
        own = slice(z * half, (z + 1) * half)
        heads = jnp.concatenate([query_sum[:, own], value_sum[:, own]], axis=1)
        none = jnp.zeros_like(heads)
        rows = [heads] + shared
        for c in (0, 1):
            last = [none if c else up_ref[z], none, none]
            for x, group in ((across, rows[:8]), (1 - across, rows[8:] + last)):
                block = jnp.concatenate(group, axis=0).astype(jnp.bfloat16)
                for y in (0, 1):
                    parts[c][y, x, z, 2 * part :] = block


def attn_grads(
    place, grad_queries, grad_keys, grad_values, mixed, grad_attn, near, attn_sums, ffn_sums, up_sums
):
    count, width = mixed.shape
    window = near.shape[0]
    depth = width // 2
    high = depth // 2 + 8
    cols = pl.BlockSpec((count, depth), lambda i, _: (0, i))
    near_cols = pl.BlockSpec((window, depth), lambda i, _: (0, i))
    return pl.pallas_call(
        attn_grads_kernel,
        grid_spec=pltpu.PrefetchScalarGridSpec(
            num_scalar_prefetch=1,
            grid=(2,),
            in_specs=[
                cols,
                near_cols,
                near_cols,
                cols,
                whole((count, width)),
                whole((window, width)),
                whole((3, width)),
                whole((3, width)),
                pl.BlockSpec((2, 1, depth), lambda i, _: (i, 0, 0)),
            ],
            out_specs=[pl.BlockSpec((2, 2, 2, high, depth), lambda i, _: (0, 0, i, 0, 0))] * 2,
            scratch_shapes=[pltpu.VMEM((depth, width), jnp.bfloat16)],
        ),
        out_shape=[jax.ShapeDtypeStruct((2, 2, 4, high, depth), jnp.bfloat16)] * 2,
        compiler_params=pltpu.CompilerParams(vmem_limit_bytes=24 << 20),
        cost_estimate=pl.CostEstimate(
            flops=4 * (window + count) * width * width, bytes_accessed=16 << 20, transcendentals=0
        ),
        name="attn_grads",
    )(
        place,
        grad_queries,
        grad_keys,
        grad_values,
        mixed,
        grad_attn,
        near,
        attn_sums,
        ffn_sums,
        up_sums,
    )


def span_grads_kernel(
    place_ref,
    dq_ref,
    dk_ref,
    dv_ref,
    w_ref,
    base_ref,
    own_ref,
    first_ref,
    second_ref,
    give_ref,
    near,
):
    core = place_ref[0]
    count, reach = own_ref.shape[0], give_ref.shape[0]
    far = count + reach
    size = near.shape[0] // 4

    @pl.loop(0, 4)
    def _(step):
        rows = pl.ds(pl.multiple_of(step * size, 32), size)
        near[rows] = dot32(dk_ref[rows], w_ref[1]) + dot32(dv_ref[rows], w_ref[2])

    def rows_at(start, size):
        return near[pl.ds(pl.multiple_of(start, QBLOCK), size)].astype(jnp.bfloat16)

    give_ref[...] = rows_at((1 - core) * far, reach)
    first_ref[...] = rows_at(jnp.where(core == 0, reach - count, far), count)
    second_ref[...] = rows_at(jnp.where(core == 0, 0, far + count), reach - count)
    own_ref[...] = base_ref[...] + dot32(dq_ref[...], w_ref[0]) + near[reach:far]


def span_grads(place, grad_queries, grad_keys, grad_values, weights, base):
    count, width = base.shape
    reach = (grad_keys.shape[0] - count) // 2
    vmem = pl.BlockSpec(memory_space=pltpu.VMEM)
    return pl.pallas_call(
        span_grads_kernel,
        in_specs=[pl.BlockSpec(memory_space=pltpu.SMEM)] + [vmem] * 5,
        out_specs=[vmem] * 4,
        out_shape=[
            jax.ShapeDtypeStruct((count, width), jnp.float32),
            jax.ShapeDtypeStruct((count, width), jnp.bfloat16),
            jax.ShapeDtypeStruct((reach - count, width), jnp.bfloat16),
            jax.ShapeDtypeStruct((reach, width), jnp.bfloat16),
        ],
        scratch_shapes=[pltpu.VMEM(grad_keys.shape, jnp.float32)],
        compiler_params=pltpu.CompilerParams(vmem_limit_bytes=16 << 20),
        cost_estimate=pl.CostEstimate(
            flops=4 * (count + 2 * reach) * width * width,
            bytes_accessed=12 << 20,
            transcendentals=0,
        ),
        name="span_grads",
    )(place, grad_queries, grad_keys, grad_values, weights, base)


def assemble_kernel(place_ref, one, two, three, four, halves, out_ref):
    core, tp, across = place_ref[0], place_ref[2], place_ref[3]
    block = out_ref.shape[1]
    part = block // 2
    mine = pl.ds(pl.multiple_of(core * part, part), part)
    other = pl.ds(pl.multiple_of((1 - core) * part, part), part)
    for k, source in enumerate((one, two, three, four)):
        z = (tp + 4 - k) & 3
        group, side = 3 * (z >> 1), z & 1
        out_ref[group + jnp.where(side == 1, 1, 2 * across)] = source[:block].astype(out_ref.dtype)
        foreign = group + 2 - 2 * across

        @pl.when(((side + across + core) & 1) == 1)
        def _():
            out_ref[foreign, mine] = source[block:].astype(out_ref.dtype)
            out_ref[foreign, other] = halves[k].astype(out_ref.dtype)


def assemble_late_kernel(place_ref, one, two, three, four, middle, foreign, out_ref):
    core, tp, across = place_ref[0], place_ref[2], place_ref[3]
    block = out_ref.shape[1]
    part = block // 2
    for k, source in enumerate((one, two, three, four)):
        z = (tp + 4 - k) & 3
        group, side = 3 * (z >> 1), z & 1
        at = group + jnp.where(side == 1, 1, 2 * across)
        odd = (across + side) & 1

        @pl.when(jnp.logical_and(odd == 0, core == 0))
        def _():
            out_ref[at] = source[:block]

        @pl.when(jnp.logical_and(odd == 0, core == 1))
        def _():
            out_ref[at, :part] = middle[k]
            out_ref[at, part:] = source[:part]

        @pl.when(jnp.logical_and(odd == 1, core == 0))
        def _():
            out_ref[at, :part] = source[block:]
            out_ref[at, part:] = middle[k]

        @pl.when(jnp.logical_and(odd == 1, core == 1))
        def _():
            out_ref[at] = source[part:]

        @pl.when(((side + across + core) & 1) == 1)
        def _():
            out_ref[group + 2 - 2 * across] = foreign[k // 2]


def assemble(kernel, place, pieces, others, seqs, dtype):
    rows, width = pieces[0].shape
    vmem = pl.BlockSpec(memory_space=pltpu.VMEM)
    return pl.pallas_call(
        kernel,
        in_specs=[pl.BlockSpec(memory_space=pltpu.SMEM)] + [vmem] * (4 + len(others)),
        out_specs=vmem,
        out_shape=jax.ShapeDtypeStruct((seqs, rows * 2 // 3, width), dtype),
        compiler_params=pltpu.CompilerParams(vmem_limit_bytes=10 << 20),
        cost_estimate=pl.CostEstimate(flops=1 << 20, bytes_accessed=8 << 20, transcendentals=0),
        name="assemble",
    )(place, *pieces, *others)


def finish_ffn_kernel(place_ref, mine, across_got, core_got, both_got, up_ref, down_ref):
    core, across = place_ref[0], place_ref[3]
    depth = mine.shape[1]
    part = depth // 2
    for c, x, source in (
        (core, across, mine),
        (core, 1 - across, across_got),
        (1 - core, across, core_got),
        (1 - core, 1 - across, both_got),
    ):
        rows = pl.ds(pl.multiple_of(x * part, part), part)
        up_ref[rows, half_cols(c, depth)] = source[:part].astype(jnp.float32)
        rows = pl.ds(pl.multiple_of(c * depth + x * part, part), part)
        down_ref[rows] = source[part:].astype(jnp.float32)


def finish_attn_kernel(
    place_ref, mine, across_got, core_got, both_got, q_ref, k_ref, v_ref, o_ref, *refs
):
    *vectors, sums_ref = refs
    core, across = place_ref[0], place_ref[3]
    part = q_ref.shape[0] // 2
    for c, x, source in (
        (core, across, mine),
        (core, 1 - across, across_got),
        (1 - core, across, core_got),
        (1 - core, 1 - across, both_got),
    ):
        rows = pl.ds(pl.multiple_of(c * part, part), part)
        one = source[:part].astype(jnp.float32)
        two = source[part : 2 * part].astype(jnp.float32)
        sums_ref[c, x] = source[2 * part :].astype(jnp.float32)

        @pl.when(x == 0)
        def _():
            q_ref[rows], k_ref[rows] = one, two

        @pl.when(x == 1)
        def _():
            v_ref[rows], o_ref[rows] = one, two

    def flat(*rows):
        return jnp.concatenate(rows, axis=1).reshape(-1)

    sums = sums_ref[core].reshape(16, 4 * part)
    for r, to in enumerate(vectors[:6]):
        to[...] = flat(sums[2 * r + 1 : 2 * r + 2], sums[2 * r + 2 : 2 * r + 3])
    vectors[6][...] = flat(sums_ref[0, 1, 5:6], sums_ref[1, 1, 5:6])
    vectors[7][...] = sums[0:1, : 2 * part].reshape(-1)
    vectors[8][...] = sums[0:1, 2 * part :].reshape(-1)


def finish(kernel, place, pieces, shapes, name, scratch=()):
    vmem = pl.BlockSpec(memory_space=pltpu.VMEM)
    return pl.pallas_call(
        kernel,
        in_specs=[pl.BlockSpec(memory_space=pltpu.SMEM)] + [vmem] * 4,
        out_specs=[vmem] * len(shapes),
        out_shape=[jax.ShapeDtypeStruct(shape, jnp.float32) for shape in shapes],
        scratch_shapes=scratch,
        compiler_params=pltpu.CompilerParams(vmem_limit_bytes=8 << 20),
        cost_estimate=pl.CostEstimate(flops=1 << 20, bytes_accessed=4 << 20, transcendentals=0),
        name=name,
    )(place, *pieces)


def ctx_swap(array, bit):
    return lax.ppermute(array, "ctx", [(i, i ^ bit) for i in range(4)])


def core_swap(array):
    return ctx_swap(array, 1)


def tie(*arrays):
    return lax.optimization_barrier(arrays)


def across_swap(array):
    return ctx_swap(array, 2)


def in_order(flag, mine, other):
    return jnp.where(flag == 0, mine, other), jnp.where(flag == 0, other, mine)


def at(across, core, tp):
    return (2 * across + core) * 4 + tp


def across_pairs():
    pairs = []
    for tp in range(4):
        for across in (0, 1):
            core = across ^ (tp & 1)
            pairs.append((at(1 - across, core, tp), at(across, core, tp)))
    return pairs


def tp_shifts(array, cuts=(slice(None), slice(None), slice(None))):
    return [
        lax.ppermute(array[cut], "tp", [(i, (i + shift) % 4) for i in range(4)])
        for shift, cut in zip((1, 2, 3), cuts)
        if cut is not None
    ]


def by_tp(array, shifted):
    one, two, three = shifted
    line = jnp.stack([three, two, one, array, three, two, one])
    return lax.dynamic_slice_in_dim(line, 3 - lax.axis_index("tp"), 4, 0)


def shard_swap(array):
    return lax.ppermute(array, "shard", [(0, 1), (1, 0)])


def low_sum(left, right):
    return (left.astype(jnp.float32) + right.astype(jnp.float32)).astype(jnp.bfloat16)


def scatter_tp_start(parts):
    tp = lax.axis_index("tp")
    moved = [lax.dynamic_index_in_dim(parts, tp, 0, keepdims=False)]
    for shift in (1, 2, 3):
        sent = lax.dynamic_index_in_dim(parts, (tp + shift) & 3, 0, keepdims=False)
        moved.append(lax.ppermute(sent, "tp", [(i, (i + shift) % 4) for i in range(4)]))
    return moved


def scatter_tp_end(moved):
    return sum(part.astype(jnp.float32) for part in moved).astype(jnp.bfloat16)


def chain_pairs(turn):
    pairs = []
    for group in (0, 2):
        path = [(0, group), (0, group + 1), (1, group + 1), (1, group)]
        for (across, tp), (next_across, next_tp) in zip(path[:-1], path[1:]):
            pairs.append((at(across, 1, tp), at(next_across, 1 ^ turn, next_tp)))
            pairs.append((at(next_across, 0, next_tp), at(across, turn, tp)))
    return pairs


def block_pairs(core):
    pairs = []
    for tp in range(4):
        for across in (0, 1):
            source = 1 ^ across ^ (tp & 1)
            pairs.append((at(across, source, tp), at(1 - across, core, tp)))
    return pairs


def span_shards(
    layer_input,
    segment_ids,
    query_proj,
    query_bias,
    key_proj,
    value_proj,
    value_bias,
    out_proj,
    out_bias,
    attn_gain,
    attn_shift,
    up_proj,
    up_bias,
    down_proj,
    down_bias,
    ffn_gain,
    ffn_shift,
    out_cotangent,
):
    seqs, block, width = layer_input.shape
    length = segment_ids.shape[1]
    reach = length // 2
    count = seqs * block // 4
    window = count + 2 * reach
    bf16, f32 = jnp.bfloat16, jnp.float32
    ctx, tp = lax.axis_index("ctx"), lax.axis_index("tp")
    shard = lax.axis_index("shard")
    core, across, side = ctx & 1, ctx >> 1, tp & 1
    place = 2 * across + (side ^ across)
    odd = across ^ side

    heads = query_proj.shape[1]
    half = heads // 2
    depth = query_proj.shape[0]
    cut = up_proj.shape[1] // 2
    own_in = lax.dynamic_slice_in_dim(
        jnp.stack([query_proj.T, key_proj.T, value_proj.T]), core * half, half, 1
    ).reshape(3 * half, depth)
    own_biases = jnp.stack(
        [
            jnp.concatenate([query_bias, value_bias]),
            lax.dynamic_slice_in_dim(up_bias, core * cut, cut, 0),
        ]
    )
    own_in = jnp.concatenate([own_in, own_biases, jnp.zeros((14, depth), bf16)], axis=0)
    out_half = out_proj.shape[0] // 2
    own_rest = jnp.concatenate(
        [
            lax.dynamic_slice_in_dim(up_proj, core * cut, cut, 1),
            lax.dynamic_slice_in_dim(down_proj, core * cut, cut, 0),
            lax.dynamic_slice_in_dim(out_proj, core * out_half, out_half, 0),
        ],
        axis=0,
    )
    first_seq = 3 * (tp >> 1)
    mine = lax.dynamic_slice_in_dim(layer_input, first_seq + across, 2, 0)
    theirs = across_swap(lax.dynamic_slice_in_dim(layer_input, first_seq + 1 - across, 2, 0))
    in_shifted = tp_shifts(own_in)
    far_rest = shard_swap(own_rest)
    *in_shifted, theirs, far_rest = tie(*in_shifted, theirs, far_rest)
    in_near = jnp.stack([own_in] + in_shifted)
    (rest_one,) = tp_shifts(tie(own_rest, in_near)[0], (slice(None), None, None))
    own_pair = jnp.stack([own_rest[: 2 * cut], far_rest[: 2 * cut]])
    near_cot = lax.dynamic_index_in_dim(
        out_cotangent, first_seq + odd + across, 0, keepdims=False
    )
    far_cot = lax.ppermute(
        lax.dynamic_index_in_dim(
            tie(out_cotangent, theirs)[0], first_seq + 2 - 2 * across, 0, keepdims=False
        ),
        ("ctx", "tp"),
        across_pairs(),
    )
    in_far, rest_one, own_pair, far_cot = tie(shard_swap(in_near), rest_one, own_pair, far_cot)
    in_mine = jnp.stack([in_near, in_far])
    (rest_three,) = tp_shifts(tie(own_rest, in_near)[0], (None, None, slice(None)))
    in_other, rest_three = tie(core_swap(in_mine), rest_three)
    own_late = tie(own_rest, rest_three)[0]
    (some_two,) = tp_shifts(own_late, (None, slice(cut, None), None))
    (up_two,) = tp_shifts(own_late, (None, slice(cut), None))
    far_three = shard_swap(rest_three)
    bias_rows = in_mine[0, :, 3 * half]
    in_biases = by_tp(bias_rows[0], [bias_rows[1], bias_rows[2], bias_rows[3]]).astype(f32)
    in_biases = jnp.stack([in_biases[:, :heads].reshape(-1), in_biases[:, heads:].reshape(-1)])
    up_bias_here = in_mine[0, :, 3 * half + 1].reshape(4, 1, cut).astype(f32)

    pair = jnp.stack([mine, theirs])
    pair_other = core_swap(pair)
    start = 2 * count * place + count * core - length * across
    ids = lax.dynamic_slice_in_dim(segment_ids, first_seq + across, 2, 0)
    ids = (ids + jnp.array([[0], [1 << 16]], jnp.int32)).reshape(-1)
    no_doc = jnp.full((reach,), -1, jnp.int32)
    window_docs = lax.dynamic_slice_in_dim(
        jnp.concatenate([no_doc, ids, no_doc]), start, window, 0
    )
    key_docs = window_docs[None]
    query_docs = jnp.broadcast_to(window_docs[reach : reach + count, None], (count, QBLOCK))

    place = jnp.stack([core, shard, tp, across, start])
    far_one = shard_swap(rest_one)
    queries, keys, values, in_window, weights_t = project(
        place, in_mine, in_other, pair, pair_other, in_biases, count, window
    )
    attention = queries, keys, values, key_docs, query_docs, reach
    plan = key_plan(window_docs, reach, count)
    mixed, logs = attend(*attention, 0)
    mixed, far_one, far_three, some_two = tie(mixed, far_one, far_three, some_two)
    far_some_two = shard_swap(some_two)
    mixed, logs = attend(*attention, 1, (plan, mixed, logs))
    mixed, far_some_two, up_two = tie(mixed, far_some_two, up_two)
    far_up_two = shard_swap(up_two)
    out_mine = jnp.stack(
        [
            jnp.stack([one[-out_half:], two[-out_half:]])
            for one, two in (
                (own_rest, far_rest),
                (rest_one, far_one),
                (some_two, far_some_two),
                (rest_three, far_three),
            )
        ]
    )
    attn_vectors = jnp.stack([out_bias, attn_gain, attn_shift]).astype(f32)
    hidden_low, normed_one, inv_one, full_out = attend_out(
        place, mixed, in_window, reach, out_mine, core_swap(out_mine), attn_vectors
    )
    hidden_other = core_swap(hidden_low)
    hidden_both = hidden_low, hidden_other
    ffn_weights = jnp.stack(
        [
            own_pair,
            jnp.stack([rest_one[: 2 * cut], far_one[: 2 * cut]]),
            jnp.stack([rest_three[: 2 * cut], far_three[: 2 * cut]]),
            own_pair,
        ]
    )
    ffn_bias = jnp.stack([up_bias_here[k] for k in (0, 1, 3, 2)])
    acts, slope, ffn_sum = ffn(place, *hidden_both, ffn_weights, ffn_bias)
    ffn_sum, far_up_two = tie(ffn_sum, far_up_two)
    rest = ffn_weights.at[3].set(
        jnp.stack(
            [
                jnp.concatenate([up_two, some_two[:cut]], axis=0),
                jnp.concatenate([far_up_two, far_some_two[:cut]], axis=0),
            ]
        )
    )
    acts, slope, ffn_own, ffn_other = ffn(
        place, *hidden_both, rest, ffn_bias, (ffn_sum, acts, slope)
    )

    half_block = block // 2

    def deliver_start(rows):
        far_rows = jnp.where(odd == 0, rows[-block:], rows[:block])
        return (
            core_swap(jnp.where(odd == 0, rows[block:], rows[:half_block])),
            lax.ppermute(far_rows[:half_block], ("ctx", "tp"), block_pairs(0)),
            lax.ppermute(far_rows[half_block:], ("ctx", "tp"), block_pairs(1)),
        )

    def deliver_pack(rows, middle, low, high):
        where_kept = [
            rows[:block],
            jnp.concatenate([middle, rows[:half_block]], axis=0),
            jnp.concatenate([rows[block:], middle], axis=0),
            rows[half_block:],
        ]
        kept = jnp.where(
            odd == 0,
            jnp.where(core == 0, where_kept[0], where_kept[1]),
            jnp.where(core == 0, where_kept[2], where_kept[3]),
        )
        return jnp.concatenate([kept, low + high], axis=0)

    cot_pair = tie(jnp.stack([near_cot, far_cot]), queries)[0]
    cot_swapped = core_swap(cot_pair)

    ffn_vectors = jnp.stack([down_bias, ffn_gain, ffn_shift]).astype(f32)
    output_rows, grad_ffn, ffn_sums = ffn_norm(
        place, hidden_low, ffn_own, core_swap(ffn_other), cot_pair, cot_swapped, ffn_vectors
    )
    grad_other = core_swap(grad_ffn)
    out_pieces = [output_rows] + tp_shifts(output_rows)
    back_own, back_other, up_keep, up_give, down_keep, down_give, up_sums = ffn_back(
        place, grad_ffn, grad_other, *hidden_both, acts, slope, rest
    )
    back_own, out_pieces[1] = tie(back_own, out_pieces[1])
    grad_one, grad_attn, grad_mixed, attn_sums = attend_norm(
        grad_ffn, back_own, core_swap(back_other), normed_one, inv_one, attn_vectors, full_out
    )
    up_got = across_swap(up_give)
    down_got = shard_swap(down_give)
    grad_scaled, grad_keys, grad_values = attend_back(plan, *attention, grad_mixed, logs)
    own_sum, first, second, give = span_grads(
        place, grad_scaled, grad_keys, grad_values, weights_t, grad_one
    )
    first, up_got, down_got, out_pieces[2] = tie(first, up_got, down_got, out_pieces[2])
    up_parts = [low_sum(up_keep[i], up_got[i]) for i in (0, 1)]
    down_parts = [low_sum(down_keep[i], down_got[i]) for i in (0, 1)]
    up_got, down_got = shard_swap(up_parts[1]), across_swap(down_parts[1])
    got = core_swap(give)
    shared = reach - count
    to_own = lax.dynamic_slice_in_dim(got, (1 - core) * shared, count, 0)
    to_next = lax.dynamic_slice_in_dim(got, core * count, shared, 0)
    no_rows = jnp.zeros((count - shared, width), bf16)
    first = low_sum(
        first,
        jnp.where(
            core == 0,
            jnp.concatenate([no_rows, to_next], axis=0),
            jnp.concatenate([to_next, no_rows], axis=0),
        ),
    )
    first_now, up_got, down_got, out_pieces[3] = tie(first, up_got, down_got, out_pieces[3])
    ffn_parts = jnp.concatenate(
        [low_sum(up_parts[0], up_got), low_sum(down_parts[0], down_got)], axis=1
    )
    ffn_near = scatter_tp_start(ffn_parts)
    first_got = lax.ppermute(first, ("ctx", "tp"), chain_pairs(1))
    second_got = lax.ppermute(second, ("ctx", "tp"), chain_pairs(0))
    grad_keys, first_now = tie(grad_keys, first)
    attn_parts = attn_grads(
        place,
        grad_scaled,
        grad_keys,
        grad_values,
        mixed,
        grad_attn,
        in_window,
        attn_sums,
        ffn_sums,
        up_sums,
    )
    first_got, second_got, attn_keep, attn_give, ffn_near[1], ffn_near[3] = tie(
        first_got, second_got, *attn_parts, ffn_near[1], ffn_near[3]
    )
    attn_core = core_swap(attn_give)
    own_sum += to_own.astype(f32) + first_got.astype(f32)
    own_sum += jnp.where(
        core == 0,
        jnp.concatenate([no_rows, second_got], axis=0),
        jnp.concatenate([second_got, no_rows], axis=0),
    ).astype(f32)
    own_low = own_sum.astype(bf16)
    in_moves = deliver_start(own_low)
    *in_moves, attn_core, ffn_near[2] = tie(*in_moves, attn_core, ffn_near[2])
    in_packed = deliver_pack(own_low, *in_moves)
    in_pieces = [in_packed] + tp_shifts(in_packed)
    attn_parts = [low_sum(attn_keep[i], attn_core[i]) for i in (0, 1)]
    attn_got = shard_swap(attn_parts[1])
    parity = (tp + 1 + across + core) & 1
    out_sent = [
        jnp.where(
            core == 0,
            jnp.where(parity == 0, even[:block], odd_one[:block]),
            jnp.where(parity == 0, even[-block:], odd_one[-block:]),
        )
        for even, odd_one in (out_pieces[:2], out_pieces[2:])
    ]
    out_foreign = lax.ppermute(jnp.stack(out_sent), "ctx", [(i, 3 - i) for i in range(4)])
    out_middle = core_swap(
        jnp.stack(
            [
                jnp.where(((across + tp + k) & 1) == 0, piece[block:], piece[:half_block])
                for k, piece in enumerate(out_pieces)
            ]
        )
    )
    attn_got, in_pieces[1], in_pieces[3] = tie(attn_got, in_pieces[1], in_pieces[3])
    attn_mid = [low_sum(attn_parts[0][i], attn_got[i]) for i in (0, 1)]
    attn_got = across_swap(attn_mid[1])
    ffn_low = scatter_tp_end(ffn_near)
    ffn_got = across_swap(ffn_low)
    attn_got, out_foreign, out_middle = tie(attn_got, out_foreign, out_middle)
    attn_near = scatter_tp_start(low_sum(attn_mid[0], attn_got))
    layer_output = assemble(
        assemble_late_kernel, place, out_pieces, (out_middle, out_foreign), seqs, bf16
    )
    layer_output, in_pieces[2], attn_near[3], ffn_got = tie(
        layer_output, in_pieces[2], attn_near[3], ffn_got
    )
    in_halves = core_swap(jnp.stack([piece[block:] for piece in in_pieces]))
    input_grad = assemble(assemble_kernel, place, in_pieces, (in_halves,), seqs, f32)
    up_grad, down_grad = finish(
        finish_ffn_kernel,
        place,
        (ffn_low, ffn_got, core_swap(ffn_low), core_swap(ffn_got)),
        ((cut, 2 * cut), (2 * cut, cut)),
        "finish_ffn",
    )
    attn_low = scatter_tp_end(attn_near)
    attn_got, input_grad = tie(across_swap(attn_low), input_grad)
    finished = finish(
        finish_attn_kernel,
        place,
        (attn_low, attn_got, core_swap(attn_low), core_swap(attn_got)),
        ((heads, depth),) * 4 + ((width,),) * 6 + ((2 * cut,), (heads,), (heads,)),
        "finish_attn",
        [pltpu.VMEM((2, 2, 8, depth), f32)],
    )
    weight_grads, row_sums = finished[:4], finished[4:10]
    up_bias_grad, query_bias_grad, value_bias_grad = finished[10:]
    return (
        layer_output,
        input_grad,
        weight_grads[0].T,
        query_bias_grad,
        weight_grads[1].T,
        weight_grads[2].T,
        value_bias_grad,
        weight_grads[3],
        row_sums[0],
        row_sums[1],
        row_sums[2],
        up_grad,
        up_bias_grad,
        down_grad,
        row_sums[3],
        row_sums[4],
        row_sums[5],
    )


def pick_plan(mesh):
    shape = dict(mesh.shape)

    def plan(layer_input, segment_ids, *others):
        seqs, block, _ = layer_input.shape
        fits = (
            (shape["shard"], shape["ctx"], shape["tp"]) == (2, 4, 4)
            and seqs == 6
            and segment_ids.shape[1] == 4 * block
            and block == 2 * QBLOCK
        )
        chosen = span_shards if fits else general_shards
        return chosen(layer_input, segment_ids, *others)

    return plan


def solution(mesh):
    return jax.shard_map(
        pick_plan(mesh),
        mesh=mesh,
        in_specs=(
            P("shard", "ctx", None),
            P("shard", None),
            P("shard", "tp"),
            P("tp"),
            P("shard", "tp"),
            P("shard", "tp"),
            P("tp"),
            P("tp", "shard"),
            P(),
            P(),
            P(),
            P("shard", "tp"),
            P("tp"),
            P("tp", "shard"),
            P(),
            P(),
            P(),
            P("shard", "ctx", None),
        ),
        out_specs=(
            P("shard", "ctx", None),
            P("shard", "ctx", None),
            P("shard", "tp"),
            P("tp"),
            P("shard", "tp"),
            P("shard", "tp"),
            P("tp"),
            P("tp", "shard"),
            P(),
            P(),
            P(),
            P("shard", "tp"),
            P("tp"),
            P("tp", "shard"),
            P(),
            P(),
            P(),
        ),
        check_vma=False,
    )
```
